32 devices in a mesh: ctx: 8 (over z, x), heads: 4 (over y, core).
Axes of the slice: x: 2, y: 2, z: 4, core: 2. Of those that a mesh axis runs over, the one named last changes fastest.
Arguments:
- tokens: bfloat16 [4096, 1024], P(('ctx', 'heads')), may hold values from -6 to 6
- d_out: bfloat16 [4096, 1024], P(('ctx', 'heads')), may hold values from -6 to 6
- segment_ids: int32 [4096], P(('ctx', 'heads')), may hold values from 0 to 2, as said below
- position_ids: int32 [4096], P(('ctx', 'heads')), may hold values from 0 to 2047, as said below
- w_qkv: bfloat16 [1024, 3072], P('ctx'), may hold values from -0.1875 to 0.1875
- w_attn: bfloat16 [1024, 1024], P('ctx'), may hold values from -1.5 to 1.5
- w_in: bfloat16 [1024, 5248], P('ctx'), may hold values from -0.1875 to 0.1875
- w_out: bfloat16 [2624, 1024], P(None, 'ctx'), may hold values from -0.25 to 0.25
- gain_attn: bfloat16 [1024], P('ctx'), may hold values from 0.25 to 1.75
- gain_mlp: bfloat16 [1024], P('ctx'), may hold values from 0.25 to 1.75
Outputs:
- out: bfloat16 [4096, 1024], P(('ctx', 'heads'))
- grad_input: float32 [4096, 1024], P(('ctx', 'heads'))
- grad_w_qkv: float32 [1024, 3072], P('ctx')
- grad_w_attn: float32 [1024, 1024], P('ctx')
- grad_w_in: float32 [1024, 5248], P('ctx')
- grad_w_out: float32 [2624, 1024], P(None, 'ctx')
- grad_gain_attn: float32 [1024], P('ctx')
- grad_gain_mlp: float32 [1024], P('ctx')
The draws below stay inside these ranges and needn't reach their ends.
Inputs may be any that keep to these rules, and one draw needn't show every extreme that they name: `segment_ids`: starts at 0 and rises by 0 or 1 from one token to the next. The tokens fall into aligned blocks of 2048; one block, at a drawn place, is one sequence of exactly 2048 tokens, every other block holds two sequences split at a drawn point, each of 512 tokens or more. `position_ids`: the number of earlier tokens with the same segment id.
All inputs are finite; a program needn't handle non-finite values.
Results may differ from the reference program's by a relative error of at most 0.02.
Values may be sent and summed in bfloat16 or wider, within the bound.
A program may use at most 192 MiB of HBM per device.

```python
import jax
import jax.numpy as jnp
from jax import lax

D = 1024
H = 16
HD = 64
FF = 2624
TOK_DEV = 128
SEQ_MAX = 2048
TOKENS = 4096
N_HEADS = 4


def segment_layout(key):
    folded = jax.random.fold_in(key, 11)
    cut_key, pick_key = jax.random.split(folded)
    block_total = TOKENS // SEQ_MAX
    cuts = jax.random.randint(cut_key, (block_total,), SEQ_MAX // 4, 3 * SEQ_MAX // 4 + 1).astype(jnp.int32)
    whole_block = jax.random.randint(pick_key, (), 0, block_total).astype(jnp.int32)
    places = jnp.arange(TOKENS, dtype=jnp.int32)
    block_of = (places // SEQ_MAX).astype(jnp.int32)
    within = (places % SEQ_MAX).astype(jnp.int32)
    block_cut = jnp.take(cuts, block_of)
    second = jnp.logical_and(within >= block_cut, block_of != whole_block).astype(jnp.int32)
    later = (block_of > whole_block).astype(jnp.int32)
    ids = 2 * block_of - later + second
    positions = within - second * block_cut
    return (ids.astype(jnp.int32), positions.astype(jnp.int32))


def draw_segment_ids(key, part):
    return segment_layout(key)[0]


def draw_position_ids(key, part):
    return segment_layout(key)[1]


def level_of(rng, shape, shards, least, top_value):
    gain, own = 1.0, jax.random.fold_in(rng, 6)
    for axis_at, parts in shards:
        heights = jnp.exp(jax.random.uniform(jax.random.fold_in(own, axis_at), (parts,), jnp.float32, least / len(shards), top_value / len(shards)))
        gain = gain * jnp.repeat(heights, shape[axis_at] // parts).reshape([-1 if axis == axis_at else 1 for axis in range(len(shape))])
    return gain


def noise(rng, extent, width, limit, cuts=(), held_as=jnp.bfloat16):
    factor_of = level_of(rng, extent, cuts, -0.22, 0.18) if cuts else 1.0
    entries = jax.random.normal(rng, extent, jnp.float32) * width * factor_of
    return jnp.minimum(jnp.maximum(entries, -limit), limit).astype(held_as)


def setup_inputs(seed: int = 0) -> dict:
    key_of = jax.random.split(jax.random.key(seed), 11)
    return {
        "tokens": noise(key_of[0], (TOKENS, D), 1.0, 6.0, ((0, 32),)),
        "d_out": noise(key_of[1], (TOKENS, D), 1.0, 6.0, ((0, 32),)),
        "segment_ids": draw_segment_ids(jax.random.fold_in(key_of[10], 71), 0),
        "position_ids": draw_position_ids(jax.random.fold_in(key_of[10], 71), 0),
        "w_qkv": noise(key_of[4], (D, 3 * D), D ** -0.5, 0.1875, ((0, 8),)),
        "w_attn": noise(key_of[5], (D, D), (D // 64) ** -0.5, 1.5, ((0, 8),)),
        "w_in": noise(key_of[6], (D, 2 * FF), D ** -0.5, 0.1875, ((0, 8),)),
        "w_out": noise(key_of[7], (FF, D), (FF // 4) ** -0.5, 0.25, ((1, 8),)),
        "gain_attn": jnp.clip(1.0 + 0.15 * jax.random.normal(key_of[8], (D,), jnp.float32), 0.25, 1.75).astype(jnp.bfloat16),
        "gain_mlp": jnp.clip(1.0 + 0.15 * jax.random.normal(key_of[9], (D,), jnp.float32), 0.25, 1.75).astype(jnp.bfloat16),
    }


@jax.custom_vjp
def low(v):
    return lax.optimization_barrier(v.astype(jnp.bfloat16)).astype(jnp.float32)

@jax.custom_vjp
def low_back(v):
    return v

def low_keep(v):
    return (low(v), None)

def low_pass(kept, grad):
    return (grad,)

def back_keep(v):
    return (v, None)

def back_low(kept, grad):
    return (low(grad),)
low.defvjp(low_keep, low_pass)
low_back.defvjp(back_keep, back_low)

def layer_norm(values, scale_gain):
    average = lax.optimization_barrier(jnp.mean(values, axis=-1, keepdims=True))
    centred = values - average
    inverse_std = lax.rsqrt(lax.optimization_barrier(jnp.mean(centred * centred, axis=-1, keepdims=True)) + 1e-05)
    return centred * inverse_std * scale_gain

def rope_tables(positions, head_dim):
    half_dim = head_dim // 2
    freqs = jnp.power(160000.0, -(2.0 * jnp.arange(half_dim, dtype=jnp.float32)) / head_dim)
    angles = positions.astype(jnp.float32)[:, None] * freqs[None, :]
    cosine = jnp.concatenate([jnp.cos(angles), jnp.cos(angles)], axis=-1)[:, None, :]
    sine = jnp.concatenate([jnp.sin(angles), jnp.sin(angles)], axis=-1)[:, None, :]
    return (cosine, sine)

def rotate(values, cosine, sine):
    half_dim = values.shape[-1] // 2
    turned = jnp.concatenate([-values[..., half_dim:], values[..., :half_dim]], axis=-1)
    return values * cosine + turned * sine

def attention(queries, keys, values, segments):
    block_rows = TOK_DEV * N_HEADS
    window = min(block_rows + 2 * SEQ_MAX, TOKENS)
    highest = lax.Precision.HIGHEST

    def one_block(block_index):
        start = (block_index * block_rows).astype(jnp.int32)
        key_start = jnp.clip(start - SEQ_MAX, 0, TOKENS - window).astype(jnp.int32)
        query_block = lax.dynamic_slice_in_dim(queries, start, block_rows, 0)
        query_marks = lax.dynamic_slice_in_dim(segments, start, block_rows, 0)
        key_block = lax.dynamic_slice_in_dim(keys, key_start, window, 0)
        value_block = lax.dynamic_slice_in_dim(values, key_start, window, 0)
        key_marks = lax.dynamic_slice_in_dim(segments, key_start, window, 0)
        raw = jnp.einsum('qhd,khd->hqk', query_block, key_block, precision=highest) * 0.125
        allowed = (query_marks[:, None] == key_marks[None, :])[None]
        scores = low_back(jnp.where(allowed, raw, -1e+30))
        shifted = jnp.exp(scores - lax.optimization_barrier(jnp.max(scores, axis=-1, keepdims=True)))
        probability = shifted / lax.optimization_barrier(jnp.sum(shifted, axis=-1, keepdims=True))
        mixed = jnp.einsum('hqk,khd->qhd', low(probability), value_block, precision=highest)
        return mixed.reshape(block_rows, H * HD)
    blocks = lax.map(jax.checkpoint(one_block), jnp.arange(TOKENS // block_rows, dtype=jnp.int32))
    return blocks.reshape(TOKENS, H * HD)

def reference(tokens, d_out, segment_ids, position_ids, w_qkv, w_attn, w_in, w_out, gain_attn, gain_mlp):
    cosine, sine = rope_tables(position_ids, HD)
    highest = lax.Precision.HIGHEST

    def forward(residual_in, mat_qkv, mat_attn, mat_in, mat_out, gain_one, gain_two):
        attn_input = low(layer_norm(residual_in, gain_one))
        projected = low_back(jnp.dot(attn_input, mat_qkv, precision=highest)).reshape(TOKENS, 3, H, HD)
        queries = low_back(low(rotate(projected[:, 0], cosine, sine)))
        keys = low_back(low(rotate(projected[:, 1], cosine, sine)))
        values = low_back(low(projected[:, 2]))
        attended = low_back(low(attention(queries, keys, values, segment_ids)))
        middle = residual_in + low_back(jnp.dot(attended, mat_attn, precision=highest))
        mlp_input = low(layer_norm(middle, gain_two))
        gate_up = low_back(jnp.dot(mlp_input, mat_in, precision=highest))
        mixed = low(jax.nn.gelu(gate_up[:, :FF], approximate=False) * gate_up[:, FF:])
        return middle + low_back(jnp.dot(mixed, mat_out, precision=highest))
    result, pull = jax.vjp(forward, tokens.astype(jnp.float32), w_qkv.astype(jnp.float32), w_attn.astype(jnp.float32), w_in.astype(jnp.float32), w_out.astype(jnp.float32), gain_attn.astype(jnp.float32), gain_mlp.astype(jnp.float32))
    grads = pull(d_out.astype(jnp.float32))
    return (result.astype(jnp.bfloat16), grads[0], grads[1], grads[2], grads[3], grads[4], grads[5], grads[6])
```

```python
import functools

import jax
import jax.numpy as jnp
from jax import lax
from jax.experimental import pallas as pl
from jax.experimental.pallas import tpu as pltpu
from jax.sharding import PartitionSpec as P

H = 16
HD = 64
HALF = HD // 2
FF = 2624
SEQ_MAX = 2048
MASKED = -1e30
MARKS = 16
QM_END = HD + MARKS
K_END = QM_END + HD
KM_END = K_END + MARKS
V_END = KM_END + HD
SLICE = 384
BF = jnp.bfloat16
F32 = jnp.float32
MESH = pl.DeviceIdType.MESH
VMEM = pl.BlockSpec(memory_space=pltpu.VMEM)
ANY = pl.BlockSpec(memory_space=pl.ANY)
DMA = pltpu.SemaphoreType.DMA
LIMIT = 48 << 20


def dot(left, right, left_dim, right_dim):
    return lax.dot_general(
        left, right, (((left_dim,), (right_dim,)), ((), ())), preferred_element_type=F32
    )


def norm_parts(values):
    average = jnp.mean(values, axis=-1, keepdims=True)
    centred = values - average
    inverse_std = lax.rsqrt(jnp.mean(centred * centred, axis=-1, keepdims=True) + 1e-05)
    return centred * inverse_std, inverse_std


def norm_back(upstream, normed, inverse_std, gain):
    scaled = upstream * gain
    return inverse_std * (
        scaled
        - jnp.mean(scaled, axis=-1, keepdims=True)
        - normed * jnp.mean(scaled * normed, axis=-1, keepdims=True)
    )


def flip(value, bit):
    return value + bit - 2 * bit * (value // bit % 2)


class Place:
    def __init__(self, groups, reach):
        self.groups, self.reach = groups, reach
        self.ctx = lax.axis_index("ctx")
        self.head = lax.axis_index("heads")
        self.local = self.ctx % reach
        self.base = self.ctx - self.local
        self.idx = self.local * groups + self.head

    def member(self, j):
        return {"ctx": self.base + j // self.groups, "heads": j % self.groups}


def meet(devices):
    barrier = pltpu.get_barrier_semaphore()
    for device in devices:
        pl.semaphore_signal(barrier, inc=1, device_id=device, device_id_type=MESH)
    pl.semaphore_wait(barrier, len(devices))


def push(source, target, device, send, recv):
    copy = pltpu.make_async_remote_copy(
        src_ref=source,
        dst_ref=target,
        send_sem=send,
        recv_sem=recv,
        device_id=device,
        device_id_type=MESH,
    )
    copy.start()
    return copy


def tree_parts(axes, rows):
    part = -(-rows // axes // 16) * 16
    starts = [min(part * a, rows) for a in range(axes + 1)]
    return [(starts[a], starts[a + 1] - starts[a]) for a in range(axes)]


class Tree:
    def __init__(self, place, axes, source, target, sems):
        self.place, self.axes, self.source, self.target = place, axes, source, target
        self.send, self.recv, self.core_send, self.core_recv, self.own = sems
        self.slots = 2 << axes
        self.levels, self.cores = [], []

    @staticmethod
    def scratch(axes):
        far, near = axes * axes, axes * axes + 1
        return [DMA((far,)), DMA((far,)), DMA((near,)), DMA((near,)), DMA]

    def origin(self, level, first):
        value = self.place.idx
        for k in range(level):
            value = flip(value, 2 << ((first + k) % self.axes))
        return value % self.slots

    def neighbour(self, axis):
        return self.place.member(flip(self.place.idx, 2 << (axis % self.axes)))

    def piece(self, slot, part):
        return self.target.at[slot] if part is None else self.target.at[slot, pl.ds(*part)]

    def to_core(self, source, slot, part):
        at = len(self.cores)
        self.cores.append(
            push(
                source,
                self.piece(slot, part),
                self.place.member(flip(self.place.idx, 1)),
                self.core_send.at[at],
                self.core_recv.at[at],
            )
        )

    def start(self):
        me = self.place.idx % self.slots
        self.levels.append(
            [
                push(
                    self.source, self.target.at[me], self.neighbour(a), self.send.at[a], self.recv.at[a]
                )
                for a in range(self.axes)
            ]
        )
        self.to_core(self.source, me, None)
        self.local = pltpu.make_async_copy(self.source, self.target.at[me], self.own)
        self.local.start()

    def forward(self, level):
        axes = self.axes
        parts = tree_parts(axes, self.target.shape[1])
        onward = []
        for a in range(axes):
            self.levels[level - 1][a].wait_recv()
            slot = self.origin(level, a)
            if level < axes:
                part = parts[a] if level + 1 == axes else None
                at = level * axes + a
                piece = self.piece(slot, part)
                onward.append(
                    push(piece, piece, self.neighbour(a + level), self.send.at[at], self.recv.at[at])
                )
                self.to_core(self.target.at[slot], slot, None)
            else:
                self.to_core(self.piece(slot, parts[a]), slot, parts[a])
        self.levels.append(onward)

    def finish(self):
        self.local.wait()
        for level in self.levels:
            for copy in level:
                copy.wait_send()
        for copy in self.cores:
            copy.wait()


class Halving:
    def __init__(self, place, axes, value, scratch):
        self.place, self.axes, self.value = place, axes, value
        self.other, self.held, self.land, self.send, self.recv, self.send0, self.recv0 = scratch
        self.blocks = 1 << axes
        width = value.shape[-1]
        part = -(-width // axes // 128) * 128
        starts = [min(part * a, width) for a in range(axes + 1)]
        self.columns = [pl.ds(starts[a], starts[a + 1] - starts[a]) for a in range(axes)]
        self.core = place.idx % 2
        self.chip = place.idx // 2 % self.blocks
        self.first, self.copies = [], {}

    @staticmethod
    def scratch(axes, rows, width):
        blocks = 1 << axes
        return [
            pltpu.VMEM((blocks, rows, width), BF),
            pltpu.VMEM((blocks, rows, width), BF),
            pltpu.VMEM((blocks, rows, width), BF),
            DMA((axes, blocks)),
            DMA((axes, blocks)),
            DMA((axes,)),
            DMA((axes,)),
        ]

    def sent(self, part, step):
        seen = [1 << ((part + s) % self.axes) for s in range(step)]
        bit = 1 << ((part + step) % self.axes)
        return bit, [j for j in range(self.blocks) if j & bit and not any(j & s for s in seen)]

    def start(self):
        for p in range(self.axes):
            self.first.append(
                push(
                    self.value.at[:, 1 - self.core, :, self.columns[p]],
                    self.other.at[:, :, self.columns[p]],
                    self.place.member(flip(self.place.idx, 1)),
                    self.send0.at[p],
                    self.recv0.at[p],
                )
            )

    def ship(self, p, step, j):
        piece = lambda ref: ref.at[j, :, self.columns[p]]
        bit, _ = self.sent(p, step)
        self.copies[p, j] = push(
            piece(self.held),
            piece(self.land),
            self.place.member(flip(self.place.idx, 2 * bit)),
            self.send.at[p, j],
            self.recv.at[p, j],
        )

    def pair(self):
        for p in range(self.axes):
            cols = self.columns[p]
            self.first[p].wait_recv()
            _, early = self.sent(p, 0)
            for j in early + [j for j in range(self.blocks) if j not in early]:
                k = self.chip
                for a in range(self.axes):
                    if j >> a & 1:
                        k = flip(k, 1 << a)
                self.held[j, :, cols] = (
                    self.value[k, self.core, :, cols].astype(F32) + self.other[k, :, cols].astype(F32)
                ).astype(BF)
                if j in early:
                    self.ship(p, 0, j)

    def halve(self, step):
        for p in range(self.axes):
            cols = self.columns[p]
            bit, arrived = self.sent(p, step)
            onward = self.sent(p, step + 1)[1] if step + 1 < self.axes else []
            for j in sorted(arrived, key=lambda j: (j - bit) not in onward):
                self.copies[p, j].wait_recv()
                k = j - bit
                total = self.held[k, :, cols].astype(F32) + self.land[j, :, cols].astype(F32)
                if step + 1 < self.axes:
                    self.held[k, :, cols] = total.astype(BF)
                    if k in onward:
                        self.ship(p, step + 1, k)
                else:
                    self.result[:, cols] = total

    def run(self, result):
        self.result = result
        self.start()
        self.pair()
        for step in range(self.axes):
            self.halve(step)
        self.finish()

    def finish(self):
        for copy in self.first:
            copy.wait_send()
        for copy in self.copies.values():
            copy.wait_send()


def spread(place, source, target, sems, me=None):
    send, recv, own = sems
    count = target.shape[0]
    copies = []
    for step in range(1, count):
        peer = (place.idx + step) % count
        copies.append(
            push(
                source.at[peer],
                target.at[place.idx],
                place.member(peer),
                send.at[step - 1],
                recv.at[step - 1],
            )
        )
    local = pltpu.make_async_copy(source.at[place.idx], target.at[place.idx], own)
    local.start()
    copies.append(local)
    return copies


def begin_kernel(
    groups,
    reach,
    count,
    tokens,
    gains,
    ids,
    w_qkv,
    w_attn,
    input_all,
    ids_all,
    gains_all,
    slab,
    attn_all,
    mine,
    gain_land,
    own_sems,
    ids_send,
    ids_recv,
    gain_send,
    gain_recv,
    slab_send,
    slab_recv,
    wide_send,
    wide_recv,
    side_send,
    side_recv,
    core_send,
    core_recv,
    *tree_sems,
):
    place = Place(groups, reach)
    group = reach * groups
    ctx, head, idx = place.ctx, place.head, place.idx
    lanes = attn_all.shape[2] // groups
    mates = [place.member((idx + step) % group) for step in range(1, group)]
    lines = [{"ctx": (ctx + step) % count} for step in range(1, count)]
    outside = [
        {"ctx": (place.base + reach + step) % count} for step in range(count - reach)
    ]
    meet(mates + outside)
    copies = []
    for step in range(1, count):
        copies.append(
            push(
                gains,
                gain_land.at[ctx],
                lines[step - 1],
                gain_send.at[step - 1],
                gain_recv.at[step - 1],
            )
        )
    for step in range(1, group):
        copies.append(
            push(ids, ids_all.at[idx], mates[step - 1], ids_send.at[step - 1], ids_recv.at[step - 1])
        )
    late = []
    for step in range(1, count):
        peer = (ctx + step) % count
        column = ((peer % reach) * groups + head) // 2 * 128
        for third in range(3):
            start = pl.multiple_of(third * 1024 + column, 128)
            late.append(
                push(
                    w_qkv.at[:, pl.ds(start, 128)],
                    slab.at[ctx, :, pl.ds(third * 128, 128)],
                    lines[step - 1],
                    slab_send.at[step - 1, third],
                    slab_recv.at[step - 1, third],
                )
            )
    gain_land[ctx] = gains[...]
    own = []
    for third in range(3):
        start = pl.multiple_of(third * 1024 + idx // 2 * 128, 128)
        own.append(
            pltpu.make_async_copy(
                w_qkv.at[:, pl.ds(start, 128)],
                slab.at[ctx, :, pl.ds(third * 128, 128)],
                own_sems.at[third],
            )
        )
    own.append(pltpu.make_async_copy(ids, ids_all.at[idx], own_sems.at[3]))
    own.append(pltpu.make_async_copy(w_attn, attn_all.at[ctx], own_sems.at[4]))
    for copy in own:
        copy.start()
    for copy in copies[: count - 1]:
        copy.wait_recv()
    shard = w_qkv.shape[0]
    gain, gain_two = (
        jnp.concatenate([gain_land[c, k : k + 1, :shard] for c in range(count)], axis=1)
        for k in range(2)
    )
    normed, _ = norm_parts(tokens[...].astype(F32))
    mine[...] = (normed * gain).astype(BF)
    tree = Tree(place, 3, mine, input_all, tree_sems)
    tree.start()
    gains_all[0:1, :] = gain
    gains_all[1:2, :] = gain_two
    slices = []
    across = pl.ds(pl.multiple_of(head * lanes, 128), lanes)
    for step in range(1, count):
        slices.append(
            push(
                w_attn.at[:, pl.ds(pl.multiple_of(head * lanes, 128), lanes)],
                attn_all.at[ctx, :, across],
                lines[step - 1],
                wide_send.at[step - 1],
                wide_recv.at[step - 1],
            )
        )
    tree.forward(1)
    tree.forward(2)
    half = groups // 2
    sides = []
    for step in range(1, count):
        slices[step - 1].wait_recv()
        source = (ctx - step + count) % count
        piece = attn_all.at[source, :, across]
        for k in range(1, half):
            sides.append(
                push(
                    piece,
                    piece,
                    {"heads": (head + 2 * k) % groups},
                    side_send.at[step - 1, k - 1],
                    side_recv.at[step - 1, k - 1],
                )
            )
    tree.forward(3)
    cores = []
    for k in range(half):
        if k:
            for step in range(1, count):
                sides[(step - 1) * (half - 1) + k - 1].wait_recv()
        column = pl.multiple_of((head - 2 * k + groups) % groups * lanes, 128)
        for step in range(1, count):
            piece = attn_all.at[(ctx - step + count) % count, :, pl.ds(column, lanes)]
            cores.append(
                push(
                    piece,
                    piece,
                    {"heads": flip(head, 1)},
                    core_send.at[step - 1, k],
                    core_recv.at[step - 1, k],
                )
            )
    tree.finish()
    for copy in own:
        copy.wait()
    for copy in copies[: count - 1] + slices + sides:
        copy.wait_send()
    for copy in copies[count - 1 :] + late + cores:
        copy.wait()


def begin(tokens, gains, ids, w_qkv, w_attn, count, groups, reach):
    rows, width = tokens.shape
    shard = w_qkv.shape[0]
    group = groups * reach
    sems = lambda *shape: [DMA(shape), DMA(shape)]
    return pl.pallas_call(
        functools.partial(begin_kernel, groups, reach, count),
        in_specs=[VMEM, VMEM, ANY, ANY, ANY],
        out_specs=[ANY, ANY, VMEM, ANY, ANY],
        out_shape=[
            jax.ShapeDtypeStruct((group, rows, width), BF),
            jax.ShapeDtypeStruct((group, 8, rows), jnp.int32),
            jax.ShapeDtypeStruct((8, width), F32),
            jax.ShapeDtypeStruct((count, shard, 3 * 128), BF),
            jax.ShapeDtypeStruct((count, shard, width), BF),
        ],
        scratch_shapes=[
            pltpu.VMEM((rows, width), BF),
            pltpu.VMEM((count, 8, gains.shape[1]), F32),
            DMA((5,)),
            *sems(group - 1),
            *sems(count - 1),
            *sems(count - 1, 3),
            *sems(count - 1),
            *sems(count - 1, max(groups // 2 - 1, 1)),
            *sems(count - 1, groups // 2),
            *Tree.scratch(3),
        ],
        compiler_params=pltpu.CompilerParams(
            collective_id=0, has_side_effects=True, vmem_limit_bytes=LIMIT
        ),
        cost_estimate=pl.CostEstimate(flops=0, bytes_accessed=30 << 20, transcendentals=0),
        name="begin",
    )(tokens, gains, ids, w_qkv, w_attn)


def attend_kernel(tile, x_ref, w_ref, cos_ref, sin_ref, mark_ref, out_ref, wide_ref, lse_ref, qkv_ref):
    count = x_ref.shape[0]
    step = pl.program_id(0)
    steps = count // tile

    @pl.when(step == 0)
    def _():
        qkv_ref[HD:QM_END, :] = mark_ref[:MARKS, :]
        qkv_ref[K_END:KM_END, :] = mark_ref[MARKS:, :]

        @pl.loop(0, steps)
        def _(i):
            at = pl.ds(pl.multiple_of(i * tile, tile), tile)
            cosine, sine = cos_ref[:, at], sin_ref[:, at]
            part = dot(w_ref[...], x_ref[at, :], 0, 1)

            def turn(value):
                front, back = value[:HALF], value[HALF:]
                return jnp.concatenate(
                    [front * cosine - back * sine, back * cosine + front * sine], axis=0
                )

            qkv_ref[:HD, at] = (turn(part[:HD]) * 0.125).astype(BF)
            qkv_ref[QM_END:K_END, at] = turn(part[HD : 2 * HD]).astype(BF)
            qkv_ref[KM_END:, at] = part[2 * HD :].astype(BF)

    here = pl.ds(pl.multiple_of(step * tile, tile), tile)
    query = qkv_ref[:QM_END, here]
    keys = [slice(j * tile, (j + 1) * tile) for j in range(steps)]
    scores = [dot(qkv_ref[QM_END:KM_END, at], query, 0, 0) for at in keys]
    top = functools.reduce(jnp.maximum, [jnp.max(s, axis=0, keepdims=True) for s in scores])
    raised = [jnp.exp(s - top) for s in scores]
    total = functools.reduce(jnp.add, [jnp.sum(e, axis=0, keepdims=True) for e in raised])
    scale = 1.0 / total
    result = jnp.zeros((HD, tile), F32)
    for j in range(steps):
        result += dot(qkv_ref[KM_END:, keys[j]], (raised[j] * scale).astype(BF), 1, 0)
    rows = out_ref.shape[2]
    for k in range(tile // rows):
        out_ref[step * (tile // rows) + k] = result[:, k * rows : (k + 1) * rows].astype(BF)
    wide_ref[:, here] = result
    lse_ref[:, here] = top + jnp.log(total)


def attend(x, w, cosine, sine, marks, rows, tile):
    count, width = x.shape
    whole = lambda *shape: pl.BlockSpec(shape, lambda i: (0,) * len(shape))
    return pl.pallas_call(
        functools.partial(attend_kernel, tile),
        grid=(count // tile,),
        in_specs=[
            whole(count, width),
            whole(*w.shape),
            whole(HALF, count),
            whole(HALF, count),
            whole(2 * MARKS, count),
        ],
        out_specs=[
            whole(count // rows, HD, rows),
            whole(HD, count),
            whole(1, count),
            whole(V_END, count),
        ],
        out_shape=[
            jax.ShapeDtypeStruct((count // rows, HD, rows), BF),
            jax.ShapeDtypeStruct((HD, count), F32),
            jax.ShapeDtypeStruct((1, count), F32),
            jax.ShapeDtypeStruct((V_END, count), BF),
        ],
        compiler_params=pltpu.CompilerParams(vmem_limit_bytes=LIMIT),
        cost_estimate=pl.CostEstimate(
            flops=count * count * HD * 8, bytes_accessed=count * 4096, transcendentals=count * count
        ),
        name="attend",
    )(x, w, cosine, sine, marks)


def middle_kernel(
    groups,
    reach,
    outgoing,
    tokens,
    d_out,
    w_attn,
    gains,
    mlp_all,
    upstream_all,
    middle,
    attended,
    land,
    mine,
    a2a_send,
    a2a_recv,
    own,
    *tree_sems,
):
    place = Place(groups, reach)
    group = groups * reach
    meet([place.member((place.idx + step) % group) for step in range(1, group)])
    copies = spread(place, outgoing, land, (a2a_send, a2a_recv, own))
    up = Tree(place, 2, d_out, upstream_all, tree_sems[5:])
    up.start()
    up.forward(1)
    for copy in copies:
        copy.wait()
    attended[...] = land[...]
    value = tokens[...].astype(F32) + dot(
        land[...].reshape(group * HD, tokens.shape[0]), w_attn[...], 0, 0
    )
    middle[...] = value
    normed, _ = norm_parts(value)
    mine[...] = (normed * gains[1:2, :]).astype(BF)
    tree = Tree(place, 2, mine, mlp_all, tree_sems[:5])
    tree.start()
    up.forward(2)
    tree.forward(1)
    tree.forward(2)
    up.finish()
    tree.finish()


def middle_step(outgoing, tokens, d_out, w_attn, gains, groups, reach):
    rows, width = tokens.shape
    group = groups * reach
    return pl.pallas_call(
        functools.partial(middle_kernel, groups, reach),
        in_specs=[ANY, VMEM, ANY, VMEM, VMEM],
        out_specs=[ANY, ANY, VMEM, VMEM],
        out_shape=[
            jax.ShapeDtypeStruct((8, rows, width), BF),
            jax.ShapeDtypeStruct((8, rows, width), BF),
            jax.ShapeDtypeStruct((rows, width), F32),
            jax.ShapeDtypeStruct((group, HD, rows), BF),
        ],
        scratch_shapes=[
            pltpu.VMEM((group, HD, rows), BF),
            pltpu.VMEM((rows, width), BF),
            DMA((group - 1,)),
            DMA((group - 1,)),
            DMA,
            *Tree.scratch(2),
            *Tree.scratch(2),
        ],
        compiler_params=pltpu.CompilerParams(
            collective_id=1, has_side_effects=True, vmem_limit_bytes=LIMIT
        ),
        cost_estimate=pl.CostEstimate(flops=1 << 28, bytes_accessed=12 << 20, transcendentals=0),
        name="middle_step",
    )(outgoing, tokens, d_out, w_attn, gains)


def turn_kernel(
    groups,
    reach,
    partial,
    middle,
    d_out,
    w_attn,
    gains,
    grads,
    columns,
    grad_middle,
    gain_sum,
    total,
    outgoing,
    branch,
    a2a_send,
    a2a_recv,
    own,
    side_send,
    side_recv,
    side_own,
    *halving,
):
    place = Place(groups, reach)
    group = groups * reach
    lanes = branch.shape[2]
    meet([place.member((place.idx + step) % group) for step in range(1, group)])
    Halving(place, 2, partial, halving).run(total)
    normed, inverse_std = norm_parts(middle[...])
    upstream = total[...]
    gain_sum[0:1, :] = jnp.sum(upstream * normed, axis=0, keepdims=True)
    grad = d_out[...].astype(F32) + norm_back(upstream, normed, inverse_std, gains[1:2, :])
    grad_middle[...] = grad
    low = grad.astype(BF)
    for g in range(groups):
        branch[g] = low[:, g * lanes : (g + 1) * lanes]
    outgoing[...] = dot(w_attn[...], low, 1, 1).astype(BF).reshape(outgoing.shape)
    copies = spread(place, outgoing, grads, (a2a_send, a2a_recv, own))
    for step in range(1, groups):
        peer = (place.head + step) % groups
        copies.append(
            push(
                branch.at[peer],
                columns.at[place.head],
                {"heads": peer},
                side_send.at[step - 1],
                side_recv.at[step - 1],
            )
        )
    local = pltpu.make_async_copy(branch.at[place.head], columns.at[place.head], side_own)
    local.start()
    for copy in copies:
        copy.wait()
    local.wait()


def turn_step(partial, middle, d_out, w_attn, gains, groups, reach):
    rows, width = middle.shape
    group = groups * reach
    return pl.pallas_call(
        functools.partial(turn_kernel, groups, reach),
        in_specs=[VMEM] * 5,
        out_specs=[ANY, ANY, VMEM, VMEM],
        out_shape=[
            jax.ShapeDtypeStruct((group, HD, rows), BF),
            jax.ShapeDtypeStruct((groups, rows, width // groups), BF),
            jax.ShapeDtypeStruct((rows, width), F32),
            jax.ShapeDtypeStruct((8, width), F32),
        ],
        scratch_shapes=[
            pltpu.VMEM((rows, width), F32),
            pltpu.VMEM((group, HD, rows), BF),
            pltpu.VMEM((groups, rows, width // groups), BF),
            DMA((group - 1,)),
            DMA((group - 1,)),
            DMA,
            DMA((groups - 1,)),
            DMA((groups - 1,)),
            DMA,
            *Halving.scratch(2, rows, width),
        ],
        compiler_params=pltpu.CompilerParams(
            collective_id=2, has_side_effects=True, vmem_limit_bytes=LIMIT
        ),
        cost_estimate=pl.CostEstimate(flops=1 << 28, bytes_accessed=12 << 20, transcendentals=0),
        name="turn_step",
    )(partial, middle, d_out, w_attn, gains)


def attend_back_kernel(
    tile,
    qkv_ref,
    grad_ref,
    wide_ref,
    lse_ref,
    x_ref,
    w_ref,
    cos_ref,
    sin_ref,
    out_ref,
    weight_ref,
    sums,
    queries,
    weight,
):
    count = x_ref.shape[0]
    rows = grad_ref.shape[2]
    steps, per_tile = count // tile, tile // rows
    step = pl.program_id(0)

    @pl.when(step == 0)
    def _():
        sums[...] = jnp.zeros_like(sums)

    here = pl.ds(pl.multiple_of(step * tile, tile), tile)
    query = qkv_ref[:QM_END, here]
    grad = jnp.concatenate([grad_ref[step * per_tile + k] for k in range(per_tile)], axis=1)
    delta = jnp.sum(grad.astype(F32) * wide_ref[:, here], axis=0, keepdims=True)
    lse = lse_ref[:, here]
    grad_query = jnp.zeros((HD, tile), F32)
    for j in range(steps):
        keys = slice(j * tile, (j + 1) * tile)
        prob = jnp.exp(dot(qkv_ref[QM_END:KM_END, keys], query, 0, 0) - lse)
        grad_prob = dot(qkv_ref[KM_END:, keys], grad, 0, 0)
        grad_score = (prob * (grad_prob - delta)).astype(BF)
        grad_query += dot(qkv_ref[QM_END:K_END, keys], grad_score, 1, 0)
        sums[:HD, keys] += dot(query[:HD], grad_score, 1, 1)
        sums[HD:, keys] += dot(grad, prob.astype(BF), 1, 1)
    queries[:, here] = (grad_query * 0.125).astype(BF)

    @pl.when(step == steps - 1)
    def _():
        weight[...] = jnp.zeros_like(weight)

        @pl.loop(0, steps)
        def _(i):
            at = pl.ds(pl.multiple_of(i * tile, tile), tile)
            cosine, sine = cos_ref[:, at], sin_ref[:, at]

            def turn_back(value):
                front, back = value[:HALF], value[HALF:]
                return [front * cosine + back * sine, back * cosine - front * sine]

            low = lambda value: value.astype(BF).astype(F32)
            projected = jnp.concatenate(
                [
                    *turn_back(queries[:, at].astype(F32)),
                    *turn_back(low(sums[:HD, at])),
                    low(sums[HD:, at]),
                ],
                axis=0,
            ).astype(BF)
            part = dot(projected, w_ref[...], 0, 1).astype(BF)
            for k in range(per_tile):
                out_ref[i * per_tile + k] = part[k * rows : (k + 1) * rows]
            weight[...] += dot(projected, x_ref[at, :], 1, 0)

        weight_ref[...] = weight[...].astype(BF)


def attend_back(qkv, grad, wide, lse, x, w, cosine, sine, tile):
    count, width = x.shape
    blocks, _, rows = grad.shape
    whole = lambda *shape: pl.BlockSpec(shape, lambda i: (0,) * len(shape))
    operands = (qkv, grad, wide, lse, x, w, cosine, sine)
    return pl.pallas_call(
        functools.partial(attend_back_kernel, tile),
        grid=(count // tile,),
        in_specs=[whole(*operand.shape) for operand in operands],
        out_specs=[whole(blocks, rows, width), whole(3 * HD, width)],
        out_shape=[
            jax.ShapeDtypeStruct((blocks, rows, width), BF),
            jax.ShapeDtypeStruct((3 * HD, width), BF),
        ],
        scratch_shapes=[
            pltpu.VMEM((2 * HD, count), F32),
            pltpu.VMEM((HD, count), BF),
            pltpu.VMEM((3 * HD, width), F32),
        ],
        compiler_params=pltpu.CompilerParams(vmem_limit_bytes=LIMIT),
        cost_estimate=pl.CostEstimate(
            flops=count * count * HD * 20, bytes_accessed=count * 6144, transcendentals=count * count
        ),
        name="attend_back",
    )(*operands)


def end_kernel(groups, reach, partial, forward, tokens, grad_middle, gains, grad, gain_sum, ahead, total, *rest):
    place = Place(groups, reach)
    group = groups * reach
    meet([place.member((place.idx + step) % group) for step in range(1, group)])
    wide = Halving(place, 3, partial, rest[:7])
    small = Halving(place, 2, forward, rest[7:])
    wide.result, small.result = total, ahead
    wide.start()
    small.start()
    wide.pair()
    small.pair()
    for step in range(3):
        wide.halve(step)
        if step < 2:
            small.halve(step)
    wide.finish()
    small.finish()
    normed, inverse_std = norm_parts(tokens[...].astype(F32))
    upstream = total[...]
    gain_sum[0:1, :] = jnp.sum(upstream * normed, axis=0, keepdims=True)
    grad[...] = grad_middle[...] + norm_back(upstream, normed, inverse_std, gains[0:1, :])


def end_step(partial, forward, tokens, grad_middle, gains, groups, reach):
    rows, width = tokens.shape
    return pl.pallas_call(
        functools.partial(end_kernel, groups, reach),
        in_specs=[VMEM] * 5,
        out_specs=[VMEM] * 3,
        out_shape=[
            jax.ShapeDtypeStruct((rows, width), F32),
            jax.ShapeDtypeStruct((8, width), F32),
            jax.ShapeDtypeStruct((rows, width), F32),
        ],
        scratch_shapes=[
            pltpu.VMEM((rows, width), F32),
            *Halving.scratch(3, rows, width),
            *Halving.scratch(2, rows, width),
        ],
        compiler_params=pltpu.CompilerParams(
            collective_id=3, has_side_effects=True, vmem_limit_bytes=LIMIT
        ),
        cost_estimate=pl.CostEstimate(flops=0, bytes_accessed=24 << 20, transcendentals=0),
        name="end_step",
    )(partial, forward, tokens, grad_middle, gains)


def lines_kernel(count, source, target, send, recv, local):
    me = lax.axis_index("ctx")
    meet([{"ctx": (me + step) % count} for step in range(1, count)])
    copies = []
    for step in range(1, count):
        peer = (me + step) % count
        copies.append(
            push(source.at[peer], target.at[me], {"ctx": peer}, send.at[step - 1], recv.at[step - 1])
        )
    own = pltpu.make_async_copy(source.at[me], target.at[me], local)
    own.start()
    own.wait()
    for copy in copies:
        copy.wait()


def lines_swap(value, count):
    return pl.pallas_call(
        functools.partial(lines_kernel, count),
        in_specs=[ANY],
        out_specs=ANY,
        out_shape=jax.ShapeDtypeStruct(value.shape, BF),
        scratch_shapes=[DMA((count - 1,)), DMA((count - 1,)), DMA],
        compiler_params=pltpu.CompilerParams(collective_id=4, has_side_effects=True),
        cost_estimate=pl.CostEstimate(flops=0, bytes_accessed=2 << 20, transcendentals=0),
        name="lines_swap",
    )(value)


def collect_kernel(
    groups, sub, mlp, rest, mlp_all, rest_all, swap_send, swap_recv, own, far_send, far_recv, near_send, near_recv
):
    ctx, head = lax.axis_index("ctx"), lax.axis_index("heads")
    half = groups // 2
    pair = flip(head, 1)
    mine = ctx % sub
    line = [{"ctx": ctx - mine + (mine + step) % sub} for step in range(1, sub)]
    meet([{"heads": (head + step) % groups} for step in range(1, groups)] + line)
    waits, near = [], []
    swaps = []
    for step in range(1, sub):
        other = (mine + step) % sub
        swaps.append(
            push(
                mlp.at[other],
                mlp_all.at[mine, head],
                line[step - 1],
                swap_send.at[step - 1],
                swap_recv.at[step - 1],
            )
        )
    pieces = [(mlp.at[mine], lambda h: mlp_all.at[mine, h]), (rest, lambda h: rest_all.at[h])]
    for step in range(1, sub):
        source = (mine - step + sub) % sub
        pieces.append(
            (mlp_all.at[source, head], lambda h, source=source: mlp_all.at[source, h])
        )
    local = [
        pltpu.make_async_copy(mlp.at[mine], mlp_all.at[mine, head], own.at[0]),
        pltpu.make_async_copy(rest, rest_all.at[head], own.at[1]),
    ]
    for copy in local:
        copy.start()
    far = []
    for n, (piece, where) in enumerate(pieces):
        if n >= 2:
            swaps[n - 2].wait_recv()
        for k in range(1, half):
            far.append(
                push(
                    piece,
                    where(head),
                    {"heads": (head + 2 * k) % groups},
                    far_send.at[n, k - 1],
                    far_recv.at[n, k - 1],
                )
            )
        near.append(push(piece, where(head), {"heads": pair}, near_send.at[n, 0], near_recv.at[n, 0]))
    for n, (piece, where) in enumerate(pieces):
        for k in range(1, half):
            far[n * (half - 1) + k - 1].wait_recv()
            got = where((head - 2 * k + groups) % groups)
            near.append(push(got, got, {"heads": pair}, near_send.at[n, k], near_recv.at[n, k]))
    for copy in local + near:
        copy.wait()
    for copy in far + swaps:
        copy.wait_send()


def collect(mlp, rest, groups, sub):
    count = sub + 1
    sems = lambda *shape: [DMA(shape), DMA(shape)]
    return pl.pallas_call(
        functools.partial(collect_kernel, groups, sub),
        in_specs=[ANY, ANY],
        out_specs=[ANY, ANY],
        out_shape=[
            jax.ShapeDtypeStruct((sub, groups, *mlp.shape[1:]), BF),
            jax.ShapeDtypeStruct((groups, *rest.shape), BF),
        ],
        scratch_shapes=[
            *sems(max(sub - 1, 1)),
            DMA((2,)),
            *sems(count, max(groups // 2 - 1, 1)),
            *sems(count, groups // 2),
        ],
        compiler_params=pltpu.CompilerParams(collective_id=5, has_side_effects=True),
        cost_estimate=pl.CostEstimate(flops=0, bytes_accessed=6 << 20, transcendentals=0),
        name="collect",
    )(mlp, rest)


def slice_start(t):
    return 128 * jnp.minimum(3 * t, 2 * t + 5)


def slice_place(t):
    start = 128 * min(3 * t, 2 * t + 5)
    return start, min(128 * min(3 * t + 3, 2 * t + 7), FF) - start


def body(count, tokens, d_out, segment_ids, position_ids, w_qkv, w_attn, w_in, w_out, gain_attn, gain_mlp):
    groups = lax.axis_size("heads")
    rows, width = tokens.shape
    shard = w_qkv.shape[0]
    reach = SEQ_MAX // (rows * groups)
    group = reach * groups
    sub = 8 // groups
    ctx, head = lax.axis_index("ctx"), lax.axis_index("heads")
    assert group == H and sub * groups == 8
    total = group * rows
    tile = 512

    def mlp_slice(value, axis, start, t):
        pads = [(0, 0), (0, 0)]
        pads[axis] = (0, SLICE)
        piece = lax.dynamic_slice_in_dim(jnp.pad(value, pads), start + slice_start(t), SLICE, axis)
        wide = jnp.minimum(slice_start(t + 1), FF) - slice_start(t)
        shape = [1, 1]
        shape[axis] = SLICE
        return jnp.where(jnp.arange(SLICE).reshape(shape) < wide, piece, jnp.zeros_like(piece))

    def mlp_part(t):
        return jnp.concatenate(
            [mlp_slice(w_in, 1, 0, t), mlp_slice(w_in, 1, FF, t), mlp_slice(w_out, 0, 0, t).T], axis=1
        )

    mine = ctx % sub
    own_part = mlp_part(mine * groups + head)
    parts = [own_part]
    for step in range(1, sub):
        send = mlp_part((mine + step) % sub * groups + head)
        got = lax.ppermute(send, "ctx", [(c, c // sub * sub + (c + step) % sub) for c in range(count)])
        parts.append(got)
    if sub == 2:
        low = jnp.where(mine == 0, parts[0], parts[1])
        high = jnp.where(mine == 0, parts[1], parts[0])
        parts = [low, high]
    lines = [list(range(k, count, sub)) for k in range(sub)]
    mlp_weights = lax.all_gather(
        jnp.concatenate(parts, axis=0), "ctx", axis=0, tiled=True, axis_index_groups=lines
    )

    gains_own = jnp.pad(jnp.stack([gain_attn, gain_mlp]).astype(F32), ((0, 6), (0, -shard % 128)))
    ids = jnp.pad(jnp.stack([position_ids, segment_ids]), ((0, 6), (0, 0)))
    input_all, ids_all, gains, slab, attn_weights = begin(
        tokens, gains_own, ids, w_qkv, w_attn, count, groups, reach
    )
    x = input_all.reshape(total, width)
    attn_weights = attn_weights.reshape(width, width)
    slab = slab.reshape(width, 3, 2, HD)
    w_head = jnp.where(head % 2 == 0, slab[:, :, 0], slab[:, :, 1]).reshape(width, 3 * HD)
    positions = ids_all[:, 0].reshape(1, total).astype(F32)
    parity = (ids_all[:, 1].reshape(1, total) % 2).astype(F32)
    freqs = jnp.power(160000.0, -(2.0 * jnp.arange(HALF, dtype=F32)) / HD)
    angles = freqs[:, None] * positions
    cosine, sine = jnp.cos(angles), jnp.sin(angles)
    blank = jnp.zeros((MARKS - 2, total), F32)
    marks = jnp.concatenate(
        [parity, 1.0 - parity, blank, (1.0 - parity) * MASKED, parity * MASKED, blank]
    ).astype(BF)

    attended, wide, lse, qkv = attend(x, w_head, cosine, sine, marks, rows, tile)
    mlp_all, upstream, middle, attended = middle_step(
        attended, tokens, d_out, attn_weights, gains, groups, reach
    )
    mlp_input = mlp_all.reshape(8 * rows, width)
    upstream = upstream.reshape(8 * rows, width)
    attended_all = lax.all_gather(attended.reshape(width, rows), "heads", axis=0)

    in_weights, out_weights = mlp_weights[:, : 2 * SLICE], mlp_weights[:, 2 * SLICE :]
    gate_up = dot(mlp_input, in_weights, 1, 0)
    gate_left, gate_right = gate_up[:, :SLICE], gate_up[:, SLICE:]
    normal_cdf = 0.5 * (1.0 + lax.erf(gate_left * 0.7071067811865476))
    gelu = gate_left * normal_cdf
    density = jnp.exp(-0.5 * gate_left * gate_left) * 0.3989422804014327
    mixed = (gelu * gate_right).astype(BF)
    grad_mixed = dot(upstream, out_weights, 1, 0)
    grad_left = grad_mixed * gate_right * (normal_cdf + gate_left * density)
    grad_gate_up = jnp.concatenate([grad_left, grad_mixed * gelu], axis=1).astype(BF)
    split = lambda value, blocks: value.astype(BF).reshape(blocks // 2, 2, rows, width)
    grad_mlp = split(dot(grad_gate_up, in_weights, 1, 1), 8)
    grad_out_part = dot(upstream, mixed, 0, 0)
    grad_in_part = dot(mlp_input, grad_gate_up, 0, 0)
    mlp_sum = lax.psum_scatter(
        jnp.concatenate([grad_in_part, grad_out_part], axis=1).astype(BF),
        "ctx",
        scatter_dimension=0,
        tiled=True,
        axis_index_groups=lines,
    )
    grad_heads, branch, grad_middle, gain_two = turn_step(
        grad_mlp, middle, d_out, attn_weights, gains, groups, reach
    )
    grad_attn_part = jnp.einsum(
        "gdt,gtn->dn", attended_all, branch, preferred_element_type=F32
    ).astype(BF)
    attn_sum = lax.psum_scatter(grad_attn_part, "ctx", scatter_dimension=0, tiled=True)
    forward = split(dot(mixed, out_weights, 1, 1), 8)
    grad_input_parts, weight = attend_back(qkv, grad_heads, wide, lse, x, w_head, cosine, sine, tile)
    grad_input, gain_one, ahead = end_step(
        split(grad_input_parts, group), forward, tokens, grad_middle, gains, groups, reach
    )
    result = (middle + ahead).astype(BF)

    last = jnp.concatenate(
        [
            weight.T,
            gain_one[:1].T.astype(BF),
            gain_two[:1].T.astype(BF),
            jnp.zeros((width, 62), BF),
        ],
        axis=1,
    ).reshape(count, shard, 256)
    lined = lines_swap(last, count).astype(F32).reshape(count // reach, reach, shard, 256)
    heads_sum = jnp.sum(lined, axis=0)
    gain_sum = jnp.sum(heads_sum[:, :, 3 * HD : 3 * HD + 2], axis=0)
    rest = jnp.concatenate(
        [
            heads_sum[:, :, : 3 * HD].transpose(1, 0, 2).reshape(shard, reach * 3 * HD),
            gain_sum,
            jnp.zeros((shard, -(reach * 3 * HD + 2) % 128), F32),
            attn_sum.astype(F32),
        ],
        axis=1,
    ).astype(BF)
    mlp_rest, rest_all = collect(mlp_sum.reshape(sub, shard, 3 * SLICE), rest, groups, sub)
    qkv_all = rest_all[:, :, : reach * 3 * HD].reshape(groups, shard, reach, 3, HD)
    sum_qkv = qkv_all.transpose(1, 3, 2, 0, 4).reshape(shard, 3 * width).astype(F32)
    gain_at = reach * 3 * HD
    gain_sums = jnp.sum(rest_all[:, :, gain_at : gain_at + 2].astype(F32), axis=0)
    sum_attn = (
        rest_all[:, :, -(width // groups) :].transpose(1, 0, 2).reshape(shard, width).astype(F32)
    )
    mlp_rest = mlp_rest.reshape(8, shard, 3 * SLICE)

    def columns(at):
        return [mlp_rest[t, :, at : at + slice_place(t)[1]] for t in range(8)]

    sum_in = jnp.concatenate(columns(0) + columns(SLICE), axis=1).astype(F32)
    sum_out = jnp.concatenate([piece.T for piece in columns(2 * SLICE)], axis=0).astype(F32)
    return (
        result,
        grad_input,
        sum_qkv,
        sum_attn,
        sum_in,
        sum_out,
        gain_sums[:, 0],
        gain_sums[:, 1],
    )


def solution(mesh):
    return jax.shard_map(
        functools.partial(body, mesh.shape["ctx"]),
        mesh=mesh,
        in_specs=(
            P(("ctx", "heads"), None),
            P(("ctx", "heads"), None),
            P(("ctx", "heads")),
            P(("ctx", "heads")),
            P("ctx", None),
            P("ctx", None),
            P("ctx", None),
            P(None, "ctx"),
            P("ctx"),
            P("ctx"),
        ),
        out_specs=(
            P(("ctx", "heads"), None),
            P(("ctx", "heads"), None),
            P("ctx", None),
            P("ctx", None),
            P("ctx", None),
            P(None, "ctx"),
            P("ctx"),
            P("ctx"),
        ),
        check_vma=False,
    )
```

```python
import functools

import jax
import jax.numpy as jnp
from jax import lax
from jax.experimental import pallas as pl
from jax.experimental.pallas import tpu as pltpu
from jax.sharding import PartitionSpec as P

H = 16
HD = 64
HALF = HD // 2
FF = 2624
SEQ_MAX = 2048
MASKED = -1e30
MARKS = 16
QM_END = HD + MARKS
K_END = QM_END + HD
KM_END = K_END + MARKS
V_END = KM_END + HD
SLICE = 384
BF = jnp.bfloat16
F32 = jnp.float32
MESH = pl.DeviceIdType.MESH
VMEM = pl.BlockSpec(memory_space=pltpu.VMEM)
ANY = pl.BlockSpec(memory_space=pl.ANY)
DMA = pltpu.SemaphoreType.DMA
LIMIT = 48 << 20


def dot(left, right, left_dim, right_dim):
    return lax.dot_general(
        left, right, (((left_dim,), (right_dim,)), ((), ())), preferred_element_type=F32
    )


def norm_parts(values):
    average = jnp.mean(values, axis=-1, keepdims=True)
    centred = values - average
    inverse_std = lax.rsqrt(jnp.mean(centred * centred, axis=-1, keepdims=True) + 1e-05)
    return centred * inverse_std, inverse_std


def norm_back(upstream, normed, inverse_std, gain):
    scaled = upstream * gain
    return inverse_std * (
        scaled
        - jnp.mean(scaled, axis=-1, keepdims=True)
        - normed * jnp.mean(scaled * normed, axis=-1, keepdims=True)
    )


def flip(value, bit):
    return value + bit - 2 * bit * (value // bit % 2)


class Place:
    def __init__(self, groups, reach):
        self.groups, self.reach = groups, reach
        self.ctx = lax.axis_index("ctx")
        self.head = lax.axis_index("heads")
        self.local = self.ctx % reach
        self.base = self.ctx - self.local
        self.idx = self.local * groups + self.head

    def member(self, j):
        return {"ctx": self.base + j // self.groups, "heads": j % self.groups}


def meet(devices):
    barrier = pltpu.get_barrier_semaphore()
    for device in devices:
        pl.semaphore_signal(barrier, inc=1, device_id=device, device_id_type=MESH)
    pl.semaphore_wait(barrier, len(devices))


def remote(source, target, device, send, recv):
    return pltpu.make_async_remote_copy(
        src_ref=source,
        dst_ref=target,
        send_sem=send,
        recv_sem=recv,
        device_id=device,
        device_id_type=MESH,
    )


def push(*operands):
    copy = remote(*operands)
    copy.start()
    return copy


def tree_parts(axes, rows):
    part = -(-rows // axes // 16) * 16
    starts = [min(part * a, rows) for a in range(axes + 1)]
    return [(starts[a], starts[a + 1] - starts[a]) for a in range(axes)]


class Tree:
    def __init__(self, place, axes, source, target, sems):
        self.place, self.axes, self.source, self.target = place, axes, source, target
        self.send, self.recv, self.core_send, self.core_recv, self.own = sems
        self.slots = 2 << axes
        self.levels, self.cores = [], []

    @staticmethod
    def scratch(axes):
        far, near = axes * axes, axes * axes + 1
        return [DMA((far,)), DMA((far,)), DMA((near,)), DMA((near,)), DMA]

    def origin(self, level, first):
        value = self.place.idx
        for k in range(level):
            value = flip(value, 2 << ((first + k) % self.axes))
        return value % self.slots

    def neighbour(self, axis):
        return self.place.member(flip(self.place.idx, 2 << (axis % self.axes)))

    def piece(self, slot, part):
        return self.target.at[slot] if part is None else self.target.at[slot, pl.ds(*part)]

    def to_core(self, source, slot, part):
        at = len(self.cores)
        self.cores.append(
            push(
                source,
                self.piece(slot, part),
                self.place.member(flip(self.place.idx, 1)),
                self.core_send.at[at],
                self.core_recv.at[at],
            )
        )

    def start(self):
        me = self.place.idx % self.slots
        self.levels.append(
            [
                push(
                    self.source, self.target.at[me], self.neighbour(a), self.send.at[a], self.recv.at[a]
                )
                for a in range(self.axes)
            ]
        )
        self.to_core(self.source, me, None)
        self.local = pltpu.make_async_copy(self.source, self.target.at[me], self.own)
        self.local.start()

    def forward(self, level):
        axes = self.axes
        parts = tree_parts(axes, self.target.shape[1])
        onward = []
        for a in range(axes):
            self.levels[level - 1][a].wait_recv()
            slot = self.origin(level, a)
            if level < axes:
                part = parts[a] if level + 1 == axes else None
                at = level * axes + a
                piece = self.piece(slot, part)
                onward.append(
                    push(piece, piece, self.neighbour(a + level), self.send.at[at], self.recv.at[at])
                )
                self.to_core(self.target.at[slot], slot, None)
            else:
                self.to_core(self.piece(slot, parts[a]), slot, parts[a])
        self.levels.append(onward)

    def finish(self):
        self.local.wait()
        for level in self.levels:
            for copy in level:
                copy.wait_send()
        for copy in self.cores:
            copy.wait()


class Halving:
    def __init__(self, place, axes, value, result, scratch):
        self.axes, self.value, self.result = axes, value, result
        self.other, self.held, self.land, send, recv, send0, recv0 = scratch
        self.blocks = 1 << axes
        width = value.shape[-1]
        part = -(-width // axes // 128) * 128
        starts = [min(part * a, width) for a in range(axes + 1)]
        self.columns = [pl.ds(starts[a], starts[a + 1] - starts[a]) for a in range(axes)]
        self.core = place.idx % 2
        self.chip = place.idx // 2 % self.blocks
        self.sources = []
        for j in range(self.blocks):
            k = self.chip
            for a in range(axes):
                if j >> a & 1:
                    k = flip(k, 1 << a)
            self.sources.append(k)
        self.first, self.copies = [], {}
        for p in range(axes):
            self.first.append(
                remote(
                    value.at[:, 1 - self.core, :, self.columns[p]],
                    self.other.at[:, :, self.columns[p]],
                    place.member(flip(place.idx, 1)),
                    send0.at[p],
                    recv0.at[p],
                )
            )
            for step in range(axes):
                bit, sent = self.sent(p, step)
                for j in sent:
                    self.copies[p, j] = remote(
                        self.held.at[j, :, self.columns[p]],
                        self.land.at[j, :, self.columns[p]],
                        place.member(flip(place.idx, 2 * bit)),
                        send.at[p, j],
                        recv.at[p, j],
                    )

    @staticmethod
    def scratch(axes, rows, width):
        blocks = 1 << axes
        return [
            pltpu.VMEM((blocks, rows, width), BF),
            pltpu.VMEM((blocks, rows, width), BF),
            pltpu.VMEM((blocks, rows, width), BF),
            DMA((axes, blocks)),
            DMA((axes, blocks)),
            DMA((axes,)),
            DMA((axes,)),
        ]

    def sent(self, part, step):
        seen = [1 << ((part + s) % self.axes) for s in range(step)]
        bit = 1 << ((part + step) % self.axes)
        return bit, [j for j in range(self.blocks) if j & bit and not any(j & s for s in seen)]

    def start(self):
        for copy in self.first:
            copy.start()

    def pair(self):
        for p in range(self.axes):
            cols = self.columns[p]
            self.first[p].wait_recv()
            _, early = self.sent(p, 0)
            for j in early + [j for j in range(self.blocks) if j not in early]:
                k = self.sources[j]
                self.held[j, :, cols] = (
                    self.value[k, self.core, :, cols].astype(F32) + self.other[k, :, cols].astype(F32)
                ).astype(BF)
                if j in early:
                    self.copies[p, j].start()

    def halve(self, step):
        for p in range(self.axes):
            cols = self.columns[p]
            bit, arrived = self.sent(p, step)
            onward = self.sent(p, step + 1)[1] if step + 1 < self.axes else []
            for j in sorted(arrived, key=lambda j: (j - bit) not in onward):
                self.copies[p, j].wait_recv()
                k = j - bit
                total = self.held[k, :, cols].astype(F32) + self.land[j, :, cols].astype(F32)
                if step + 1 < self.axes:
                    self.held[k, :, cols] = total.astype(BF)
                    if k in onward:
                        self.copies[p, k].start()
                else:
                    self.result[:, cols] = total

    def run(self):
        self.start()
        self.pair()
        for step in range(self.axes):
            self.halve(step)
        self.finish()

    def finish(self):
        for copy in self.first:
            copy.wait_send()
        for copy in self.copies.values():
            copy.wait_send()


class Lines:
    def __init__(self, count, source, target, send, recv, own):
        me = lax.axis_index("ctx")
        self.copies = [pltpu.make_async_copy(source.at[me], target.at[me], own)]
        for step in range(1, count):
            peer = (me + step) % count
            self.copies.append(
                remote(source.at[peer], target.at[me], {"ctx": peer}, send.at[step - 1], recv.at[step - 1])
            )

    @staticmethod
    def scratch(count):
        return [DMA((count - 1,)), DMA((count - 1,)), DMA]

    def start(self):
        for copy in self.copies:
            copy.start()

    def finish(self):
        for copy in self.copies:
            copy.wait()


def everyone(place, count):
    group = place.reach * place.groups
    mates = [place.member((place.idx + step) % group) for step in range(1, group)]
    outside = [{"ctx": (place.base + place.reach + step) % count} for step in range(count - place.reach)]
    return mates + outside


def spread(place, source, target, sems, me=None):
    send, recv, own = sems
    count = target.shape[0]
    copies = []
    for step in range(1, count):
        peer = (place.idx + step) % count
        copies.append(
            push(
                source.at[peer],
                target.at[place.idx],
                place.member(peer),
                send.at[step - 1],
                recv.at[step - 1],
            )
        )
    local = pltpu.make_async_copy(source.at[place.idx], target.at[place.idx], own)
    local.start()
    copies.append(local)
    return copies


def begin_kernel(
    groups,
    reach,
    count,
    tokens,
    gains,
    ids,
    w_qkv,
    w_attn,
    input_all,
    ids_all,
    gains_all,
    slab,
    attn_all,
    mine,
    gain_land,
    own_sems,
    ids_send,
    ids_recv,
    gain_send,
    gain_recv,
    slab_send,
    slab_recv,
    wide_send,
    wide_recv,
    side_send,
    side_recv,
    core_send,
    core_recv,
    *tree_sems,
):
    place = Place(groups, reach)
    group = reach * groups
    ctx, head, idx = place.ctx, place.head, place.idx
    lanes = attn_all.shape[2] // groups
    mates = [place.member((idx + step) % group) for step in range(1, group)]
    lines = [{"ctx": (ctx + step) % count} for step in range(1, count)]
    outside = [
        {"ctx": (place.base + reach + step) % count} for step in range(count - reach)
    ]
    meet(mates + outside)
    copies = []
    for step in range(1, count):
        copies.append(
            push(
                gains,
                gain_land.at[ctx],
                lines[step - 1],
                gain_send.at[step - 1],
                gain_recv.at[step - 1],
            )
        )
    for step in range(1, group):
        copies.append(
            push(ids, ids_all.at[idx], mates[step - 1], ids_send.at[step - 1], ids_recv.at[step - 1])
        )
    late = []
    for step in range(1, count):
        peer = (ctx + step) % count
        column = ((peer % reach) * groups + head) // 2 * 128
        for third in range(3):
            start = pl.multiple_of(third * 1024 + column, 128)
            late.append(
                push(
                    w_qkv.at[:, pl.ds(start, 128)],
                    slab.at[ctx, :, pl.ds(third * 128, 128)],
                    lines[step - 1],
                    slab_send.at[step - 1, third],
                    slab_recv.at[step - 1, third],
                )
            )
    gain_land[ctx] = gains[...]
    own = []
    for third in range(3):
        start = pl.multiple_of(third * 1024 + idx // 2 * 128, 128)
        own.append(
            pltpu.make_async_copy(
                w_qkv.at[:, pl.ds(start, 128)],
                slab.at[ctx, :, pl.ds(third * 128, 128)],
                own_sems.at[third],
            )
        )
    own.append(pltpu.make_async_copy(ids, ids_all.at[idx], own_sems.at[3]))
    own.append(pltpu.make_async_copy(w_attn, attn_all.at[ctx], own_sems.at[4]))
    for copy in own:
        copy.start()
    for copy in copies[: count - 1]:
        copy.wait_recv()
    shard = w_qkv.shape[0]
    gain, gain_two = (
        jnp.concatenate([gain_land[c, k : k + 1, :shard] for c in range(count)], axis=1)
        for k in range(2)
    )
    normed, _ = norm_parts(tokens[...].astype(F32))
    mine[...] = (normed * gain).astype(BF)
    tree = Tree(place, 3, mine, input_all, tree_sems)
    tree.start()
    gains_all[0:1, :] = gain
    gains_all[1:2, :] = gain_two
    slices = []
    across = pl.ds(pl.multiple_of(head * lanes, 128), lanes)
    for step in range(1, count):
        slices.append(
            push(
                w_attn.at[:, pl.ds(pl.multiple_of(head * lanes, 128), lanes)],
                attn_all.at[ctx, :, across],
                lines[step - 1],
                wide_send.at[step - 1],
                wide_recv.at[step - 1],
            )
        )
    tree.forward(1)
    tree.forward(2)
    half = groups // 2
    sides = []
    for step in range(1, count):
        slices[step - 1].wait_recv()
        source = (ctx - step + count) % count
        piece = attn_all.at[source, :, across]
        for k in range(1, half):
            sides.append(
                push(
                    piece,
                    piece,
                    {"heads": (head + 2 * k) % groups},
                    side_send.at[step - 1, k - 1],
                    side_recv.at[step - 1, k - 1],
                )
            )
    tree.forward(3)
    cores = []
    for k in range(half):
        if k:
            for step in range(1, count):
                sides[(step - 1) * (half - 1) + k - 1].wait_recv()
        column = pl.multiple_of((head - 2 * k + groups) % groups * lanes, 128)
        for step in range(1, count):
            piece = attn_all.at[(ctx - step + count) % count, :, pl.ds(column, lanes)]
            cores.append(
                push(
                    piece,
                    piece,
                    {"heads": flip(head, 1)},
                    core_send.at[step - 1, k],
                    core_recv.at[step - 1, k],
                )
            )
    tree.finish()
    for copy in own:
        copy.wait()
    for copy in copies[: count - 1] + slices + sides:
        copy.wait_send()
    for copy in copies[count - 1 :] + late + cores:
        copy.wait()


def begin(tokens, gains, ids, w_qkv, w_attn, count, groups, reach):
    rows, width = tokens.shape
    shard = w_qkv.shape[0]
    group = groups * reach
    sems = lambda *shape: [DMA(shape), DMA(shape)]
    return pl.pallas_call(
        functools.partial(begin_kernel, groups, reach, count),
        in_specs=[VMEM, VMEM, ANY, ANY, ANY],
        out_specs=[ANY, ANY, VMEM, ANY, ANY],
        out_shape=[
            jax.ShapeDtypeStruct((group, rows, width), BF),
            jax.ShapeDtypeStruct((group, 8, rows), jnp.int32),
            jax.ShapeDtypeStruct((8, width), F32),
            jax.ShapeDtypeStruct((count, shard, 3 * 128), BF),
            jax.ShapeDtypeStruct((count, shard, width), BF),
        ],
        scratch_shapes=[
            pltpu.VMEM((rows, width), BF),
            pltpu.VMEM((count, 8, gains.shape[1]), F32),
            DMA((5,)),
            *sems(group - 1),
            *sems(count - 1),
            *sems(count - 1, 3),
            *sems(count - 1),
            *sems(count - 1, max(groups // 2 - 1, 1)),
            *sems(count - 1, groups // 2),
            *Tree.scratch(3),
        ],
        compiler_params=pltpu.CompilerParams(
            collective_id=0, has_side_effects=True, vmem_limit_bytes=LIMIT
        ),
        cost_estimate=pl.CostEstimate(flops=0, bytes_accessed=30 << 20, transcendentals=0),
        name="begin",
    )(tokens, gains, ids, w_qkv, w_attn)


def attend_kernel(tile, x_ref, w_ref, cos_ref, sin_ref, mark_ref, out_ref, wide_ref, lse_ref, qkv_ref):
    count = x_ref.shape[0]
    step = pl.program_id(0)
    steps = count // tile

    @pl.when(step == 0)
    def _():
        qkv_ref[HD:QM_END, :] = mark_ref[:MARKS, :]
        qkv_ref[K_END:KM_END, :] = mark_ref[MARKS:, :]

        @pl.loop(0, steps)
        def _(i):
            at = pl.ds(pl.multiple_of(i * tile, tile), tile)
            cosine, sine = cos_ref[:, at], sin_ref[:, at]
            part = dot(w_ref[...], x_ref[at, :], 0, 1)

            def turn(value):
                front, back = value[:HALF], value[HALF:]
                return jnp.concatenate(
                    [front * cosine - back * sine, back * cosine + front * sine], axis=0
                )

            qkv_ref[:HD, at] = (turn(part[:HD]) * 0.125).astype(BF)
            qkv_ref[QM_END:K_END, at] = turn(part[HD : 2 * HD]).astype(BF)
            qkv_ref[KM_END:, at] = part[2 * HD :].astype(BF)

    here = pl.ds(pl.multiple_of(step * tile, tile), tile)
    query = qkv_ref[:QM_END, here]
    keys = [slice(j * tile, (j + 1) * tile) for j in range(steps)]
    scores = [dot(qkv_ref[QM_END:KM_END, at], query, 0, 0) for at in keys]
    top = functools.reduce(jnp.maximum, [jnp.max(s, axis=0, keepdims=True) for s in scores])
    raised = [jnp.exp(s - top) for s in scores]
    total = functools.reduce(jnp.add, [jnp.sum(e, axis=0, keepdims=True) for e in raised])
    scale = 1.0 / total
    result = jnp.zeros((HD, tile), F32)
    for j in range(steps):
        result += dot(qkv_ref[KM_END:, keys[j]], (raised[j] * scale).astype(BF), 1, 0)
    rows = out_ref.shape[2]
    for k in range(tile // rows):
        out_ref[step * (tile // rows) + k] = result[:, k * rows : (k + 1) * rows].astype(BF)
    wide_ref[:, here] = result
    lse_ref[:, here] = top + jnp.log(total)


def attend(x, w, cosine, sine, marks, rows, tile):
    count, width = x.shape
    whole = lambda *shape: pl.BlockSpec(shape, lambda i: (0,) * len(shape))
    return pl.pallas_call(
        functools.partial(attend_kernel, tile),
        grid=(count // tile,),
        in_specs=[
            whole(count, width),
            whole(*w.shape),
            whole(HALF, count),
            whole(HALF, count),
            whole(2 * MARKS, count),
        ],
        out_specs=[
            whole(count // rows, HD, rows),
            whole(HD, count),
            whole(1, count),
            whole(V_END, count),
        ],
        out_shape=[
            jax.ShapeDtypeStruct((count // rows, HD, rows), BF),
            jax.ShapeDtypeStruct((HD, count), F32),
            jax.ShapeDtypeStruct((1, count), F32),
            jax.ShapeDtypeStruct((V_END, count), BF),
        ],
        compiler_params=pltpu.CompilerParams(vmem_limit_bytes=LIMIT),
        cost_estimate=pl.CostEstimate(
            flops=count * count * HD * 8, bytes_accessed=count * 4096, transcendentals=count * count
        ),
        name="attend",
    )(x, w, cosine, sine, marks)


def middle_kernel(
    groups,
    reach,
    outgoing,
    tokens,
    d_out,
    w_attn,
    gains,
    mlp_all,
    upstream_all,
    middle,
    attended,
    land,
    mine,
    a2a_send,
    a2a_recv,
    own,
    *tree_sems,
):
    place = Place(groups, reach)
    group = groups * reach
    meet([place.member((place.idx + step) % group) for step in range(1, group)])
    copies = spread(place, outgoing, land, (a2a_send, a2a_recv, own))
    up = Tree(place, 2, d_out, upstream_all, tree_sems[5:])
    up.start()
    up.forward(1)
    for copy in copies:
        copy.wait()
    attended[...] = land[...]
    value = tokens[...].astype(F32) + dot(
        land[...].reshape(group * HD, tokens.shape[0]), w_attn[...], 0, 0
    )
    middle[...] = value
    normed, _ = norm_parts(value)
    mine[...] = (normed * gains[1:2, :]).astype(BF)
    tree = Tree(place, 2, mine, mlp_all, tree_sems[:5])
    tree.start()
    up.forward(2)
    tree.forward(1)
    tree.forward(2)
    up.finish()
    tree.finish()


def middle_step(outgoing, tokens, d_out, w_attn, gains, groups, reach):
    rows, width = tokens.shape
    group = groups * reach
    return pl.pallas_call(
        functools.partial(middle_kernel, groups, reach),
        in_specs=[ANY, VMEM, ANY, VMEM, VMEM],
        out_specs=[ANY, ANY, VMEM, VMEM],
        out_shape=[
            jax.ShapeDtypeStruct((8, rows, width), BF),
            jax.ShapeDtypeStruct((8, rows, width), BF),
            jax.ShapeDtypeStruct((rows, width), F32),
            jax.ShapeDtypeStruct((group, HD, rows), BF),
        ],
        scratch_shapes=[
            pltpu.VMEM((group, HD, rows), BF),
            pltpu.VMEM((rows, width), BF),
            DMA((group - 1,)),
            DMA((group - 1,)),
            DMA,
            *Tree.scratch(2),
            *Tree.scratch(2),
        ],
        compiler_params=pltpu.CompilerParams(
            collective_id=1, has_side_effects=True, vmem_limit_bytes=LIMIT
        ),
        cost_estimate=pl.CostEstimate(flops=1 << 28, bytes_accessed=12 << 20, transcendentals=0),
        name="middle_step",
    )(outgoing, tokens, d_out, w_attn, gains)


def turn_kernel(
    groups,
    reach,
    partial,
    middle,
    d_out,
    w_attn,
    gains,
    grads,
    columns,
    grad_middle,
    total,
    outgoing,
    branch,
    a2a_send,
    a2a_recv,
    own,
    side_send,
    side_recv,
    side_own,
    *halving,
):
    place = Place(groups, reach)
    group = groups * reach
    lanes = branch.shape[2]
    meet([place.member((place.idx + step) % group) for step in range(1, group)])
    Halving(place, 2, partial, total, halving).run()
    normed, inverse_std = norm_parts(middle[...])
    upstream = total[...]
    grad = d_out[...].astype(F32) + norm_back(upstream, normed, inverse_std, gains[1:2, :])
    grad_middle[...] = grad
    low = grad.astype(BF)
    for g in range(groups):
        branch[g] = low[:, g * lanes : (g + 1) * lanes]
    outgoing[...] = dot(w_attn[...], low, 1, 1).astype(BF).reshape(outgoing.shape)
    copies = spread(place, outgoing, grads, (a2a_send, a2a_recv, own))
    for step in range(1, groups):
        peer = (place.head + step) % groups
        copies.append(
            push(
                branch.at[peer],
                columns.at[place.head],
                {"heads": peer},
                side_send.at[step - 1],
                side_recv.at[step - 1],
            )
        )
    local = pltpu.make_async_copy(branch.at[place.head], columns.at[place.head], side_own)
    local.start()
    for copy in copies:
        copy.wait()
    local.wait()


def turn_step(partial, middle, d_out, w_attn, gains, groups, reach):
    rows, width = middle.shape
    group = groups * reach
    return pl.pallas_call(
        functools.partial(turn_kernel, groups, reach),
        in_specs=[VMEM] * 5,
        out_specs=[ANY, ANY, VMEM],
        out_shape=[
            jax.ShapeDtypeStruct((group, HD, rows), BF),
            jax.ShapeDtypeStruct((groups, rows, width // groups), BF),
            jax.ShapeDtypeStruct((rows, width), F32),
        ],
        scratch_shapes=[
            pltpu.VMEM((rows, width), F32),
            pltpu.VMEM((group, HD, rows), BF),
            pltpu.VMEM((groups, rows, width // groups), BF),
            DMA((group - 1,)),
            DMA((group - 1,)),
            DMA,
            DMA((groups - 1,)),
            DMA((groups - 1,)),
            DMA,
            *Halving.scratch(2, rows, width),
        ],
        compiler_params=pltpu.CompilerParams(
            collective_id=2, has_side_effects=True, vmem_limit_bytes=LIMIT
        ),
        cost_estimate=pl.CostEstimate(flops=1 << 28, bytes_accessed=12 << 20, transcendentals=0),
        name="turn_step",
    )(partial, middle, d_out, w_attn, gains)


def attend_back_kernel(
    groups,
    reach,
    lines,
    tile,
    qkv_ref,
    grad_ref,
    wide_ref,
    lse_ref,
    x_ref,
    w_ref,
    cos_ref,
    sin_ref,
    forward_ref,
    attn_ref,
    out_ref,
    weight_ref,
    ahead_ref,
    attn_out_ref,
    sums,
    queries,
    weight,
    attn_land,
    *sems,
):
    count = x_ref.shape[0]
    rows = grad_ref.shape[2]
    steps, per_tile = count // tile, tile // rows
    step = pl.program_id(0)
    place = Place(groups, reach)
    halving = Halving(place, 2, forward_ref, ahead_ref, sems[:7])
    swap = Lines(lines, attn_ref, attn_land, *sems[7:])

    @pl.when(step == 0)
    def _():
        meet(everyone(place, lines))
        halving.start()
        swap.start()
        sums[...] = jnp.zeros_like(sums)

    here = pl.ds(pl.multiple_of(step * tile, tile), tile)
    query = qkv_ref[:QM_END, here]
    grad = jnp.concatenate([grad_ref[step * per_tile + k] for k in range(per_tile)], axis=1)
    delta = jnp.sum(grad.astype(F32) * wide_ref[:, here], axis=0, keepdims=True)
    lse = lse_ref[:, here]
    grad_query = jnp.zeros((HD, tile), F32)
    for j in range(steps):
        keys = slice(j * tile, (j + 1) * tile)
        prob = jnp.exp(dot(qkv_ref[QM_END:KM_END, keys], query, 0, 0) - lse)
        grad_prob = dot(qkv_ref[KM_END:, keys], grad, 0, 0)
        grad_score = (prob * (grad_prob - delta)).astype(BF)
        grad_query += dot(qkv_ref[QM_END:K_END, keys], grad_score, 1, 0)
        sums[:HD, keys] += dot(query[:HD], grad_score, 1, 1)
        sums[HD:, keys] += dot(grad, prob.astype(BF), 1, 1)
    queries[:, here] = (grad_query * 0.125).astype(BF)

    for k, stage in enumerate([halving.pair, lambda: halving.halve(0), lambda: halving.halve(1)]):
        pl.when(step == min(k, steps - 1))(stage)

    @pl.when(step == steps - 1)
    def _():
        weight[...] = jnp.zeros_like(weight)

        @pl.loop(0, steps)
        def _(i):
            at = pl.ds(pl.multiple_of(i * tile, tile), tile)
            cosine, sine = cos_ref[:, at], sin_ref[:, at]

            def turn_back(value):
                front, back = value[:HALF], value[HALF:]
                return [front * cosine + back * sine, back * cosine - front * sine]

            low = lambda value: value.astype(BF).astype(F32)
            projected = jnp.concatenate(
                [
                    *turn_back(queries[:, at].astype(F32)),
                    *turn_back(low(sums[:HD, at])),
                    low(sums[HD:, at]),
                ],
                axis=0,
            ).astype(BF)
            part = dot(projected, w_ref[...], 0, 1).astype(BF)
            for k in range(per_tile):
                out_ref[i * per_tile + k] = part[k * rows : (k + 1) * rows]
            weight[...] += dot(projected, x_ref[at, :], 1, 0)

        shard = weight_ref.shape[2]
        for c in range(lines):
            weight_ref[c] = weight[:, c * shard : (c + 1) * shard].astype(BF)
        swap.finish()
        attn_out_ref[...] = functools.reduce(
            jnp.add, [attn_land[c].astype(F32) for c in range(lines)]
        ).astype(BF)
        halving.finish()


def attend_back(qkv, grad, wide, lse, x, w, cosine, sine, forward, attn, groups, reach, tile):
    count, width = x.shape
    blocks, _, rows = grad.shape
    lines, shard, lanes = attn.shape
    whole = lambda *shape: pl.BlockSpec(shape, lambda i: (0,) * len(shape))
    operands = (qkv, grad, wide, lse, x, w, cosine, sine, forward)
    return pl.pallas_call(
        functools.partial(attend_back_kernel, groups, reach, lines, tile),
        grid=(count // tile,),
        in_specs=[*[whole(*operand.shape) for operand in operands], ANY],
        out_specs=[
            whole(blocks, rows, width),
            whole(lines, 3 * HD, shard),
            whole(rows, width),
            whole(shard, lanes),
        ],
        out_shape=[
            jax.ShapeDtypeStruct((blocks, rows, width), BF),
            jax.ShapeDtypeStruct((lines, 3 * HD, shard), BF),
            jax.ShapeDtypeStruct((rows, width), F32),
            jax.ShapeDtypeStruct((shard, lanes), BF),
        ],
        scratch_shapes=[
            pltpu.VMEM((2 * HD, count), F32),
            pltpu.VMEM((HD, count), BF),
            pltpu.VMEM((3 * HD, width), F32),
            pltpu.VMEM((lines, shard, lanes), BF),
            *Halving.scratch(2, rows, width),
            *Lines.scratch(lines),
        ],
        compiler_params=pltpu.CompilerParams(
            collective_id=4, has_side_effects=True, vmem_limit_bytes=56 << 20
        ),
        cost_estimate=pl.CostEstimate(
            flops=count * count * HD * 20, bytes_accessed=count * 6144, transcendentals=count * count
        ),
        name="attend_back",
    )(*operands, attn)


class Collect:
    def __init__(self, groups, pieces, far_send, far_recv, near_send, near_recv):
        head = lax.axis_index("heads")
        self.half = half = groups // 2
        pair = {"heads": flip(head, 1)}
        self.far, self.near = [], []
        for n, (piece, where) in enumerate(pieces):
            self.far.append(
                [
                    remote(
                        piece,
                        where(head),
                        {"heads": (head + 2 * k) % groups},
                        far_send.at[n, k - 1],
                        far_recv.at[n, k - 1],
                    )
                    for k in range(1, half)
                ]
            )
            sides = [(piece, where(head))]
            for k in range(1, half):
                got = where((head - 2 * k + groups) % groups)
                sides.append((got, got))
            self.near.append(
                [
                    remote(source, target, pair, near_send.at[n, k], near_recv.at[n, k])
                    for k, (source, target) in enumerate(sides)
                ]
            )

    @staticmethod
    def scratch(count, groups):
        far, near = (count, max(groups // 2 - 1, 1)), (count, groups // 2)
        return [DMA(far), DMA(far), DMA(near), DMA(near)]

    def start(self, n):
        for copy in self.far[n]:
            copy.start()
        self.near[n][0].start()

    def forward(self, n):
        for k, copy in enumerate(self.far[n]):
            copy.wait_recv()
            self.near[n][k + 1].start()

    def finish(self):
        for copies in self.far:
            for copy in copies:
                copy.wait_send()
        for copies in self.near:
            for copy in copies:
                copy.wait()


def end_kernel(
    groups,
    reach,
    lines,
    partial,
    weight,
    mlp,
    attn,
    total,
    mlp_all,
    weight_all,
    attn_all,
    lined,
    summed,
    swap_send,
    swap_recv,
    own,
    *rest,
):
    place = Place(groups, reach)
    sub = mlp.shape[0]
    mine, head = place.ctx % sub, place.head
    meet(everyone(place, lines))
    wide = Halving(place, 3, partial, total, rest[:7])
    swap = Lines(lines, weight, lined, *rest[7:10])
    wide.start()
    swaps = []
    for step in range(1, sub):
        peer = (mine + step) % sub
        swaps.append(
            push(
                mlp.at[peer],
                mlp_all.at[mine, head],
                {"ctx": place.ctx - mine + peer},
                swap_send.at[step - 1],
                swap_recv.at[step - 1],
            )
        )
    pieces = [(mlp.at[mine], lambda h: mlp_all.at[mine, h]), (attn, lambda h: attn_all.at[h])]
    for step in range(1, sub):
        source = (mine - step + sub) % sub
        pieces.append(
            (mlp_all.at[source, head], lambda h, source=source: mlp_all.at[source, h])
        )
    pieces.append((summed, lambda h: weight_all.at[h]))
    collect = Collect(groups, pieces, *rest[10:14])
    swap.start()
    local = [
        pltpu.make_async_copy(mlp.at[mine], mlp_all.at[mine, head], own.at[0]),
        pltpu.make_async_copy(attn, attn_all.at[head], own.at[1]),
        pltpu.make_async_copy(summed, weight_all.at[head], own.at[2]),
    ]
    local[0].start()
    local[1].start()
    collect.start(0)
    collect.start(1)
    wide.pair()
    for step in range(1, sub):
        swaps[step - 1].wait_recv()
        collect.start(step + 1)
    swap.finish()
    for r in range(reach):
        summed[r] = functools.reduce(
            jnp.add, [lined[r + reach * g].astype(F32) for g in range(lines // reach)]
        ).astype(BF)
    local[2].start()
    collect.start(sub + 1)
    for step in range(3):
        wide.halve(step)
        if step == 1:
            for n in range(sub + 1):
                collect.forward(n)
    collect.forward(sub + 1)
    for copy in local:
        copy.wait()
    for copy in swaps:
        copy.wait_send()
    collect.finish()
    wide.finish()


def end_step(partial, weight, mlp, attn, groups, reach):
    rows, width = partial.shape[2:]
    lines, _, shard = weight.shape
    sub = mlp.shape[0]
    return pl.pallas_call(
        functools.partial(end_kernel, groups, reach, lines),
        in_specs=[VMEM, ANY, ANY, ANY],
        out_specs=[VMEM, ANY, ANY, ANY],
        out_shape=[
            jax.ShapeDtypeStruct((rows, width), F32),
            jax.ShapeDtypeStruct((sub, groups, *mlp.shape[1:]), BF),
            jax.ShapeDtypeStruct((groups, reach, 3 * HD, shard), BF),
            jax.ShapeDtypeStruct((groups, *attn.shape), BF),
        ],
        scratch_shapes=[
            pltpu.VMEM((lines, 3 * HD, shard), BF),
            pltpu.VMEM((reach, 3 * HD, shard), BF),
            DMA((max(sub - 1, 1),)),
            DMA((max(sub - 1, 1),)),
            DMA((3,)),
            *Halving.scratch(3, rows, width),
            *Lines.scratch(lines),
            *Collect.scratch(sub + 2, groups),
        ],
        compiler_params=pltpu.CompilerParams(
            collective_id=3, has_side_effects=True, vmem_limit_bytes=LIMIT
        ),
        cost_estimate=pl.CostEstimate(flops=0, bytes_accessed=24 << 20, transcendentals=0),
        name="end_step",
    )(partial, weight, mlp, attn)


def assemble_kernel(
    upstream,
    tokens,
    grad_middle,
    gains,
    middle,
    ahead,
    weight_all,
    attn_all,
    mlp_all,
    w_qkv,
    w_in,
    own_gains,
    result,
    grad,
    sum_qkv,
    sum_attn,
    sum_in,
    sum_out,
    gain_sums,
):
    groups, reach, _, shard = weight_all.shape
    lanes = attn_all.shape[2]
    result[...] = (middle[...] + ahead[...]).astype(BF)
    normed, inverse_std = norm_parts(tokens[...].astype(F32))
    grad[...] = grad_middle[...] + norm_back(upstream[...], normed, inverse_std, gains[0:1, :])
    for g in range(groups):
        sum_attn[:, g * lanes : (g + 1) * lanes] = attn_all[g].astype(F32)
    gain_one = jnp.zeros((shard, 128), F32)
    for third in range(3):
        part = slice(third * HD, (third + 1) * HD)
        for pair in range(H // 2):
            r, g = 2 * pair // groups, 2 * pair % groups
            tile = (
                jnp.concatenate([weight_all[g, r, part], weight_all[g + 1, r, part]], axis=0)
                .astype(F32)
                .T
            )
            at = third * H * HD + pair * 2 * HD
            sum_qkv[:, at : at + 2 * HD] = tile
            gain_one += tile * w_qkv[:, at : at + 2 * HD].astype(F32)
    gain_two = jnp.zeros((shard, 1), F32)
    for t in range(8):
        start, wide = slice_place(t)
        for half in range(2):
            piece = mlp_all[t, :, half * SLICE : half * SLICE + wide].astype(F32)
            at = half * FF + start
            sum_in[:, at : at + wide] = piece
            gain_two += jnp.sum(
                piece * w_in[:, at : at + wide].astype(F32), axis=1, keepdims=True
            )
        sum_out[start : start + wide, :] = (
            mlp_all[t, :, 2 * SLICE : 3 * SLICE].astype(F32).T[:wide]
        )
    one = jnp.sum(gain_one, axis=1, keepdims=True)
    lane = lax.broadcasted_iota(jnp.int32, (shard, 128), 1)
    both = jnp.where(lane == 0, one, gain_two).T
    gain_sums[...] = both[:8] / own_gains[...]


def assemble(upstream, tokens, grad_middle, gains, middle, ahead, weight_all, attn_all, mlp_all, w_qkv, w_in, own_gains):
    rows, width = tokens.shape
    shard = w_qkv.shape[0]
    return pl.pallas_call(
        assemble_kernel,
        in_specs=[VMEM] * 12,
        out_specs=[VMEM] * 7,
        out_shape=[
            jax.ShapeDtypeStruct((rows, width), BF),
            jax.ShapeDtypeStruct((rows, width), F32),
            jax.ShapeDtypeStruct((shard, 3 * width), F32),
            jax.ShapeDtypeStruct((shard, width), F32),
            jax.ShapeDtypeStruct((shard, 2 * FF), F32),
            jax.ShapeDtypeStruct((FF, shard), F32),
            jax.ShapeDtypeStruct((8, shard), F32),
        ],
        compiler_params=pltpu.CompilerParams(vmem_limit_bytes=LIMIT),
        cost_estimate=pl.CostEstimate(flops=1 << 24, bytes_accessed=20 << 20, transcendentals=0),
        name="assemble",
    )(upstream, tokens, grad_middle, gains, middle, ahead, weight_all, attn_all, mlp_all, w_qkv, w_in, own_gains)


def slice_start(t):
    return 128 * jnp.minimum(3 * t, 2 * t + 5)


def slice_place(t):
    start = 128 * min(3 * t, 2 * t + 5)
    return start, min(128 * min(3 * t + 3, 2 * t + 7), FF) - start


def body(count, tokens, d_out, segment_ids, position_ids, w_qkv, w_attn, w_in, w_out, gain_attn, gain_mlp):
    groups = lax.axis_size("heads")
    rows, width = tokens.shape
    shard = w_qkv.shape[0]
    reach = SEQ_MAX // (rows * groups)
    group = reach * groups
    sub = 8 // groups
    ctx, head = lax.axis_index("ctx"), lax.axis_index("heads")
    assert group == H and sub * groups == 8
    total = group * rows
    tile = 512

    def mlp_slice(value, axis, start, t):
        pads = [(0, 0), (0, 0)]
        pads[axis] = (0, SLICE)
        piece = lax.dynamic_slice_in_dim(jnp.pad(value, pads), start + slice_start(t), SLICE, axis)
        wide = jnp.minimum(slice_start(t + 1), FF) - slice_start(t)
        shape = [1, 1]
        shape[axis] = SLICE
        return jnp.where(jnp.arange(SLICE).reshape(shape) < wide, piece, jnp.zeros_like(piece))

    def mlp_part(t):
        return jnp.concatenate(
            [mlp_slice(w_in, 1, 0, t), mlp_slice(w_in, 1, FF, t), mlp_slice(w_out, 0, 0, t).T], axis=1
        )

    mine = ctx % sub
    own_part = mlp_part(mine * groups + head)
    parts = [own_part]
    for step in range(1, sub):
        send = mlp_part((mine + step) % sub * groups + head)
        got = lax.ppermute(send, "ctx", [(c, c // sub * sub + (c + step) % sub) for c in range(count)])
        parts.append(got)
    if sub == 2:
        low = jnp.where(mine == 0, parts[0], parts[1])
        high = jnp.where(mine == 0, parts[1], parts[0])
        parts = [low, high]
    lines = [list(range(k, count, sub)) for k in range(sub)]
    mlp_weights = lax.all_gather(
        jnp.concatenate(parts, axis=0), "ctx", axis=0, tiled=True, axis_index_groups=lines
    )

    gains_own = jnp.pad(jnp.stack([gain_attn, gain_mlp]).astype(F32), ((0, 6), (0, -shard % 128)))
    ids = jnp.pad(jnp.stack([position_ids, segment_ids]), ((0, 6), (0, 0)))
    input_all, ids_all, gains, slab, attn_weights = begin(
        tokens, gains_own, ids, w_qkv, w_attn, count, groups, reach
    )
    x = input_all.reshape(total, width)
    attn_weights = attn_weights.reshape(width, width)
    slab = slab.reshape(width, 3, 2, HD)
    w_head = jnp.where(head % 2 == 0, slab[:, :, 0], slab[:, :, 1]).reshape(width, 3 * HD)
    positions = ids_all[:, 0].reshape(1, total).astype(F32)
    parity = (ids_all[:, 1].reshape(1, total) % 2).astype(F32)
    freqs = jnp.power(160000.0, -(2.0 * jnp.arange(HALF, dtype=F32)) / HD)
    angles = freqs[:, None] * positions
    cosine, sine = jnp.cos(angles), jnp.sin(angles)
    blank = jnp.zeros((MARKS - 2, total), F32)
    marks = jnp.concatenate(
        [parity, 1.0 - parity, blank, (1.0 - parity) * MASKED, parity * MASKED, blank]
    ).astype(BF)

    attended, wide, lse, qkv = attend(x, w_head, cosine, sine, marks, rows, tile)
    mlp_all, upstream, middle, attended = middle_step(
        attended, tokens, d_out, attn_weights, gains, groups, reach
    )
    mlp_input = mlp_all.reshape(8 * rows, width)
    upstream = upstream.reshape(8 * rows, width)
    attended_all = lax.all_gather(attended.reshape(width, rows), "heads", axis=0)

    in_weights, out_weights = mlp_weights[:, : 2 * SLICE], mlp_weights[:, 2 * SLICE :]
    gate_up = dot(mlp_input, in_weights, 1, 0)
    gate_left, gate_right = gate_up[:, :SLICE], gate_up[:, SLICE:]
    normal_cdf = 0.5 * (1.0 + lax.erf(gate_left * 0.7071067811865476))
    gelu = gate_left * normal_cdf
    density = jnp.exp(-0.5 * gate_left * gate_left) * 0.3989422804014327
    mixed = (gelu * gate_right).astype(BF)
    grad_mixed = dot(upstream, out_weights, 1, 0)
    grad_left = grad_mixed * gate_right * (normal_cdf + gate_left * density)
    grad_gate_up = jnp.concatenate([grad_left, grad_mixed * gelu], axis=1).astype(BF)
    split = lambda value, blocks: value.astype(BF).reshape(blocks // 2, 2, rows, width)
    grad_mlp = split(dot(grad_gate_up, in_weights, 1, 1), 8)
    grad_out_part = dot(upstream, mixed, 0, 0)
    grad_in_part = dot(mlp_input, grad_gate_up, 0, 0)
    mlp_terms = jnp.concatenate([grad_in_part, grad_out_part], axis=1).astype(BF)
    grad_mlp, mlp_terms = lax.optimization_barrier((grad_mlp, mlp_terms))
    mlp_sum = lax.psum_scatter(
        mlp_terms, "ctx", scatter_dimension=0, tiled=True, axis_index_groups=lines
    ).reshape(sub, shard, 3 * SLICE)
    grad_heads, branch, grad_middle = turn_step(
        grad_mlp, middle, d_out, attn_weights, gains, groups, reach
    )
    attn_part = jnp.einsum("gdt,gtn->dn", attended_all, branch, preferred_element_type=F32)
    attn_part = attn_part.astype(BF).reshape(count, shard, width // groups)
    forward = split(dot(mixed, out_weights, 1, 1), 8)
    grad_input_parts, weight, ahead, attn_sum = attend_back(
        qkv, grad_heads, wide, lse, x, w_head, cosine, sine, forward, attn_part, groups, reach, tile
    )
    upstream_in, mlp_all, weight_all, attn_all = end_step(
        split(grad_input_parts, group), weight, mlp_sum, attn_sum, groups, reach
    )
    result, grad_input, sum_qkv, sum_attn, sum_in, sum_out, gain_sums = assemble(
        upstream_in,
        tokens,
        grad_middle,
        gains,
        middle,
        ahead,
        weight_all,
        attn_all,
        mlp_all.reshape(8, shard, 3 * SLICE),
        w_qkv,
        w_in,
        jnp.pad(gains_own[:2, :shard], ((0, 6), (0, 0)), constant_values=1.0),
    )
    return (
        result,
        grad_input,
        sum_qkv,
        sum_attn,
        sum_in,
        sum_out,
        gain_sums[0],
        gain_sums[1],
    )


def solution(mesh):
    return jax.shard_map(
        functools.partial(body, mesh.shape["ctx"]),
        mesh=mesh,
        in_specs=(
            P(("ctx", "heads"), None),
            P(("ctx", "heads"), None),
            P(("ctx", "heads")),
            P(("ctx", "heads")),
            P("ctx", None),
            P("ctx", None),
            P("ctx", None),
            P(None, "ctx"),
            P("ctx"),
            P("ctx"),
        ),
        out_specs=(
            P(("ctx", "heads"), None),
            P(("ctx", "heads"), None),
            P("ctx", None),
            P("ctx", None),
            P("ctx", None),
            P(None, "ctx"),
            P("ctx"),
            P("ctx"),
        ),
        check_vma=False,
    )
```

```python
import functools

import jax
import jax.numpy as jnp
from jax import lax
from jax.experimental import pallas as pl
from jax.experimental.pallas import tpu as pltpu
from jax.sharding import PartitionSpec as P

H = 16
HD = 64
HALF = HD // 2
FF = 2624
SEQ_MAX = 2048
MASKED = -1e30
MARKS = 16
QM_END = HD + MARKS
K_END = QM_END + HD
KM_END = K_END + MARKS
V_END = KM_END + HD
SLICE = 384
BF = jnp.bfloat16
F32 = jnp.float32
MESH = pl.DeviceIdType.MESH
VMEM = pl.BlockSpec(memory_space=pltpu.VMEM)
ANY = pl.BlockSpec(memory_space=pl.ANY)
DMA = pltpu.SemaphoreType.DMA
LIMIT = 48 << 20


def dot(left, right, left_dim, right_dim):
    return lax.dot_general(
        left, right, (((left_dim,), (right_dim,)), ((), ())), preferred_element_type=F32
    )


def norm_parts(values):
    average = jnp.mean(values, axis=-1, keepdims=True)
    centred = values - average
    inverse_std = lax.rsqrt(jnp.mean(centred * centred, axis=-1, keepdims=True) + 1e-05)
    return centred * inverse_std, inverse_std


def norm_back(upstream, normed, inverse_std, gain):
    scaled = upstream * gain
    return inverse_std * (
        scaled
        - jnp.mean(scaled, axis=-1, keepdims=True)
        - normed * jnp.mean(scaled * normed, axis=-1, keepdims=True)
    )


def flip(value, bit):
    return value + bit - 2 * bit * (value // bit % 2)


class Place:
    def __init__(self, groups, reach):
        self.groups, self.reach = groups, reach
        self.ctx = lax.axis_index("ctx")
        self.head = lax.axis_index("heads")
        self.local = self.ctx % reach
        self.base = self.ctx - self.local
        self.idx = self.local * groups + self.head

    def member(self, j):
        return {"ctx": self.base + j // self.groups, "heads": j % self.groups}


def meet(devices):
    barrier = pltpu.get_barrier_semaphore()
    for device in devices:
        pl.semaphore_signal(barrier, inc=1, device_id=device, device_id_type=MESH)
    pl.semaphore_wait(barrier, len(devices))


def remote(source, target, device, send, recv):
    return pltpu.make_async_remote_copy(
        src_ref=source,
        dst_ref=target,
        send_sem=send,
        recv_sem=recv,
        device_id=device,
        device_id_type=MESH,
    )


def push(*operands):
    copy = remote(*operands)
    copy.start()
    return copy


def tree_parts(axes, rows):
    part = -(-rows // axes // 16) * 16
    starts = [min(part * a, rows) for a in range(axes + 1)]
    return [(starts[a], starts[a + 1] - starts[a]) for a in range(axes)]


class Tree:
    def __init__(self, place, axes, source, target, sems):
        self.place, self.axes, self.source, self.target = place, axes, source, target
        self.send, self.recv, self.core_send, self.core_recv, self.own = sems
        self.slots = 2 << axes
        self.levels, self.cores = [], []

    @staticmethod
    def scratch(axes):
        far, near = axes * axes, axes * axes + 1
        return [DMA((far,)), DMA((far,)), DMA((near,)), DMA((near,)), DMA]

    def origin(self, level, first):
        value = self.place.idx
        for k in range(level):
            value = flip(value, 2 << ((first + k) % self.axes))
        return value % self.slots

    def neighbour(self, axis):
        return self.place.member(flip(self.place.idx, 2 << (axis % self.axes)))

    def piece(self, slot, part):
        return self.target.at[slot] if part is None else self.target.at[slot, pl.ds(*part)]

    def to_core(self, source, slot, part):
        at = len(self.cores)
        self.cores.append(
            push(
                source,
                self.piece(slot, part),
                self.place.member(flip(self.place.idx, 1)),
                self.core_send.at[at],
                self.core_recv.at[at],
            )
        )

    def start(self):
        me = self.place.idx % self.slots
        self.levels.append(
            [
                push(
                    self.source, self.target.at[me], self.neighbour(a), self.send.at[a], self.recv.at[a]
                )
                for a in range(self.axes)
            ]
        )
        self.to_core(self.source, me, None)
        self.local = pltpu.make_async_copy(self.source, self.target.at[me], self.own)
        self.local.start()

    def forward(self, level):
        axes = self.axes
        parts = tree_parts(axes, self.target.shape[1])
        onward = []
        for a in range(axes):
            self.levels[level - 1][a].wait_recv()
            slot = self.origin(level, a)
            if level < axes:
                part = parts[a] if level + 1 == axes else None
                at = level * axes + a
                piece = self.piece(slot, part)
                onward.append(
                    push(piece, piece, self.neighbour(a + level), self.send.at[at], self.recv.at[at])
                )
                self.to_core(self.target.at[slot], slot, None)
            else:
                self.to_core(self.piece(slot, parts[a]), slot, parts[a])
        self.levels.append(onward)

    def finish(self):
        self.local.wait()
        for level in self.levels:
            for copy in level:
                copy.wait_send()
        for copy in self.cores:
            copy.wait()


class Halving:
    def __init__(self, place, axes, value, result, scratch):
        self.axes, self.value, self.result = axes, value, result
        self.other, self.held, self.land, send, recv, send0, recv0 = scratch
        self.blocks = 1 << axes
        width = value.shape[-1]
        part = -(-width // axes // 128) * 128
        starts = [min(part * a, width) for a in range(axes + 1)]
        self.columns = [pl.ds(starts[a], starts[a + 1] - starts[a]) for a in range(axes)]
        self.core = place.idx % 2
        self.chip = place.idx // 2 % self.blocks
        self.sources = []
        for j in range(self.blocks):
            k = self.chip
            for a in range(axes):
                if j >> a & 1:
                    k = flip(k, 1 << a)
            self.sources.append(k)
        self.first, self.copies = [], {}
        for p in range(axes):
            self.first.append(
                remote(
                    value.at[:, 1 - self.core, :, self.columns[p]],
                    self.other.at[:, :, self.columns[p]],
                    place.member(flip(place.idx, 1)),
                    send0.at[p],
                    recv0.at[p],
                )
            )
            for step in range(axes):
                bit, sent = self.sent(p, step)
                for j in sent:
                    self.copies[p, j] = remote(
                        self.held.at[j, :, self.columns[p]],
                        self.land.at[j, :, self.columns[p]],
                        place.member(flip(place.idx, 2 * bit)),
                        send.at[p, j],
                        recv.at[p, j],
                    )

    @staticmethod
    def scratch(axes, rows, width):
        blocks = 1 << axes
        return [
            pltpu.VMEM((blocks, rows, width), BF),
            pltpu.VMEM((blocks, rows, width), BF),
            pltpu.VMEM((blocks, rows, width), BF),
            DMA((axes, blocks)),
            DMA((axes, blocks)),
            DMA((axes,)),
            DMA((axes,)),
        ]

    def sent(self, part, step):
        seen = [1 << ((part + s) % self.axes) for s in range(step)]
        bit = 1 << ((part + step) % self.axes)
        return bit, [j for j in range(self.blocks) if j & bit and not any(j & s for s in seen)]

    def start(self):
        for copy in self.first:
            copy.start()

    def pair(self):
        for p in range(self.axes):
            cols = self.columns[p]
            self.first[p].wait_recv()
            _, early = self.sent(p, 0)
            for j in early + [j for j in range(self.blocks) if j not in early]:
                k = self.sources[j]
                self.held[j, :, cols] = (
                    self.value[k, self.core, :, cols].astype(F32) + self.other[k, :, cols].astype(F32)
                ).astype(BF)
                if j in early:
                    self.copies[p, j].start()

    def halve(self, step):
        for p in range(self.axes):
            cols = self.columns[p]
            bit, arrived = self.sent(p, step)
            onward = self.sent(p, step + 1)[1] if step + 1 < self.axes else []
            for j in sorted(arrived, key=lambda j: (j - bit) not in onward):
                self.copies[p, j].wait_recv()
                k = j - bit
                total = self.held[k, :, cols].astype(F32) + self.land[j, :, cols].astype(F32)
                if step + 1 < self.axes:
                    self.held[k, :, cols] = total.astype(BF)
                    if k in onward:
                        self.copies[p, k].start()
                else:
                    self.result[:, cols] = total

    def run(self):
        self.start()
        self.pair()
        for step in range(self.axes):
            self.halve(step)
        self.finish()

    def finish(self):
        for copy in self.first:
            copy.wait_send()
        for copy in self.copies.values():
            copy.wait_send()


class Lines:
    def __init__(self, count, source, target, send, recv, own):
        me = lax.axis_index("ctx")
        self.copies = [pltpu.make_async_copy(source.at[me], target.at[me], own)]
        for step in range(1, count):
            peer = (me + step) % count
            self.copies.append(
                remote(source.at[peer], target.at[me], {"ctx": peer}, send.at[step - 1], recv.at[step - 1])
            )

    @staticmethod
    def scratch(count):
        return [DMA((count - 1,)), DMA((count - 1,)), DMA]

    def start(self):
        for copy in self.copies:
            copy.start()

    def finish(self):
        for copy in self.copies:
            copy.wait()


def everyone(place, count):
    group = place.reach * place.groups
    mates = [place.member((place.idx + step) % group) for step in range(1, group)]
    outside = [{"ctx": (place.base + place.reach + step) % count} for step in range(count - place.reach)]
    return mates + outside


def spread(place, source, target, sems, me=None):
    send, recv, own = sems
    count = target.shape[0]
    copies = []
    for step in range(1, count):
        peer = (place.idx + step) % count
        copies.append(
            push(
                source.at[peer],
                target.at[place.idx],
                place.member(peer),
                send.at[step - 1],
                recv.at[step - 1],
            )
        )
    local = pltpu.make_async_copy(source.at[place.idx], target.at[place.idx], own)
    local.start()
    copies.append(local)
    return copies


def begin_kernel(
    groups,
    reach,
    count,
    tokens,
    gains,
    ids,
    w_qkv,
    w_attn,
    mlp,
    input_all,
    ids_all,
    gains_all,
    slab,
    attn_part,
    mlp_pair,
    mine,
    gain_land,
    own_sems,
    ids_send,
    ids_recv,
    gain_send,
    gain_recv,
    slab_send,
    slab_recv,
    wide_send,
    wide_recv,
    swap_send,
    swap_recv,
    core_send,
    core_recv,
    *tree_sems,
):
    place = Place(groups, reach)
    group = reach * groups
    ctx, head, idx = place.ctx, place.head, place.idx
    shard = w_qkv.shape[0]
    sub = mlp.shape[0]
    ring = count // sub
    side, spot = ctx % sub, ctx // sub
    lanes = attn_part.shape[2]
    core = {"heads": flip(head, 1)}
    mates = [place.member((idx + step) % group) for step in range(1, group)]
    lines = [{"ctx": (ctx + step) % count} for step in range(1, count)]
    meet(everyone(place, count))
    first = [
        push(gains, gain_land.at[ctx], lines[step - 1], gain_send.at[step - 1], gain_recv.at[step - 1])
        for step in range(1, count)
    ]
    small = [
        push(ids, ids_all.at[idx], mates[step - 1], ids_send.at[step - 1], ids_recv.at[step - 1])
        for step in range(1, group)
    ]
    half = pl.ds(pl.multiple_of(head % 2 * (shard // 2), 16), shard // 2)
    thirds = []
    for step in range(1, count):
        peer = (ctx + step) % count
        column = ((peer % reach) * groups + head) // 2 * 128
        for third in range(3):
            start = pl.multiple_of(third * 1024 + column, 128)
            thirds.append(
                push(
                    w_qkv.at[half, pl.ds(start, 128)],
                    slab.at[ctx, half, pl.ds(third * 128, 128)],
                    lines[step - 1],
                    slab_send.at[step - 1, third],
                    slab_recv.at[step - 1, third],
                )
            )
    gain_land[ctx] = gains[...]
    across = pl.ds(pl.multiple_of(head * lanes, 128), lanes)
    own = [
        pltpu.make_async_copy(ids, ids_all.at[idx], own_sems.at[3]),
        pltpu.make_async_copy(w_attn.at[:, across], attn_part.at[spot], own_sems.at[4]),
        pltpu.make_async_copy(mlp.at[side], mlp_pair.at[side], own_sems.at[5]),
    ]
    for third in range(3):
        start = pl.multiple_of(third * 1024 + idx // 2 * 128, 128)
        own.append(
            pltpu.make_async_copy(
                w_qkv.at[half, pl.ds(start, 128)],
                slab.at[ctx, half, pl.ds(third * 128, 128)],
                own_sems.at[third],
            )
        )
    for copy in own:
        copy.start()
    for copy in first:
        copy.wait_recv()
    gain, gain_two = (
        jnp.concatenate([gain_land[c, k : k + 1, :shard] for c in range(count)], axis=1)
        for k in range(2)
    )
    normed, _ = norm_parts(tokens[...].astype(F32))
    mine[...] = (normed * gain).astype(BF)
    tree = Tree(place, 3, mine, input_all, tree_sems)
    tree.start()
    gains_all[0:1, :] = gain
    gains_all[1:2, :] = gain_two
    late = []
    for step in range(1, sub):
        peer = (side + step) % sub
        late.append(
            push(
                mlp.at[peer],
                mlp_pair.at[side],
                {"ctx": ctx - side + peer},
                swap_send.at[step - 1],
                swap_recv.at[step - 1],
            )
        )
    for step in range(1, ring):
        late.append(
            push(
                w_attn.at[:, across],
                attn_part.at[spot],
                {"ctx": (spot + step) % ring * sub + side},
                wide_send.at[step - 1],
                wide_recv.at[step - 1],
            )
        )
    tree.forward(1)
    for copy in own:
        copy.wait()
    for copy in thirds:
        copy.wait_recv()
    late.append(push(slab.at[:, half], slab.at[:, half], core, core_send, core_recv))
    tree.forward(2)
    tree.forward(3)
    tree.finish()
    for copy in first + thirds:
        copy.wait_send()
    for copy in small + late:
        copy.wait()


def begin(tokens, gains, ids, w_qkv, w_attn, mlp, count, groups, reach):
    rows, width = tokens.shape
    shard = w_qkv.shape[0]
    sub = mlp.shape[0]
    ring = count // sub
    group = groups * reach
    sems = lambda *shape: [DMA(shape), DMA(shape)]
    return pl.pallas_call(
        functools.partial(begin_kernel, groups, reach, count),
        in_specs=[VMEM, VMEM, ANY, ANY, ANY, ANY],
        out_specs=[ANY, ANY, VMEM, ANY, ANY, ANY],
        out_shape=[
            jax.ShapeDtypeStruct((group, rows, width), BF),
            jax.ShapeDtypeStruct((group, 8, rows), jnp.int32),
            jax.ShapeDtypeStruct((8, width), F32),
            jax.ShapeDtypeStruct((count, shard, 3 * 128), BF),
            jax.ShapeDtypeStruct((ring, shard, width // groups), BF),
            jax.ShapeDtypeStruct(mlp.shape, BF),
        ],
        scratch_shapes=[
            pltpu.VMEM((rows, width), BF),
            pltpu.VMEM((count, 8, gains.shape[1]), F32),
            DMA((6,)),
            *sems(group - 1),
            *sems(count - 1),
            *sems(count - 1, 3),
            *sems(ring - 1),
            *sems(max(sub - 1, 1)),
            DMA,
            DMA,
            *Tree.scratch(3),
        ],
        compiler_params=pltpu.CompilerParams(
            collective_id=0, has_side_effects=True, vmem_limit_bytes=LIMIT
        ),
        cost_estimate=pl.CostEstimate(flops=0, bytes_accessed=30 << 20, transcendentals=0),
        name="begin",
    )(tokens, gains, ids, w_qkv, w_attn, mlp)


class Ring:
    def __init__(self, ring, sub, blocks, arrivals, send, recv):
        ctx = lax.axis_index("ctx")
        right = {"ctx": (ctx // sub + 1) % ring * sub + ctx % sub}
        self.copies = [
            remote(source, target, right, send.at[s], recv.at[s])
            for s, (source, target) in enumerate(zip(blocks, arrivals))
        ]

    def start(self, s):
        if s:
            self.copies[s - 1].wait_recv()
        self.copies[s].start()

    def finish(self):
        self.copies[-1].wait_recv()
        for copy in self.copies:
            copy.wait_send()


class Columns:
    def __init__(self, place, part, whole, own, side_send, side_recv, far_send, far_recv, near_send, near_recv):
        groups = place.groups
        _, sub, _, width = whole.shape
        lanes = width // groups
        head, side = place.head, place.ctx % sub
        half = groups // 2
        at = lambda h: pl.ds(pl.multiple_of(h * lanes, 128), lanes)
        self.own = pltpu.make_async_copy(part, whole.at[:, side, :, at(head)], own)
        self.sides, self.far, self.near = [], [], []
        for step in range(1, sub):
            peer = (side + step) % sub
            self.sides.append(
                remote(
                    part,
                    whole.at[:, side, :, at(head)],
                    {"ctx": place.ctx - side + peer},
                    side_send.at[step - 1],
                    side_recv.at[step - 1],
                )
            )
        for step in range(sub):
            x = (side - step + sub) % sub
            here = whole.at[:, x, :, at(head)]
            self.far.append(
                [
                    remote(
                        here if step else part,
                        here,
                        {"heads": (head + 2 * k) % groups},
                        far_send.at[step, k - 1],
                        far_recv.at[step, k - 1],
                    )
                    for k in range(1, half)
                ]
            )
        for k in range(half):
            here = whole.at[:, :, :, at((head - 2 * k + groups) % groups)]
            self.near.append(
                remote(here, here, {"heads": flip(head, 1)}, near_send.at[k], near_recv.at[k])
            )

    @staticmethod
    def scratch(sub, groups):
        side, far, near = (max(sub - 1, 1),), (sub, max(groups // 2 - 1, 1)), (groups // 2,)
        return [DMA, DMA(side), DMA(side), DMA(far), DMA(far), DMA(near), DMA(near)]

    def start(self):
        self.own.start()
        for copy in self.sides + self.far[0]:
            copy.start()

    def forward(self):
        for step, copy in enumerate(self.sides):
            copy.wait_recv()
            for far in self.far[step + 1]:
                far.start()

    def across(self):
        self.own.wait()
        self.near[0].start()
        for k in range(1, len(self.near)):
            for far in self.far:
                far[k - 1].wait_recv()
            self.near[k].start()

    def finish(self):
        for copies in [self.sides, *self.far]:
            for copy in copies:
                copy.wait_send()
        for copy in self.near:
            copy.wait()


def attend_kernel(
    groups,
    reach,
    lines,
    tile,
    x_ref,
    w_ref,
    cos_ref,
    sin_ref,
    mark_ref,
    attn_part,
    mlp_pair,
    out_ref,
    wide_ref,
    lse_ref,
    qkv_ref,
    attn_all,
    mlp_near,
    ring_send,
    ring_recv,
    *sems,
):
    count = x_ref.shape[0]
    step = pl.program_id(0)
    steps = count // tile
    place = Place(groups, reach)
    sub = mlp_pair.shape[0]
    early = mlp_near.shape[0]
    ring = Ring(
        lines // sub,
        sub,
        [mlp_pair] + [mlp_near.at[s] for s in range(early - 1)],
        [mlp_near.at[s] for s in range(early)],
        ring_send,
        ring_recv,
    )
    columns = Columns(place, attn_part, attn_all, *sems)

    @pl.when(step == 0)
    def _():
        meet(everyone(place, lines))
        ring.start(0)
        columns.start()
        qkv_ref[HD:QM_END, :] = mark_ref[:MARKS, :]
        qkv_ref[K_END:KM_END, :] = mark_ref[MARKS:, :]

        @pl.loop(0, steps)
        def _(i):
            at = pl.ds(pl.multiple_of(i * tile, tile), tile)
            cosine, sine = cos_ref[:, at], sin_ref[:, at]
            part = dot(w_ref[...], x_ref[at, :], 0, 1)

            def turn(value):
                front, back = value[:HALF], value[HALF:]
                return jnp.concatenate(
                    [front * cosine - back * sine, back * cosine + front * sine], axis=0
                )

            qkv_ref[:HD, at] = (turn(part[:HD]) * 0.125).astype(BF)
            qkv_ref[QM_END:K_END, at] = turn(part[HD : 2 * HD]).astype(BF)
            qkv_ref[KM_END:, at] = part[2 * HD :].astype(BF)

    here = pl.ds(pl.multiple_of(step * tile, tile), tile)
    query = qkv_ref[:QM_END, here]
    keys = [slice(j * tile, (j + 1) * tile) for j in range(steps)]
    scores = [dot(qkv_ref[QM_END:KM_END, at], query, 0, 0) for at in keys]
    top = functools.reduce(jnp.maximum, [jnp.max(s, axis=0, keepdims=True) for s in scores])
    raised = [jnp.exp(s - top) for s in scores]
    total = functools.reduce(jnp.add, [jnp.sum(e, axis=0, keepdims=True) for e in raised])
    scale = 1.0 / total
    result = jnp.zeros((HD, tile), F32)
    for j in range(steps):
        result += dot(qkv_ref[KM_END:, keys[j]], (raised[j] * scale).astype(BF), 1, 0)
    rows = out_ref.shape[2]
    for k in range(tile // rows):
        out_ref[step * (tile // rows) + k] = result[:, k * rows : (k + 1) * rows].astype(BF)
    wide_ref[:, here] = result
    lse_ref[:, here] = top + jnp.log(total)

    pl.when(step == min(1, steps - 1))(columns.forward)

    @pl.when(step == steps - 1)
    def _():
        columns.across()
        for s in range(1, early):
            ring.start(s)
        ring.finish()
        columns.finish()


def attend(x, w, cosine, sine, marks, attn_part, mlp_pair, lines, groups, reach, rows, tile):
    count, width = x.shape
    sub = mlp_pair.shape[0]
    ring, shard, _ = attn_part.shape
    early = (ring - 1) // 3
    whole = lambda *shape: pl.BlockSpec(shape, lambda i: (0,) * len(shape))
    return pl.pallas_call(
        functools.partial(attend_kernel, groups, reach, lines, tile),
        grid=(count // tile,),
        in_specs=[
            whole(count, width),
            whole(*w.shape),
            whole(HALF, count),
            whole(HALF, count),
            whole(2 * MARKS, count),
            ANY,
            ANY,
        ],
        out_specs=[
            whole(count // rows, HD, rows),
            whole(HD, count),
            whole(1, count),
            whole(V_END, count),
            ANY,
            ANY,
        ],
        out_shape=[
            jax.ShapeDtypeStruct((count // rows, HD, rows), BF),
            jax.ShapeDtypeStruct((HD, count), F32),
            jax.ShapeDtypeStruct((1, count), F32),
            jax.ShapeDtypeStruct((V_END, count), BF),
            jax.ShapeDtypeStruct((ring, sub, shard, width), BF),
            jax.ShapeDtypeStruct((early, *mlp_pair.shape), BF),
        ],
        scratch_shapes=[DMA((early,)), DMA((early,)), *Columns.scratch(sub, groups)],
        compiler_params=pltpu.CompilerParams(
            collective_id=5, has_side_effects=True, vmem_limit_bytes=LIMIT
        ),
        cost_estimate=pl.CostEstimate(
            flops=count * count * HD * 8, bytes_accessed=count * 4096, transcendentals=count * count
        ),
        name="attend",
    )(x, w, cosine, sine, marks, attn_part, mlp_pair)


def middle_kernel(
    groups,
    reach,
    lines,
    outgoing,
    tokens,
    d_out,
    w_attn,
    gains,
    mlp_pair,
    mlp_near,
    mlp_all,
    upstream_all,
    middle,
    attended,
    mlp_weights,
    land,
    mine,
    a2a_send,
    a2a_recv,
    own,
    ring_send,
    ring_recv,
    ring_own,
    *tree_sems,
):
    place = Place(groups, reach)
    group = groups * reach
    early, sub = mlp_near.shape[:2]
    count = lines // sub
    spot = place.ctx // sub
    slot = lambda s: mlp_weights.at[(spot - s + count) % count]
    left = count - 1 - early
    ring = Ring(
        count,
        sub,
        [mlp_near.at[early - 1]] + [slot(early + s) for s in range(1, left)],
        [mlp_weights.at[(spot - early - s + count) % count] for s in range(left)],
        ring_send,
        ring_recv,
    )
    local = [pltpu.make_async_copy(mlp_pair, slot(0), ring_own.at[0])]
    for s in range(early):
        local.append(pltpu.make_async_copy(mlp_near.at[s], slot(s + 1), ring_own.at[s + 1]))
    meet(everyone(place, lines))
    copies = spread(place, outgoing, land, (a2a_send, a2a_recv, own))
    ring.start(0)
    up = Tree(place, 2, d_out, upstream_all, tree_sems[5:])
    up.start()
    for copy in local:
        copy.start()
    for copy in copies:
        copy.wait()
    attended[...] = land[...]
    value = tokens[...].astype(F32) + dot(
        land[...].reshape(group * HD, tokens.shape[0]), w_attn[...], 0, 0
    )
    middle[...] = value
    normed, _ = norm_parts(value)
    mine[...] = (normed * gains[1:2, :]).astype(BF)
    tree = Tree(place, 2, mine, mlp_all, tree_sems[:5])
    tree.start()
    up.forward(1)
    for s in range(1, left):
        ring.start(s)
    tree.forward(1)
    up.forward(2)
    tree.forward(2)
    up.finish()
    tree.finish()
    for copy in local:
        copy.wait()
    ring.finish()


def middle_step(outgoing, tokens, d_out, w_attn, gains, mlp_pair, mlp_near, lines, groups, reach):
    rows, width = tokens.shape
    group = groups * reach
    early, sub = mlp_near.shape[:2]
    ring = lines // sub
    left = ring - 1 - early
    return pl.pallas_call(
        functools.partial(middle_kernel, groups, reach, lines),
        in_specs=[ANY, VMEM, ANY, VMEM, VMEM, ANY, ANY],
        out_specs=[ANY, ANY, VMEM, VMEM, ANY],
        out_shape=[
            jax.ShapeDtypeStruct((8, rows, width), BF),
            jax.ShapeDtypeStruct((8, rows, width), BF),
            jax.ShapeDtypeStruct((rows, width), F32),
            jax.ShapeDtypeStruct((group, HD, rows), BF),
            jax.ShapeDtypeStruct((ring, *mlp_pair.shape), BF),
        ],
        scratch_shapes=[
            pltpu.VMEM((group, HD, rows), BF),
            pltpu.VMEM((rows, width), BF),
            DMA((group - 1,)),
            DMA((group - 1,)),
            DMA,
            DMA((left,)),
            DMA((left,)),
            DMA((early + 1,)),
            *Tree.scratch(2),
            *Tree.scratch(2),
        ],
        compiler_params=pltpu.CompilerParams(
            collective_id=1, has_side_effects=True, vmem_limit_bytes=LIMIT
        ),
        cost_estimate=pl.CostEstimate(flops=1 << 28, bytes_accessed=12 << 20, transcendentals=0),
        name="middle_step",
    )(outgoing, tokens, d_out, w_attn, gains, mlp_pair, mlp_near)


def turn_kernel(
    groups,
    reach,
    partial,
    middle,
    d_out,
    w_attn,
    gains,
    grads,
    columns,
    grad_middle,
    total,
    outgoing,
    branch,
    a2a_send,
    a2a_recv,
    own,
    side_send,
    side_recv,
    side_own,
    *halving,
):
    place = Place(groups, reach)
    group = groups * reach
    lanes = branch.shape[2]
    meet([place.member((place.idx + step) % group) for step in range(1, group)])
    Halving(place, 2, partial, total, halving).run()
    normed, inverse_std = norm_parts(middle[...])
    upstream = total[...]
    grad = d_out[...].astype(F32) + norm_back(upstream, normed, inverse_std, gains[1:2, :])
    grad_middle[...] = grad
    low = grad.astype(BF)
    for g in range(groups):
        branch[g] = low[:, g * lanes : (g + 1) * lanes]
    outgoing[...] = dot(w_attn[...], low, 1, 1).astype(BF).reshape(outgoing.shape)
    copies = spread(place, outgoing, grads, (a2a_send, a2a_recv, own))
    for step in range(1, groups):
        peer = (place.head + step) % groups
        copies.append(
            push(
                branch.at[peer],
                columns.at[place.head],
                {"heads": peer},
                side_send.at[step - 1],
                side_recv.at[step - 1],
            )
        )
    local = pltpu.make_async_copy(branch.at[place.head], columns.at[place.head], side_own)
    local.start()
    for copy in copies:
        copy.wait()
    local.wait()


def turn_step(partial, middle, d_out, w_attn, gains, groups, reach):
    rows, width = middle.shape
    group = groups * reach
    return pl.pallas_call(
        functools.partial(turn_kernel, groups, reach),
        in_specs=[VMEM] * 5,
        out_specs=[ANY, ANY, VMEM],
        out_shape=[
            jax.ShapeDtypeStruct((group, HD, rows), BF),
            jax.ShapeDtypeStruct((groups, rows, width // groups), BF),
            jax.ShapeDtypeStruct((rows, width), F32),
        ],
        scratch_shapes=[
            pltpu.VMEM((rows, width), F32),
            pltpu.VMEM((group, HD, rows), BF),
            pltpu.VMEM((groups, rows, width // groups), BF),
            DMA((group - 1,)),
            DMA((group - 1,)),
            DMA,
            DMA((groups - 1,)),
            DMA((groups - 1,)),
            DMA,
            *Halving.scratch(2, rows, width),
        ],
        compiler_params=pltpu.CompilerParams(
            collective_id=2, has_side_effects=True, vmem_limit_bytes=LIMIT
        ),
        cost_estimate=pl.CostEstimate(flops=1 << 28, bytes_accessed=12 << 20, transcendentals=0),
        name="turn_step",
    )(partial, middle, d_out, w_attn, gains)


def attend_back_kernel(
    groups,
    reach,
    lines,
    tile,
    qkv_ref,
    grad_ref,
    wide_ref,
    lse_ref,
    x_ref,
    w_ref,
    cos_ref,
    sin_ref,
    forward_ref,
    attn_ref,
    out_ref,
    weight_ref,
    ahead_ref,
    attn_out_ref,
    sums,
    queries,
    weight,
    attn_land,
    *sems,
):
    count = x_ref.shape[0]
    rows = grad_ref.shape[2]
    steps, per_tile = count // tile, tile // rows
    step = pl.program_id(0)
    place = Place(groups, reach)
    halving = Halving(place, 2, forward_ref, ahead_ref, sems[:7])
    swap = Lines(lines, attn_ref, attn_land, *sems[7:])

    @pl.when(step == 0)
    def _():
        meet(everyone(place, lines))
        halving.start()
        swap.start()
        sums[...] = jnp.zeros_like(sums)

    here = pl.ds(pl.multiple_of(step * tile, tile), tile)
    query = qkv_ref[:QM_END, here]
    grad = jnp.concatenate([grad_ref[step * per_tile + k] for k in range(per_tile)], axis=1)
    delta = jnp.sum(grad.astype(F32) * wide_ref[:, here], axis=0, keepdims=True)
    lse = lse_ref[:, here]
    grad_query = jnp.zeros((HD, tile), F32)
    for j in range(steps):
        keys = slice(j * tile, (j + 1) * tile)
        prob = jnp.exp(dot(qkv_ref[QM_END:KM_END, keys], query, 0, 0) - lse)
        grad_prob = dot(qkv_ref[KM_END:, keys], grad, 0, 0)
        grad_score = (prob * (grad_prob - delta)).astype(BF)
        grad_query += dot(qkv_ref[QM_END:K_END, keys], grad_score, 1, 0)
        sums[:HD, keys] += dot(query[:HD], grad_score, 1, 1)
        sums[HD:, keys] += dot(grad, prob.astype(BF), 1, 1)
    queries[:, here] = (grad_query * 0.125).astype(BF)

    for k, stage in enumerate([halving.pair, lambda: halving.halve(0), lambda: halving.halve(1)]):
        pl.when(step == min(k, steps - 1))(stage)

    @pl.when(step == steps - 1)
    def _():
        weight[...] = jnp.zeros_like(weight)

        @pl.loop(0, steps)
        def _(i):
            at = pl.ds(pl.multiple_of(i * tile, tile), tile)
            cosine, sine = cos_ref[:, at], sin_ref[:, at]

            def turn_back(value):
                front, back = value[:HALF], value[HALF:]
                return [front * cosine + back * sine, back * cosine - front * sine]

            low = lambda value: value.astype(BF).astype(F32)
            projected = jnp.concatenate(
                [
                    *turn_back(queries[:, at].astype(F32)),
                    *turn_back(low(sums[:HD, at])),
                    low(sums[HD:, at]),
                ],
                axis=0,
            ).astype(BF)
            part = dot(projected, w_ref[...], 0, 1).astype(BF)
            for k in range(per_tile):
                out_ref[i * per_tile + k] = part[k * rows : (k + 1) * rows]
            weight[...] += dot(projected, x_ref[at, :], 1, 0)

        shard = weight_ref.shape[2]
        for c in range(lines):
            weight_ref[c] = weight[:, c * shard : (c + 1) * shard].astype(BF)
        swap.finish()
        attn_out_ref[...] = functools.reduce(
            jnp.add, [attn_land[c].astype(F32) for c in range(lines)]
        ).astype(BF)
        halving.finish()


def attend_back(qkv, grad, wide, lse, x, w, cosine, sine, forward, attn, groups, reach, tile):
    count, width = x.shape
    blocks, _, rows = grad.shape
    lines, shard, lanes = attn.shape
    whole = lambda *shape: pl.BlockSpec(shape, lambda i: (0,) * len(shape))
    operands = (qkv, grad, wide, lse, x, w, cosine, sine, forward)
    return pl.pallas_call(
        functools.partial(attend_back_kernel, groups, reach, lines, tile),
        grid=(count // tile,),
        in_specs=[*[whole(*operand.shape) for operand in operands], ANY],
        out_specs=[
            whole(blocks, rows, width),
            whole(lines, 3 * HD, shard),
            whole(rows, width),
            whole(shard, lanes),
        ],
        out_shape=[
            jax.ShapeDtypeStruct((blocks, rows, width), BF),
            jax.ShapeDtypeStruct((lines, 3 * HD, shard), BF),
            jax.ShapeDtypeStruct((rows, width), F32),
            jax.ShapeDtypeStruct((shard, lanes), BF),
        ],
        scratch_shapes=[
            pltpu.VMEM((2 * HD, count), F32),
            pltpu.VMEM((HD, count), BF),
            pltpu.VMEM((3 * HD, width), F32),
            pltpu.VMEM((lines, shard, lanes), BF),
            *Halving.scratch(2, rows, width),
            *Lines.scratch(lines),
        ],
        compiler_params=pltpu.CompilerParams(
            collective_id=4, has_side_effects=True, vmem_limit_bytes=56 << 20
        ),
        cost_estimate=pl.CostEstimate(
            flops=count * count * HD * 20, bytes_accessed=count * 6144, transcendentals=count * count
        ),
        name="attend_back",
    )(*operands, attn)


class Collect:
    def __init__(self, groups, pieces, far_send, far_recv, near_send, near_recv):
        head = lax.axis_index("heads")
        self.half = half = groups // 2
        pair = {"heads": flip(head, 1)}
        self.far, self.near = [], []
        for n, (piece, where) in enumerate(pieces):
            self.far.append(
                [
                    remote(
                        piece,
                        where(head),
                        {"heads": (head + 2 * k) % groups},
                        far_send.at[n, k - 1],
                        far_recv.at[n, k - 1],
                    )
                    for k in range(1, half)
                ]
            )
            sides = [(piece, where(head))]
            for k in range(1, half):
                got = where((head - 2 * k + groups) % groups)
                sides.append((got, got))
            self.near.append(
                [
                    remote(source, target, pair, near_send.at[n, k], near_recv.at[n, k])
                    for k, (source, target) in enumerate(sides)
                ]
            )

    @staticmethod
    def scratch(count, groups):
        far, near = (count, max(groups // 2 - 1, 1)), (count, groups // 2)
        return [DMA(far), DMA(far), DMA(near), DMA(near)]

    def start(self, n):
        for copy in self.far[n]:
            copy.start()
        self.near[n][0].start()

    def forward(self, n):
        for k, copy in enumerate(self.far[n]):
            copy.wait_recv()
            self.near[n][k + 1].start()

    def finish(self):
        for copies in self.far:
            for copy in copies:
                copy.wait_send()
        for copies in self.near:
            for copy in copies:
                copy.wait()


def end_kernel(
    groups,
    reach,
    lines,
    partial,
    weight,
    mlp,
    attn,
    total,
    mlp_all,
    weight_all,
    attn_all,
    lined,
    summed,
    swap_send,
    swap_recv,
    own,
    *rest,
):
    place = Place(groups, reach)
    sub = mlp.shape[0]
    mine, head = place.ctx % sub, place.head
    meet(everyone(place, lines))
    wide = Halving(place, 3, partial, total, rest[:7])
    swap = Lines(lines, weight, lined, *rest[7:10])
    wide.start()
    swaps = []
    for step in range(1, sub):
        peer = (mine + step) % sub
        swaps.append(
            push(
                mlp.at[peer],
                mlp_all.at[mine, head],
                {"ctx": place.ctx - mine + peer},
                swap_send.at[step - 1],
                swap_recv.at[step - 1],
            )
        )
    pieces = [(mlp.at[mine], lambda h: mlp_all.at[mine, h]), (attn, lambda h: attn_all.at[h])]
    for step in range(1, sub):
        source = (mine - step + sub) % sub
        pieces.append(
            (mlp_all.at[source, head], lambda h, source=source: mlp_all.at[source, h])
        )
    pieces.append((summed, lambda h: weight_all.at[h]))
    collect = Collect(groups, pieces, *rest[10:14])
    swap.start()
    local = [
        pltpu.make_async_copy(mlp.at[mine], mlp_all.at[mine, head], own.at[0]),
        pltpu.make_async_copy(attn, attn_all.at[head], own.at[1]),
        pltpu.make_async_copy(summed, weight_all.at[head], own.at[2]),
    ]
    local[0].start()
    local[1].start()
    collect.start(0)
    collect.start(1)
    wide.pair()
    for step in range(1, sub):
        swaps[step - 1].wait_recv()
        collect.start(step + 1)
    swap.finish()
    for r in range(reach):
        summed[r] = functools.reduce(
            jnp.add, [lined[r + reach * g].astype(F32) for g in range(lines // reach)]
        ).astype(BF)
    local[2].start()
    collect.start(sub + 1)
    for step in range(3):
        wide.halve(step)
        if step == 1:
            for n in range(sub + 1):
                collect.forward(n)
    collect.forward(sub + 1)
    for copy in local:
        copy.wait()
    for copy in swaps:
        copy.wait_send()
    collect.finish()
    wide.finish()


def end_step(partial, weight, mlp, attn, groups, reach):
    rows, width = partial.shape[2:]
    lines, _, shard = weight.shape
    sub = mlp.shape[0]
    return pl.pallas_call(
        functools.partial(end_kernel, groups, reach, lines),
        in_specs=[VMEM, ANY, ANY, ANY],
        out_specs=[VMEM, ANY, ANY, ANY],
        out_shape=[
            jax.ShapeDtypeStruct((rows, width), F32),
            jax.ShapeDtypeStruct((sub, groups, *mlp.shape[1:]), BF),
            jax.ShapeDtypeStruct((groups, reach, 3 * HD, shard), BF),
            jax.ShapeDtypeStruct((groups, *attn.shape), BF),
        ],
        scratch_shapes=[
            pltpu.VMEM((lines, 3 * HD, shard), BF),
            pltpu.VMEM((reach, 3 * HD, shard), BF),
            DMA((max(sub - 1, 1),)),
            DMA((max(sub - 1, 1),)),
            DMA((3,)),
            *Halving.scratch(3, rows, width),
            *Lines.scratch(lines),
            *Collect.scratch(sub + 2, groups),
        ],
        compiler_params=pltpu.CompilerParams(
            collective_id=3, has_side_effects=True, vmem_limit_bytes=LIMIT
        ),
        cost_estimate=pl.CostEstimate(flops=0, bytes_accessed=24 << 20, transcendentals=0),
        name="end_step",
    )(partial, weight, mlp, attn)


def assemble_kernel(
    upstream,
    tokens,
    grad_middle,
    gains,
    middle,
    ahead,
    weight_all,
    attn_all,
    mlp_all,
    w_qkv,
    w_in,
    own_gains,
    result,
    grad,
    sum_qkv,
    sum_attn,
    sum_in,
    sum_out,
    gain_sums,
):
    groups, reach, _, shard = weight_all.shape
    lanes = attn_all.shape[2]
    result[...] = (middle[...] + ahead[...]).astype(BF)
    normed, inverse_std = norm_parts(tokens[...].astype(F32))
    grad[...] = grad_middle[...] + norm_back(upstream[...], normed, inverse_std, gains[0:1, :])
    for g in range(groups):
        sum_attn[:, g * lanes : (g + 1) * lanes] = attn_all[g].astype(F32)
    gain_one = jnp.zeros((shard, 128), F32)
    for third in range(3):
        part = slice(third * HD, (third + 1) * HD)
        for pair in range(H // 2):
            r, g = 2 * pair // groups, 2 * pair % groups
            tile = (
                jnp.concatenate([weight_all[g, r, part], weight_all[g + 1, r, part]], axis=0)
                .astype(F32)
                .T
            )
            at = third * H * HD + pair * 2 * HD
            sum_qkv[:, at : at + 2 * HD] = tile
            gain_one += tile * w_qkv[:, at : at + 2 * HD].astype(F32)
    gain_two = jnp.zeros((shard, 1), F32)
    for t in range(8):
        start, wide = slice_place(t)
        for half in range(2):
            piece = mlp_all[t, :, half * SLICE : half * SLICE + wide].astype(F32)
            at = half * FF + start
            sum_in[:, at : at + wide] = piece
            gain_two += jnp.sum(
                piece * w_in[:, at : at + wide].astype(F32), axis=1, keepdims=True
            )
        sum_out[start : start + wide, :] = (
            mlp_all[t, :, 2 * SLICE : 3 * SLICE].astype(F32).T[:wide]
        )
    one = jnp.sum(gain_one, axis=1, keepdims=True)
    lane = lax.broadcasted_iota(jnp.int32, (shard, 128), 1)
    both = jnp.where(lane == 0, one, gain_two).T
    gain_sums[...] = both[:8] / own_gains[...]


def assemble(upstream, tokens, grad_middle, gains, middle, ahead, weight_all, attn_all, mlp_all, w_qkv, w_in, own_gains):
    rows, width = tokens.shape
    shard = w_qkv.shape[0]
    return pl.pallas_call(
        assemble_kernel,
        in_specs=[VMEM] * 12,
        out_specs=[VMEM] * 7,
        out_shape=[
            jax.ShapeDtypeStruct((rows, width), BF),
            jax.ShapeDtypeStruct((rows, width), F32),
            jax.ShapeDtypeStruct((shard, 3 * width), F32),
            jax.ShapeDtypeStruct((shard, width), F32),
            jax.ShapeDtypeStruct((shard, 2 * FF), F32),
            jax.ShapeDtypeStruct((FF, shard), F32),
            jax.ShapeDtypeStruct((8, shard), F32),
        ],
        compiler_params=pltpu.CompilerParams(vmem_limit_bytes=LIMIT),
        cost_estimate=pl.CostEstimate(flops=1 << 24, bytes_accessed=20 << 20, transcendentals=0),
        name="assemble",
    )(upstream, tokens, grad_middle, gains, middle, ahead, weight_all, attn_all, mlp_all, w_qkv, w_in, own_gains)


def slice_start(t):
    return 128 * jnp.minimum(3 * t, 2 * t + 5)


def slice_place(t):
    start = 128 * min(3 * t, 2 * t + 5)
    return start, min(128 * min(3 * t + 3, 2 * t + 7), FF) - start


def body(count, tokens, d_out, segment_ids, position_ids, w_qkv, w_attn, w_in, w_out, gain_attn, gain_mlp):
    groups = lax.axis_size("heads")
    rows, width = tokens.shape
    shard = w_qkv.shape[0]
    reach = SEQ_MAX // (rows * groups)
    group = reach * groups
    sub = 8 // groups
    ctx, head = lax.axis_index("ctx"), lax.axis_index("heads")
    assert group == H and sub * groups == 8
    total = group * rows
    tile = 512

    def mlp_slice(value, axis, start, t):
        pads = [(0, 0), (0, 0)]
        pads[axis] = (0, SLICE)
        piece = lax.dynamic_slice_in_dim(jnp.pad(value, pads), start + slice_start(t), SLICE, axis)
        wide = jnp.minimum(slice_start(t + 1), FF) - slice_start(t)
        shape = [1, 1]
        shape[axis] = SLICE
        return jnp.where(jnp.arange(SLICE).reshape(shape) < wide, piece, jnp.zeros_like(piece))

    def mlp_part(t):
        return jnp.concatenate(
            [mlp_slice(w_in, 1, 0, t), mlp_slice(w_in, 1, FF, t), mlp_slice(w_out, 0, 0, t).T], axis=1
        )

    mlp = jnp.stack([mlp_part(x * groups + head) for x in range(sub)])
    lines = [list(range(k, count, sub)) for k in range(sub)]
    gains_own = jnp.pad(jnp.stack([gain_attn, gain_mlp]).astype(F32), ((0, 6), (0, -shard % 128)))
    ids = jnp.pad(jnp.stack([position_ids, segment_ids]), ((0, 6), (0, 0)))
    input_all, ids_all, gains, slab, attn_part, mlp_pair = begin(
        tokens, gains_own, ids, w_qkv, w_attn, mlp, count, groups, reach
    )
    x = input_all.reshape(total, width)
    slab = slab.reshape(width, 3, 2, HD)
    w_head = jnp.where(head % 2 == 0, slab[:, :, 0], slab[:, :, 1]).reshape(width, 3 * HD)
    positions = ids_all[:, 0].reshape(1, total).astype(F32)
    parity = (ids_all[:, 1].reshape(1, total) % 2).astype(F32)
    freqs = jnp.power(160000.0, -(2.0 * jnp.arange(HALF, dtype=F32)) / HD)
    angles = freqs[:, None] * positions
    cosine, sine = jnp.cos(angles), jnp.sin(angles)
    blank = jnp.zeros((MARKS - 2, total), F32)
    marks = jnp.concatenate(
        [parity, 1.0 - parity, blank, (1.0 - parity) * MASKED, parity * MASKED, blank]
    ).astype(BF)

    attended, wide, lse, qkv, attn_weights, mlp_near = attend(
        x, w_head, cosine, sine, marks, attn_part, mlp_pair, count, groups, reach, rows, tile
    )
    attn_weights = attn_weights.reshape(width, width)
    mlp_all, upstream, middle, attended, mlp_weights = middle_step(
        attended, tokens, d_out, attn_weights, gains, mlp_pair, mlp_near, count, groups, reach
    )
    mlp_weights = mlp_weights.reshape(width, 3 * SLICE)
    mlp_input = mlp_all.reshape(8 * rows, width)
    upstream = upstream.reshape(8 * rows, width)
    attended_all = lax.all_gather(attended.reshape(width, rows), "heads", axis=0)

    in_weights, out_weights = mlp_weights[:, : 2 * SLICE], mlp_weights[:, 2 * SLICE :]
    gate_up = dot(mlp_input, in_weights, 1, 0)
    gate_left, gate_right = gate_up[:, :SLICE], gate_up[:, SLICE:]
    normal_cdf = 0.5 * (1.0 + lax.erf(gate_left * 0.7071067811865476))
    gelu = gate_left * normal_cdf
    density = jnp.exp(-0.5 * gate_left * gate_left) * 0.3989422804014327
    mixed = (gelu * gate_right).astype(BF)
    grad_mixed = dot(upstream, out_weights, 1, 0)
    grad_left = grad_mixed * gate_right * (normal_cdf + gate_left * density)
    grad_gate_up = jnp.concatenate([grad_left, grad_mixed * gelu], axis=1).astype(BF)
    split = lambda value, blocks: value.astype(BF).reshape(blocks // 2, 2, rows, width)
    grad_mlp = split(dot(grad_gate_up, in_weights, 1, 1), 8)
    grad_out_part = dot(upstream, mixed, 0, 0)
    grad_in_part = dot(mlp_input, grad_gate_up, 0, 0)
    mlp_terms = jnp.concatenate([grad_in_part, grad_out_part], axis=1).astype(BF)
    grad_mlp, mlp_terms = lax.optimization_barrier((grad_mlp, mlp_terms))
    mlp_sum = lax.psum_scatter(
        mlp_terms, "ctx", scatter_dimension=0, tiled=True, axis_index_groups=lines
    ).reshape(sub, shard, 3 * SLICE)
    grad_heads, branch, grad_middle = turn_step(
        grad_mlp, middle, d_out, attn_weights, gains, groups, reach
    )
    attn_part = jnp.einsum("gdt,gtn->dn", attended_all, branch, preferred_element_type=F32)
    attn_part = attn_part.astype(BF).reshape(count, shard, width // groups)
    forward = split(dot(mixed, out_weights, 1, 1), 8)
    grad_input_parts, weight, ahead, attn_sum = attend_back(
        qkv, grad_heads, wide, lse, x, w_head, cosine, sine, forward, attn_part, groups, reach, tile
    )
    upstream_in, mlp_all, weight_all, attn_all = end_step(
        split(grad_input_parts, group), weight, mlp_sum, attn_sum, groups, reach
    )
    result, grad_input, sum_qkv, sum_attn, sum_in, sum_out, gain_sums = assemble(
        upstream_in,
        tokens,
        grad_middle,
        gains,
        middle,
        ahead,
        weight_all,
        attn_all,
        mlp_all.reshape(8, shard, 3 * SLICE),
        w_qkv,
        w_in,
        jnp.pad(gains_own[:2, :shard], ((0, 6), (0, 0)), constant_values=1.0),
    )
    return (
        result,
        grad_input,
        sum_qkv,
        sum_attn,
        sum_in,
        sum_out,
        gain_sums[0],
        gain_sums[1],
    )


def solution(mesh):
    return jax.shard_map(
        functools.partial(body, mesh.shape["ctx"]),
        mesh=mesh,
        in_specs=(
            P(("ctx", "heads"), None),
            P(("ctx", "heads"), None),
            P(("ctx", "heads")),
            P(("ctx", "heads")),
            P("ctx", None),
            P("ctx", None),
            P("ctx", None),
            P(None, "ctx"),
            P("ctx"),
            P("ctx"),
        ),
        out_specs=(
            P(("ctx", "heads"), None),
            P(("ctx", "heads"), None),
            P("ctx", None),
            P("ctx", None),
            P("ctx", None),
            P(None, "ctx"),
            P("ctx"),
            P("ctx"),
        ),
        check_vma=False,
    )
```

```python
import functools

import jax
import jax.numpy as jnp
from jax import lax
from jax.experimental import pallas as pl
from jax.experimental.pallas import tpu as pltpu
from jax.sharding import PartitionSpec as P

H = 16
HD = 64
HALF = HD // 2
FF = 2624
SEQ_MAX = 2048
MASKED = -1e30
MARKS = 16
QM_END = HD + MARKS
K_END = QM_END + HD
KM_END = K_END + MARKS
V_END = KM_END + HD
SLICE = 384
BF = jnp.bfloat16
F32 = jnp.float32
MESH = pl.DeviceIdType.MESH
VMEM = pl.BlockSpec(memory_space=pltpu.VMEM)
ANY = pl.BlockSpec(memory_space=pl.ANY)
DMA = pltpu.SemaphoreType.DMA
LIMIT = 48 << 20


def dot(left, right, left_dim, right_dim):
    return lax.dot_general(
        left, right, (((left_dim,), (right_dim,)), ((), ())), preferred_element_type=F32
    )


def norm_parts(values):
    average = jnp.mean(values, axis=-1, keepdims=True)
    centred = values - average
    inverse_std = lax.rsqrt(jnp.mean(centred * centred, axis=-1, keepdims=True) + 1e-05)
    return centred * inverse_std, inverse_std


def norm_back(upstream, normed, inverse_std, gain):
    scaled = upstream * gain
    return inverse_std * (
        scaled
        - jnp.mean(scaled, axis=-1, keepdims=True)
        - normed * jnp.mean(scaled * normed, axis=-1, keepdims=True)
    )


def flip(value, bit):
    return value + bit - 2 * bit * (value // bit % 2)


class Place:
    def __init__(self, groups, reach):
        self.groups, self.reach = groups, reach
        self.ctx = lax.axis_index("ctx")
        self.head = lax.axis_index("heads")
        self.local = self.ctx % reach
        self.base = self.ctx - self.local
        self.idx = self.local * groups + self.head

    def member(self, j):
        return {"ctx": self.base + j // self.groups, "heads": j % self.groups}


def greet(devices):
    barrier = pltpu.get_barrier_semaphore()
    for device in devices:
        pl.semaphore_signal(barrier, inc=1, device_id=device, device_id_type=MESH)


def meet(devices):
    greet(devices)
    pl.semaphore_wait(pltpu.get_barrier_semaphore(), len(devices))


def remote(source, target, device, send, recv):
    return pltpu.make_async_remote_copy(
        src_ref=source,
        dst_ref=target,
        send_sem=send,
        recv_sem=recv,
        device_id=device,
        device_id_type=MESH,
    )


def push(*operands):
    copy = remote(*operands)
    copy.start()
    return copy


def tree_parts(axes, rows):
    part = -(-rows // axes // 16) * 16
    starts = [min(part * a, rows) for a in range(axes + 1)]
    return [(starts[a], starts[a + 1] - starts[a]) for a in range(axes)]


class Tree:
    def __init__(self, place, axes, source, target, sems):
        self.place, self.axes, self.source, self.target = place, axes, source, target
        self.send, self.recv, self.core_send, self.core_recv, self.own = sems
        self.slots = 2 << axes
        self.levels, self.cores = [], []

    @staticmethod
    def scratch(axes):
        far, near = axes * axes, axes * axes + 1
        return [DMA((far,)), DMA((far,)), DMA((near,)), DMA((near,)), DMA]

    def origin(self, level, first):
        value = self.place.idx
        for k in range(level):
            value = flip(value, 2 << ((first + k) % self.axes))
        return value % self.slots

    def neighbour(self, axis):
        return self.place.member(flip(self.place.idx, 2 << (axis % self.axes)))

    def piece(self, slot, part):
        return self.target.at[slot] if part is None else self.target.at[slot, pl.ds(*part)]

    def to_core(self, source, slot, part):
        at = len(self.cores)
        self.cores.append(
            push(
                source,
                self.piece(slot, part),
                self.place.member(flip(self.place.idx, 1)),
                self.core_send.at[at],
                self.core_recv.at[at],
            )
        )

    def start(self):
        me = self.place.idx % self.slots
        self.levels.append(
            [
                push(
                    self.source, self.target.at[me], self.neighbour(a), self.send.at[a], self.recv.at[a]
                )
                for a in range(self.axes)
            ]
        )
        self.to_core(self.source, me, None)
        self.local = pltpu.make_async_copy(self.source, self.target.at[me], self.own)
        self.local.start()

    def forward(self, level):
        axes = self.axes
        parts = tree_parts(axes, self.target.shape[1])
        onward = []
        for a in range(axes):
            self.levels[level - 1][a].wait_recv()
            slot = self.origin(level, a)
            if level < axes:
                part = parts[a] if level + 1 == axes else None
                at = level * axes + a
                piece = self.piece(slot, part)
                onward.append(
                    push(piece, piece, self.neighbour(a + level), self.send.at[at], self.recv.at[at])
                )
                self.to_core(self.target.at[slot], slot, None)
            else:
                self.to_core(self.piece(slot, parts[a]), slot, parts[a])
        self.levels.append(onward)

    def finish(self):
        self.local.wait()
        for level in self.levels:
            for copy in level:
                copy.wait_send()
        for copy in self.cores:
            copy.wait()


class Halving:
    def __init__(self, place, axes, value, result, scratch):
        self.axes, self.value, self.result = axes, value, result
        self.other, self.held, self.land, send, recv, send0, recv0 = scratch
        self.blocks = 1 << axes
        width = value.shape[-1]
        part = -(-width // axes // 128) * 128
        starts = [0] + [width - part * (axes - a) for a in range(1, axes + 1)]
        self.columns = [pl.ds(starts[a], starts[a + 1] - starts[a]) for a in range(axes)]
        self.core = place.idx % 2
        self.chip = place.idx // 2 % self.blocks
        self.sources = []
        for j in range(self.blocks):
            k = self.chip
            for a in range(axes):
                if j >> a & 1:
                    k = flip(k, 1 << a)
            self.sources.append(k)
        self.first, self.copies = [], {}
        for p in range(axes):
            self.first.append(
                remote(
                    value.at[:, 1 - self.core, :, self.columns[p]],
                    self.other.at[:, :, self.columns[p]],
                    place.member(flip(place.idx, 1)),
                    send0.at[p],
                    recv0.at[p],
                )
            )
            for step in range(axes):
                bit, sent = self.sent(p, step)
                for j in sent:
                    self.copies[p, j] = remote(
                        self.held.at[j, :, self.columns[p]],
                        self.land.at[j, :, self.columns[p]],
                        place.member(flip(place.idx, 2 * bit)),
                        send.at[p, j],
                        recv.at[p, j],
                    )

    @staticmethod
    def scratch(axes, rows, width):
        blocks = 1 << axes
        return [
            pltpu.VMEM((blocks, rows, width), BF),
            pltpu.VMEM((blocks, rows, width), BF),
            pltpu.VMEM((blocks, rows, width), BF),
            DMA((axes, blocks)),
            DMA((axes, blocks)),
            DMA((axes,)),
            DMA((axes,)),
        ]

    def sent(self, part, step):
        seen = [1 << ((part + s) % self.axes) for s in range(step)]
        bit = 1 << ((part + step) % self.axes)
        return bit, [j for j in range(self.blocks) if j & bit and not any(j & s for s in seen)]

    def start(self):
        for copy in self.first:
            copy.start()

    def pair(self):
        for p in range(self.axes):
            cols = self.columns[p]
            self.first[p].wait_recv()
            _, early = self.sent(p, 0)
            for j in early + [j for j in range(self.blocks) if j not in early]:
                k = self.sources[j]
                self.held[j, :, cols] = (
                    self.value[k, self.core, :, cols].astype(F32) + self.other[k, :, cols].astype(F32)
                ).astype(BF)
                if j in early:
                    self.copies[p, j].start()

    def halve(self, step):
        for p in range(self.axes):
            cols = self.columns[p]
            bit, arrived = self.sent(p, step)
            onward = self.sent(p, step + 1)[1] if step + 1 < self.axes else []
            for j in sorted(arrived, key=lambda j: (j - bit) not in onward):
                self.copies[p, j].wait_recv()
                k = j - bit
                total = self.held[k, :, cols].astype(F32) + self.land[j, :, cols].astype(F32)
                if step + 1 < self.axes:
                    self.held[k, :, cols] = total.astype(BF)
                    if k in onward:
                        self.copies[p, k].start()
                else:
                    self.result[:, cols] = total

    def run(self):
        self.start()
        self.pair()
        for step in range(self.axes):
            self.halve(step)
        self.finish()

    def finish(self):
        for copy in self.first:
            copy.wait_send()
        for copy in self.copies.values():
            copy.wait_send()


class Lines:
    def __init__(self, count, source, target, send, recv, own):
        me = lax.axis_index("ctx")
        self.copies = [pltpu.make_async_copy(source.at[me], target.at[me], own)]
        for step in range(1, count):
            peer = (me + step) % count
            self.copies.append(
                remote(source.at[peer], target.at[me], {"ctx": peer}, send.at[step - 1], recv.at[step - 1])
            )

    @staticmethod
    def scratch(count):
        return [DMA((count - 1,)), DMA((count - 1,)), DMA]

    def start(self):
        for copy in self.copies:
            copy.start()

    def finish(self):
        for copy in self.copies:
            copy.wait()


def everyone(place, count):
    group = place.reach * place.groups
    mates = [place.member((place.idx + step) % group) for step in range(1, group)]
    outside = [{"ctx": (place.base + place.reach + step) % count} for step in range(count - place.reach)]
    return mates + outside


def spread(place, source, target, sems, me=None):
    send, recv, own = sems
    count = target.shape[0]
    copies = []
    for step in range(1, count):
        peer = (place.idx + step) % count
        copies.append(
            push(
                source.at[peer],
                target.at[place.idx],
                place.member(peer),
                send.at[step - 1],
                recv.at[step - 1],
            )
        )
    local = pltpu.make_async_copy(source.at[place.idx], target.at[place.idx], own)
    local.start()
    copies.append(local)
    return copies


def begin_kernel(
    groups,
    reach,
    count,
    tokens,
    gains,
    ids,
    w_qkv,
    w_attn,
    mlp,
    freqs,
    input_all,
    gains_all,
    w_head,
    cosine,
    sine,
    marks,
    attn_part,
    mlp_pair,
    ids_all,
    slab,
    mine,
    gain_land,
    own_sems,
    ids_send,
    ids_recv,
    gain_send,
    gain_recv,
    slab_send,
    slab_recv,
    wide_send,
    wide_recv,
    swap_send,
    swap_recv,
    core_send,
    core_recv,
    *tree_sems,
):
    place = Place(groups, reach)
    group = reach * groups
    ctx, head, idx = place.ctx, place.head, place.idx
    shard = w_qkv.shape[0]
    sub = mlp.shape[0]
    ring = count // sub
    side, spot = ctx % sub, ctx // sub
    lanes = attn_part.shape[2]
    core = {"heads": flip(head, 1)}
    mates = [place.member((idx + step) % group) for step in range(1, group)]
    lines = [{"ctx": (ctx + step) % count} for step in range(1, count)]
    meet(everyone(place, count))
    first = [
        push(gains, gain_land.at[ctx], lines[step - 1], gain_send.at[step - 1], gain_recv.at[step - 1])
        for step in range(1, count)
    ]
    small = [
        push(ids, ids_all.at[idx], mates[step - 1], ids_send.at[step - 1], ids_recv.at[step - 1])
        for step in range(1, group)
    ]
    half = pl.ds(pl.multiple_of(head % 2 * (shard // 2), 16), shard // 2)
    thirds = []
    for step in range(1, count):
        peer = (ctx + step) % count
        column = ((peer % reach) * groups + head) // 2 * 128
        for third in range(3):
            start = pl.multiple_of(third * 1024 + column, 128)
            thirds.append(
                push(
                    w_qkv.at[half, pl.ds(start, 128)],
                    slab.at[ctx, half, pl.ds(third * 128, 128)],
                    lines[step - 1],
                    slab_send.at[step - 1, third],
                    slab_recv.at[step - 1, third],
                )
            )
    gain_land[ctx] = gains[...]
    across = pl.ds(pl.multiple_of(head * lanes, 128), lanes)
    own = [
        pltpu.make_async_copy(ids, ids_all.at[idx], own_sems.at[3]),
        pltpu.make_async_copy(w_attn.at[:, across], attn_part.at[spot], own_sems.at[4]),
        pltpu.make_async_copy(mlp.at[side], mlp_pair.at[side], own_sems.at[5]),
    ]
    for third in range(3):
        start = pl.multiple_of(third * 1024 + idx // 2 * 128, 128)
        own.append(
            pltpu.make_async_copy(
                w_qkv.at[half, pl.ds(start, 128)],
                slab.at[ctx, half, pl.ds(third * 128, 128)],
                own_sems.at[third],
            )
        )
    for copy in own:
        copy.start()
    for copy in first:
        copy.wait_recv()
    gain, gain_two = (
        jnp.concatenate([gain_land[c, k : k + 1, :shard] for c in range(count)], axis=1)
        for k in range(2)
    )
    normed, _ = norm_parts(tokens[...].astype(F32))
    mine[...] = (normed * gain).astype(BF)
    tree = Tree(place, 3, mine, input_all, tree_sems)
    tree.start()
    gains_all[0:1, :] = gain
    gains_all[1:2, :] = gain_two
    late = []
    for step in range(1, sub):
        peer = (side + step) % sub
        late.append(
            push(
                mlp.at[peer],
                mlp_pair.at[side],
                {"ctx": ctx - side + peer},
                swap_send.at[step - 1],
                swap_recv.at[step - 1],
            )
        )
    for step in range(1, ring):
        late.append(
            push(
                w_attn.at[:, across],
                attn_part.at[spot],
                {"ctx": (spot + step) % ring * sub + side},
                wide_send.at[step - 1],
                wide_recv.at[step - 1],
            )
        )
    tree.forward(1)
    for copy in own:
        copy.wait()
    for copy in thirds:
        copy.wait_recv()
    shared = push(slab.at[:, half], slab.at[:, half], core, core_send, core_recv)
    for copy in small:
        copy.wait()
    row = lambda k: jnp.concatenate([ids_all[j, k : k + 1, :] for j in range(group)], axis=1)
    angles = freqs[...] * row(0).astype(F32)
    cosine[...] = jnp.cos(angles)
    sine[...] = jnp.sin(angles)
    parity = (row(1) % 2).astype(F32)
    blank = jnp.zeros((MARKS - 2, parity.shape[1]), F32)
    marks[...] = jnp.concatenate(
        [parity, 1.0 - parity, blank, (1.0 - parity) * MASKED, parity * MASKED, blank], axis=0
    ).astype(BF)
    tree.forward(2)
    shared.wait()
    odd = head % 2 == 1
    for c in range(count):
        rows = slice(c * shard, (c + 1) * shard)
        block = slab[c].astype(F32)
        parts = []
        for third in range(3):
            at = third * 128
            parts.append(jnp.where(odd, block[:, at + HD : at + 128], block[:, at : at + HD]))
        w_head[rows] = jnp.concatenate(parts, axis=1).astype(BF)
    tree.forward(3)
    tree.finish()
    for copy in first + thirds:
        copy.wait_send()
    for copy in late:
        copy.wait()


def begin(tokens, gains, ids, w_qkv, w_attn, mlp, freqs, count, groups, reach):
    rows, width = tokens.shape
    shard = w_qkv.shape[0]
    sub = mlp.shape[0]
    ring = count // sub
    group = groups * reach
    sems = lambda *shape: [DMA(shape), DMA(shape)]
    return pl.pallas_call(
        functools.partial(begin_kernel, groups, reach, count),
        in_specs=[VMEM, VMEM, ANY, ANY, ANY, ANY, VMEM],
        out_specs=[ANY, VMEM, VMEM, VMEM, VMEM, VMEM, ANY, ANY],
        out_shape=[
            jax.ShapeDtypeStruct((group, rows, width), BF),
            jax.ShapeDtypeStruct((8, width), F32),
            jax.ShapeDtypeStruct((width, 3 * HD), BF),
            jax.ShapeDtypeStruct((HALF, group * rows), F32),
            jax.ShapeDtypeStruct((HALF, group * rows), F32),
            jax.ShapeDtypeStruct((2 * MARKS, group * rows), BF),
            jax.ShapeDtypeStruct((ring, shard, width // groups), BF),
            jax.ShapeDtypeStruct(mlp.shape, BF),
        ],
        scratch_shapes=[
            pltpu.VMEM((group, 8, rows), jnp.int32),
            pltpu.VMEM((count, shard, 3 * 128), BF),
            pltpu.VMEM((rows, width), BF),
            pltpu.VMEM((count, 8, gains.shape[1]), F32),
            DMA((6,)),
            *sems(group - 1),
            *sems(count - 1),
            *sems(count - 1, 3),
            *sems(ring - 1),
            *sems(max(sub - 1, 1)),
            DMA,
            DMA,
            *Tree.scratch(3),
        ],
        compiler_params=pltpu.CompilerParams(
            collective_id=0, has_side_effects=True, vmem_limit_bytes=LIMIT
        ),
        cost_estimate=pl.CostEstimate(flops=0, bytes_accessed=30 << 20, transcendentals=0),
        name="begin",
    )(tokens, gains, ids, w_qkv, w_attn, mlp, freqs)


class Ring:
    def __init__(self, ring, sub, blocks, arrivals, send, recv):
        ctx = lax.axis_index("ctx")
        right = {"ctx": (ctx // sub + 1) % ring * sub + ctx % sub}
        self.copies = [
            remote(source, target, right, send.at[s], recv.at[s])
            for s, (source, target) in enumerate(zip(blocks, arrivals))
        ]

    def start(self, s):
        if s:
            self.copies[s - 1].wait_recv()
        self.copies[s].start()

    def finish(self):
        self.copies[-1].wait_recv()
        for copy in self.copies:
            copy.wait_send()


class Columns:
    def __init__(self, place, part, whole, own, side_send, side_recv, far_send, far_recv, near_send, near_recv):
        groups = place.groups
        _, sub, _, width = whole.shape
        lanes = width // groups
        head, side = place.head, place.ctx % sub
        half = groups // 2
        at = lambda h: pl.ds(pl.multiple_of(h * lanes, 128), lanes)
        self.own = pltpu.make_async_copy(part, whole.at[:, side, :, at(head)], own)
        self.sides, self.far, self.near = [], [], []
        for step in range(1, sub):
            peer = (side + step) % sub
            self.sides.append(
                remote(
                    part,
                    whole.at[:, side, :, at(head)],
                    {"ctx": place.ctx - side + peer},
                    side_send.at[step - 1],
                    side_recv.at[step - 1],
                )
            )
        for step in range(sub):
            x = (side - step + sub) % sub
            here = whole.at[:, x, :, at(head)]
            self.far.append(
                [
                    remote(
                        here if step else part,
                        here,
                        {"heads": (head + 2 * k) % groups},
                        far_send.at[step, k - 1],
                        far_recv.at[step, k - 1],
                    )
                    for k in range(1, half)
                ]
            )
        for k in range(half):
            here = whole.at[:, :, :, at((head - 2 * k + groups) % groups)]
            self.near.append(
                remote(here, here, {"heads": flip(head, 1)}, near_send.at[k], near_recv.at[k])
            )

    @staticmethod
    def scratch(sub, groups):
        side, far, near = (max(sub - 1, 1),), (sub, max(groups // 2 - 1, 1)), (groups // 2,)
        return [DMA, DMA(side), DMA(side), DMA(far), DMA(far), DMA(near), DMA(near)]

    def start(self):
        self.own.start()
        for copy in self.sides + self.far[0]:
            copy.start()

    def forward(self):
        for step, copy in enumerate(self.sides):
            copy.wait_recv()
            for far in self.far[step + 1]:
                far.start()

    def across(self):
        self.own.wait()
        self.near[0].start()

    def onward(self):
        for k in range(1, len(self.near)):
            for far in self.far:
                far[k - 1].wait_recv()
            self.near[k].start()

    def finish(self):
        for copies in [self.sides, *self.far]:
            for copy in copies:
                copy.wait_send()
        for copy in self.near:
            copy.wait()


def attend_kernel(
    groups,
    reach,
    lines,
    tile,
    x_ref,
    w_ref,
    cos_ref,
    sin_ref,
    mark_ref,
    attn_part,
    mlp_pair,
    out_ref,
    wide_ref,
    lse_ref,
    qkv_ref,
    attn_all,
    mlp_near,
    ring_send,
    ring_recv,
    *sems,
):
    count = x_ref.shape[0]
    step = pl.program_id(0)
    steps = count // tile
    place = Place(groups, reach)
    sub = mlp_pair.shape[0]
    early = mlp_near.shape[0]
    ring = Ring(
        lines // sub,
        sub,
        [mlp_pair] + [mlp_near.at[s] for s in range(early - 1)],
        [mlp_near.at[s] for s in range(early)],
        ring_send,
        ring_recv,
    )
    columns = Columns(place, attn_part, attn_all, *sems)

    @pl.when(step == 0)
    def _():
        meet(everyone(place, lines))
        ring.start(0)
        columns.start()
        qkv_ref[HD:QM_END, :] = mark_ref[:MARKS, :]
        qkv_ref[K_END:KM_END, :] = mark_ref[MARKS:, :]

        @pl.loop(0, steps)
        def _(i):
            at = pl.ds(pl.multiple_of(i * tile, tile), tile)
            cosine, sine = cos_ref[:, at], sin_ref[:, at]
            part = dot(w_ref[...], x_ref[at, :], 0, 1)

            def turn(value):
                front, back = value[:HALF], value[HALF:]
                return jnp.concatenate(
                    [front * cosine - back * sine, back * cosine + front * sine], axis=0
                )

            qkv_ref[:HD, at] = (turn(part[:HD]) * 0.125).astype(BF)
            qkv_ref[QM_END:K_END, at] = turn(part[HD : 2 * HD]).astype(BF)
            qkv_ref[KM_END:, at] = part[2 * HD :].astype(BF)

    here = pl.ds(pl.multiple_of(step * tile, tile), tile)
    query = qkv_ref[:QM_END, here]
    keys = [slice(j * tile, (j + 1) * tile) for j in range(steps)]
    scores = [dot(qkv_ref[QM_END:KM_END, at], query, 0, 0) for at in keys]
    top = functools.reduce(jnp.maximum, [jnp.max(s, axis=0, keepdims=True) for s in scores])
    raised = [jnp.exp(s - top) for s in scores]
    total = functools.reduce(jnp.add, [jnp.sum(e, axis=0, keepdims=True) for e in raised])
    scale = 1.0 / total
    result = jnp.zeros((HD, tile), F32)
    for j in range(steps):
        result += dot(qkv_ref[KM_END:, keys[j]], (raised[j] * scale).astype(BF), 1, 0)
    rows = out_ref.shape[2]
    for k in range(tile // rows):
        out_ref[step * (tile // rows) + k] = result[:, k * rows : (k + 1) * rows].astype(BF)
    wide_ref[:, here] = result
    lse_ref[:, here] = top + jnp.log(total)

    pl.when(step == min(1, steps - 1))(columns.forward)
    pl.when(step == min(2, steps - 1))(columns.across)

    @pl.when(step == steps - 1)
    def _():
        columns.onward()
        for s in range(1, early):
            ring.start(s)
        ring.finish()
        columns.finish()


def attend(x, w, cosine, sine, marks, attn_part, mlp_pair, lines, groups, reach, rows, tile):
    count, width = x.shape
    sub = mlp_pair.shape[0]
    ring, shard, _ = attn_part.shape
    early = (ring - 1) // 3
    whole = lambda *shape: pl.BlockSpec(shape, lambda i: (0,) * len(shape))
    return pl.pallas_call(
        functools.partial(attend_kernel, groups, reach, lines, tile),
        grid=(count // tile,),
        in_specs=[
            whole(count, width),
            whole(*w.shape),
            whole(HALF, count),
            whole(HALF, count),
            whole(2 * MARKS, count),
            ANY,
            ANY,
        ],
        out_specs=[
            whole(count // rows, HD, rows),
            whole(HD, count),
            whole(1, count),
            whole(V_END, count),
            ANY,
            ANY,
        ],
        out_shape=[
            jax.ShapeDtypeStruct((count // rows, HD, rows), BF),
            jax.ShapeDtypeStruct((HD, count), F32),
            jax.ShapeDtypeStruct((1, count), F32),
            jax.ShapeDtypeStruct((V_END, count), BF),
            jax.ShapeDtypeStruct((ring, sub, shard, width), BF),
            jax.ShapeDtypeStruct((early, *mlp_pair.shape), BF),
        ],
        scratch_shapes=[DMA((early,)), DMA((early,)), *Columns.scratch(sub, groups)],
        compiler_params=pltpu.CompilerParams(
            collective_id=5, has_side_effects=True, vmem_limit_bytes=LIMIT
        ),
        cost_estimate=pl.CostEstimate(
            flops=count * count * HD * 8, bytes_accessed=count * 4096, transcendentals=count * count
        ),
        name="attend",
    )(x, w, cosine, sine, marks, attn_part, mlp_pair)


def middle_kernel(
    groups,
    reach,
    lines,
    outgoing,
    tokens,
    d_out,
    w_attn,
    gains,
    mlp_pair,
    mlp_near,
    mlp_all,
    upstream_all,
    middle,
    attended,
    mlp_weights,
    land,
    mine,
    a2a_send,
    a2a_recv,
    own,
    ring_send,
    ring_recv,
    ring_own,
    land_own,
    *tree_sems,
):
    place = Place(groups, reach)
    group = groups * reach
    early, sub = mlp_near.shape[:2]
    count = lines // sub
    spot = place.ctx // sub
    slot = lambda s: mlp_weights.at[(spot - s + count) % count]
    left = count - 1 - early
    ring = Ring(
        count,
        sub,
        [mlp_near.at[early - 1]] + [slot(early + s) for s in range(1, left)],
        [mlp_weights.at[(spot - early - s + count) % count] for s in range(left)],
        ring_send,
        ring_recv,
    )
    local = [pltpu.make_async_copy(mlp_pair, slot(0), ring_own.at[0])]
    for s in range(early):
        local.append(pltpu.make_async_copy(mlp_near.at[s], slot(s + 1), ring_own.at[s + 1]))
    meet(everyone(place, lines))
    copies = spread(place, outgoing, land, (a2a_send, a2a_recv, own))
    ring.start(0)
    up = Tree(place, 2, d_out, upstream_all, tree_sems[5:10])
    up.start()
    for copy in local:
        copy.start()
    for copy in copies:
        copy.wait()
    collect = Collect(groups, [(land, lambda h: attended.at[h])], *tree_sems[10:])
    collect.start(0)
    local.append(pltpu.make_async_copy(land, attended.at[place.head], land_own))
    local[-1].start()
    value = tokens[...].astype(F32) + dot(
        land[...].reshape(group * HD, tokens.shape[0]), w_attn[...], 0, 0
    )
    middle[...] = value
    normed, _ = norm_parts(value)
    mine[...] = (normed * gains[1:2, :]).astype(BF)
    tree = Tree(place, 2, mine, mlp_all, tree_sems[:5])
    tree.start()
    up.forward(1)
    for s in range(1, left):
        ring.start(s)
    tree.forward(1)
    up.forward(2)
    tree.forward(2)
    collect.forward(0)
    up.finish()
    tree.finish()
    collect.finish()
    for copy in local:
        copy.wait()
    ring.finish()


def middle_step(outgoing, tokens, d_out, w_attn, gains, mlp_pair, mlp_near, lines, groups, reach):
    rows, width = tokens.shape
    group = groups * reach
    early, sub = mlp_near.shape[:2]
    ring = lines // sub
    left = ring - 1 - early
    return pl.pallas_call(
        functools.partial(middle_kernel, groups, reach, lines),
        in_specs=[ANY, VMEM, ANY, VMEM, VMEM, ANY, ANY],
        out_specs=[ANY, ANY, VMEM, ANY, ANY],
        out_shape=[
            jax.ShapeDtypeStruct((8, rows, width), BF),
            jax.ShapeDtypeStruct((8, rows, width), BF),
            jax.ShapeDtypeStruct((rows, width), F32),
            jax.ShapeDtypeStruct((groups, group, HD, rows), BF),
            jax.ShapeDtypeStruct((ring, *mlp_pair.shape), BF),
        ],
        scratch_shapes=[
            pltpu.VMEM((group, HD, rows), BF),
            pltpu.VMEM((rows, width), BF),
            DMA((group - 1,)),
            DMA((group - 1,)),
            DMA,
            DMA((left,)),
            DMA((left,)),
            DMA((early + 1,)),
            DMA,
            *Tree.scratch(2),
            *Tree.scratch(2),
            *Collect.scratch(1, groups),
        ],
        compiler_params=pltpu.CompilerParams(
            collective_id=1, has_side_effects=True, vmem_limit_bytes=LIMIT
        ),
        cost_estimate=pl.CostEstimate(flops=1 << 28, bytes_accessed=12 << 20, transcendentals=0),
        name="middle_step",
    )(outgoing, tokens, d_out, w_attn, gains, mlp_pair, mlp_near)


def mlp_kernel(chunk, x_ref, up_ref, w_ref, back_ref, forward_ref, terms_ref, kept):
    count, width = x_ref.shape

    @pl.loop(0, count // chunk)
    def _(i):
        at = pl.ds(pl.multiple_of(i * chunk, chunk), chunk)
        gate_up = dot(x_ref[at, :], w_ref[:, : 2 * SLICE], 1, 0)
        left, right = gate_up[:, :SLICE], gate_up[:, SLICE:]
        grad_mixed = dot(up_ref[at, :], w_ref[:, 2 * SLICE :], 1, 0)
        normal_cdf = 0.5 * (1.0 + lax.erf(left * 0.7071067811865476))
        gelu = left * normal_cdf
        density = jnp.exp(-0.5 * left * left) * 0.3989422804014327
        kept[at, :SLICE] = (grad_mixed * right * (normal_cdf + left * density)).astype(BF)
        kept[at, SLICE : 2 * SLICE] = (grad_mixed * gelu).astype(BF)
        kept[at, 2 * SLICE :] = (gelu * right).astype(BF)
        back_ref[at, :] = dot(kept[at, : 2 * SLICE], w_ref[:, : 2 * SLICE], 1, 1).astype(BF)
        forward_ref[at, :] = dot(kept[at, 2 * SLICE :], w_ref[:, 2 * SLICE :], 1, 1).astype(BF)

    @pl.loop(0, width // chunk)
    def _(i):
        at = pl.ds(pl.multiple_of(i * chunk, chunk), chunk)
        terms_ref[at, : 2 * SLICE] = dot(x_ref[:, at], kept[:, : 2 * SLICE], 0, 0).astype(BF)
        terms_ref[at, 2 * SLICE :] = dot(up_ref[:, at], kept[:, 2 * SLICE :], 0, 0).astype(BF)


def mlp_step(x, up, w, chunk):
    count, width = x.shape
    return pl.pallas_call(
        functools.partial(mlp_kernel, chunk),
        in_specs=[VMEM] * 3,
        out_specs=[VMEM] * 3,
        out_shape=[
            jax.ShapeDtypeStruct((count, width), BF),
            jax.ShapeDtypeStruct((count, width), BF),
            jax.ShapeDtypeStruct((width, 3 * SLICE), BF),
        ],
        scratch_shapes=[pltpu.VMEM((count, 3 * SLICE), BF)],
        compiler_params=pltpu.CompilerParams(vmem_limit_bytes=LIMIT),
        cost_estimate=pl.CostEstimate(
            flops=18 * count * width * SLICE, bytes_accessed=14 << 20, transcendentals=2 * count * SLICE
        ),
        name="mlp_step",
    )(x, up, w)


def turn_kernel(
    groups,
    reach,
    partial,
    middle,
    d_out,
    w_attn,
    gains,
    attended,
    grads,
    grad_middle,
    attn_part,
    columns,
    total,
    outgoing,
    branch,
    a2a_send,
    a2a_recv,
    own,
    side_send,
    side_recv,
    side_own,
    *halving,
):
    place = Place(groups, reach)
    group = groups * reach
    lanes = branch.shape[2]
    meet([place.member((place.idx + step) % group) for step in range(1, group)])
    Halving(place, 2, partial, total, halving).run()
    normed, inverse_std = norm_parts(middle[...])
    upstream = total[...]
    grad = d_out[...].astype(F32) + norm_back(upstream, normed, inverse_std, gains[1:2, :])
    grad_middle[...] = grad
    low = grad.astype(BF)
    for g in range(groups):
        branch[g] = low[:, g * lanes : (g + 1) * lanes]
    outgoing[...] = dot(w_attn[...], low, 1, 1).astype(BF).reshape(outgoing.shape)
    copies = spread(place, outgoing, grads, (a2a_send, a2a_recv, own))
    for step in range(1, groups):
        peer = (place.head + step) % groups
        copies.append(
            push(
                branch.at[peer],
                columns.at[place.head],
                {"heads": peer},
                side_send.at[step - 1],
                side_recv.at[step - 1],
            )
        )
    local = pltpu.make_async_copy(branch.at[place.head], columns.at[place.head], side_own)
    local.start()
    for copy in copies[-(groups - 1) :]:
        copy.wait()
    local.wait()
    attn_part[...] = functools.reduce(
        jnp.add, [dot(attended[g], columns[g], 1, 0) for g in range(groups)]
    ).astype(BF)
    for copy in copies[: -(groups - 1)]:
        copy.wait()


def turn_step(partial, middle, d_out, w_attn, gains, attended, groups, reach):
    rows, width = middle.shape
    group = groups * reach
    return pl.pallas_call(
        functools.partial(turn_kernel, groups, reach),
        in_specs=[VMEM] * 6,
        out_specs=[ANY, VMEM, VMEM],
        out_shape=[
            jax.ShapeDtypeStruct((group, HD, rows), BF),
            jax.ShapeDtypeStruct((rows, width), F32),
            jax.ShapeDtypeStruct((width, width // groups), BF),
        ],
        scratch_shapes=[
            pltpu.VMEM((groups, rows, width // groups), BF),
            pltpu.VMEM((rows, width), F32),
            pltpu.VMEM((group, HD, rows), BF),
            pltpu.VMEM((groups, rows, width // groups), BF),
            DMA((group - 1,)),
            DMA((group - 1,)),
            DMA,
            DMA((groups - 1,)),
            DMA((groups - 1,)),
            DMA,
            *Halving.scratch(2, rows, width),
        ],
        compiler_params=pltpu.CompilerParams(
            collective_id=2, has_side_effects=True, vmem_limit_bytes=LIMIT
        ),
        cost_estimate=pl.CostEstimate(flops=1 << 28, bytes_accessed=12 << 20, transcendentals=0),
        name="turn_step",
    )(partial, middle, d_out, w_attn, gains, attended)


def attend_back_kernel(
    groups,
    reach,
    lines,
    tile,
    qkv_ref,
    grad_ref,
    wide_ref,
    lse_ref,
    x_ref,
    w_ref,
    cos_ref,
    sin_ref,
    forward_ref,
    attn_ref,
    out_ref,
    weight_ref,
    ahead_ref,
    attn_out_ref,
    sums,
    queries,
    weight,
    attn_land,
    *sems,
):
    count = x_ref.shape[0]
    rows = grad_ref.shape[2]
    steps, per_tile = count // tile, tile // rows
    step = pl.program_id(0)
    place = Place(groups, reach)
    halving = Halving(place, 2, forward_ref, ahead_ref, sems[:7])
    swap = Lines(lines, attn_ref, attn_land, *sems[7:])

    @pl.when(step == 0)
    def _():
        greet(everyone(place, lines))
        sums[...] = jnp.zeros_like(sums)

    here = pl.ds(pl.multiple_of(step * tile, tile), tile)
    query = qkv_ref[:QM_END, here]
    grad = jnp.concatenate([grad_ref[step * per_tile + k] for k in range(per_tile)], axis=1)
    delta = jnp.sum(grad.astype(F32) * wide_ref[:, here], axis=0, keepdims=True)
    lse = lse_ref[:, here]
    grad_query = jnp.zeros((HD, tile), F32)
    for j in range(steps):
        keys = slice(j * tile, (j + 1) * tile)
        prob = jnp.exp(dot(qkv_ref[QM_END:KM_END, keys], query, 0, 0) - lse)
        grad_prob = dot(qkv_ref[KM_END:, keys], grad, 0, 0)
        grad_score = (prob * (grad_prob - delta)).astype(BF)
        grad_query += dot(qkv_ref[QM_END:K_END, keys], grad_score, 1, 0)
        sums[:HD, keys] += dot(query[:HD], grad_score, 1, 1)
        sums[HD:, keys] += dot(grad, prob.astype(BF), 1, 1)
    queries[:, here] = (grad_query * 0.125).astype(BF)

    @pl.when(step == 0)
    def _():
        pl.semaphore_wait(pltpu.get_barrier_semaphore(), len(everyone(place, lines)))
        halving.start()
        swap.start()

    pl.when(step == min(1, steps - 1))(halving.pair)
    pl.when(step == min(2, steps - 1))(lambda: halving.halve(0))

    @pl.when(step == steps - 1)
    def _():
        weight[...] = jnp.zeros_like(weight)

        @pl.loop(0, steps)
        def _(i):
            at = pl.ds(pl.multiple_of(i * tile, tile), tile)
            cosine, sine = cos_ref[:, at], sin_ref[:, at]

            def turn_back(value):
                front, back = value[:HALF], value[HALF:]
                return [front * cosine + back * sine, back * cosine - front * sine]

            low = lambda value: value.astype(BF).astype(F32)
            projected = jnp.concatenate(
                [
                    *turn_back(queries[:, at].astype(F32)),
                    *turn_back(low(sums[:HD, at])),
                    low(sums[HD:, at]),
                ],
                axis=0,
            ).astype(BF)
            part = dot(projected, w_ref[...], 0, 1).astype(BF)
            for k in range(per_tile):
                out_ref[i * per_tile + k] = part[k * rows : (k + 1) * rows]
            weight[...] += dot(projected, x_ref[at, :], 1, 0)

        shard = weight_ref.shape[2]
        for c in range(lines):
            weight_ref[c] = weight[:, c * shard : (c + 1) * shard].astype(BF)
        halving.halve(1)
        swap.finish()
        attn_out_ref[...] = functools.reduce(
            jnp.add, [attn_land[c].astype(F32) for c in range(lines)]
        ).astype(BF)
        halving.finish()


def attend_back(qkv, grad, wide, lse, x, w, cosine, sine, forward, attn, groups, reach, tile):
    count, width = x.shape
    blocks, _, rows = grad.shape
    lines, shard, lanes = attn.shape
    whole = lambda *shape: pl.BlockSpec(shape, lambda i: (0,) * len(shape))
    operands = (qkv, grad, wide, lse, x, w, cosine, sine, forward)
    return pl.pallas_call(
        functools.partial(attend_back_kernel, groups, reach, lines, tile),
        grid=(count // tile,),
        in_specs=[*[whole(*operand.shape) for operand in operands], ANY],
        out_specs=[
            whole(blocks, rows, width),
            whole(lines, 3 * HD, shard),
            whole(rows, width),
            whole(shard, lanes),
        ],
        out_shape=[
            jax.ShapeDtypeStruct((blocks, rows, width), BF),
            jax.ShapeDtypeStruct((lines, 3 * HD, shard), BF),
            jax.ShapeDtypeStruct((rows, width), F32),
            jax.ShapeDtypeStruct((shard, lanes), BF),
        ],
        scratch_shapes=[
            pltpu.VMEM((2 * HD, count), F32),
            pltpu.VMEM((HD, count), BF),
            pltpu.VMEM((3 * HD, width), F32),
            pltpu.VMEM((lines, shard, lanes), BF),
            *Halving.scratch(2, rows, width),
            *Lines.scratch(lines),
        ],
        compiler_params=pltpu.CompilerParams(
            collective_id=4, has_side_effects=True, vmem_limit_bytes=56 << 20
        ),
        cost_estimate=pl.CostEstimate(
            flops=count * count * HD * 20, bytes_accessed=count * 6144, transcendentals=count * count
        ),
        name="attend_back",
    )(*operands, attn)


class Collect:
    def __init__(self, groups, pieces, far_send, far_recv, near_send, near_recv):
        head = lax.axis_index("heads")
        self.half = half = groups // 2
        pair = {"heads": flip(head, 1)}
        self.far, self.near = [], []
        for n, (piece, where) in enumerate(pieces):
            self.far.append(
                [
                    remote(
                        piece,
                        where(head),
                        {"heads": (head + 2 * k) % groups},
                        far_send.at[n, k - 1],
                        far_recv.at[n, k - 1],
                    )
                    for k in range(1, half)
                ]
            )
            sides = [(piece, where(head))]
            for k in range(1, half):
                got = where((head - 2 * k + groups) % groups)
                sides.append((got, got))
            self.near.append(
                [
                    remote(source, target, pair, near_send.at[n, k], near_recv.at[n, k])
                    for k, (source, target) in enumerate(sides)
                ]
            )

    @staticmethod
    def scratch(count, groups):
        far, near = (count, max(groups // 2 - 1, 1)), (count, groups // 2)
        return [DMA(far), DMA(far), DMA(near), DMA(near)]

    def start(self, n):
        for copy in self.far[n]:
            copy.start()
        self.near[n][0].start()

    def forward(self, n):
        for k, copy in enumerate(self.far[n]):
            copy.wait_recv()
            self.near[n][k + 1].start()

    def finish(self):
        for copies in self.far:
            for copy in copies:
                copy.wait_send()
        for copies in self.near:
            for copy in copies:
                copy.wait()


def end_kernel(
    groups,
    reach,
    lines,
    partial,
    weight,
    mlp,
    attn,
    total,
    mlp_all,
    weight_all,
    attn_all,
    lined,
    summed,
    swap_send,
    swap_recv,
    own,
    *rest,
):
    place = Place(groups, reach)
    sub = mlp.shape[0]
    mine, head = place.ctx % sub, place.head
    meet(everyone(place, lines))
    wide = Halving(place, 3, partial, total, rest[:7])
    swap = Lines(lines, weight, lined, *rest[7:10])
    wide.start()
    swaps = []
    for step in range(1, sub):
        peer = (mine + step) % sub
        swaps.append(
            push(
                mlp.at[peer],
                mlp_all.at[mine, head],
                {"ctx": place.ctx - mine + peer},
                swap_send.at[step - 1],
                swap_recv.at[step - 1],
            )
        )
    pieces = [(mlp.at[mine], lambda h: mlp_all.at[mine, h]), (attn, lambda h: attn_all.at[h])]
    for step in range(1, sub):
        source = (mine - step + sub) % sub
        pieces.append(
            (mlp_all.at[source, head], lambda h, source=source: mlp_all.at[source, h])
        )
    pieces.append((summed, lambda h: weight_all.at[h]))
    collect = Collect(groups, pieces, *rest[10:14])
    swap.start()
    local = [
        pltpu.make_async_copy(mlp.at[mine], mlp_all.at[mine, head], own.at[0]),
        pltpu.make_async_copy(attn, attn_all.at[head], own.at[1]),
        pltpu.make_async_copy(summed, weight_all.at[head], own.at[2]),
    ]
    local[0].start()
    local[1].start()
    collect.start(0)
    collect.start(1)
    wide.pair()
    for step in range(1, sub):
        swaps[step - 1].wait_recv()
        collect.start(step + 1)
    swap.finish()
    for r in range(reach):
        summed[r] = functools.reduce(
            jnp.add, [lined[r + reach * g].astype(F32) for g in range(lines // reach)]
        ).astype(BF)
    local[2].start()
    collect.start(sub + 1)
    for step in range(3):
        wide.halve(step)
        if step == 1:
            for n in range(sub + 1):
                collect.forward(n)
    collect.forward(sub + 1)
    for copy in local:
        copy.wait()
    for copy in swaps:
        copy.wait_send()
    collect.finish()
    wide.finish()


def end_step(partial, weight, mlp, attn, groups, reach):
    rows, width = partial.shape[2:]
    lines, _, shard = weight.shape
    sub = mlp.shape[0]
    return pl.pallas_call(
        functools.partial(end_kernel, groups, reach, lines),
        in_specs=[VMEM, ANY, ANY, ANY],
        out_specs=[VMEM, ANY, ANY, ANY],
        out_shape=[
            jax.ShapeDtypeStruct((rows, width), F32),
            jax.ShapeDtypeStruct((sub, groups, *mlp.shape[1:]), BF),
            jax.ShapeDtypeStruct((groups, reach, 3 * HD, shard), BF),
            jax.ShapeDtypeStruct((groups, *attn.shape), BF),
        ],
        scratch_shapes=[
            pltpu.VMEM((lines, 3 * HD, shard), BF),
            pltpu.VMEM((reach, 3 * HD, shard), BF),
            DMA((max(sub - 1, 1),)),
            DMA((max(sub - 1, 1),)),
            DMA((3,)),
            *Halving.scratch(3, rows, width),
            *Lines.scratch(lines),
            *Collect.scratch(sub + 2, groups),
        ],
        compiler_params=pltpu.CompilerParams(
            collective_id=3, has_side_effects=True, vmem_limit_bytes=LIMIT
        ),
        cost_estimate=pl.CostEstimate(flops=0, bytes_accessed=24 << 20, transcendentals=0),
        name="end_step",
    )(partial, weight, mlp, attn)


def assemble_kernel(
    upstream,
    tokens,
    grad_middle,
    gains,
    middle,
    ahead,
    weight_all,
    attn_all,
    mlp_all,
    w_qkv,
    w_in,
    own_gains,
    result,
    grad,
    sum_qkv,
    sum_attn,
    sum_in,
    sum_out,
    gain_sums,
):
    groups, reach, _, shard = weight_all.shape
    lanes = attn_all.shape[2]
    result[...] = (middle[...] + ahead[...]).astype(BF)
    normed, inverse_std = norm_parts(tokens[...].astype(F32))
    grad[...] = grad_middle[...] + norm_back(upstream[...], normed, inverse_std, gains[0:1, :])
    for g in range(groups):
        sum_attn[:, g * lanes : (g + 1) * lanes] = attn_all[g].astype(F32)
    gain_one = jnp.zeros((shard, 128), F32)
    for third in range(3):
        part = slice(third * HD, (third + 1) * HD)
        for pair in range(H // 2):
            r, g = 2 * pair // groups, 2 * pair % groups
            tile = (
                jnp.concatenate([weight_all[g, r, part], weight_all[g + 1, r, part]], axis=0)
                .astype(F32)
                .T
            )
            at = third * H * HD + pair * 2 * HD
            sum_qkv[:, at : at + 2 * HD] = tile
            gain_one += tile * w_qkv[:, at : at + 2 * HD].astype(F32)
    gain_two = jnp.zeros((shard, 1), F32)
    for t in range(8):
        start, wide = slice_place(t)
        for half in range(2):
            piece = mlp_all[t, :, half * SLICE : half * SLICE + wide].astype(F32)
            at = half * FF + start
            sum_in[:, at : at + wide] = piece
            gain_two += jnp.sum(
                piece * w_in[:, at : at + wide].astype(F32), axis=1, keepdims=True
            )
        sum_out[start : start + wide, :] = (
            mlp_all[t, :, 2 * SLICE : 3 * SLICE].astype(F32).T[:wide]
        )
    one = jnp.sum(gain_one, axis=1, keepdims=True)
    lane = lax.broadcasted_iota(jnp.int32, (shard, 128), 1)
    both = jnp.where(lane == 0, one, gain_two).T
    gain_sums[...] = both[:8] / own_gains[...]


def assemble(upstream, tokens, grad_middle, gains, middle, ahead, weight_all, attn_all, mlp_all, w_qkv, w_in, own_gains):
    rows, width = tokens.shape
    shard = w_qkv.shape[0]
    return pl.pallas_call(
        assemble_kernel,
        in_specs=[VMEM] * 12,
        out_specs=[VMEM] * 7,
        out_shape=[
            jax.ShapeDtypeStruct((rows, width), BF),
            jax.ShapeDtypeStruct((rows, width), F32),
            jax.ShapeDtypeStruct((shard, 3 * width), F32),
            jax.ShapeDtypeStruct((shard, width), F32),
            jax.ShapeDtypeStruct((shard, 2 * FF), F32),
            jax.ShapeDtypeStruct((FF, shard), F32),
            jax.ShapeDtypeStruct((8, shard), F32),
        ],
        compiler_params=pltpu.CompilerParams(vmem_limit_bytes=LIMIT),
        cost_estimate=pl.CostEstimate(flops=1 << 24, bytes_accessed=20 << 20, transcendentals=0),
        name="assemble",
    )(upstream, tokens, grad_middle, gains, middle, ahead, weight_all, attn_all, mlp_all, w_qkv, w_in, own_gains)


def slice_start(t):
    return 128 * jnp.minimum(3 * t, 2 * t + 5)


def slice_place(t):
    start = 128 * min(3 * t, 2 * t + 5)
    return start, min(128 * min(3 * t + 3, 2 * t + 7), FF) - start


def body(count, tokens, d_out, segment_ids, position_ids, w_qkv, w_attn, w_in, w_out, gain_attn, gain_mlp):
    groups = lax.axis_size("heads")
    rows, width = tokens.shape
    shard = w_qkv.shape[0]
    reach = SEQ_MAX // (rows * groups)
    group = reach * groups
    sub = 8 // groups
    ctx, head = lax.axis_index("ctx"), lax.axis_index("heads")
    assert group == H and sub * groups == 8
    total = group * rows
    tile = 512

    def mlp_slice(value, axis, start, t):
        pads = [(0, 0), (0, 0)]
        pads[axis] = (0, SLICE)
        piece = lax.dynamic_slice_in_dim(jnp.pad(value, pads), start + slice_start(t), SLICE, axis)
        wide = jnp.minimum(slice_start(t + 1), FF) - slice_start(t)
        shape = [1, 1]
        shape[axis] = SLICE
        return jnp.where(jnp.arange(SLICE).reshape(shape) < wide, piece, jnp.zeros_like(piece))

    def mlp_part(t):
        return jnp.concatenate(
            [mlp_slice(w_in, 1, 0, t), mlp_slice(w_in, 1, FF, t), mlp_slice(w_out, 0, 0, t).T], axis=1
        )

    mlp = jnp.stack([mlp_part(x * groups + head) for x in range(sub)])
    lines = [list(range(k, count, sub)) for k in range(sub)]
    gains_own = jnp.pad(jnp.stack([gain_attn, gain_mlp]).astype(F32), ((0, 6), (0, -shard % 128)))
    ids = jnp.pad(jnp.stack([position_ids, segment_ids]), ((0, 6), (0, 0)))
    freqs = jnp.power(160000.0, -(2.0 * jnp.arange(HALF, dtype=F32)) / HD)[:, None]
    input_all, gains, w_head, cosine, sine, marks, attn_part, mlp_pair = begin(
        tokens, gains_own, ids, w_qkv, w_attn, mlp, freqs, count, groups, reach
    )
    x = input_all.reshape(total, width)

    attended, wide, lse, qkv, attn_weights, mlp_near = attend(
        x, w_head, cosine, sine, marks, attn_part, mlp_pair, count, groups, reach, rows, tile
    )
    attn_weights = attn_weights.reshape(width, width)
    mlp_all, upstream, middle, attended, mlp_weights = middle_step(
        attended, tokens, d_out, attn_weights, gains, mlp_pair, mlp_near, count, groups, reach
    )
    mlp_weights = mlp_weights.reshape(width, 3 * SLICE)
    split = lambda value, blocks: value.reshape(blocks // 2, 2, rows, width)
    back, forward, mlp_terms = mlp_step(
        mlp_all.reshape(8 * rows, width), upstream.reshape(8 * rows, width), mlp_weights, 512
    )
    mlp_sum = lax.psum_scatter(
        mlp_terms, "ctx", scatter_dimension=0, tiled=True, axis_index_groups=lines
    ).reshape(sub, shard, 3 * SLICE)
    grad_heads, grad_middle, attn_part = turn_step(
        split(back, 8),
        middle,
        d_out,
        attn_weights,
        gains,
        attended.reshape(groups, width, rows),
        groups,
        reach,
    )
    attn_part = attn_part.reshape(count, shard, width // groups)
    forward = split(forward, 8)
    grad_input_parts, weight, ahead, attn_sum = attend_back(
        qkv, grad_heads, wide, lse, x, w_head, cosine, sine, forward, attn_part, groups, reach, tile
    )
    upstream_in, mlp_all, weight_all, attn_all = end_step(
        split(grad_input_parts, group), weight, mlp_sum, attn_sum, groups, reach
    )
    result, grad_input, sum_qkv, sum_attn, sum_in, sum_out, gain_sums = assemble(
        upstream_in,
        tokens,
        grad_middle,
        gains,
        middle,
        ahead,
        weight_all,
        attn_all,
        mlp_all.reshape(8, shard, 3 * SLICE),
        w_qkv,
        w_in,
        jnp.pad(gains_own[:2, :shard], ((0, 6), (0, 0)), constant_values=1.0),
    )
    return (
        result,
        grad_input,
        sum_qkv,
        sum_attn,
        sum_in,
        sum_out,
        gain_sums[0],
        gain_sums[1],
    )


def solution(mesh):
    return jax.shard_map(
        functools.partial(body, mesh.shape["ctx"]),
        mesh=mesh,
        in_specs=(
            P(("ctx", "heads"), None),
            P(("ctx", "heads"), None),
            P(("ctx", "heads")),
            P(("ctx", "heads")),
            P("ctx", None),
            P("ctx", None),
            P("ctx", None),
            P(None, "ctx"),
            P("ctx"),
            P("ctx"),
        ),
        out_specs=(
            P(("ctx", "heads"), None),
            P(("ctx", "heads"), None),
            P("ctx", None),
            P("ctx", None),
            P("ctx", None),
            P(None, "ctx"),
            P("ctx"),
            P("ctx"),
        ),
        check_vma=False,
    )
```

```python
import functools

import jax
import jax.numpy as jnp
from jax import lax
from jax.experimental import pallas as pl
from jax.experimental.pallas import tpu as pltpu
from jax.sharding import PartitionSpec as P

H = 16
HD = 64
HALF = HD // 2
FF = 2624
SEQ_MAX = 2048
MASKED = -1e30
MARKS = 16
QM_END = HD + MARKS
K_END = QM_END + HD
KM_END = K_END + MARKS
V_END = KM_END + HD
SLICE = 384
BF = jnp.bfloat16
F32 = jnp.float32
MESH = pl.DeviceIdType.MESH
VMEM = pl.BlockSpec(memory_space=pltpu.VMEM)
ANY = pl.BlockSpec(memory_space=pl.ANY)
DMA = pltpu.SemaphoreType.DMA


def dot(left, right, left_dim, right_dim):
    return lax.dot_general(
        left, right, (((left_dim,), (right_dim,)), ((), ())), preferred_element_type=F32
    )


def norm_parts(values):
    average = jnp.mean(values, axis=-1, keepdims=True)
    centred = values - average
    inverse_std = lax.rsqrt(jnp.mean(centred * centred, axis=-1, keepdims=True) + 1e-05)
    return centred * inverse_std, inverse_std


def norm_back(upstream, normed, inverse_std, gain):
    scaled = upstream * gain
    return inverse_std * (
        scaled
        - jnp.mean(scaled, axis=-1, keepdims=True)
        - normed * jnp.mean(scaled * normed, axis=-1, keepdims=True)
    )


def flip(value, bit):
    return value + bit - 2 * bit * (value // bit % 2)


class Place:
    def __init__(self, groups, reach):
        self.groups, self.reach = groups, reach
        self.ctx = lax.axis_index("ctx")
        self.head = lax.axis_index("heads")
        self.local = self.ctx % reach
        self.base = self.ctx - self.local
        self.idx = self.local * groups + self.head

    def member(self, j):
        return {"ctx": self.base + j // self.groups, "heads": j % self.groups}


def greet(devices):
    barrier = pltpu.get_barrier_semaphore()
    for device in devices:
        pl.semaphore_signal(barrier, inc=1, device_id=device, device_id_type=MESH)


def meet(devices):
    greet(devices)
    pl.semaphore_wait(pltpu.get_barrier_semaphore(), len(devices))


def remote(source, target, device, send, recv):
    return pltpu.make_async_remote_copy(
        src_ref=source,
        dst_ref=target,
        send_sem=send,
        recv_sem=recv,
        device_id=device,
        device_id_type=MESH,
    )


def push(*operands):
    copy = remote(*operands)
    copy.start()
    return copy


def tree_parts(axes, rows):
    if axes == 3:
        return [None, (0, rows), None]
    part = -(-rows // axes // 16) * 16
    starts = [min(part * a, rows) for a in range(axes + 1)]
    return [(starts[a], starts[a + 1] - starts[a]) for a in range(axes)]


class Tree:
    def __init__(self, place, axes, source, target, sems):
        self.place, self.axes, self.source, self.target = place, axes, source, target
        self.send, self.recv, self.core_send, self.core_recv, self.own = sems
        self.slots = 2 << axes
        self.levels, self.cores = [], []

    @staticmethod
    def scratch(axes):
        far, near = axes * axes, axes * axes + 1
        return [DMA((far,)), DMA((far,)), DMA((near,)), DMA((near,)), DMA]

    def origin(self, level, first):
        value = self.place.idx
        for k in range(level):
            value = flip(value, 2 << ((first + k) % self.axes))
        return value % self.slots

    def neighbour(self, axis):
        return self.place.member(flip(self.place.idx, 2 << (axis % self.axes)))

    def piece(self, slot, part):
        return self.target.at[slot] if part is None else self.target.at[slot, pl.ds(*part)]

    def to_core(self, source, slot, part):
        at = len(self.cores)
        self.cores.append(
            push(
                source,
                self.piece(slot, part),
                self.place.member(flip(self.place.idx, 1)),
                self.core_send.at[at],
                self.core_recv.at[at],
            )
        )

    def start(self):
        me = self.place.idx % self.slots
        self.levels.append(
            [
                push(
                    self.source, self.target.at[me], self.neighbour(a), self.send.at[a], self.recv.at[a]
                )
                for a in range(self.axes)
            ]
        )
        self.to_core(self.source, me, None)
        self.local = pltpu.make_async_copy(self.source, self.target.at[me], self.own)
        self.local.start()

    def forward(self, level):
        axes = self.axes
        parts = tree_parts(axes, self.target.shape[1])
        onward = []
        for a in range(axes):
            if self.levels[level - 1][a] is None:
                continue
            self.levels[level - 1][a].wait_recv()
            slot = self.origin(level, a)
            if level < axes:
                part = parts[a] if level + 1 == axes else None
                if level + 1 == axes and part is None:
                    onward.append(None)
                    self.to_core(self.target.at[slot], slot, None)
                    continue
                at = level * axes + a
                piece = self.piece(slot, part)
                onward.append(
                    push(piece, piece, self.neighbour(a + level), self.send.at[at], self.recv.at[at])
                )
                self.to_core(self.target.at[slot], slot, None)
            else:
                self.to_core(self.piece(slot, parts[a]), slot, parts[a])
        self.levels.append(onward)

    def finish(self):
        self.local.wait()
        for level in self.levels:
            for copy in level:
                if copy is not None:
                    copy.wait_send()
        for copy in self.cores:
            copy.wait()


class Halving:
    def __init__(self, place, axes, value, result, scratch, widths=None):
        self.axes, self.value, self.result = axes, value, result
        self.other, self.held, self.land, send, recv, send0, recv0 = scratch
        self.blocks = 1 << axes
        width = value.shape[-1]
        widths = widths or [width // axes] * axes
        self.columns = [pl.ds(sum(widths[:a]), widths[a]) for a in range(axes)]
        self.core = place.idx % 2
        self.chip = place.idx // 2 % self.blocks
        self.sources = []
        for j in range(self.blocks):
            k = self.chip
            for a in range(axes):
                if j >> a & 1:
                    k = flip(k, 1 << a)
            self.sources.append(k)
        self.first, self.copies = [], {}
        for p in range(axes):
            self.first.append(
                remote(
                    value.at[:, 1 - self.core, :, self.columns[p]],
                    self.other.at[:, :, self.columns[p]],
                    place.member(flip(place.idx, 1)),
                    send0.at[p],
                    recv0.at[p],
                )
            )
            for step in range(axes):
                bit, sent = self.sent(p, step)
                for j in sent:
                    self.copies[p, j] = remote(
                        self.held.at[j, :, self.columns[p]],
                        self.land.at[j, :, self.columns[p]],
                        place.member(flip(place.idx, 2 * bit)),
                        send.at[p, j],
                        recv.at[p, j],
                    )

    @staticmethod
    def scratch(axes, rows, width):
        blocks = 1 << axes
        return [
            pltpu.VMEM((blocks, rows, width), BF),
            pltpu.VMEM((blocks, rows, width), BF),
            pltpu.VMEM((blocks, rows, width), BF),
            DMA((axes, blocks)),
            DMA((axes, blocks)),
            DMA((axes,)),
            DMA((axes,)),
        ]

    def sent(self, part, step):
        seen = [1 << ((part + s) % self.axes) for s in range(step)]
        bit = 1 << ((part + step) % self.axes)
        return bit, [j for j in range(self.blocks) if j & bit and not any(j & s for s in seen)]

    def start(self):
        for copy in self.first:
            copy.start()

    def pair(self):
        for p in range(self.axes):
            cols = self.columns[p]
            self.first[p].wait_recv()
            _, early = self.sent(p, 0)
            for j in early + [j for j in range(self.blocks) if j not in early]:
                k = self.sources[j]
                self.held[j, :, cols] = (
                    self.value[k, self.core, :, cols].astype(F32) + self.other[k, :, cols].astype(F32)
                ).astype(BF)
                if j in early:
                    self.copies[p, j].start()

    def halve(self, step):
        for p in range(self.axes):
            cols = self.columns[p]
            bit, arrived = self.sent(p, step)
            onward = self.sent(p, step + 1)[1] if step + 1 < self.axes else []
            for j in sorted(arrived, key=lambda j: (j - bit) not in onward):
                self.copies[p, j].wait_recv()
                k = j - bit
                total = self.held[k, :, cols].astype(F32) + self.land[j, :, cols].astype(F32)
                if step + 1 < self.axes:
                    self.held[k, :, cols] = total.astype(BF)
                    if k in onward:
                        self.copies[p, k].start()
                else:
                    self.result[:, cols] = total

    def run(self):
        self.start()
        self.pair()
        for step in range(self.axes):
            self.halve(step)
        self.finish()

    def finish(self):
        for copy in self.first:
            copy.wait_send()
        for copy in self.copies.values():
            copy.wait_send()


class Lines:
    def __init__(self, count, source, target, send, recv, own):
        me = lax.axis_index("ctx")
        self.copies = [pltpu.make_async_copy(source.at[me], target.at[me], own)]
        for step in range(1, count):
            peer = (me + step) % count
            self.copies.append(
                remote(source.at[peer], target.at[me], {"ctx": peer}, send.at[step - 1], recv.at[step - 1])
            )

    @staticmethod
    def scratch(count):
        return [DMA((count - 1,)), DMA((count - 1,)), DMA]

    def start(self):
        for copy in self.copies:
            copy.start()

    def finish(self):
        for copy in self.copies:
            copy.wait()


def everyone(place, count):
    group = place.reach * place.groups
    mates = [place.member((place.idx + step) % group) for step in range(1, group)]
    outside = [{"ctx": (place.base + place.reach + step) % count} for step in range(count - place.reach)]
    return mates + outside


def spread(place, source, target, sems, me=None):
    send, recv, own = sems
    count = target.shape[0]
    copies = []
    for step in range(1, count):
        peer = (place.idx + step) % count
        copies.append(
            push(
                source.at[peer],
                target.at[place.idx],
                place.member(peer),
                send.at[step - 1],
                recv.at[step - 1],
            )
        )
    local = pltpu.make_async_copy(source.at[place.idx], target.at[place.idx], own)
    local.start()
    copies.append(local)
    return copies


def begin_kernel(
    groups,
    reach,
    count,
    tokens,
    gains,
    ids,
    w_qkv,
    w_attn,
    freqs,
    input_all,
    gains_all,
    w_head,
    cosine,
    sine,
    marks,
    attn_half,
    ids_all,
    slab,
    mine,
    gain_land,
    own_sems,
    ids_send,
    ids_recv,
    gain_send,
    gain_recv,
    slab_send,
    slab_recv,
    wide_send,
    wide_recv,
    core_send,
    core_recv,
    *tree_sems,
):
    place = Place(groups, reach)
    group = reach * groups
    ctx, head, idx = place.ctx, place.head, place.idx
    shard = w_qkv.shape[0]
    ring = attn_half.shape[0]
    sub = count // ring
    side, spot = ctx % sub, ctx // sub
    lanes = attn_half.shape[2] // groups
    core = {"heads": flip(head, 1)}
    mates = [place.member((idx + step) % group) for step in range(1, group)]
    lines = [{"ctx": (ctx + step) % count} for step in range(1, count)]
    meet(everyone(place, count))
    first = [
        push(gains, gain_land.at[ctx], lines[step - 1], gain_send.at[step - 1], gain_recv.at[step - 1])
        for step in range(1, count)
    ]
    small = [
        push(ids, ids_all.at[idx], mates[step - 1], ids_send.at[step - 1], ids_recv.at[step - 1])
        for step in range(1, group)
    ]
    half = pl.ds(pl.multiple_of(head % 2 * (shard // 2), 16), shard // 2)
    thirds = []
    for step in range(1, count):
        peer = (ctx + step) % count
        column = ((peer % reach) * groups + head) // 2 * 128
        for third in range(3):
            start = pl.multiple_of(third * 1024 + column, 128)
            thirds.append(
                push(
                    w_qkv.at[half, pl.ds(start, 128)],
                    slab.at[ctx, half, pl.ds(third * 128, 128)],
                    lines[step - 1],
                    slab_send.at[step - 1, third],
                    slab_recv.at[step - 1, third],
                )
            )
    gain_land[ctx] = gains[...]
    where = lambda h: pl.ds(pl.multiple_of(h * lanes, 128), lanes)
    across = where(head)
    own = [
        pltpu.make_async_copy(ids, ids_all.at[idx], own_sems.at[3]),
        pltpu.make_async_copy(w_attn.at[:, across], attn_half.at[spot, :, across], own_sems.at[4]),
    ]
    for third in range(3):
        start = pl.multiple_of(third * 1024 + idx // 2 * 128, 128)
        own.append(
            pltpu.make_async_copy(
                w_qkv.at[half, pl.ds(start, 128)],
                slab.at[ctx, half, pl.ds(third * 128, 128)],
                own_sems.at[third],
            )
        )
    for copy in own:
        copy.start()
    for copy in first:
        copy.wait_recv()
    gain, gain_two = (
        jnp.concatenate([gain_land[c, k : k + 1, :shard] for c in range(count)], axis=1)
        for k in range(2)
    )
    normed, _ = norm_parts(tokens[...].astype(F32))
    mine[...] = (normed * gain).astype(BF)
    tree = Tree(place, 3, mine, input_all, tree_sems[:5])
    tree.start()
    gains_all[0:1, :] = gain
    gains_all[1:2, :] = gain_two
    late = []
    for step in range(1, ring):
        late.append(
            push(
                w_attn.at[:, across],
                attn_half.at[spot, :, across],
                {"ctx": (spot + step) % ring * sub + side},
                wide_send.at[step - 1],
                wide_recv.at[step - 1],
            )
        )
    tree.forward(1)
    for copy in own:
        copy.wait()
    for copy in thirds:
        copy.wait_recv()
    for copy in late:
        copy.wait_recv()
    collect = Collect(
        groups, [(attn_half.at[:, :, across], lambda h: attn_half.at[:, :, where(h)])], *tree_sems[5:]
    )
    collect.start(0)
    shared = push(slab.at[:, half], slab.at[:, half], core, core_send, core_recv)
    for copy in small:
        copy.wait()
    row = lambda k: jnp.concatenate([ids_all[j, k : k + 1, :] for j in range(group)], axis=1)
    angles = freqs[...] * row(0).astype(F32)
    cosine[...] = jnp.cos(angles)
    sine[...] = jnp.sin(angles)
    parity = (row(1) % 2).astype(F32)
    blank = jnp.zeros((MARKS - 2, parity.shape[1]), F32)
    marks[...] = jnp.concatenate(
        [parity, 1.0 - parity, blank, (1.0 - parity) * MASKED, parity * MASKED, blank], axis=0
    ).astype(BF)
    tree.forward(2)
    shared.wait()
    odd = head % 2 == 1
    for c in range(count):
        rows = slice(c * shard, (c + 1) * shard)
        block = slab[c].astype(F32)
        parts = []
        for third in range(3):
            at = third * 128
            parts.append(jnp.where(odd, block[:, at + HD : at + 128], block[:, at : at + HD]))
        w_head[rows] = jnp.concatenate(parts, axis=1).astype(BF)
    collect.forward(0)
    tree.forward(3)
    tree.finish()
    collect.finish()
    for copy in first + thirds + late:
        copy.wait_send()


def begin(tokens, gains, ids, w_qkv, w_attn, freqs, ring, count, groups, reach):
    rows, width = tokens.shape
    shard = w_qkv.shape[0]
    group = groups * reach
    sems = lambda *shape: [DMA(shape), DMA(shape)]
    return pl.pallas_call(
        functools.partial(begin_kernel, groups, reach, count),
        in_specs=[VMEM, VMEM, ANY, ANY, ANY, VMEM],
        out_specs=[ANY, VMEM, VMEM, VMEM, VMEM, VMEM, ANY],
        out_shape=[
            jax.ShapeDtypeStruct((group, rows, width), BF),
            jax.ShapeDtypeStruct((8, width), F32),
            jax.ShapeDtypeStruct((width, 3 * HD), BF),
            jax.ShapeDtypeStruct((HALF, group * rows), F32),
            jax.ShapeDtypeStruct((HALF, group * rows), F32),
            jax.ShapeDtypeStruct((2 * MARKS, group * rows), BF),
            jax.ShapeDtypeStruct((ring, shard, width), BF),
        ],
        scratch_shapes=[
            pltpu.VMEM((group, 8, rows), jnp.int32),
            pltpu.VMEM((count, shard, 3 * 128), BF),
            pltpu.VMEM((rows, width), BF),
            pltpu.VMEM((count, 8, gains.shape[1]), F32),
            DMA((5,)),
            *sems(group - 1),
            *sems(count - 1),
            *sems(count - 1, 3),
            *sems(ring - 1),
            DMA,
            DMA,
            *Tree.scratch(3),
            *Collect.scratch(1, groups),
        ],
        compiler_params=pltpu.CompilerParams(
            collective_id=0, has_side_effects=True, vmem_limit_bytes=12 << 20
        ),
        cost_estimate=pl.CostEstimate(flops=0, bytes_accessed=30 << 20, transcendentals=0),
        name="begin",
    )(tokens, gains, ids, w_qkv, w_attn, freqs)


class Ring:
    def __init__(self, ring, sub, first, blocks, arrivals, send, recv):
        ctx = lax.axis_index("ctx")
        right = {"ctx": (ctx // sub + 1) % ring * sub + ctx % sub}
        self.first = first
        self.waited = set()
        self.copies = [
            remote(source, target, right, send.at[q], recv.at[q])
            for q, (source, target) in enumerate(zip(blocks, arrivals))
        ]

    def start(self, q):
        if q >= 2:
            self.copies[q - 2].wait_recv()
            self.waited.add(q - 2)
        self.copies[q].start()

    def finish(self):
        for q, copy in enumerate(self.copies):
            if q not in self.waited:
                copy.wait_recv()
            copy.wait_send()


def ring_half(sub, side, k):
    return (side + k) % 2 if sub == 2 else k


class Columns:
    def __init__(self, place, part, whole, own, side_send, side_recv, near_send, near_recv):
        _, sub, _, width = whole.shape
        side = place.ctx % sub
        half = pl.ds(pl.multiple_of(place.head % 2 * (width // 2), 128), width // 2)
        self.own = pltpu.make_async_copy(part, whole.at[:, side], own)
        self.sides, self.near = [], []
        for step in range(1, sub):
            peer, source = (side + step) % sub, (side - step + sub) % sub
            self.sides.append(
                remote(
                    part.at[:, :, half],
                    whole.at[:, side, :, half],
                    {"ctx": place.ctx - side + peer},
                    side_send.at[step - 1],
                    side_recv.at[step - 1],
                )
            )
            here = whole.at[:, source, :, half]
            self.near.append(
                remote(
                    here, here, {"heads": flip(place.head, 1)}, near_send.at[step - 1], near_recv.at[step - 1]
                )
            )

    @staticmethod
    def scratch(sub):
        count = (max(sub - 1, 1),)
        return [DMA, DMA(count), DMA(count), DMA(count), DMA(count)]

    def start(self):
        self.own.start()
        for copy in self.sides:
            copy.start()

    def across(self):
        for side, near in zip(self.sides, self.near):
            side.wait_recv()
            near.start()

    def finish(self):
        self.own.wait()
        for side, near in zip(self.sides, self.near):
            side.wait_send()
            near.wait()


def attend_kernel(
    groups,
    reach,
    lines,
    tile,
    x_ref,
    w_ref,
    cos_ref,
    sin_ref,
    mark_ref,
    attn_half,
    mlp,
    out_ref,
    wide_ref,
    lse_ref,
    qkv_ref,
    attn_all,
    mlp_pair,
    mlp_near,
    ring_send,
    ring_recv,
    swap_send,
    swap_recv,
    swap_own,
    *sems,
):
    count = x_ref.shape[0]
    step = pl.program_id(0)
    steps = count // tile
    place = Place(groups, reach)
    ring_size, sub = attn_all.shape[:2]
    side = place.ctx % sub
    early = mlp_near.shape[0]
    if sub == 2:
        kept = pltpu.make_async_copy(mlp.at[side], mlp_pair.at[side], swap_own)
        swap = [
            remote(
                mlp.at[1 - side],
                mlp_pair.at[side],
                {"ctx": place.ctx + 1 - 2 * side},
                swap_send,
                swap_recv,
            )
        ]
        sources = [mlp.at[side], mlp_pair.at[1 - side]]
    else:
        kept = pltpu.make_async_copy(mlp, mlp_pair, swap_own)
        swap = []
        sources = [mlp.at[0], mlp.at[1]]
    ring = Ring(
        ring_size,
        sub,
        0,
        sources + [mlp_near.at[q] for q in range(early - 2)],
        [mlp_near.at[q] for q in range(early)],
        ring_send,
        ring_recv,
    )
    columns = Columns(place, attn_half, attn_all, *sems)

    @pl.when(step == 0)
    def _():
        meet(everyone(place, lines))
        for copy in swap:
            copy.start()
        ring.start(0)
        kept.start()
        columns.start()
        qkv_ref[HD:QM_END, :] = mark_ref[:MARKS, :]
        qkv_ref[K_END:KM_END, :] = mark_ref[MARKS:, :]

        @pl.loop(0, steps)
        def _(i):
            at = pl.ds(pl.multiple_of(i * tile, tile), tile)
            cosine, sine = cos_ref[:, at], sin_ref[:, at]
            part = dot(w_ref[...], x_ref[at, :], 0, 1)

            def turn(value):
                front, back = value[:HALF], value[HALF:]
                return jnp.concatenate(
                    [front * cosine - back * sine, back * cosine + front * sine], axis=0
                )

            qkv_ref[:HD, at] = (turn(part[:HD]) * 0.125).astype(BF)
            qkv_ref[QM_END:K_END, at] = turn(part[HD : 2 * HD]).astype(BF)
            qkv_ref[KM_END:, at] = part[2 * HD :].astype(BF)

    here = pl.ds(pl.multiple_of(step * tile, tile), tile)
    query = qkv_ref[:QM_END, here]
    keys = [slice(j * tile, (j + 1) * tile) for j in range(steps)]
    scores = [dot(qkv_ref[QM_END:KM_END, at], query, 0, 0) for at in keys]
    top = functools.reduce(jnp.maximum, [jnp.max(s, axis=0, keepdims=True) for s in scores])
    raised = [jnp.exp(s - top) for s in scores]
    total = functools.reduce(jnp.add, [jnp.sum(e, axis=0, keepdims=True) for e in raised])
    scale = 1.0 / total
    result = jnp.zeros((HD, tile), F32)
    for j in range(steps):
        result += dot(qkv_ref[KM_END:, keys[j]], (raised[j] * scale).astype(BF), 1, 0)
    rows = out_ref.shape[2]
    for k in range(tile // rows):
        out_ref[step * (tile // rows) + k] = result[:, k * rows : (k + 1) * rows].astype(BF)
    wide_ref[:, here] = result
    lse_ref[:, here] = top + jnp.log(total)

    @pl.when(step == min(1, steps - 1))
    def _():
        for copy in swap:
            copy.wait_recv()
        for q in range(1, min(early, 3)):
            ring.start(q)

    @pl.when(step == steps - 1)
    def _():
        columns.across()
        for q in range(3, early):
            ring.start(q)
        ring.waited.update(range(early - 2))
        ring.finish()
        for copy in swap:
            copy.wait_send()
        kept.wait()
        columns.finish()


def attend(x, w, cosine, sine, marks, attn_half, mlp, lines, groups, reach, rows, tile):
    count, width = x.shape
    ring, shard, _ = attn_half.shape
    sub = lines // ring
    early = ring - 1
    whole = lambda *shape: pl.BlockSpec(shape, lambda i: (0,) * len(shape))
    return pl.pallas_call(
        functools.partial(attend_kernel, groups, reach, lines, tile),
        grid=(count // tile,),
        in_specs=[
            whole(count, width),
            whole(*w.shape),
            whole(HALF, count),
            whole(HALF, count),
            whole(2 * MARKS, count),
            ANY,
            ANY,
        ],
        out_specs=[
            whole(count // rows, HD, rows),
            whole(HD, count),
            whole(1, count),
            whole(V_END, count),
            ANY,
            ANY,
            ANY,
        ],
        out_shape=[
            jax.ShapeDtypeStruct((count // rows, HD, rows), BF),
            jax.ShapeDtypeStruct((HD, count), F32),
            jax.ShapeDtypeStruct((1, count), F32),
            jax.ShapeDtypeStruct((V_END, count), BF),
            jax.ShapeDtypeStruct((ring, sub, shard, width), BF),
            jax.ShapeDtypeStruct(mlp.shape, BF),
            jax.ShapeDtypeStruct((early, *mlp.shape[1:]), BF),
        ],
        scratch_shapes=[DMA((early,)), DMA((early,)), DMA, DMA, DMA, *Columns.scratch(sub)],
        compiler_params=pltpu.CompilerParams(
            collective_id=5, has_side_effects=True, vmem_limit_bytes=32 << 20
        ),
        cost_estimate=pl.CostEstimate(
            flops=count * count * HD * 8, bytes_accessed=count * 4096, transcendentals=count * count
        ),
        name="attend",
    )(x, w, cosine, sine, marks, attn_half, mlp)


def middle_kernel(
    groups,
    reach,
    lines,
    outgoing,
    tokens,
    d_out,
    w_attn,
    gains,
    mlp_pair,
    mlp_near,
    mlp_all,
    upstream_all,
    middle,
    attended,
    mlp_weights,
    land,
    mine,
    a2a_send,
    a2a_recv,
    own,
    ring_send,
    ring_recv,
    ring_own,
    land_own,
    *tree_sems,
):
    place = Place(groups, reach)
    group = groups * reach
    early, count = mlp_near.shape[0], mlp_weights.shape[0]
    sub = lines // count
    spot, side = place.ctx // sub, place.ctx % sub
    slot = lambda q: mlp_weights.at[(spot - q // 2 - 1 + count) % count, ring_half(sub, side, q % 2)]
    rest = range(early, 2 * (count - 1))
    ring = Ring(
        count,
        sub,
        early,
        [mlp_near.at[q - 2] if q - 2 < early else slot(q - 2) for q in rest],
        [slot(q - 2) for q in rest],
        ring_send,
        ring_recv,
    )
    local = [pltpu.make_async_copy(mlp_pair, mlp_weights.at[spot], ring_own.at[0])]
    for q in range(early):
        local.append(pltpu.make_async_copy(mlp_near.at[q], slot(q), ring_own.at[q + 1]))
    meet(everyone(place, lines))
    copies = spread(place, outgoing, land, (a2a_send, a2a_recv, own))
    ring.start(0)
    ring.start(1)
    up = Tree(place, 2, d_out, upstream_all, tree_sems[5:10])
    up.start()
    for copy in local:
        copy.start()
    for copy in copies:
        copy.wait()
    collect = Collect(groups, [(land, lambda h: attended.at[h])], *tree_sems[10:])
    collect.start(0)
    local.append(pltpu.make_async_copy(land, attended.at[place.head], land_own))
    local[-1].start()
    value = tokens[...].astype(F32) + dot(
        land[...].reshape(group * HD, tokens.shape[0]), w_attn[...], 0, 0
    )
    middle[...] = value
    normed, _ = norm_parts(value)
    mine[...] = (normed * gains[1:2, :]).astype(BF)
    tree = Tree(place, 2, mine, mlp_all, tree_sems[:5])
    tree.start()
    up.forward(1)
    for q in range(2, len(rest)):
        ring.start(q)
    tree.forward(1)
    up.forward(2)
    tree.forward(2)
    collect.forward(0)
    up.finish()
    tree.finish()
    collect.finish()
    for copy in local:
        copy.wait()
    ring.finish()


def middle_step(outgoing, tokens, d_out, w_attn, gains, mlp_pair, mlp_near, lines, groups, reach):
    rows, width = tokens.shape
    group = groups * reach
    early, sub = mlp_near.shape[0], 8 // groups
    ring = lines // sub
    left = 2 * (ring - 1) - early
    return pl.pallas_call(
        functools.partial(middle_kernel, groups, reach, lines),
        in_specs=[ANY, VMEM, ANY, VMEM, VMEM, ANY, ANY],
        out_specs=[ANY, ANY, VMEM, ANY, ANY],
        out_shape=[
            jax.ShapeDtypeStruct((8, rows, width), BF),
            jax.ShapeDtypeStruct((8, rows, width), BF),
            jax.ShapeDtypeStruct((rows, width), F32),
            jax.ShapeDtypeStruct((groups, group, HD, rows), BF),
            jax.ShapeDtypeStruct((ring, *mlp_pair.shape), BF),
        ],
        scratch_shapes=[
            pltpu.VMEM((group, HD, rows), BF),
            pltpu.VMEM((rows, width), BF),
            DMA((group - 1,)),
            DMA((group - 1,)),
            DMA,
            DMA((left,)),
            DMA((left,)),
            DMA((early + 1,)),
            DMA,
            *Tree.scratch(2),
            *Tree.scratch(2),
            *Collect.scratch(1, groups),
        ],
        compiler_params=pltpu.CompilerParams(
            collective_id=1, has_side_effects=True, vmem_limit_bytes=12 << 20
        ),
        cost_estimate=pl.CostEstimate(flops=1 << 28, bytes_accessed=12 << 20, transcendentals=0),
        name="middle_step",
    )(outgoing, tokens, d_out, w_attn, gains, mlp_pair, mlp_near)


def mlp_kernel(chunk, x_ref, up_ref, w_ref, back_ref, forward_ref, terms_ref, kept):
    count, width = x_ref.shape

    @pl.loop(0, count // chunk)
    def _(i):
        at = pl.ds(pl.multiple_of(i * chunk, chunk), chunk)
        gate_up = dot(x_ref[at, :], w_ref[:, : 2 * SLICE], 1, 0)
        left, right = gate_up[:, :SLICE], gate_up[:, SLICE:]
        grad_mixed = dot(up_ref[at, :], w_ref[:, 2 * SLICE :], 1, 0)
        normal_cdf = 0.5 * (1.0 + lax.erf(left * 0.7071067811865476))
        gelu = left * normal_cdf
        density = jnp.exp(-0.5 * left * left) * 0.3989422804014327
        kept[at, :SLICE] = (grad_mixed * right * (normal_cdf + left * density)).astype(BF)
        kept[at, SLICE : 2 * SLICE] = (grad_mixed * gelu).astype(BF)
        kept[at, 2 * SLICE :] = (gelu * right).astype(BF)
        back_ref[at, :] = dot(kept[at, : 2 * SLICE], w_ref[:, : 2 * SLICE], 1, 1).astype(BF)
        forward_ref[at, :] = dot(kept[at, 2 * SLICE :], w_ref[:, 2 * SLICE :], 1, 1).astype(BF)

    @pl.loop(0, width // chunk)
    def _(i):
        at = pl.ds(pl.multiple_of(i * chunk, chunk), chunk)
        terms_ref[at, : 2 * SLICE] = dot(x_ref[:, at], kept[:, : 2 * SLICE], 0, 0).astype(BF)
        terms_ref[at, 2 * SLICE :] = dot(up_ref[:, at], kept[:, 2 * SLICE :], 0, 0).astype(BF)


def mlp_step(x, up, w, chunk):
    count, width = x.shape
    return pl.pallas_call(
        functools.partial(mlp_kernel, chunk),
        in_specs=[VMEM] * 3,
        out_specs=[VMEM] * 3,
        out_shape=[
            jax.ShapeDtypeStruct((count, width), BF),
            jax.ShapeDtypeStruct((count, width), BF),
            jax.ShapeDtypeStruct((width, 3 * SLICE), BF),
        ],
        scratch_shapes=[pltpu.VMEM((count, 3 * SLICE), BF)],
        compiler_params=pltpu.CompilerParams(vmem_limit_bytes=28 << 20),
        cost_estimate=pl.CostEstimate(
            flops=18 * count * width * SLICE, bytes_accessed=14 << 20, transcendentals=2 * count * SLICE
        ),
        name="mlp_step",
    )(x, up, w)


def turn_kernel(
    groups,
    reach,
    partial,
    middle,
    d_out,
    w_attn,
    gains,
    attended,
    grads,
    grad_middle,
    attn_part,
    columns,
    total,
    outgoing,
    branch,
    a2a_send,
    a2a_recv,
    own,
    side_send,
    side_recv,
    side_own,
    *halving,
):
    place = Place(groups, reach)
    group = groups * reach
    lanes = branch.shape[2]
    meet([place.member((place.idx + step) % group) for step in range(1, group)])
    Halving(place, 2, partial, total, halving).run()
    normed, inverse_std = norm_parts(middle[...])
    upstream = total[...]
    grad = d_out[...].astype(F32) + norm_back(upstream, normed, inverse_std, gains[1:2, :])
    grad_middle[...] = grad
    low = grad.astype(BF)
    for g in range(groups):
        branch[g] = low[:, g * lanes : (g + 1) * lanes]
    outgoing[...] = dot(w_attn[...], low, 1, 1).astype(BF).reshape(outgoing.shape)
    copies = spread(place, outgoing, grads, (a2a_send, a2a_recv, own))
    for step in range(1, groups):
        peer = (place.head + step) % groups
        copies.append(
            push(
                branch.at[peer],
                columns.at[place.head],
                {"heads": peer},
                side_send.at[step - 1],
                side_recv.at[step - 1],
            )
        )
    local = pltpu.make_async_copy(branch.at[place.head], columns.at[place.head], side_own)
    local.start()
    for copy in copies[-(groups - 1) :]:
        copy.wait()
    local.wait()
    attn_part[...] = functools.reduce(
        jnp.add, [dot(attended[g], columns[g], 1, 0) for g in range(groups)]
    ).astype(BF)
    for copy in copies[: -(groups - 1)]:
        copy.wait()


def turn_step(partial, middle, d_out, w_attn, gains, attended, groups, reach):
    rows, width = middle.shape
    group = groups * reach
    return pl.pallas_call(
        functools.partial(turn_kernel, groups, reach),
        in_specs=[VMEM] * 6,
        out_specs=[ANY, VMEM, VMEM],
        out_shape=[
            jax.ShapeDtypeStruct((group, HD, rows), BF),
            jax.ShapeDtypeStruct((rows, width), F32),
            jax.ShapeDtypeStruct((width, width // groups), BF),
        ],
        scratch_shapes=[
            pltpu.VMEM((groups, rows, width // groups), BF),
            pltpu.VMEM((rows, width), F32),
            pltpu.VMEM((group, HD, rows), BF),
            pltpu.VMEM((groups, rows, width // groups), BF),
            DMA((group - 1,)),
            DMA((group - 1,)),
            DMA,
            DMA((groups - 1,)),
            DMA((groups - 1,)),
            DMA,
            *Halving.scratch(2, rows, width),
        ],
        compiler_params=pltpu.CompilerParams(
            collective_id=2, has_side_effects=True, vmem_limit_bytes=16 << 20
        ),
        cost_estimate=pl.CostEstimate(flops=1 << 28, bytes_accessed=12 << 20, transcendentals=0),
        name="turn_step",
    )(partial, middle, d_out, w_attn, gains, attended)


def attend_back_kernel(
    groups,
    reach,
    lines,
    tile,
    qkv_ref,
    grad_ref,
    wide_ref,
    lse_ref,
    x_ref,
    w_ref,
    cos_ref,
    sin_ref,
    forward_ref,
    attn_ref,
    out_ref,
    weight_ref,
    ahead_ref,
    attn_out_ref,
    sums,
    queries,
    weight,
    attn_land,
    *sems,
):
    count = x_ref.shape[0]
    rows = grad_ref.shape[2]
    steps, per_tile = count // tile, tile // rows
    step = pl.program_id(0)
    place = Place(groups, reach)
    halving = Halving(place, 2, forward_ref, ahead_ref, sems[:7])
    swap = Lines(lines, attn_ref, attn_land, *sems[7:])

    @pl.when(step == 0)
    def _():
        greet(everyone(place, lines))
        sums[...] = jnp.zeros_like(sums)

    here = pl.ds(pl.multiple_of(step * tile, tile), tile)
    query = qkv_ref[:QM_END, here]
    grad = jnp.concatenate([grad_ref[step * per_tile + k] for k in range(per_tile)], axis=1)
    delta = jnp.sum(grad.astype(F32) * wide_ref[:, here], axis=0, keepdims=True)
    lse = lse_ref[:, here]
    grad_query = jnp.zeros((HD, tile), F32)
    for j in range(steps):
        keys = slice(j * tile, (j + 1) * tile)
        prob = jnp.exp(dot(qkv_ref[QM_END:KM_END, keys], query, 0, 0) - lse)
        grad_prob = dot(qkv_ref[KM_END:, keys], grad, 0, 0)
        grad_score = (prob * (grad_prob - delta)).astype(BF)
        grad_query += dot(qkv_ref[QM_END:K_END, keys], grad_score, 1, 0)
        sums[:HD, keys] += dot(query[:HD], grad_score, 1, 1)
        sums[HD:, keys] += dot(grad, prob.astype(BF), 1, 1)
    queries[:, here] = (grad_query * 0.125).astype(BF)

    @pl.when(step == 0)
    def _():
        pl.semaphore_wait(pltpu.get_barrier_semaphore(), len(everyone(place, lines)))
        halving.start()
        swap.start()

    pl.when(step == min(1, steps - 1))(halving.pair)
    pl.when(step == min(2, steps - 1))(lambda: halving.halve(0))

    @pl.when(step == steps - 1)
    def _():
        weight[...] = jnp.zeros_like(weight)

        @pl.loop(0, steps)
        def _(i):
            at = pl.ds(pl.multiple_of(i * tile, tile), tile)
            cosine, sine = cos_ref[:, at], sin_ref[:, at]

            def turn_back(value):
                front, back = value[:HALF], value[HALF:]
                return [front * cosine + back * sine, back * cosine - front * sine]

            low = lambda value: value.astype(BF).astype(F32)
            projected = jnp.concatenate(
                [
                    *turn_back(queries[:, at].astype(F32)),
                    *turn_back(low(sums[:HD, at])),
                    low(sums[HD:, at]),
                ],
                axis=0,
            ).astype(BF)
            part = dot(projected, w_ref[...], 0, 1).astype(BF)
            for k in range(per_tile):
                out_ref[i * per_tile + k] = part[k * rows : (k + 1) * rows]
            weight[...] += dot(projected, x_ref[at, :], 1, 0)

        shard = weight_ref.shape[2]
        for c in range(lines):
            weight_ref[c] = weight[:, c * shard : (c + 1) * shard].astype(BF)
        halving.halve(1)
        swap.finish()
        attn_out_ref[...] = functools.reduce(
            jnp.add, [attn_land[c].astype(F32) for c in range(lines)]
        ).astype(BF)
        halving.finish()


def attend_back(qkv, grad, wide, lse, x, w, cosine, sine, forward, attn, groups, reach, tile):
    count, width = x.shape
    blocks, _, rows = grad.shape
    lines, shard, lanes = attn.shape
    whole = lambda *shape: pl.BlockSpec(shape, lambda i: (0,) * len(shape))
    operands = (qkv, grad, wide, lse, x, w, cosine, sine, forward)
    return pl.pallas_call(
        functools.partial(attend_back_kernel, groups, reach, lines, tile),
        grid=(count // tile,),
        in_specs=[*[whole(*operand.shape) for operand in operands], ANY],
        out_specs=[
            whole(blocks, rows, width),
            whole(lines, 3 * HD, shard),
            whole(rows, width),
            whole(shard, lanes),
        ],
        out_shape=[
            jax.ShapeDtypeStruct((blocks, rows, width), BF),
            jax.ShapeDtypeStruct((lines, 3 * HD, shard), BF),
            jax.ShapeDtypeStruct((rows, width), F32),
            jax.ShapeDtypeStruct((shard, lanes), BF),
        ],
        scratch_shapes=[
            pltpu.VMEM((2 * HD, count), F32),
            pltpu.VMEM((HD, count), BF),
            pltpu.VMEM((3 * HD, width), F32),
            pltpu.VMEM((lines, shard, lanes), BF),
            *Halving.scratch(2, rows, width),
            *Lines.scratch(lines),
        ],
        compiler_params=pltpu.CompilerParams(
            collective_id=4, has_side_effects=True, vmem_limit_bytes=44 << 20
        ),
        cost_estimate=pl.CostEstimate(
            flops=count * count * HD * 20, bytes_accessed=count * 6144, transcendentals=count * count
        ),
        name="attend_back",
    )(*operands, attn)


class Collect:
    def __init__(self, groups, pieces, far_send, far_recv, near_send, near_recv):
        head = lax.axis_index("heads")
        self.half = half = groups // 2
        pair = {"heads": flip(head, 1)}
        self.far, self.near = [], []
        for n, (piece, where) in enumerate(pieces):
            self.far.append(
                [
                    remote(
                        piece,
                        where(head),
                        {"heads": (head + 2 * k) % groups},
                        far_send.at[n, k - 1],
                        far_recv.at[n, k - 1],
                    )
                    for k in range(1, half)
                ]
            )
            sides = [(piece, where(head))]
            for k in range(1, half):
                got = where((head - 2 * k + groups) % groups)
                sides.append((got, got))
            self.near.append(
                [
                    remote(source, target, pair, near_send.at[n, k], near_recv.at[n, k])
                    for k, (source, target) in enumerate(sides)
                ]
            )

    @staticmethod
    def scratch(count, groups):
        far, near = (count, max(groups // 2 - 1, 1)), (count, groups // 2)
        return [DMA(far), DMA(far), DMA(near), DMA(near)]

    def start(self, n):
        for copy in self.far[n]:
            copy.start()
        self.near[n][0].start()

    def forward(self, n):
        for k, copy in enumerate(self.far[n]):
            copy.wait_recv()
            self.near[n][k + 1].start()

    def finish(self):
        for copies in self.far:
            for copy in copies:
                copy.wait_send()
        for copies in self.near:
            for copy in copies:
                copy.wait()


def end_kernel(
    groups,
    reach,
    lines,
    partial,
    weight,
    mlp,
    attn,
    total,
    mlp_all,
    weight_all,
    attn_all,
    lined,
    summed,
    swap_send,
    swap_recv,
    own,
    *rest,
):
    place = Place(groups, reach)
    sub = mlp.shape[0]
    mine, head = place.ctx % sub, place.head
    meet(everyone(place, lines))
    width = total.shape[1]
    wide = Halving(place, 3, partial, total, rest[:7], [width // 8, width // 8 * 3, width // 2])
    swap = Lines(lines, weight, lined, *rest[7:10])
    wide.start()
    swaps = []
    for step in range(1, sub):
        peer = (mine + step) % sub
        swaps.append(
            push(
                mlp.at[peer],
                mlp_all.at[mine, head],
                {"ctx": place.ctx - mine + peer},
                swap_send.at[step - 1],
                swap_recv.at[step - 1],
            )
        )
    pieces = [(mlp.at[mine], lambda h: mlp_all.at[mine, h]), (attn, lambda h: attn_all.at[h])]
    for step in range(1, sub):
        source = (mine - step + sub) % sub
        pieces.append(
            (mlp_all.at[source, head], lambda h, source=source: mlp_all.at[source, h])
        )
    pieces.append((summed, lambda h: weight_all.at[h]))
    collect = Collect(groups, pieces, *rest[10:14])
    swap.start()
    local = [
        pltpu.make_async_copy(mlp.at[mine], mlp_all.at[mine, head], own.at[0]),
        pltpu.make_async_copy(attn, attn_all.at[head], own.at[1]),
        pltpu.make_async_copy(summed, weight_all.at[head], own.at[2]),
    ]
    local[0].start()
    local[1].start()
    collect.start(0)
    collect.start(1)
    wide.pair()
    for step in range(1, sub):
        swaps[step - 1].wait_recv()
        collect.start(step + 1)
    wide.halve(0)
    swap.finish()
    for r in range(reach):
        summed[r] = functools.reduce(
            jnp.add, [lined[r + reach * g].astype(F32) for g in range(lines // reach)]
        ).astype(BF)
    local[2].start()
    collect.start(sub + 1)
    wide.halve(1)
    collect.forward(0)
    collect.forward(1)
    wide.halve(2)
    for n in range(2, sub + 2):
        collect.forward(n)
    for copy in local:
        copy.wait()
    for copy in swaps:
        copy.wait_send()
    collect.finish()
    wide.finish()


def end_step(partial, weight, mlp, attn, groups, reach):
    rows, width = partial.shape[2:]
    lines, _, shard = weight.shape
    sub = mlp.shape[0]
    return pl.pallas_call(
        functools.partial(end_kernel, groups, reach, lines),
        in_specs=[VMEM, ANY, ANY, ANY],
        out_specs=[VMEM, ANY, ANY, ANY],
        out_shape=[
            jax.ShapeDtypeStruct((rows, width), F32),
            jax.ShapeDtypeStruct((sub, groups, *mlp.shape[1:]), BF),
            jax.ShapeDtypeStruct((groups, reach, 3 * HD, shard), BF),
            jax.ShapeDtypeStruct((groups, *attn.shape), BF),
        ],
        scratch_shapes=[
            pltpu.VMEM((lines, 3 * HD, shard), BF),
            pltpu.VMEM((reach, 3 * HD, shard), BF),
            DMA((max(sub - 1, 1),)),
            DMA((max(sub - 1, 1),)),
            DMA((3,)),
            *Halving.scratch(3, rows, width),
            *Lines.scratch(lines),
            *Collect.scratch(sub + 2, groups),
        ],
        compiler_params=pltpu.CompilerParams(
            collective_id=3, has_side_effects=True, vmem_limit_bytes=20 << 20
        ),
        cost_estimate=pl.CostEstimate(flops=0, bytes_accessed=24 << 20, transcendentals=0),
        name="end_step",
    )(partial, weight, mlp, attn)


def assemble_kernel(
    upstream,
    tokens,
    grad_middle,
    gains,
    middle,
    ahead,
    weight_all,
    attn_all,
    mlp_all,
    w_qkv,
    w_in,
    own_gains,
    result,
    grad,
    sum_qkv,
    sum_attn,
    sum_in,
    sum_out,
    gain_sums,
):
    groups, reach, _, shard = weight_all.shape
    lanes = attn_all.shape[2]
    result[...] = (middle[...] + ahead[...]).astype(BF)
    normed, inverse_std = norm_parts(tokens[...].astype(F32))
    grad[...] = grad_middle[...] + norm_back(upstream[...], normed, inverse_std, gains[0:1, :])
    for g in range(groups):
        sum_attn[:, g * lanes : (g + 1) * lanes] = attn_all[g].astype(F32)
    gain_one = jnp.zeros((shard, 128), F32)
    for third in range(3):
        part = slice(third * HD, (third + 1) * HD)
        for pair in range(H // 2):
            r, g = 2 * pair // groups, 2 * pair % groups
            tile = (
                jnp.concatenate([weight_all[g, r, part], weight_all[g + 1, r, part]], axis=0)
                .astype(F32)
                .T
            )
            at = third * H * HD + pair * 2 * HD
            sum_qkv[:, at : at + 2 * HD] = tile
            gain_one += tile * w_qkv[:, at : at + 2 * HD].astype(F32)
    gain_two = jnp.zeros((shard, 1), F32)
    for t in range(8):
        start, wide = slice_place(t)
        for half in range(2):
            piece = mlp_all[t, :, half * SLICE : half * SLICE + wide].astype(F32)
            at = half * FF + start
            sum_in[:, at : at + wide] = piece
            gain_two += jnp.sum(
                piece * w_in[:, at : at + wide].astype(F32), axis=1, keepdims=True
            )
        sum_out[start : start + wide, :] = (
            mlp_all[t, :, 2 * SLICE : 3 * SLICE].astype(F32).T[:wide]
        )
    one = jnp.sum(gain_one, axis=1, keepdims=True)
    lane = lax.broadcasted_iota(jnp.int32, (shard, 128), 1)
    both = jnp.where(lane == 0, one, gain_two).T
    gain_sums[...] = both[:8] / own_gains[...]


def assemble(upstream, tokens, grad_middle, gains, middle, ahead, weight_all, attn_all, mlp_all, w_qkv, w_in, own_gains):
    rows, width = tokens.shape
    shard = w_qkv.shape[0]
    return pl.pallas_call(
        assemble_kernel,
        in_specs=[VMEM] * 12,
        out_specs=[VMEM] * 7,
        out_shape=[
            jax.ShapeDtypeStruct((rows, width), BF),
            jax.ShapeDtypeStruct((rows, width), F32),
            jax.ShapeDtypeStruct((shard, 3 * width), F32),
            jax.ShapeDtypeStruct((shard, width), F32),
            jax.ShapeDtypeStruct((shard, 2 * FF), F32),
            jax.ShapeDtypeStruct((FF, shard), F32),
            jax.ShapeDtypeStruct((8, shard), F32),
        ],
        compiler_params=pltpu.CompilerParams(vmem_limit_bytes=24 << 20),
        cost_estimate=pl.CostEstimate(flops=1 << 24, bytes_accessed=20 << 20, transcendentals=0),
        name="assemble",
    )(upstream, tokens, grad_middle, gains, middle, ahead, weight_all, attn_all, mlp_all, w_qkv, w_in, own_gains)


def slice_start(t):
    return 128 * jnp.minimum(3 * t, 2 * t + 5)


def slice_place(t):
    start = 128 * min(3 * t, 2 * t + 5)
    return start, min(128 * min(3 * t + 3, 2 * t + 7), FF) - start


def body(count, tokens, d_out, segment_ids, position_ids, w_qkv, w_attn, w_in, w_out, gain_attn, gain_mlp):
    groups = lax.axis_size("heads")
    rows, width = tokens.shape
    shard = w_qkv.shape[0]
    reach = SEQ_MAX // (rows * groups)
    group = reach * groups
    sub = 8 // groups
    ctx, head = lax.axis_index("ctx"), lax.axis_index("heads")
    assert group == H and sub * groups == 8
    total = group * rows
    tile = 512

    def mlp_slice(value, axis, start, t):
        pads = [(0, 0), (0, 0)]
        pads[axis] = (0, SLICE)
        piece = lax.dynamic_slice_in_dim(jnp.pad(value, pads), start + slice_start(t), SLICE, axis)
        wide = jnp.minimum(slice_start(t + 1), FF) - slice_start(t)
        shape = [1, 1]
        shape[axis] = SLICE
        return jnp.where(jnp.arange(SLICE).reshape(shape) < wide, piece, jnp.zeros_like(piece))

    def mlp_part(t):
        return jnp.concatenate(
            [mlp_slice(w_in, 1, 0, t), mlp_slice(w_in, 1, FF, t), mlp_slice(w_out, 0, 0, t).T], axis=1
        )

    mlp = jnp.stack([mlp_part(x * groups + head) for x in range(sub)])
    lines = [list(range(k, count, sub)) for k in range(sub)]
    gains_own = jnp.pad(jnp.stack([gain_attn, gain_mlp]).astype(F32), ((0, 6), (0, -shard % 128)))
    ids = jnp.pad(jnp.stack([position_ids, segment_ids]), ((0, 6), (0, 0)))
    freqs = jnp.power(160000.0, -(2.0 * jnp.arange(HALF, dtype=F32)) / HD)[:, None]
    input_all, gains, w_head, cosine, sine, marks, attn_half = begin(
        tokens, gains_own, ids, w_qkv, w_attn, freqs, count // sub, count, groups, reach
    )
    x = input_all.reshape(total, width)

    attended, wide, lse, qkv, attn_weights, mlp_pair, mlp_near = attend(
        x,
        w_head,
        cosine,
        sine,
        marks,
        attn_half,
        mlp.reshape(2, sub * shard // 2, 3 * SLICE),
        count,
        groups,
        reach,
        rows,
        tile,
    )
    attn_weights = attn_weights.reshape(width, width)
    mlp_all, upstream, middle, attended, mlp_weights = middle_step(
        attended, tokens, d_out, attn_weights, gains, mlp_pair, mlp_near, count, groups, reach
    )
    mlp_weights = mlp_weights.reshape(width, 3 * SLICE)
    split = lambda value, blocks: value.reshape(blocks // 2, 2, rows, width)
    back, forward, mlp_terms = mlp_step(
        mlp_all.reshape(8 * rows, width), upstream.reshape(8 * rows, width), mlp_weights, 512
    )
    mlp_sum = lax.psum_scatter(
        mlp_terms, "ctx", scatter_dimension=0, tiled=True, axis_index_groups=lines
    ).reshape(sub, shard, 3 * SLICE)
    grad_heads, grad_middle, attn_part = turn_step(
        split(back, 8),
        middle,
        d_out,
        attn_weights,
        gains,
        attended.reshape(groups, width, rows),
        groups,
        reach,
    )
    attn_part = attn_part.reshape(count, shard, width // groups)
    forward = split(forward, 8)
    grad_input_parts, weight, ahead, attn_sum = attend_back(
        qkv, grad_heads, wide, lse, x, w_head, cosine, sine, forward, attn_part, groups, reach, tile
    )
    upstream_in, mlp_all, weight_all, attn_all = end_step(
        split(grad_input_parts, group), weight, mlp_sum, attn_sum, groups, reach
    )
    result, grad_input, sum_qkv, sum_attn, sum_in, sum_out, gain_sums = assemble(
        upstream_in,
        tokens,
        grad_middle,
        gains,
        middle,
        ahead,
        weight_all,
        attn_all,
        mlp_all.reshape(8, shard, 3 * SLICE),
        w_qkv,
        w_in,
        jnp.pad(gains_own[:2, :shard], ((0, 6), (0, 0)), constant_values=1.0),
    )
    return (
        result,
        grad_input,
        sum_qkv,
        sum_attn,
        sum_in,
        sum_out,
        gain_sums[0],
        gain_sums[1],
    )


def solution(mesh):
    return jax.shard_map(
        functools.partial(body, mesh.shape["ctx"]),
        mesh=mesh,
        in_specs=(
            P(("ctx", "heads"), None),
            P(("ctx", "heads"), None),
            P(("ctx", "heads")),
            P(("ctx", "heads")),
            P("ctx", None),
            P("ctx", None),
            P("ctx", None),
            P(None, "ctx"),
            P("ctx"),
            P("ctx"),
        ),
        out_specs=(
            P(("ctx", "heads"), None),
            P(("ctx", "heads"), None),
            P("ctx", None),
            P("ctx", None),
            P("ctx", None),
            P(None, "ctx"),
            P("ctx"),
            P("ctx"),
        ),
        check_vma=False,
    )
```

```python
import functools

import jax
import jax.numpy as jnp
from jax import lax
from jax.experimental import pallas as pl
from jax.experimental.pallas import tpu as pltpu
from jax.sharding import PartitionSpec as P

H = 16
HD = 64
HALF = HD // 2
FF = 2624
SEQ_MAX = 2048
MASKED = -1e30
MARKS = 16
QM_END = HD + MARKS
K_END = QM_END + HD
KM_END = K_END + MARKS
V_END = KM_END + HD
SLICE = 384
BF = jnp.bfloat16
F32 = jnp.float32
MESH = pl.DeviceIdType.MESH
VMEM = pl.BlockSpec(memory_space=pltpu.VMEM)
ANY = pl.BlockSpec(memory_space=pl.ANY)
DMA = pltpu.SemaphoreType.DMA


def dot(left, right, left_dim, right_dim):
    return lax.dot_general(
        left, right, (((left_dim,), (right_dim,)), ((), ())), preferred_element_type=F32
    )


def norm_parts(values):
    average = jnp.mean(values, axis=-1, keepdims=True)
    centred = values - average
    inverse_std = lax.rsqrt(jnp.mean(centred * centred, axis=-1, keepdims=True) + 1e-05)
    return centred * inverse_std, inverse_std


def norm_back(upstream, normed, inverse_std, gain):
    scaled = upstream * gain
    return inverse_std * (
        scaled
        - jnp.mean(scaled, axis=-1, keepdims=True)
        - normed * jnp.mean(scaled * normed, axis=-1, keepdims=True)
    )


def flip(value, bit):
    return value + bit - 2 * bit * (value // bit % 2)


class Place:
    def __init__(self, groups, reach):
        self.groups, self.reach = groups, reach
        self.ctx = lax.axis_index("ctx")
        self.head = lax.axis_index("heads")
        self.local = self.ctx % reach
        self.base = self.ctx - self.local
        self.idx = self.local * groups + self.head

    def member(self, j):
        return {"ctx": self.base + j // self.groups, "heads": j % self.groups}


def greet(devices):
    barrier = pltpu.get_barrier_semaphore()
    for device in devices:
        pl.semaphore_signal(barrier, inc=1, device_id=device, device_id_type=MESH)


def meet(devices):
    greet(devices)
    pl.semaphore_wait(pltpu.get_barrier_semaphore(), len(devices))


def remote(source, target, device, send, recv):
    return pltpu.make_async_remote_copy(
        src_ref=source,
        dst_ref=target,
        send_sem=send,
        recv_sem=recv,
        device_id=device,
        device_id_type=MESH,
    )


def push(*operands):
    copy = remote(*operands)
    copy.start()
    return copy


def tree_parts(axes, rows):
    part = -(-rows // axes // 16) * 16
    starts = [min(part * a, rows) for a in range(axes + 1)]
    return [(starts[a], starts[a + 1] - starts[a]) for a in range(axes)]


class Tree:
    def __init__(self, place, axes, source, target, sems):
        self.place, self.axes, self.source, self.target = place, axes, source, target
        self.send, self.recv, self.core_send, self.core_recv, self.own = sems
        self.slots = 2 << axes
        self.levels, self.cores = [], []

    @staticmethod
    def scratch(axes):
        far, near = axes * axes, axes * axes + 1
        return [DMA((far,)), DMA((far,)), DMA((near,)), DMA((near,)), DMA]

    def origin(self, level, first):
        value = self.place.idx
        for k in range(level):
            value = flip(value, 2 << ((first + k) % self.axes))
        return value % self.slots

    def neighbour(self, axis):
        return self.place.member(flip(self.place.idx, 2 << (axis % self.axes)))

    def piece(self, slot, part):
        return self.target.at[slot] if part is None else self.target.at[slot, pl.ds(*part)]

    def to_core(self, source, slot, part):
        at = len(self.cores)
        self.cores.append(
            push(
                source,
                self.piece(slot, part),
                self.place.member(flip(self.place.idx, 1)),
                self.core_send.at[at],
                self.core_recv.at[at],
            )
        )

    def start(self):
        me = self.place.idx % self.slots
        self.levels.append(
            [
                push(
                    self.source, self.target.at[me], self.neighbour(a), self.send.at[a], self.recv.at[a]
                )
                for a in range(self.axes)
            ]
        )
        self.to_core(self.source, me, None)
        self.local = pltpu.make_async_copy(self.source, self.target.at[me], self.own)
        self.local.start()

    def forward(self, level):
        axes = self.axes
        parts = tree_parts(axes, self.target.shape[1])
        onward = []
        for a in range(axes):
            self.levels[level - 1][a].wait_recv()
            slot = self.origin(level, a)
            if level < axes:
                part = parts[a] if level + 1 == axes else None
                at = level * axes + a
                piece = self.piece(slot, part)
                onward.append(
                    push(piece, piece, self.neighbour(a + level), self.send.at[at], self.recv.at[at])
                )
                self.to_core(self.target.at[slot], slot, None)
            else:
                self.to_core(self.piece(slot, parts[a]), slot, parts[a])
        self.levels.append(onward)

    def finish(self):
        self.local.wait()
        for level in self.levels:
            for copy in level:
                copy.wait_send()
        for copy in self.cores:
            copy.wait()


class Halving:
    def __init__(self, place, axes, value, result, scratch, firsts=None):
        self.firsts = firsts = firsts or list(range(axes))
        self.axes, self.value, self.result = axes, value, result
        self.other, self.held, self.land, send, recv, send0, recv0 = scratch
        self.blocks = 1 << axes
        width = value.shape[-1]
        part = width // len(firsts)
        self.columns = [pl.ds(part * a, part) for a in range(len(firsts))]
        self.core = place.idx % 2
        self.chip = place.idx // 2 % self.blocks
        self.sources = []
        for j in range(self.blocks):
            k = self.chip
            for a in range(axes):
                if j >> a & 1:
                    k = flip(k, 1 << a)
            self.sources.append(k)
        self.first, self.copies = [], {}
        for p in range(len(firsts)):
            self.first.append(
                remote(
                    value.at[:, 1 - self.core, :, self.columns[p]],
                    self.other.at[:, :, self.columns[p]],
                    place.member(flip(place.idx, 1)),
                    send0.at[p],
                    recv0.at[p],
                )
            )
            for step in range(axes):
                bit, sent = self.sent(p, step)
                for j in sent:
                    self.copies[p, j] = remote(
                        self.held.at[j, :, self.columns[p]],
                        self.land.at[j, :, self.columns[p]],
                        place.member(flip(place.idx, 2 * bit)),
                        send.at[p, j],
                        recv.at[p, j],
                    )

    @staticmethod
    def scratch(axes, rows, width):
        blocks = 1 << axes
        return [
            pltpu.VMEM((blocks, rows, width), BF),
            pltpu.VMEM((blocks, rows, width), BF),
            pltpu.VMEM((blocks, rows, width), BF),
            DMA((axes, blocks)),
            DMA((axes, blocks)),
            DMA((axes,)),
            DMA((axes,)),
        ]

    def sent(self, part, step):
        first = self.firsts[part]
        seen = [1 << ((first + s) % self.axes) for s in range(step)]
        bit = 1 << ((first + step) % self.axes)
        return bit, [j for j in range(self.blocks) if j & bit and not any(j & s for s in seen)]

    def start(self):
        for copy in self.first:
            copy.start()

    def pair(self):
        for p in range(len(self.firsts)):
            cols = self.columns[p]
            self.first[p].wait_recv()
            _, early = self.sent(p, 0)
            for j in early + [j for j in range(self.blocks) if j not in early]:
                k = self.sources[j]
                self.held[j, :, cols] = (
                    self.value[k, self.core, :, cols].astype(F32) + self.other[k, :, cols].astype(F32)
                ).astype(BF)
                if j in early:
                    self.copies[p, j].start()

    def halve(self, step):
        for p in range(len(self.firsts)):
            cols = self.columns[p]
            bit, arrived = self.sent(p, step)
            onward = self.sent(p, step + 1)[1] if step + 1 < self.axes else []
            for j in sorted(arrived, key=lambda j: (j - bit) not in onward):
                self.copies[p, j].wait_recv()
                k = j - bit
                total = self.held[k, :, cols].astype(F32) + self.land[j, :, cols].astype(F32)
                if step + 1 < self.axes:
                    self.held[k, :, cols] = total.astype(BF)
                    if k in onward:
                        self.copies[p, k].start()
                else:
                    self.result[:, cols] = total

    def run(self):
        self.start()
        self.pair()
        for step in range(self.axes):
            self.halve(step)
        self.finish()

    def finish(self):
        for copy in self.first:
            copy.wait_send()
        for copy in self.copies.values():
            copy.wait_send()


class Lines:
    def __init__(self, count, source, target, send, recv, own):
        me = lax.axis_index("ctx")
        self.copies = [pltpu.make_async_copy(source.at[me], target.at[me], own)]
        for step in range(1, count):
            peer = (me + step) % count
            self.copies.append(
                remote(source.at[peer], target.at[me], {"ctx": peer}, send.at[step - 1], recv.at[step - 1])
            )

    @staticmethod
    def scratch(count):
        return [DMA((count - 1,)), DMA((count - 1,)), DMA]

    def start(self):
        for copy in self.copies:
            copy.start()

    def finish(self):
        for copy in self.copies:
            copy.wait()


def everyone(place, count):
    group = place.reach * place.groups
    mates = [place.member((place.idx + step) % group) for step in range(1, group)]
    outside = [{"ctx": (place.base + place.reach + step) % count} for step in range(count - place.reach)]
    return mates + outside


def spread(place, source, target, sems, me=None):
    send, recv, own = sems
    count = target.shape[0]
    copies = []
    for step in range(1, count):
        peer = (place.idx + step) % count
        copies.append(
            push(
                source.at[peer],
                target.at[place.idx],
                place.member(peer),
                send.at[step - 1],
                recv.at[step - 1],
            )
        )
    local = pltpu.make_async_copy(source.at[place.idx], target.at[place.idx], own)
    local.start()
    copies.append(local)
    return copies


def begin_kernel(
    groups,
    reach,
    count,
    tokens,
    gains,
    ids,
    w_qkv,
    w_attn,
    freqs,
    input_all,
    gains_all,
    w_head,
    cosine,
    sine,
    marks,
    attn_half,
    ids_all,
    slab,
    mine,
    gain_land,
    own_sems,
    ids_send,
    ids_recv,
    gain_send,
    gain_recv,
    slab_send,
    slab_recv,
    wide_send,
    wide_recv,
    core_send,
    core_recv,
    *tree_sems,
):
    place = Place(groups, reach)
    group = reach * groups
    ctx, head, idx = place.ctx, place.head, place.idx
    shard = w_qkv.shape[0]
    ring = attn_half.shape[0]
    sub = count // ring
    side, spot = ctx % sub, ctx // sub
    lanes = attn_half.shape[2] // groups
    core = {"heads": flip(head, 1)}
    mates = [place.member((idx + step) % group) for step in range(1, group)]
    lines = [{"ctx": (ctx + step) % count} for step in range(1, count)]
    meet(everyone(place, count))
    first = [
        push(gains, gain_land.at[ctx], lines[step - 1], gain_send.at[step - 1], gain_recv.at[step - 1])
        for step in range(1, count)
    ]
    small = [
        push(ids, ids_all.at[idx], mates[step - 1], ids_send.at[step - 1], ids_recv.at[step - 1])
        for step in range(1, group)
    ]
    half = pl.ds(pl.multiple_of(head % 2 * (shard // 2), 16), shard // 2)
    thirds = []
    for step in range(1, count):
        peer = (ctx + step) % count
        column = ((peer % reach) * groups + head) // 2 * 128
        for third in range(3):
            start = pl.multiple_of(third * 1024 + column, 128)
            thirds.append(
                push(
                    w_qkv.at[half, pl.ds(start, 128)],
                    slab.at[ctx, half, pl.ds(third * 128, 128)],
                    lines[step - 1],
                    slab_send.at[step - 1, third],
                    slab_recv.at[step - 1, third],
                )
            )
    gain_land[ctx] = gains[...]
    where = lambda h: pl.ds(pl.multiple_of(h * lanes, 128), lanes)
    across = where(head)
    own = [
        pltpu.make_async_copy(ids, ids_all.at[idx], own_sems.at[3]),
        pltpu.make_async_copy(w_attn.at[:, across], attn_half.at[spot, :, across], own_sems.at[4]),
    ]
    for third in range(3):
        start = pl.multiple_of(third * 1024 + idx // 2 * 128, 128)
        own.append(
            pltpu.make_async_copy(
                w_qkv.at[half, pl.ds(start, 128)],
                slab.at[ctx, half, pl.ds(third * 128, 128)],
                own_sems.at[third],
            )
        )
    for copy in own:
        copy.start()
    for copy in first:
        copy.wait_recv()
    gain, gain_two = (
        jnp.concatenate([gain_land[c, k : k + 1, :shard] for c in range(count)], axis=1)
        for k in range(2)
    )
    normed, _ = norm_parts(tokens[...].astype(F32))
    mine[...] = (normed * gain).astype(BF)
    tree = Tree(place, 3, mine, input_all, tree_sems[:5])
    tree.start()
    gains_all[0:1, :] = gain
    gains_all[1:2, :] = gain_two
    late = []
    for step in range(1, ring):
        late.append(
            push(
                w_attn.at[:, across],
                attn_half.at[spot, :, across],
                {"ctx": (spot + step) % ring * sub + side},
                wide_send.at[step - 1],
                wide_recv.at[step - 1],
            )
        )
    tree.forward(1)
    for copy in own:
        copy.wait()
    for copy in thirds:
        copy.wait_recv()
    for copy in late:
        copy.wait_recv()
    collect = Collect(
        groups, [(attn_half.at[:, :, across], lambda h: attn_half.at[:, :, where(h)])], *tree_sems[5:]
    )
    collect.start(0)
    shared = push(slab.at[:, half], slab.at[:, half], core, core_send, core_recv)
    for copy in small:
        copy.wait()
    row = lambda k: jnp.concatenate([ids_all[j, k : k + 1, :] for j in range(group)], axis=1)
    angles = freqs[...] * row(0).astype(F32)
    cosine[...] = jnp.cos(angles)
    sine[...] = jnp.sin(angles)
    parity = (row(1) % 2).astype(F32)
    blank = jnp.zeros((MARKS - 2, parity.shape[1]), F32)
    marks[...] = jnp.concatenate(
        [parity, 1.0 - parity, blank, (1.0 - parity) * MASKED, parity * MASKED, blank], axis=0
    ).astype(BF)
    tree.forward(2)
    shared.wait()
    odd = head % 2 == 1
    for c in range(count):
        rows = slice(c * shard, (c + 1) * shard)
        block = slab[c].astype(F32)
        parts = []
        for third in range(3):
            at = third * 128
            parts.append(jnp.where(odd, block[:, at + HD : at + 128], block[:, at : at + HD]))
        w_head[rows] = jnp.concatenate(parts, axis=1).astype(BF)
    collect.forward(0)
    tree.forward(3)
    tree.finish()
    collect.finish()
    for copy in first + thirds + late:
        copy.wait_send()


def begin(tokens, gains, ids, w_qkv, w_attn, freqs, ring, count, groups, reach):
    rows, width = tokens.shape
    shard = w_qkv.shape[0]
    group = groups * reach
    sems = lambda *shape: [DMA(shape), DMA(shape)]
    return pl.pallas_call(
        functools.partial(begin_kernel, groups, reach, count),
        in_specs=[VMEM, VMEM, ANY, ANY, ANY, VMEM],
        out_specs=[ANY, VMEM, VMEM, VMEM, VMEM, VMEM, ANY],
        out_shape=[
            jax.ShapeDtypeStruct((group, rows, width), BF),
            jax.ShapeDtypeStruct((8, width), F32),
            jax.ShapeDtypeStruct((width, 3 * HD), BF),
            jax.ShapeDtypeStruct((HALF, group * rows), F32),
            jax.ShapeDtypeStruct((HALF, group * rows), F32),
            jax.ShapeDtypeStruct((2 * MARKS, group * rows), BF),
            jax.ShapeDtypeStruct((ring, shard, width), BF),
        ],
        scratch_shapes=[
            pltpu.VMEM((group, 8, rows), jnp.int32),
            pltpu.VMEM((count, shard, 3 * 128), BF),
            pltpu.VMEM((rows, width), BF),
            pltpu.VMEM((count, 8, gains.shape[1]), F32),
            DMA((5,)),
            *sems(group - 1),
            *sems(count - 1),
            *sems(count - 1, 3),
            *sems(ring - 1),
            DMA,
            DMA,
            *Tree.scratch(3),
            *Collect.scratch(1, groups),
        ],
        compiler_params=pltpu.CompilerParams(
            collective_id=0, has_side_effects=True, vmem_limit_bytes=12 << 20
        ),
        cost_estimate=pl.CostEstimate(flops=0, bytes_accessed=30 << 20, transcendentals=0),
        name="begin",
    )(tokens, gains, ids, w_qkv, w_attn, freqs)


class Line:
    def __init__(self, length, sub, first, sources, targets, send, recv):
        ctx = lax.axis_index("ctx")
        spot, side = ctx // sub, ctx % sub
        self.length, self.spot, self.first = length, spot, first
        self.waited = 0
        beside = [{"ctx": (spot + 1) % length * sub + side}, {"ctx": (spot + length - 1) % length * sub + side}]
        self.copies = [
            [
                remote(sources[d][q], targets[d][q], beside[d], send.at[d, q], recv.at[d, q])
                for q in range(len(sources[d]))
            ]
            for d in range(2)
        ]

    def sends(self, d, q):
        s, spot, last = (q + self.first) // 2, self.spot, self.length - 1
        if d:
            return jnp.logical_and(spot + s <= last, spot > 0)
        return jnp.logical_and(spot >= s, spot < last)

    def receives(self, d, q):
        s = (q + self.first) // 2
        return self.spot + s + 1 < self.length if d else self.spot > s

    def arrive(self, q):
        for d in range(2):
            pl.when(self.receives(d, q))(self.copies[d][q].wait_recv)
        self.waited = q + 1

    def start(self, q):
        if q >= 2:
            self.arrive(q - 2)
        for d in range(2):
            pl.when(self.sends(d, q))(self.copies[d][q].start)

    def finish(self):
        for q in range(self.waited, len(self.copies[0])):
            self.arrive(q)
        for d in range(2):
            for q, copy in enumerate(self.copies[d]):
                pl.when(self.sends(d, q))(copy.wait_send)


def ring_half(sub, side, k):
    return (side + k) % 2 if sub == 2 else k


class Columns:
    def __init__(self, place, part, whole, own, side_send, side_recv, near_send, near_recv):
        _, sub, _, width = whole.shape
        side = place.ctx % sub
        half = pl.ds(pl.multiple_of(place.head % 2 * (width // 2), 128), width // 2)
        self.own = pltpu.make_async_copy(part, whole.at[:, side], own)
        self.sides, self.near = [], []
        for step in range(1, sub):
            peer, source = (side + step) % sub, (side - step + sub) % sub
            self.sides.append(
                remote(
                    part.at[:, :, half],
                    whole.at[:, side, :, half],
                    {"ctx": place.ctx - side + peer},
                    side_send.at[step - 1],
                    side_recv.at[step - 1],
                )
            )
            here = whole.at[:, source, :, half]
            self.near.append(
                remote(
                    here, here, {"heads": flip(place.head, 1)}, near_send.at[step - 1], near_recv.at[step - 1]
                )
            )

    @staticmethod
    def scratch(sub):
        count = (max(sub - 1, 1),)
        return [DMA, DMA(count), DMA(count), DMA(count), DMA(count)]

    def start(self):
        self.own.start()
        for copy in self.sides:
            copy.start()

    def across(self):
        for side, near in zip(self.sides, self.near):
            side.wait_recv()
            near.start()

    def finish(self):
        self.own.wait()
        for side, near in zip(self.sides, self.near):
            side.wait_send()
            near.wait()


def attend_kernel(
    groups,
    reach,
    lines,
    tile,
    x_ref,
    w_ref,
    cos_ref,
    sin_ref,
    mark_ref,
    attn_half,
    mlp,
    out_ref,
    wide_ref,
    lse_ref,
    qkv_ref,
    attn_all,
    mlp_pair,
    mlp_near,
    ring_send,
    ring_recv,
    swap_send,
    swap_recv,
    swap_own,
    *sems,
):
    count = x_ref.shape[0]
    step = pl.program_id(0)
    steps = count // tile
    place = Place(groups, reach)
    ring_size, sub = attn_all.shape[:2]
    side = place.ctx % sub
    early = mlp_near.shape[1]
    if sub == 2:
        kept = pltpu.make_async_copy(mlp.at[side], mlp_pair.at[side], swap_own)
        swap = [
            remote(
                mlp.at[1 - side],
                mlp_pair.at[side],
                {"ctx": place.ctx + 1 - 2 * side},
                swap_send,
                swap_recv,
            )
        ]
        sources = [mlp.at[side], mlp_pair.at[1 - side]]
    else:
        kept = pltpu.make_async_copy(mlp, mlp_pair, swap_own)
        swap = []
        sources = [mlp.at[0], mlp.at[1]]
    ring = Line(
        ring_size,
        sub,
        0,
        [sources + [mlp_near.at[d, q] for q in range(early - 2)] for d in range(2)],
        [[mlp_near.at[d, q] for q in range(early)] for d in range(2)],
        ring_send,
        ring_recv,
    )
    columns = Columns(place, attn_half, attn_all, *sems)

    @pl.when(step == 0)
    def _():
        meet(everyone(place, lines))
        for copy in swap:
            copy.start()
        ring.start(0)
        kept.start()
        columns.start()
        qkv_ref[HD:QM_END, :] = mark_ref[:MARKS, :]
        qkv_ref[K_END:KM_END, :] = mark_ref[MARKS:, :]

        @pl.loop(0, steps)
        def _(i):
            at = pl.ds(pl.multiple_of(i * tile, tile), tile)
            cosine, sine = cos_ref[:, at], sin_ref[:, at]
            part = dot(w_ref[...], x_ref[at, :], 0, 1)

            def turn(value):
                front, back = value[:HALF], value[HALF:]
                return jnp.concatenate(
                    [front * cosine - back * sine, back * cosine + front * sine], axis=0
                )

            qkv_ref[:HD, at] = (turn(part[:HD]) * 0.125).astype(BF)
            qkv_ref[QM_END:K_END, at] = turn(part[HD : 2 * HD]).astype(BF)
            qkv_ref[KM_END:, at] = part[2 * HD :].astype(BF)

    here = pl.ds(pl.multiple_of(step * tile, tile), tile)
    query = qkv_ref[:QM_END, here]
    keys = [slice(j * tile, (j + 1) * tile) for j in range(steps)]
    scores = [dot(qkv_ref[QM_END:KM_END, at], query, 0, 0) for at in keys]
    top = functools.reduce(jnp.maximum, [jnp.max(s, axis=0, keepdims=True) for s in scores])
    raised = [jnp.exp(s - top) for s in scores]
    total = functools.reduce(jnp.add, [jnp.sum(e, axis=0, keepdims=True) for e in raised])
    scale = 1.0 / total
    result = jnp.zeros((HD, tile), F32)
    for j in range(steps):
        result += dot(qkv_ref[KM_END:, keys[j]], (raised[j] * scale).astype(BF), 1, 0)
    rows = out_ref.shape[2]
    for k in range(tile // rows):
        out_ref[step * (tile // rows) + k] = result[:, k * rows : (k + 1) * rows].astype(BF)
    wide_ref[:, here] = result
    lse_ref[:, here] = top + jnp.log(total)

    @pl.when(step == min(1, steps - 1))
    def _():
        for copy in swap:
            copy.wait_recv()
        for q in range(1, min(early, 3)):
            ring.start(q)

    @pl.when(step == steps - 1)
    def _():
        columns.across()
        for q in range(3, early):
            ring.start(q)
        ring.finish()
        for copy in swap:
            copy.wait_send()
        kept.wait()
        columns.finish()


def attend(x, w, cosine, sine, marks, attn_half, mlp, lines, groups, reach, rows, tile):
    count, width = x.shape
    ring, shard, _ = attn_half.shape
    sub = lines // ring
    early = ring - 1
    whole = lambda *shape: pl.BlockSpec(shape, lambda i: (0,) * len(shape))
    return pl.pallas_call(
        functools.partial(attend_kernel, groups, reach, lines, tile),
        grid=(count // tile,),
        in_specs=[
            whole(count, width),
            whole(*w.shape),
            whole(HALF, count),
            whole(HALF, count),
            whole(2 * MARKS, count),
            ANY,
            ANY,
        ],
        out_specs=[
            whole(count // rows, HD, rows),
            whole(HD, count),
            whole(1, count),
            whole(V_END, count),
            ANY,
            ANY,
            ANY,
        ],
        out_shape=[
            jax.ShapeDtypeStruct((count // rows, HD, rows), BF),
            jax.ShapeDtypeStruct((HD, count), F32),
            jax.ShapeDtypeStruct((1, count), F32),
            jax.ShapeDtypeStruct((V_END, count), BF),
            jax.ShapeDtypeStruct((ring, sub, shard, width), BF),
            jax.ShapeDtypeStruct(mlp.shape, BF),
            jax.ShapeDtypeStruct((2, early, *mlp.shape[1:]), BF),
        ],
        scratch_shapes=[DMA((2, early)), DMA((2, early)), DMA, DMA, DMA, *Columns.scratch(sub)],
        compiler_params=pltpu.CompilerParams(
            collective_id=5, has_side_effects=True, vmem_limit_bytes=32 << 20
        ),
        cost_estimate=pl.CostEstimate(
            flops=count * count * HD * 8, bytes_accessed=count * 4096, transcendentals=count * count
        ),
        name="attend",
    )(x, w, cosine, sine, marks, attn_half, mlp)


def middle_kernel(
    groups,
    reach,
    lines,
    outgoing,
    tokens,
    d_out,
    w_attn,
    gains,
    mlp_pair,
    mlp_near,
    mlp_all,
    upstream_all,
    middle,
    attended,
    mlp_weights,
    land,
    mine,
    a2a_send,
    a2a_recv,
    own,
    ring_send,
    ring_recv,
    ring_own,
    land_own,
    *tree_sems,
):
    place = Place(groups, reach)
    group = groups * reach
    early, count = mlp_near.shape[1], mlp_weights.shape[0]
    sub = lines // count
    spot, side = place.ctx // sub, place.ctx % sub

    def slot(d, q, ahead):
        block = (spot + (q // 2 + ahead if d else count - q // 2 - ahead)) % count
        return mlp_weights.at[block, ring_half(sub, side, q % 2)]

    rest = range(early, 2 * (count - 1))
    ring = Line(
        count,
        sub,
        early,
        [[mlp_near.at[d, q - 2] if q - 2 < early else slot(d, q, 0) for q in rest] for d in range(2)],
        [[slot(d, q, 0) for q in rest] for d in range(2)],
        ring_send,
        ring_recv,
    )
    local = [pltpu.make_async_copy(mlp_pair, mlp_weights.at[spot], ring_own.at[0])]
    near = []
    for d in range(2):
        for q in range(early):
            copy = pltpu.make_async_copy(
                mlp_near.at[d, q], slot(d, q, 1), ring_own.at[1 + d * early + q]
            )
            there = spot + q // 2 + 1 < count if d else spot > q // 2
            near.append((there, copy))
    meet(everyone(place, lines))
    copies = spread(place, outgoing, land, (a2a_send, a2a_recv, own))
    ring.start(0)
    ring.start(1)
    up = Tree(place, 2, d_out, upstream_all, tree_sems[5:10])
    up.start()
    for copy in local:
        copy.start()
    for there, copy in near:
        pl.when(there)(copy.start)
    for copy in copies:
        copy.wait()
    collect = Collect(groups, [(land, lambda h: attended.at[h])], *tree_sems[10:])
    collect.start(0)
    local.append(pltpu.make_async_copy(land, attended.at[place.head], land_own))
    local[-1].start()
    value = tokens[...].astype(F32) + dot(
        land[...].reshape(group * HD, tokens.shape[0]), w_attn[...], 0, 0
    )
    middle[...] = value
    normed, _ = norm_parts(value)
    mine[...] = (normed * gains[1:2, :]).astype(BF)
    tree = Tree(place, 2, mine, mlp_all, tree_sems[:5])
    tree.start()
    up.forward(1)
    for q in range(2, len(rest)):
        ring.start(q)
    tree.forward(1)
    up.forward(2)
    tree.forward(2)
    collect.forward(0)
    up.finish()
    tree.finish()
    collect.finish()
    for copy in local:
        copy.wait()
    for there, copy in near:
        pl.when(there)(copy.wait)
    ring.finish()


def middle_step(outgoing, tokens, d_out, w_attn, gains, mlp_pair, mlp_near, lines, groups, reach):
    rows, width = tokens.shape
    group = groups * reach
    early, sub = mlp_near.shape[1], 8 // groups
    ring = lines // sub
    left = 2 * (ring - 1) - early
    return pl.pallas_call(
        functools.partial(middle_kernel, groups, reach, lines),
        in_specs=[ANY, VMEM, ANY, VMEM, VMEM, ANY, ANY],
        out_specs=[ANY, ANY, VMEM, ANY, ANY],
        out_shape=[
            jax.ShapeDtypeStruct((8, rows, width), BF),
            jax.ShapeDtypeStruct((8, rows, width), BF),
            jax.ShapeDtypeStruct((rows, width), F32),
            jax.ShapeDtypeStruct((groups, group, HD, rows), BF),
            jax.ShapeDtypeStruct((ring, *mlp_pair.shape), BF),
        ],
        scratch_shapes=[
            pltpu.VMEM((group, HD, rows), BF),
            pltpu.VMEM((rows, width), BF),
            DMA((group - 1,)),
            DMA((group - 1,)),
            DMA,
            DMA((2, left)),
            DMA((2, left)),
            DMA((2 * early + 1,)),
            DMA,
            *Tree.scratch(2),
            *Tree.scratch(2),
            *Collect.scratch(1, groups),
        ],
        compiler_params=pltpu.CompilerParams(
            collective_id=1, has_side_effects=True, vmem_limit_bytes=12 << 20
        ),
        cost_estimate=pl.CostEstimate(flops=1 << 28, bytes_accessed=12 << 20, transcendentals=0),
        name="middle_step",
    )(outgoing, tokens, d_out, w_attn, gains, mlp_pair, mlp_near)


def mlp_kernel(chunk, x_ref, up_ref, w_ref, back_ref, forward_ref, terms_ref, kept):
    count, width = x_ref.shape

    @pl.loop(0, count // chunk)
    def _(i):
        at = pl.ds(pl.multiple_of(i * chunk, chunk), chunk)
        gate_up = dot(x_ref[at, :], w_ref[:, : 2 * SLICE], 1, 0)
        left, right = gate_up[:, :SLICE], gate_up[:, SLICE:]
        grad_mixed = dot(up_ref[at, :], w_ref[:, 2 * SLICE :], 1, 0)
        normal_cdf = 0.5 * (1.0 + lax.erf(left * 0.7071067811865476))
        gelu = left * normal_cdf
        density = jnp.exp(-0.5 * left * left) * 0.3989422804014327
        kept[at, :SLICE] = (grad_mixed * right * (normal_cdf + left * density)).astype(BF)
        kept[at, SLICE : 2 * SLICE] = (grad_mixed * gelu).astype(BF)
        kept[at, 2 * SLICE :] = (gelu * right).astype(BF)
        back_ref[at, :] = dot(kept[at, : 2 * SLICE], w_ref[:, : 2 * SLICE], 1, 1).astype(BF)
        forward_ref[at, :] = dot(kept[at, 2 * SLICE :], w_ref[:, 2 * SLICE :], 1, 1).astype(BF)

    @pl.loop(0, width // chunk)
    def _(i):
        at = pl.ds(pl.multiple_of(i * chunk, chunk), chunk)
        terms_ref[at, : 2 * SLICE] = dot(x_ref[:, at], kept[:, : 2 * SLICE], 0, 0).astype(BF)
        terms_ref[at, 2 * SLICE :] = dot(up_ref[:, at], kept[:, 2 * SLICE :], 0, 0).astype(BF)


def mlp_step(x, up, w, chunk):
    count, width = x.shape
    return pl.pallas_call(
        functools.partial(mlp_kernel, chunk),
        in_specs=[VMEM] * 3,
        out_specs=[VMEM] * 3,
        out_shape=[
            jax.ShapeDtypeStruct((count, width), BF),
            jax.ShapeDtypeStruct((count, width), BF),
            jax.ShapeDtypeStruct((width, 3 * SLICE), BF),
        ],
        scratch_shapes=[pltpu.VMEM((count, 3 * SLICE), BF)],
        compiler_params=pltpu.CompilerParams(vmem_limit_bytes=28 << 20),
        cost_estimate=pl.CostEstimate(
            flops=18 * count * width * SLICE, bytes_accessed=14 << 20, transcendentals=2 * count * SLICE
        ),
        name="mlp_step",
    )(x, up, w)


def turn_kernel(
    groups,
    reach,
    partial,
    middle,
    d_out,
    w_attn,
    gains,
    attended,
    grads,
    grad_middle,
    attn_part,
    columns,
    total,
    outgoing,
    branch,
    a2a_send,
    a2a_recv,
    own,
    side_send,
    side_recv,
    side_own,
    *halving,
):
    place = Place(groups, reach)
    group = groups * reach
    lanes = branch.shape[2]
    meet([place.member((place.idx + step) % group) for step in range(1, group)])
    Halving(place, 2, partial, total, halving).run()
    normed, inverse_std = norm_parts(middle[...])
    upstream = total[...]
    grad = d_out[...].astype(F32) + norm_back(upstream, normed, inverse_std, gains[1:2, :])
    grad_middle[...] = grad
    low = grad.astype(BF)
    for g in range(groups):
        branch[g] = low[:, g * lanes : (g + 1) * lanes]
    outgoing[...] = dot(w_attn[...], low, 1, 1).astype(BF).reshape(outgoing.shape)
    copies = spread(place, outgoing, grads, (a2a_send, a2a_recv, own))
    for step in range(1, groups):
        peer = (place.head + step) % groups
        copies.append(
            push(
                branch.at[peer],
                columns.at[place.head],
                {"heads": peer},
                side_send.at[step - 1],
                side_recv.at[step - 1],
            )
        )
    local = pltpu.make_async_copy(branch.at[place.head], columns.at[place.head], side_own)
    local.start()
    for copy in copies[-(groups - 1) :]:
        copy.wait()
    local.wait()
    attn_part[...] = functools.reduce(
        jnp.add, [dot(attended[g], columns[g], 1, 0) for g in range(groups)]
    ).astype(BF)
    for copy in copies[: -(groups - 1)]:
        copy.wait()


def turn_step(partial, middle, d_out, w_attn, gains, attended, groups, reach):
    rows, width = middle.shape
    group = groups * reach
    return pl.pallas_call(
        functools.partial(turn_kernel, groups, reach),
        in_specs=[VMEM] * 6,
        out_specs=[ANY, VMEM, VMEM],
        out_shape=[
            jax.ShapeDtypeStruct((group, HD, rows), BF),
            jax.ShapeDtypeStruct((rows, width), F32),
            jax.ShapeDtypeStruct((width, width // groups), BF),
        ],
        scratch_shapes=[
            pltpu.VMEM((groups, rows, width // groups), BF),
            pltpu.VMEM((rows, width), F32),
            pltpu.VMEM((group, HD, rows), BF),
            pltpu.VMEM((groups, rows, width // groups), BF),
            DMA((group - 1,)),
            DMA((group - 1,)),
            DMA,
            DMA((groups - 1,)),
            DMA((groups - 1,)),
            DMA,
            *Halving.scratch(2, rows, width),
        ],
        compiler_params=pltpu.CompilerParams(
            collective_id=2, has_side_effects=True, vmem_limit_bytes=16 << 20
        ),
        cost_estimate=pl.CostEstimate(flops=1 << 28, bytes_accessed=12 << 20, transcendentals=0),
        name="turn_step",
    )(partial, middle, d_out, w_attn, gains, attended)


def attend_back_kernel(
    groups,
    reach,
    lines,
    tile,
    qkv_ref,
    grad_ref,
    wide_ref,
    lse_ref,
    x_ref,
    w_ref,
    cos_ref,
    sin_ref,
    forward_ref,
    attn_ref,
    out_ref,
    weight_ref,
    ahead_ref,
    attn_out_ref,
    sums,
    queries,
    weight,
    attn_land,
    *sems,
):
    count = x_ref.shape[0]
    rows = grad_ref.shape[2]
    steps, per_tile = count // tile, tile // rows
    step = pl.program_id(0)
    place = Place(groups, reach)
    halving = Halving(place, 2, forward_ref, ahead_ref, sems[:7])
    swap = Lines(lines, attn_ref, attn_land, *sems[7:])

    @pl.when(step == 0)
    def _():
        greet(everyone(place, lines))
        sums[...] = jnp.zeros_like(sums)

    here = pl.ds(pl.multiple_of(step * tile, tile), tile)
    query = qkv_ref[:QM_END, here]
    grad = jnp.concatenate([grad_ref[step * per_tile + k] for k in range(per_tile)], axis=1)
    delta = jnp.sum(grad.astype(F32) * wide_ref[:, here], axis=0, keepdims=True)
    lse = lse_ref[:, here]
    grad_query = jnp.zeros((HD, tile), F32)
    for j in range(steps):
        keys = slice(j * tile, (j + 1) * tile)
        prob = jnp.exp(dot(qkv_ref[QM_END:KM_END, keys], query, 0, 0) - lse)
        grad_prob = dot(qkv_ref[KM_END:, keys], grad, 0, 0)
        grad_score = (prob * (grad_prob - delta)).astype(BF)
        grad_query += dot(qkv_ref[QM_END:K_END, keys], grad_score, 1, 0)
        sums[:HD, keys] += dot(query[:HD], grad_score, 1, 1)
        sums[HD:, keys] += dot(grad, prob.astype(BF), 1, 1)
    queries[:, here] = (grad_query * 0.125).astype(BF)

    @pl.when(step == 0)
    def _():
        pl.semaphore_wait(pltpu.get_barrier_semaphore(), len(everyone(place, lines)))
        halving.start()
        swap.start()

    pl.when(step == min(1, steps - 1))(halving.pair)
    pl.when(step == min(2, steps - 1))(lambda: halving.halve(0))

    @pl.when(step == steps - 1)
    def _():
        weight[...] = jnp.zeros_like(weight)

        @pl.loop(0, steps)
        def _(i):
            at = pl.ds(pl.multiple_of(i * tile, tile), tile)
            cosine, sine = cos_ref[:, at], sin_ref[:, at]

            def turn_back(value):
                front, back = value[:HALF], value[HALF:]
                return [front * cosine + back * sine, back * cosine - front * sine]

            low = lambda value: value.astype(BF).astype(F32)
            projected = jnp.concatenate(
                [
                    *turn_back(queries[:, at].astype(F32)),
                    *turn_back(low(sums[:HD, at])),
                    low(sums[HD:, at]),
                ],
                axis=0,
            ).astype(BF)
            part = dot(projected, w_ref[...], 0, 1).astype(BF)
            for k in range(per_tile):
                out_ref[i * per_tile + k] = part[k * rows : (k + 1) * rows]
            weight[...] += dot(projected, x_ref[at, :], 1, 0)

        shard = weight_ref.shape[2]
        for c in range(lines):
            weight_ref[c] = weight[:, c * shard : (c + 1) * shard].astype(BF)
        halving.halve(1)
        swap.finish()
        attn_out_ref[...] = functools.reduce(
            jnp.add, [attn_land[c].astype(F32) for c in range(lines)]
        ).astype(BF)
        halving.finish()


def attend_back(qkv, grad, wide, lse, x, w, cosine, sine, forward, attn, groups, reach, tile):
    count, width = x.shape
    blocks, _, rows = grad.shape
    lines, shard, lanes = attn.shape
    whole = lambda *shape: pl.BlockSpec(shape, lambda i: (0,) * len(shape))
    operands = (qkv, grad, wide, lse, x, w, cosine, sine, forward)
    return pl.pallas_call(
        functools.partial(attend_back_kernel, groups, reach, lines, tile),
        grid=(count // tile,),
        in_specs=[*[whole(*operand.shape) for operand in operands], ANY],
        out_specs=[
            whole(blocks, rows, width),
            whole(lines, 3 * HD, shard),
            whole(rows, width),
            whole(shard, lanes),
        ],
        out_shape=[
            jax.ShapeDtypeStruct((blocks, rows, width), BF),
            jax.ShapeDtypeStruct((lines, 3 * HD, shard), BF),
            jax.ShapeDtypeStruct((rows, width), F32),
            jax.ShapeDtypeStruct((shard, lanes), BF),
        ],
        scratch_shapes=[
            pltpu.VMEM((2 * HD, count), F32),
            pltpu.VMEM((HD, count), BF),
            pltpu.VMEM((3 * HD, width), F32),
            pltpu.VMEM((lines, shard, lanes), BF),
            *Halving.scratch(2, rows, width),
            *Lines.scratch(lines),
        ],
        compiler_params=pltpu.CompilerParams(
            collective_id=4, has_side_effects=True, vmem_limit_bytes=44 << 20
        ),
        cost_estimate=pl.CostEstimate(
            flops=count * count * HD * 20, bytes_accessed=count * 6144, transcendentals=count * count
        ),
        name="attend_back",
    )(*operands, attn)


class Collect:
    def __init__(self, groups, pieces, far_send, far_recv, near_send, near_recv):
        head = lax.axis_index("heads")
        self.half = half = groups // 2
        pair = {"heads": flip(head, 1)}
        self.far, self.near = [], []
        for n, (piece, where) in enumerate(pieces):
            self.far.append(
                [
                    remote(
                        piece,
                        where(head),
                        {"heads": (head + 2 * k) % groups},
                        far_send.at[n, k - 1],
                        far_recv.at[n, k - 1],
                    )
                    for k in range(1, half)
                ]
            )
            sides = [(piece, where(head))]
            for k in range(1, half):
                got = where((head - 2 * k + groups) % groups)
                sides.append((got, got))
            self.near.append(
                [
                    remote(source, target, pair, near_send.at[n, k], near_recv.at[n, k])
                    for k, (source, target) in enumerate(sides)
                ]
            )

    @staticmethod
    def scratch(count, groups):
        far, near = (count, max(groups // 2 - 1, 1)), (count, groups // 2)
        return [DMA(far), DMA(far), DMA(near), DMA(near)]

    def start(self, n):
        for copy in self.far[n]:
            copy.start()
        self.near[n][0].start()

    def forward(self, n):
        for k, copy in enumerate(self.far[n]):
            copy.wait_recv()
            self.near[n][k + 1].start()

    def finish(self):
        for copies in self.far:
            for copy in copies:
                copy.wait_send()
        for copies in self.near:
            for copy in copies:
                copy.wait()


def end_kernel(
    groups,
    reach,
    lines,
    partial,
    weight,
    mlp,
    attn,
    total,
    mlp_all,
    weight_all,
    attn_all,
    lined,
    summed,
    swap_send,
    swap_recv,
    own,
    *rest,
):
    place = Place(groups, reach)
    sub = mlp.shape[0]
    mine, head = place.ctx % sub, place.head
    meet(everyone(place, lines))
    wide = Halving(place, 3, partial, total, rest[:7], [2, 1])
    swap = Lines(lines, weight, lined, *rest[7:10])
    wide.start()
    swaps = []
    for step in range(1, sub):
        peer = (mine + step) % sub
        swaps.append(
            push(
                mlp.at[peer],
                mlp_all.at[mine, head],
                {"ctx": place.ctx - mine + peer},
                swap_send.at[step - 1],
                swap_recv.at[step - 1],
            )
        )
    pieces = [(mlp.at[mine], lambda h: mlp_all.at[mine, h]), (attn, lambda h: attn_all.at[h])]
    for step in range(1, sub):
        source = (mine - step + sub) % sub
        pieces.append(
            (mlp_all.at[source, head], lambda h, source=source: mlp_all.at[source, h])
        )
    pieces.append((summed, lambda h: weight_all.at[h]))
    collect = Collect(groups, pieces, *rest[10:14])
    swap.start()
    local = [
        pltpu.make_async_copy(mlp.at[mine], mlp_all.at[mine, head], own.at[0]),
        pltpu.make_async_copy(attn, attn_all.at[head], own.at[1]),
        pltpu.make_async_copy(summed, weight_all.at[head], own.at[2]),
    ]
    local[0].start()
    local[1].start()
    collect.start(0)
    collect.start(1)
    wide.pair()
    for step in range(1, sub):
        swaps[step - 1].wait_recv()
        collect.start(step + 1)
    wide.halve(0)
    swap.finish()
    for r in range(reach):
        summed[r] = functools.reduce(
            jnp.add, [lined[r + reach * g].astype(F32) for g in range(lines // reach)]
        ).astype(BF)
    local[2].start()
    collect.start(sub + 1)
    wide.halve(1)
    collect.forward(0)
    collect.forward(1)
    wide.halve(2)
    for n in range(2, sub + 2):
        collect.forward(n)
    for copy in local:
        copy.wait()
    for copy in swaps:
        copy.wait_send()
    collect.finish()
    wide.finish()


def end_step(partial, weight, mlp, attn, groups, reach):
    rows, width = partial.shape[2:]
    lines, _, shard = weight.shape
    sub = mlp.shape[0]
    return pl.pallas_call(
        functools.partial(end_kernel, groups, reach, lines),
        in_specs=[VMEM, ANY, ANY, ANY],
        out_specs=[VMEM, ANY, ANY, ANY],
        out_shape=[
            jax.ShapeDtypeStruct((rows, width), F32),
            jax.ShapeDtypeStruct((sub, groups, *mlp.shape[1:]), BF),
            jax.ShapeDtypeStruct((groups, reach, 3 * HD, shard), BF),
            jax.ShapeDtypeStruct((groups, *attn.shape), BF),
        ],
        scratch_shapes=[
            pltpu.VMEM((lines, 3 * HD, shard), BF),
            pltpu.VMEM((reach, 3 * HD, shard), BF),
            DMA((max(sub - 1, 1),)),
            DMA((max(sub - 1, 1),)),
            DMA((3,)),
            *Halving.scratch(3, rows, width),
            *Lines.scratch(lines),
            *Collect.scratch(sub + 2, groups),
        ],
        compiler_params=pltpu.CompilerParams(
            collective_id=3, has_side_effects=True, vmem_limit_bytes=20 << 20
        ),
        cost_estimate=pl.CostEstimate(flops=0, bytes_accessed=24 << 20, transcendentals=0),
        name="end_step",
    )(partial, weight, mlp, attn)


def assemble_kernel(
    upstream,
    tokens,
    grad_middle,
    gains,
    middle,
    ahead,
    weight_all,
    attn_all,
    mlp_all,
    w_qkv,
    w_in,
    own_gains,
    result,
    grad,
    sum_qkv,
    sum_attn,
    sum_in,
    sum_out,
    gain_sums,
):
    groups, reach, _, shard = weight_all.shape
    lanes = attn_all.shape[2]
    result[...] = (middle[...] + ahead[...]).astype(BF)
    normed, inverse_std = norm_parts(tokens[...].astype(F32))
    grad[...] = grad_middle[...] + norm_back(upstream[...], normed, inverse_std, gains[0:1, :])
    for g in range(groups):
        sum_attn[:, g * lanes : (g + 1) * lanes] = attn_all[g].astype(F32)
    gain_one = jnp.zeros((shard, 128), F32)
    for third in range(3):
        part = slice(third * HD, (third + 1) * HD)
        for pair in range(H // 2):
            r, g = 2 * pair // groups, 2 * pair % groups
            tile = (
                jnp.concatenate([weight_all[g, r, part], weight_all[g + 1, r, part]], axis=0)
                .astype(F32)
                .T
            )
            at = third * H * HD + pair * 2 * HD
            sum_qkv[:, at : at + 2 * HD] = tile
            gain_one += tile * w_qkv[:, at : at + 2 * HD].astype(F32)
    gain_two = jnp.zeros((shard, 1), F32)
    for t in range(8):
        start, wide = slice_place(t)
        for half in range(2):
            piece = mlp_all[t, :, half * SLICE : half * SLICE + wide].astype(F32)
            at = half * FF + start
            sum_in[:, at : at + wide] = piece
            gain_two += jnp.sum(
                piece * w_in[:, at : at + wide].astype(F32), axis=1, keepdims=True
            )
        sum_out[start : start + wide, :] = (
            mlp_all[t, :, 2 * SLICE : 3 * SLICE].astype(F32).T[:wide]
        )
    one = jnp.sum(gain_one, axis=1, keepdims=True)
    lane = lax.broadcasted_iota(jnp.int32, (shard, 128), 1)
    both = jnp.where(lane == 0, one, gain_two).T
    gain_sums[...] = both[:8] / own_gains[...]


def assemble(upstream, tokens, grad_middle, gains, middle, ahead, weight_all, attn_all, mlp_all, w_qkv, w_in, own_gains):
    rows, width = tokens.shape
    shard = w_qkv.shape[0]
    return pl.pallas_call(
        assemble_kernel,
        in_specs=[VMEM] * 12,
        out_specs=[VMEM] * 7,
        out_shape=[
            jax.ShapeDtypeStruct((rows, width), BF),
            jax.ShapeDtypeStruct((rows, width), F32),
            jax.ShapeDtypeStruct((shard, 3 * width), F32),
            jax.ShapeDtypeStruct((shard, width), F32),
            jax.ShapeDtypeStruct((shard, 2 * FF), F32),
            jax.ShapeDtypeStruct((FF, shard), F32),
            jax.ShapeDtypeStruct((8, shard), F32),
        ],
        compiler_params=pltpu.CompilerParams(vmem_limit_bytes=24 << 20),
        cost_estimate=pl.CostEstimate(flops=1 << 24, bytes_accessed=20 << 20, transcendentals=0),
        name="assemble",
    )(upstream, tokens, grad_middle, gains, middle, ahead, weight_all, attn_all, mlp_all, w_qkv, w_in, own_gains)


def slice_start(t):
    return 128 * jnp.minimum(3 * t, 2 * t + 5)


def slice_place(t):
    start = 128 * min(3 * t, 2 * t + 5)
    return start, min(128 * min(3 * t + 3, 2 * t + 7), FF) - start


def body(count, tokens, d_out, segment_ids, position_ids, w_qkv, w_attn, w_in, w_out, gain_attn, gain_mlp):
    groups = lax.axis_size("heads")
    rows, width = tokens.shape
    shard = w_qkv.shape[0]
    reach = SEQ_MAX // (rows * groups)
    group = reach * groups
    sub = 8 // groups
    ctx, head = lax.axis_index("ctx"), lax.axis_index("heads")
    assert group == H and sub * groups == 8
    total = group * rows
    tile = 512

    def mlp_slice(value, axis, start, t):
        pads = [(0, 0), (0, 0)]
        pads[axis] = (0, SLICE)
        piece = lax.dynamic_slice_in_dim(jnp.pad(value, pads), start + slice_start(t), SLICE, axis)
        wide = jnp.minimum(slice_start(t + 1), FF) - slice_start(t)
        shape = [1, 1]
        shape[axis] = SLICE
        return jnp.where(jnp.arange(SLICE).reshape(shape) < wide, piece, jnp.zeros_like(piece))

    def mlp_part(t):
        return jnp.concatenate(
            [mlp_slice(w_in, 1, 0, t), mlp_slice(w_in, 1, FF, t), mlp_slice(w_out, 0, 0, t).T], axis=1
        )

    mlp = jnp.stack([mlp_part(x * groups + head) for x in range(sub)])
    lines = [list(range(k, count, sub)) for k in range(sub)]
    gains_own = jnp.pad(jnp.stack([gain_attn, gain_mlp]).astype(F32), ((0, 6), (0, -shard % 128)))
    ids = jnp.pad(jnp.stack([position_ids, segment_ids]), ((0, 6), (0, 0)))
    freqs = jnp.power(160000.0, -(2.0 * jnp.arange(HALF, dtype=F32)) / HD)[:, None]
    input_all, gains, w_head, cosine, sine, marks, attn_half = begin(
        tokens, gains_own, ids, w_qkv, w_attn, freqs, count // sub, count, groups, reach
    )
    x = input_all.reshape(total, width)

    attended, wide, lse, qkv, attn_weights, mlp_pair, mlp_near = attend(
        x,
        w_head,
        cosine,
        sine,
        marks,
        attn_half,
        mlp.reshape(2, sub * shard // 2, 3 * SLICE),
        count,
        groups,
        reach,
        rows,
        tile,
    )
    attn_weights = attn_weights.reshape(width, width)
    mlp_all, upstream, middle, attended, mlp_weights = middle_step(
        attended, tokens, d_out, attn_weights, gains, mlp_pair, mlp_near, count, groups, reach
    )
    mlp_weights = mlp_weights.reshape(width, 3 * SLICE)
    split = lambda value, blocks: value.reshape(blocks // 2, 2, rows, width)
    back, forward, mlp_terms = mlp_step(
        mlp_all.reshape(8 * rows, width), upstream.reshape(8 * rows, width), mlp_weights, 512
    )
    mlp_sum = lax.psum_scatter(
        mlp_terms, "ctx", scatter_dimension=0, tiled=True, axis_index_groups=lines
    ).reshape(sub, shard, 3 * SLICE)
    grad_heads, grad_middle, attn_part = turn_step(
        split(back, 8),
        middle,
        d_out,
        attn_weights,
        gains,
        attended.reshape(groups, width, rows),
        groups,
        reach,
    )
    attn_part = attn_part.reshape(count, shard, width // groups)
    forward = split(forward, 8)
    grad_input_parts, weight, ahead, attn_sum = attend_back(
        qkv, grad_heads, wide, lse, x, w_head, cosine, sine, forward, attn_part, groups, reach, tile
    )
    upstream_in, mlp_all, weight_all, attn_all = end_step(
        split(grad_input_parts, group), weight, mlp_sum, attn_sum, groups, reach
    )
    result, grad_input, sum_qkv, sum_attn, sum_in, sum_out, gain_sums = assemble(
        upstream_in,
        tokens,
        grad_middle,
        gains,
        middle,
        ahead,
        weight_all,
        attn_all,
        mlp_all.reshape(8, shard, 3 * SLICE),
        w_qkv,
        w_in,
        jnp.pad(gains_own[:2, :shard], ((0, 6), (0, 0)), constant_values=1.0),
    )
    return (
        result,
        grad_input,
        sum_qkv,
        sum_attn,
        sum_in,
        sum_out,
        gain_sums[0],
        gain_sums[1],
    )


def solution(mesh):
    return jax.shard_map(
        functools.partial(body, mesh.shape["ctx"]),
        mesh=mesh,
        in_specs=(
            P(("ctx", "heads"), None),
            P(("ctx", "heads"), None),
            P(("ctx", "heads")),
            P(("ctx", "heads")),
            P("ctx", None),
            P("ctx", None),
            P("ctx", None),
            P(None, "ctx"),
            P("ctx"),
            P("ctx"),
        ),
        out_specs=(
            P(("ctx", "heads"), None),
            P(("ctx", "heads"), None),
            P("ctx", None),
            P("ctx", None),
            P("ctx", None),
            P(None, "ctx"),
            P("ctx"),
            P("ctx"),
        ),
        check_vma=False,
    )
```

```python
import functools

import jax
import jax.numpy as jnp
from jax import lax
from jax.experimental import pallas as pl
from jax.experimental.pallas import tpu as pltpu
from jax.sharding import PartitionSpec as P

H = 16
HD = 64
HALF = HD // 2
FF = 2624
SEQ_MAX = 2048
MASKED = -1e30
MARKS = 16
QM_END = HD + MARKS
K_END = QM_END + HD
KM_END = K_END + MARKS
V_END = KM_END + HD
SLICE = 384
BF = jnp.bfloat16
F32 = jnp.float32
MESH = pl.DeviceIdType.MESH
VMEM = pl.BlockSpec(memory_space=pltpu.VMEM)
ANY = pl.BlockSpec(memory_space=pl.ANY)
DMA = pltpu.SemaphoreType.DMA


def dot(left, right, left_dim, right_dim):
    return lax.dot_general(
        left, right, (((left_dim,), (right_dim,)), ((), ())), preferred_element_type=F32
    )


def norm_parts(values):
    average = jnp.mean(values, axis=-1, keepdims=True)
    centred = values - average
    inverse_std = lax.rsqrt(jnp.mean(centred * centred, axis=-1, keepdims=True) + 1e-05)
    return centred * inverse_std, inverse_std


def norm_back(upstream, normed, inverse_std, gain):
    scaled = upstream * gain
    return inverse_std * (
        scaled
        - jnp.mean(scaled, axis=-1, keepdims=True)
        - normed * jnp.mean(scaled * normed, axis=-1, keepdims=True)
    )


def flip(value, bit):
    return value + bit - 2 * bit * (value // bit % 2)


class Place:
    def __init__(self, groups, reach):
        self.groups, self.reach = groups, reach
        self.ctx = lax.axis_index("ctx")
        self.head = lax.axis_index("heads")
        self.local = self.ctx % reach
        self.base = self.ctx - self.local
        self.idx = self.local * groups + self.head

    def member(self, j):
        return {"ctx": self.base + j // self.groups, "heads": j % self.groups}


def greet(devices):
    barrier = pltpu.get_barrier_semaphore()
    for device in devices:
        pl.semaphore_signal(barrier, inc=1, device_id=device, device_id_type=MESH)


def meet(devices):
    greet(devices)
    pl.semaphore_wait(pltpu.get_barrier_semaphore(), len(devices))


def remote(source, target, device, send, recv):
    return pltpu.make_async_remote_copy(
        src_ref=source,
        dst_ref=target,
        send_sem=send,
        recv_sem=recv,
        device_id=device,
        device_id_type=MESH,
    )


def push(*operands):
    copy = remote(*operands)
    copy.start()
    return copy


def tree_parts(axes, rows):
    part = -(-rows // axes // 16) * 16
    starts = [min(part * a, rows) for a in range(axes + 1)]
    return [(starts[a], starts[a + 1] - starts[a]) for a in range(axes)]


class Tree:
    def __init__(self, place, axes, source, target, sems):
        self.place, self.axes, self.source, self.target = place, axes, source, target
        self.send, self.recv, self.core_send, self.core_recv, self.own = sems
        self.slots = 2 << axes
        self.levels, self.cores = [], []

    @staticmethod
    def scratch(axes):
        far, near = axes * axes, axes * axes + 1
        return [DMA((far,)), DMA((far,)), DMA((near,)), DMA((near,)), DMA]

    def origin(self, level, first):
        value = self.place.idx
        for k in range(level):
            value = flip(value, 2 << ((first + k) % self.axes))
        return value % self.slots

    def neighbour(self, axis):
        return self.place.member(flip(self.place.idx, 2 << (axis % self.axes)))

    def piece(self, slot, part):
        return self.target.at[slot] if part is None else self.target.at[slot, pl.ds(*part)]

    def to_core(self, source, slot, part):
        at = len(self.cores)
        self.cores.append(
            push(
                source,
                self.piece(slot, part),
                self.place.member(flip(self.place.idx, 1)),
                self.core_send.at[at],
                self.core_recv.at[at],
            )
        )

    def start(self):
        me = self.place.idx % self.slots
        self.levels.append(
            [
                push(
                    self.source, self.target.at[me], self.neighbour(a), self.send.at[a], self.recv.at[a]
                )
                for a in range(self.axes)
            ]
        )
        self.to_core(self.source, me, None)
        self.local = pltpu.make_async_copy(self.source, self.target.at[me], self.own)
        self.local.start()

    def forward(self, level):
        axes = self.axes
        parts = tree_parts(axes, self.target.shape[1])
        onward = []
        for a in range(axes):
            self.levels[level - 1][a].wait_recv()
            slot = self.origin(level, a)
            if level < axes:
                part = parts[a] if level + 1 == axes else None
                at = level * axes + a
                piece = self.piece(slot, part)
                onward.append(
                    push(piece, piece, self.neighbour(a + level), self.send.at[at], self.recv.at[at])
                )
                self.to_core(self.target.at[slot], slot, None)
            else:
                self.to_core(self.piece(slot, parts[a]), slot, parts[a])
        self.levels.append(onward)

    def finish(self):
        self.local.wait()
        for level in self.levels:
            for copy in level:
                copy.wait_send()
        for copy in self.cores:
            copy.wait()


class Halving:
    def __init__(self, place, axes, value, result, scratch, firsts=None):
        self.firsts = firsts = firsts or list(range(axes))
        self.axes, self.value, self.result = axes, value, result
        self.other, self.held, self.land, send, recv, send0, recv0 = scratch
        self.blocks = 1 << axes
        width = value.shape[-1]
        part = width // len(firsts)
        self.columns = [pl.ds(part * a, part) for a in range(len(firsts))]
        self.core = place.idx % 2
        self.chip = place.idx // 2 % self.blocks
        self.sources = []
        for j in range(self.blocks):
            k = self.chip
            for a in range(axes):
                if j >> a & 1:
                    k = flip(k, 1 << a)
            self.sources.append(k)
        self.first, self.copies = [], {}
        for p in range(len(firsts)):
            self.first.append(
                remote(
                    value.at[:, 1 - self.core, :, self.columns[p]],
                    self.other.at[:, :, self.columns[p]],
                    place.member(flip(place.idx, 1)),
                    send0.at[p],
                    recv0.at[p],
                )
            )
            for step in range(axes):
                bit, sent = self.sent(p, step)
                for j in sent:
                    self.copies[p, j] = remote(
                        self.held.at[j, :, self.columns[p]],
                        self.land.at[j, :, self.columns[p]],
                        place.member(flip(place.idx, 2 * bit)),
                        send.at[p, j],
                        recv.at[p, j],
                    )

    @staticmethod
    def scratch(axes, rows, width):
        blocks = 1 << axes
        return [
            pltpu.VMEM((blocks, rows, width), BF),
            pltpu.VMEM((blocks, rows, width), BF),
            pltpu.VMEM((blocks, rows, width), BF),
            DMA((axes, blocks)),
            DMA((axes, blocks)),
            DMA((axes,)),
            DMA((axes,)),
        ]

    def sent(self, part, step):
        first = self.firsts[part]
        seen = [1 << ((first + s) % self.axes) for s in range(step)]
        bit = 1 << ((first + step) % self.axes)
        return bit, [j for j in range(self.blocks) if j & bit and not any(j & s for s in seen)]

    def start(self):
        for copy in self.first:
            copy.start()

    def pair(self):
        for p in range(len(self.firsts)):
            cols = self.columns[p]
            self.first[p].wait_recv()
            _, early = self.sent(p, 0)
            for j in early + [j for j in range(self.blocks) if j not in early]:
                k = self.sources[j]
                self.held[j, :, cols] = (
                    self.value[k, self.core, :, cols].astype(F32) + self.other[k, :, cols].astype(F32)
                ).astype(BF)
                if j in early:
                    self.copies[p, j].start()

    def halve(self, step):
        for p in range(len(self.firsts)):
            cols = self.columns[p]
            bit, arrived = self.sent(p, step)
            onward = self.sent(p, step + 1)[1] if step + 1 < self.axes else []
            for j in sorted(arrived, key=lambda j: (j - bit) not in onward):
                self.copies[p, j].wait_recv()
                k = j - bit
                total = self.held[k, :, cols].astype(F32) + self.land[j, :, cols].astype(F32)
                if step + 1 < self.axes:
                    self.held[k, :, cols] = total.astype(BF)
                    if k in onward:
                        self.copies[p, k].start()
                else:
                    self.result[:, cols] = total

    def run(self):
        self.start()
        self.pair()
        for step in range(self.axes):
            self.halve(step)
        self.finish()

    def finish(self):
        for copy in self.first:
            copy.wait_send()
        for copy in self.copies.values():
            copy.wait_send()


class Lines:
    def __init__(self, count, source, target, send, recv, own):
        me = lax.axis_index("ctx")
        self.copies = [pltpu.make_async_copy(source.at[me], target.at[me], own)]
        for step in range(1, count):
            peer = (me + step) % count
            self.copies.append(
                remote(source.at[peer], target.at[me], {"ctx": peer}, send.at[step - 1], recv.at[step - 1])
            )

    @staticmethod
    def scratch(count):
        return [DMA((count - 1,)), DMA((count - 1,)), DMA]

    def start(self):
        for copy in self.copies:
            copy.start()

    def finish(self):
        for copy in self.copies:
            copy.wait()


def everyone(place, count):
    group = place.reach * place.groups
    mates = [place.member((place.idx + step) % group) for step in range(1, group)]
    outside = [{"ctx": (place.base + place.reach + step) % count} for step in range(count - place.reach)]
    return mates + outside


def spread(place, source, target, sems, me=None):
    send, recv, own = sems
    count = target.shape[0]
    copies = []
    for step in range(1, count):
        peer = (place.idx + step) % count
        copies.append(
            push(
                source.at[peer],
                target.at[place.idx],
                place.member(peer),
                send.at[step - 1],
                recv.at[step - 1],
            )
        )
    local = pltpu.make_async_copy(source.at[place.idx], target.at[place.idx], own)
    local.start()
    copies.append(local)
    return copies


def begin_kernel(
    groups,
    reach,
    count,
    tokens,
    gains,
    ids,
    w_qkv,
    w_attn,
    freqs,
    input_all,
    gains_all,
    w_head,
    cosine,
    sine,
    marks,
    attn_half,
    ids_all,
    slab,
    mine,
    gain_land,
    own_sems,
    ids_send,
    ids_recv,
    gain_send,
    gain_recv,
    slab_send,
    slab_recv,
    wide_send,
    wide_recv,
    core_send,
    core_recv,
    *tree_sems,
):
    place = Place(groups, reach)
    group = reach * groups
    ctx, head, idx = place.ctx, place.head, place.idx
    shard = w_qkv.shape[0]
    ring = attn_half.shape[0]
    sub = count // ring
    side, spot = ctx % sub, ctx // sub
    lanes = attn_half.shape[2] // groups
    core = {"heads": flip(head, 1)}
    mates = [place.member((idx + step) % group) for step in range(1, group)]
    lines = [{"ctx": (ctx + step) % count} for step in range(1, count)]
    meet(everyone(place, count))
    first = [
        push(gains, gain_land.at[ctx], lines[step - 1], gain_send.at[step - 1], gain_recv.at[step - 1])
        for step in range(1, count)
    ]
    small = [
        push(ids, ids_all.at[idx], mates[step - 1], ids_send.at[step - 1], ids_recv.at[step - 1])
        for step in range(1, group)
    ]
    half = pl.ds(pl.multiple_of(head % 2 * (shard // 2), 16), shard // 2)
    thirds = []
    for step in range(1, count):
        peer = (ctx + step) % count
        column = ((peer % reach) * groups + head) // 2 * 128
        for third in range(3):
            start = pl.multiple_of(third * 1024 + column, 128)
            thirds.append(
                push(
                    w_qkv.at[half, pl.ds(start, 128)],
                    slab.at[ctx, half, pl.ds(third * 128, 128)],
                    lines[step - 1],
                    slab_send.at[step - 1, third],
                    slab_recv.at[step - 1, third],
                )
            )
    gain_land[ctx] = gains[...]
    where = lambda h: pl.ds(pl.multiple_of(h * lanes, 128), lanes)
    across = where(head)
    own = [
        pltpu.make_async_copy(ids, ids_all.at[idx], own_sems.at[3]),
        pltpu.make_async_copy(w_attn.at[:, across], attn_half.at[spot, :, across], own_sems.at[4]),
    ]
    for third in range(3):
        start = pl.multiple_of(third * 1024 + idx // 2 * 128, 128)
        own.append(
            pltpu.make_async_copy(
                w_qkv.at[half, pl.ds(start, 128)],
                slab.at[ctx, half, pl.ds(third * 128, 128)],
                own_sems.at[third],
            )
        )
    for copy in own:
        copy.start()
    for copy in first:
        copy.wait_recv()
    gain, gain_two = (
        jnp.concatenate([gain_land[c, k : k + 1, :shard] for c in range(count)], axis=1)
        for k in range(2)
    )
    normed, _ = norm_parts(tokens[...].astype(F32))
    mine[...] = (normed * gain).astype(BF)
    tree = Tree(place, 3, mine, input_all, tree_sems[:5])
    tree.start()
    gains_all[0:1, :] = gain
    gains_all[1:2, :] = gain_two
    late = []
    for step in range(1, ring):
        late.append(
            push(
                w_attn.at[:, across],
                attn_half.at[spot, :, across],
                {"ctx": (spot + step) % ring * sub + side},
                wide_send.at[step - 1],
                wide_recv.at[step - 1],
            )
        )
    tree.forward(1)
    for copy in own:
        copy.wait()
    for copy in thirds:
        copy.wait_recv()
    for copy in late:
        copy.wait_recv()
    collect = Collect(
        groups, [(attn_half.at[:, :, across], lambda h: attn_half.at[:, :, where(h)])], *tree_sems[5:]
    )
    collect.start(0)
    shared = push(slab.at[:, half], slab.at[:, half], core, core_send, core_recv)
    for copy in small:
        copy.wait()
    row = lambda k: jnp.concatenate([ids_all[j, k : k + 1, :] for j in range(group)], axis=1)
    angles = freqs[...] * row(0).astype(F32)
    cosine[...] = jnp.cos(angles)
    sine[...] = jnp.sin(angles)
    parity = (row(1) % 2).astype(F32)
    blank = jnp.zeros((MARKS - 2, parity.shape[1]), F32)
    marks[...] = jnp.concatenate(
        [parity, 1.0 - parity, blank, (1.0 - parity) * MASKED, parity * MASKED, blank], axis=0
    ).astype(BF)
    tree.forward(2)
    shared.wait()
    odd = head % 2 == 1
    for c in range(count):
        rows = slice(c * shard, (c + 1) * shard)
        block = slab[c].astype(F32)
        parts = []
        for third in range(3):
            at = third * 128
            parts.append(jnp.where(odd, block[:, at + HD : at + 128], block[:, at : at + HD]))
        w_head[rows] = jnp.concatenate(parts, axis=1).astype(BF)
    collect.forward(0)
    tree.forward(3)
    tree.finish()
    collect.finish()
    for copy in first + thirds + late:
        copy.wait_send()


def begin(tokens, gains, ids, w_qkv, w_attn, freqs, ring, count, groups, reach):
    rows, width = tokens.shape
    shard = w_qkv.shape[0]
    group = groups * reach
    sems = lambda *shape: [DMA(shape), DMA(shape)]
    return pl.pallas_call(
        functools.partial(begin_kernel, groups, reach, count),
        in_specs=[VMEM, VMEM, ANY, ANY, ANY, VMEM],
        out_specs=[ANY, VMEM, VMEM, VMEM, VMEM, VMEM, ANY],
        out_shape=[
            jax.ShapeDtypeStruct((group, rows, width), BF),
            jax.ShapeDtypeStruct((8, width), F32),
            jax.ShapeDtypeStruct((width, 3 * HD), BF),
            jax.ShapeDtypeStruct((HALF, group * rows), F32),
            jax.ShapeDtypeStruct((HALF, group * rows), F32),
            jax.ShapeDtypeStruct((2 * MARKS, group * rows), BF),
            jax.ShapeDtypeStruct((ring, shard, width), BF),
        ],
        scratch_shapes=[
            pltpu.VMEM((group, 8, rows), jnp.int32),
            pltpu.VMEM((count, shard, 3 * 128), BF),
            pltpu.VMEM((rows, width), BF),
            pltpu.VMEM((count, 8, gains.shape[1]), F32),
            DMA((5,)),
            *sems(group - 1),
            *sems(count - 1),
            *sems(count - 1, 3),
            *sems(ring - 1),
            DMA,
            DMA,
            *Tree.scratch(3),
            *Collect.scratch(1, groups),
        ],
        compiler_params=pltpu.CompilerParams(
            collective_id=0, has_side_effects=True, vmem_limit_bytes=12 << 20
        ),
        cost_estimate=pl.CostEstimate(flops=0, bytes_accessed=30 << 20, transcendentals=0),
        name="begin",
    )(tokens, gains, ids, w_qkv, w_attn, freqs)


class Line:
    def __init__(self, length, sub, first, sources, targets, send, recv):
        ctx = lax.axis_index("ctx")
        spot, side = ctx // sub, ctx % sub
        self.length, self.spot, self.first = length, spot, first
        self.waited = 0
        beside = [{"ctx": (spot + 1) % length * sub + side}, {"ctx": (spot + length - 1) % length * sub + side}]
        self.copies = [
            [
                remote(sources[d][q], targets[d][q], beside[d], send.at[d, q], recv.at[d, q])
                for q in range(len(sources[d]))
            ]
            for d in range(2)
        ]

    def sends(self, d, q):
        s, spot, last = (q + self.first) // 2, self.spot, self.length - 1
        if d:
            return jnp.logical_and(spot + s <= last, spot > 0)
        return jnp.logical_and(spot >= s, spot < last)

    def receives(self, d, q):
        s = (q + self.first) // 2
        return self.spot + s + 1 < self.length if d else self.spot > s

    def arrive(self, q):
        for d in range(2):
            pl.when(self.receives(d, q))(self.copies[d][q].wait_recv)
        self.waited = q + 1

    def start(self, q):
        if q >= 2:
            self.arrive(q - 2)
        for d in range(2):
            pl.when(self.sends(d, q))(self.copies[d][q].start)

    def finish(self):
        for q in range(self.waited, len(self.copies[0])):
            self.arrive(q)
        for d in range(2):
            for q, copy in enumerate(self.copies[d]):
                pl.when(self.sends(d, q))(copy.wait_send)


def ring_half(sub, side, k):
    return (side + k) % 2 if sub == 2 else k


class Columns:
    def __init__(self, place, part, whole, own, side_send, side_recv, near_send, near_recv):
        _, sub, _, width = whole.shape
        side = place.ctx % sub
        half = pl.ds(pl.multiple_of(place.head % 2 * (width // 2), 128), width // 2)
        self.own = pltpu.make_async_copy(part, whole.at[:, side], own)
        self.sides, self.near = [], []
        for step in range(1, sub):
            peer, source = (side + step) % sub, (side - step + sub) % sub
            self.sides.append(
                remote(
                    part.at[:, :, half],
                    whole.at[:, side, :, half],
                    {"ctx": place.ctx - side + peer},
                    side_send.at[step - 1],
                    side_recv.at[step - 1],
                )
            )
            here = whole.at[:, source, :, half]
            self.near.append(
                remote(
                    here, here, {"heads": flip(place.head, 1)}, near_send.at[step - 1], near_recv.at[step - 1]
                )
            )

    @staticmethod
    def scratch(sub):
        count = (max(sub - 1, 1),)
        return [DMA, DMA(count), DMA(count), DMA(count), DMA(count)]

    def start(self):
        self.own.start()
        for copy in self.sides:
            copy.start()

    def across(self):
        for side, near in zip(self.sides, self.near):
            side.wait_recv()
            near.start()

    def finish(self):
        self.own.wait()
        for side, near in zip(self.sides, self.near):
            side.wait_send()
            near.wait()


def attend_kernel(
    groups,
    reach,
    lines,
    tile,
    x_ref,
    w_ref,
    cos_ref,
    sin_ref,
    mark_ref,
    attn_half,
    mlp,
    out_ref,
    wide_ref,
    lse_ref,
    qkv_ref,
    attn_all,
    mlp_pair,
    mlp_near,
    ring_send,
    ring_recv,
    swap_send,
    swap_recv,
    swap_own,
    *sems,
):
    count = x_ref.shape[0]
    step = pl.program_id(0)
    steps = count // tile
    place = Place(groups, reach)
    ring_size, sub = attn_all.shape[:2]
    side = place.ctx % sub
    early = mlp_near.shape[1]
    if sub == 2:
        kept = pltpu.make_async_copy(mlp.at[side], mlp_pair.at[side], swap_own)
        swap = [
            remote(
                mlp.at[1 - side],
                mlp_pair.at[side],
                {"ctx": place.ctx + 1 - 2 * side},
                swap_send,
                swap_recv,
            )
        ]
        sources = [mlp.at[side], mlp_pair.at[1 - side]]
    else:
        kept = pltpu.make_async_copy(mlp, mlp_pair, swap_own)
        swap = []
        sources = [mlp.at[0], mlp.at[1]]
    ring = Line(
        ring_size,
        sub,
        0,
        [sources + [mlp_near.at[d, q] for q in range(early - 2)] for d in range(2)],
        [[mlp_near.at[d, q] for q in range(early)] for d in range(2)],
        ring_send,
        ring_recv,
    )
    columns = Columns(place, attn_half, attn_all, *sems)

    @pl.when(step == 0)
    def _():
        meet(everyone(place, lines))
        for copy in swap:
            copy.start()
        ring.start(0)
        kept.start()
        columns.start()
        qkv_ref[HD:QM_END, :] = mark_ref[:MARKS, :]
        qkv_ref[K_END:KM_END, :] = mark_ref[MARKS:, :]

        @pl.loop(0, steps)
        def _(i):
            at = pl.ds(pl.multiple_of(i * tile, tile), tile)
            cosine, sine = cos_ref[:, at], sin_ref[:, at]
            part = dot(w_ref[...], x_ref[at, :], 0, 1)

            def turn(value):
                front, back = value[:HALF], value[HALF:]
                return jnp.concatenate(
                    [front * cosine - back * sine, back * cosine + front * sine], axis=0
                )

            qkv_ref[:HD, at] = (turn(part[:HD]) * 0.125).astype(BF)
            qkv_ref[QM_END:K_END, at] = turn(part[HD : 2 * HD]).astype(BF)
            qkv_ref[KM_END:, at] = part[2 * HD :].astype(BF)

    here = pl.ds(pl.multiple_of(step * tile, tile), tile)
    query = qkv_ref[:QM_END, here]
    keys = [slice(j * tile, (j + 1) * tile) for j in range(steps)]
    scores = [dot(qkv_ref[QM_END:KM_END, at], query, 0, 0) for at in keys]
    top = functools.reduce(jnp.maximum, [jnp.max(s, axis=0, keepdims=True) for s in scores])
    raised = [jnp.exp(s - top) for s in scores]
    total = functools.reduce(jnp.add, [jnp.sum(e, axis=0, keepdims=True) for e in raised])
    scale = 1.0 / total
    result = jnp.zeros((HD, tile), F32)
    for j in range(steps):
        result += dot(qkv_ref[KM_END:, keys[j]], (raised[j] * scale).astype(BF), 1, 0)
    rows = out_ref.shape[2]
    for k in range(tile // rows):
        out_ref[step * (tile // rows) + k] = result[:, k * rows : (k + 1) * rows].astype(BF)
    wide_ref[:, here] = result
    lse_ref[:, here] = top + jnp.log(total)

    @pl.when(step == min(1, steps - 1))
    def _():
        for copy in swap:
            copy.wait_recv()
        for q in range(1, min(early, 3)):
            ring.start(q)

    @pl.when(step == steps - 1)
    def _():
        columns.across()
        for q in range(3, early):
            ring.start(q)
        ring.finish()
        for copy in swap:
            copy.wait_send()
        kept.wait()
        columns.finish()


def attend(x, w, cosine, sine, marks, attn_half, mlp, lines, groups, reach, rows, tile):
    count, width = x.shape
    ring, shard, _ = attn_half.shape
    sub = lines // ring
    early = ring - 1
    whole = lambda *shape: pl.BlockSpec(shape, lambda i: (0,) * len(shape))
    return pl.pallas_call(
        functools.partial(attend_kernel, groups, reach, lines, tile),
        grid=(count // tile,),
        in_specs=[
            whole(count, width),
            whole(*w.shape),
            whole(HALF, count),
            whole(HALF, count),
            whole(2 * MARKS, count),
            ANY,
            ANY,
        ],
        out_specs=[
            whole(count // rows, HD, rows),
            whole(HD, count),
            whole(1, count),
            whole(V_END, count),
            ANY,
            ANY,
            ANY,
        ],
        out_shape=[
            jax.ShapeDtypeStruct((count // rows, HD, rows), BF),
            jax.ShapeDtypeStruct((HD, count), F32),
            jax.ShapeDtypeStruct((1, count), F32),
            jax.ShapeDtypeStruct((V_END, count), BF),
            jax.ShapeDtypeStruct((ring, sub, shard, width), BF),
            jax.ShapeDtypeStruct(mlp.shape, BF),
            jax.ShapeDtypeStruct((2, early, *mlp.shape[1:]), BF),
        ],
        scratch_shapes=[DMA((2, early)), DMA((2, early)), DMA, DMA, DMA, *Columns.scratch(sub)],
        compiler_params=pltpu.CompilerParams(
            collective_id=5, has_side_effects=True, vmem_limit_bytes=32 << 20
        ),
        cost_estimate=pl.CostEstimate(
            flops=count * count * HD * 8, bytes_accessed=count * 4096, transcendentals=count * count
        ),
        name="attend",
    )(x, w, cosine, sine, marks, attn_half, mlp)


def middle_kernel(
    groups,
    reach,
    lines,
    outgoing,
    tokens,
    d_out,
    w_attn,
    gains,
    mlp_pair,
    mlp_near,
    mlp_all,
    upstream_all,
    middle,
    attended,
    mlp_weights,
    land,
    mine,
    a2a_send,
    a2a_recv,
    own,
    ring_send,
    ring_recv,
    ring_own,
    land_own,
    *tree_sems,
):
    place = Place(groups, reach)
    group = groups * reach
    early, count = mlp_near.shape[1], mlp_weights.shape[0]
    sub = lines // count
    spot, side = place.ctx // sub, place.ctx % sub

    def slot(d, q, ahead):
        block = (spot + (q // 2 + ahead if d else count - q // 2 - ahead)) % count
        return mlp_weights.at[block, ring_half(sub, side, q % 2)]

    rest = range(early, 2 * (count - 1))
    ring = Line(
        count,
        sub,
        early,
        [[mlp_near.at[d, q - 2] if q - 2 < early else slot(d, q, 0) for q in rest] for d in range(2)],
        [[slot(d, q, 0) for q in rest] for d in range(2)],
        ring_send,
        ring_recv,
    )
    local = [pltpu.make_async_copy(mlp_pair, mlp_weights.at[spot], ring_own.at[0])]
    near = []
    for d in range(2):
        for q in range(early):
            copy = pltpu.make_async_copy(
                mlp_near.at[d, q], slot(d, q, 1), ring_own.at[1 + d * early + q]
            )
            there = spot + q // 2 + 1 < count if d else spot > q // 2
            near.append((there, copy))
    meet(everyone(place, lines))
    copies = spread(place, outgoing, land, (a2a_send, a2a_recv, own))
    ring.start(0)
    ring.start(1)
    up = Tree(place, 2, d_out, upstream_all, tree_sems[5:10])
    up.start()
    for copy in local:
        copy.start()
    for there, copy in near:
        pl.when(there)(copy.start)
    for copy in copies:
        copy.wait()
    collect = Collect(groups, [(land, lambda h: attended.at[h])], *tree_sems[10:])
    collect.start(0)
    local.append(pltpu.make_async_copy(land, attended.at[place.head], land_own))
    local[-1].start()
    value = tokens[...].astype(F32) + dot(
        land[...].reshape(group * HD, tokens.shape[0]), w_attn[...], 0, 0
    )
    middle[...] = value
    normed, _ = norm_parts(value)
    mine[...] = (normed * gains[1:2, :]).astype(BF)
    tree = Tree(place, 2, mine, mlp_all, tree_sems[:5])
    tree.start()
    up.forward(1)
    for q in range(2, len(rest)):
        ring.start(q)
    tree.forward(1)
    up.forward(2)
    tree.forward(2)
    collect.forward(0)
    up.finish()
    tree.finish()
    collect.finish()
    for copy in local:
        copy.wait()
    for there, copy in near:
        pl.when(there)(copy.wait)
    ring.finish()


def middle_step(outgoing, tokens, d_out, w_attn, gains, mlp_pair, mlp_near, lines, groups, reach):
    rows, width = tokens.shape
    group = groups * reach
    early, sub = mlp_near.shape[1], 8 // groups
    ring = lines // sub
    left = 2 * (ring - 1) - early
    return pl.pallas_call(
        functools.partial(middle_kernel, groups, reach, lines),
        in_specs=[ANY, VMEM, ANY, VMEM, VMEM, ANY, ANY],
        out_specs=[ANY, ANY, VMEM, ANY, ANY],
        out_shape=[
            jax.ShapeDtypeStruct((8, rows, width), BF),
            jax.ShapeDtypeStruct((8, rows, width), BF),
            jax.ShapeDtypeStruct((rows, width), F32),
            jax.ShapeDtypeStruct((groups, group, HD, rows), BF),
            jax.ShapeDtypeStruct((ring, *mlp_pair.shape), BF),
        ],
        scratch_shapes=[
            pltpu.VMEM((group, HD, rows), BF),
            pltpu.VMEM((rows, width), BF),
            DMA((group - 1,)),
            DMA((group - 1,)),
            DMA,
            DMA((2, left)),
            DMA((2, left)),
            DMA((2 * early + 1,)),
            DMA,
            *Tree.scratch(2),
            *Tree.scratch(2),
            *Collect.scratch(1, groups),
        ],
        compiler_params=pltpu.CompilerParams(
            collective_id=1, has_side_effects=True, vmem_limit_bytes=12 << 20
        ),
        cost_estimate=pl.CostEstimate(flops=1 << 28, bytes_accessed=12 << 20, transcendentals=0),
        name="middle_step",
    )(outgoing, tokens, d_out, w_attn, gains, mlp_pair, mlp_near)


class Sum:
    def __init__(self, place, terms, first, held, stage, land, send, recv):
        self.terms, self.first, self.stage, self.land = terms, first, stage, land
        length = terms.shape[0]
        lines_sub = 8 // place.groups
        spot, side = place.ctx // lines_sub, place.ctx % lines_sub
        self.length, self.spot = length, spot
        self.held = lambda d, q: land.at[d, q] if q >= 0 else held.at[d, q + 2]
        beside = [
            {"ctx": (spot + 1) % length * lines_sub + side},
            {"ctx": (spot + length - 1) % length * lines_sub + side},
        ]
        self.copies = [
            [
                remote(stage.at[d, q], land.at[d, q], beside[d], send.at[d, q], recv.at[d, q])
                for q in range(stage.shape[1])
            ]
            for d in range(2)
        ]

    @staticmethod
    def scratch(count, half):
        return [
            pltpu.VMEM((2, count, *half), BF),
            pltpu.VMEM((2, count, *half), BF),
            DMA((2, count)),
            DMA((2, count)),
        ]

    def sends(self, d, q):
        s, spot, last = (q + self.first) // 2, self.spot, self.length - 1
        if d:
            return jnp.logical_and(spot >= last - s, spot > 0)
        return jnp.logical_and(spot <= s, spot < last)

    def receives(self, d, q):
        s, spot, last = (q + self.first) // 2, self.spot, self.length - 1
        if d:
            return jnp.logical_and(spot >= last - 1 - s, spot < last)
        return jnp.logical_and(spot <= s + 1, spot > 0)

    def clear(self):
        for d in range(2):
            for q in range(len(self.copies[d])):

                @pl.when(jnp.logical_not(self.receives(d, q)))
                def _():
                    self.land[d, q] = jnp.zeros(self.land.shape[2:], BF)

    def arrive(self, q):
        for d in range(2):
            pl.when(self.receives(d, q))(self.copies[d][q].wait_recv)

    def start(self, q):
        if q >= 2:
            self.arrive(q - 2)
        step, k = (q + self.first) // 2, (q + self.first) % 2
        for d in range(2):
            at = self.spot + (step + 1 if d else self.length - 1 - step)

            @pl.when(self.sends(d, q))
            def _():
                value = self.terms[at % self.length, k]
                if q + self.first >= 2:
                    value = (value.astype(F32) + self.held(d, q - 2)[...].astype(F32)).astype(BF)
                self.stage[d, q] = value
                self.copies[d][q].start()

    def finish(self):
        count = len(self.copies[0])
        for q in range(max(count - 2, 0), count):
            self.arrive(q)
        for d in range(2):
            for q, copy in enumerate(self.copies[d]):
                pl.when(self.sends(d, q))(copy.wait_send)


def mlp_kernel(chunk, x_ref, up_ref, w_ref, back_ref, forward_ref, terms_ref, kept):
    count, width = x_ref.shape

    @pl.loop(0, count // chunk)
    def _(i):
        at = pl.ds(pl.multiple_of(i * chunk, chunk), chunk)
        gate_up = dot(x_ref[at, :], w_ref[:, : 2 * SLICE], 1, 0)
        left, right = gate_up[:, :SLICE], gate_up[:, SLICE:]
        grad_mixed = dot(up_ref[at, :], w_ref[:, 2 * SLICE :], 1, 0)
        normal_cdf = 0.5 * (1.0 + lax.erf(left * 0.7071067811865476))
        gelu = left * normal_cdf
        density = jnp.exp(-0.5 * left * left) * 0.3989422804014327
        kept[at, :SLICE] = (grad_mixed * right * (normal_cdf + left * density)).astype(BF)
        kept[at, SLICE : 2 * SLICE] = (grad_mixed * gelu).astype(BF)
        kept[at, 2 * SLICE :] = (gelu * right).astype(BF)
        back_ref[at, :] = dot(kept[at, : 2 * SLICE], w_ref[:, : 2 * SLICE], 1, 1).astype(BF)
        forward_ref[at, :] = dot(kept[at, 2 * SLICE :], w_ref[:, 2 * SLICE :], 1, 1).astype(BF)

    @pl.loop(0, width // chunk)
    def _(i):
        at = pl.ds(pl.multiple_of(i * chunk, chunk), chunk)
        terms_ref[at, : 2 * SLICE] = dot(x_ref[:, at], kept[:, : 2 * SLICE], 0, 0).astype(BF)
        terms_ref[at, 2 * SLICE :] = dot(up_ref[:, at], kept[:, 2 * SLICE :], 0, 0).astype(BF)


def mlp_step(x, up, w, chunk):
    count, width = x.shape
    return pl.pallas_call(
        functools.partial(mlp_kernel, chunk),
        in_specs=[VMEM] * 3,
        out_specs=[VMEM] * 3,
        out_shape=[
            jax.ShapeDtypeStruct((count, width), BF),
            jax.ShapeDtypeStruct((count, width), BF),
            jax.ShapeDtypeStruct((width, 3 * SLICE), BF),
        ],
        scratch_shapes=[pltpu.VMEM((count, 3 * SLICE), BF)],
        compiler_params=pltpu.CompilerParams(vmem_limit_bytes=28 << 20),
        cost_estimate=pl.CostEstimate(
            flops=18 * count * width * SLICE, bytes_accessed=14 << 20, transcendentals=2 * count * SLICE
        ),
        name="mlp_step",
    )(x, up, w)


def turn_kernel(
    groups,
    reach,
    partial,
    middle,
    d_out,
    w_attn,
    gains,
    attended,
    terms,
    grads,
    grad_middle,
    attn_part,
    carry,
    columns,
    total,
    outgoing,
    branch,
    a2a_send,
    a2a_recv,
    own,
    side_send,
    side_recv,
    side_own,
    *rest,
):
    place = Place(groups, reach)
    group = groups * reach
    lanes = branch.shape[2]
    lines = terms.shape[0] * (8 // groups)
    sums = Sum(place, terms, 0, None, *rest[7:])
    count = rest[7].shape[1]
    devices = everyone(place, lines)
    sums.clear()
    meet(devices)
    halving = Halving(place, 2, partial, total, rest[:7])
    halving.start()
    sums.start(0)
    sums.start(1)
    halving.pair()
    halving.halve(0)
    halving.halve(1)
    for q in range(2, count):
        sums.start(q)
    halving.finish()
    normed, inverse_std = norm_parts(middle[...])
    upstream = total[...]
    grad = d_out[...].astype(F32) + norm_back(upstream, normed, inverse_std, gains[1:2, :])
    grad_middle[...] = grad
    low = grad.astype(BF)
    for g in range(groups):
        branch[g] = low[:, g * lanes : (g + 1) * lanes]
    outgoing[...] = dot(w_attn[...], low, 1, 1).astype(BF).reshape(outgoing.shape)
    copies = spread(place, outgoing, grads, (a2a_send, a2a_recv, own))
    for step in range(1, groups):
        peer = (place.head + step) % groups
        copies.append(
            push(
                branch.at[peer],
                columns.at[place.head],
                {"heads": peer},
                side_send.at[step - 1],
                side_recv.at[step - 1],
            )
        )
    local = pltpu.make_async_copy(branch.at[place.head], columns.at[place.head], side_own)
    local.start()
    for copy in copies[-(groups - 1) :]:
        copy.wait()
    local.wait()
    attn_part[...] = functools.reduce(
        jnp.add, [dot(attended[g], columns[g], 1, 0) for g in range(groups)]
    ).astype(BF)
    for copy in copies[: -(groups - 1)]:
        copy.wait()
    sums.finish()
    for d in range(2):
        for q in range(2):
            carry[d, q] = sums.land[d, count - 2 + q]


def turn_step(partial, middle, d_out, w_attn, gains, attended, terms, groups, reach):
    rows, width = middle.shape
    count = terms.shape[0] - 1
    group = groups * reach
    return pl.pallas_call(
        functools.partial(turn_kernel, groups, reach),
        in_specs=[VMEM] * 7,
        out_specs=[ANY, VMEM, VMEM, VMEM],
        out_shape=[
            jax.ShapeDtypeStruct((group, HD, rows), BF),
            jax.ShapeDtypeStruct((rows, width), F32),
            jax.ShapeDtypeStruct((width, width // groups), BF),
            jax.ShapeDtypeStruct((2, 2, *terms.shape[2:]), BF),
        ],
        scratch_shapes=[
            pltpu.VMEM((groups, rows, width // groups), BF),
            pltpu.VMEM((rows, width), F32),
            pltpu.VMEM((group, HD, rows), BF),
            pltpu.VMEM((groups, rows, width // groups), BF),
            DMA((group - 1,)),
            DMA((group - 1,)),
            DMA,
            DMA((groups - 1,)),
            DMA((groups - 1,)),
            DMA,
            *Halving.scratch(2, rows, width),
            *Sum.scratch(count, terms.shape[2:]),
        ],
        compiler_params=pltpu.CompilerParams(
            collective_id=2, has_side_effects=True, vmem_limit_bytes=16 << 20
        ),
        cost_estimate=pl.CostEstimate(flops=1 << 28, bytes_accessed=12 << 20, transcendentals=0),
        name="turn_step",
    )(partial, middle, d_out, w_attn, gains, attended, terms)


def attend_back_kernel(
    groups,
    reach,
    lines,
    tile,
    qkv_ref,
    grad_ref,
    wide_ref,
    lse_ref,
    x_ref,
    w_ref,
    cos_ref,
    sin_ref,
    forward_ref,
    terms,
    carry,
    attn_ref,
    out_ref,
    weight_ref,
    ahead_ref,
    attn_out_ref,
    mlp_ref,
    sums,
    queries,
    weight,
    attn_land,
    *sems,
):
    count = x_ref.shape[0]
    rows = grad_ref.shape[2]
    steps, per_tile = count // tile, tile // rows
    step = pl.program_id(0)
    place = Place(groups, reach)
    halving = Halving(place, 2, forward_ref, ahead_ref, sems[:7])
    swap = Lines(lines, attn_ref, attn_land, *sems[7:10])
    length = terms.shape[0]
    line = Sum(place, terms, length - 1, carry, *sems[10:])

    @pl.when(step == 0)
    def _():
        line.clear()
        greet(everyone(place, lines))
        sums[...] = jnp.zeros_like(sums)

    here = pl.ds(pl.multiple_of(step * tile, tile), tile)
    query = qkv_ref[:QM_END, here]
    grad = jnp.concatenate([grad_ref[step * per_tile + k] for k in range(per_tile)], axis=1)
    delta = jnp.sum(grad.astype(F32) * wide_ref[:, here], axis=0, keepdims=True)
    lse = lse_ref[:, here]
    grad_query = jnp.zeros((HD, tile), F32)
    for j in range(steps):
        keys = slice(j * tile, (j + 1) * tile)
        prob = jnp.exp(dot(qkv_ref[QM_END:KM_END, keys], query, 0, 0) - lse)
        grad_prob = dot(qkv_ref[KM_END:, keys], grad, 0, 0)
        grad_score = (prob * (grad_prob - delta)).astype(BF)
        grad_query += dot(qkv_ref[QM_END:K_END, keys], grad_score, 1, 0)
        sums[:HD, keys] += dot(query[:HD], grad_score, 1, 1)
        sums[HD:, keys] += dot(grad, prob.astype(BF), 1, 1)
    queries[:, here] = (grad_query * 0.125).astype(BF)

    @pl.when(step == 0)
    def _():
        pl.semaphore_wait(pltpu.get_barrier_semaphore(), len(everyone(place, lines)))
        halving.start()
        swap.start()
        line.start(0)
        line.start(1)

    pl.when(step == min(1, steps - 1))(halving.pair)

    @pl.when(step == min(2, steps - 1))
    def _():
        halving.halve(0)
        for q in range(2, length - 1):
            line.start(q)


    @pl.when(step == steps - 1)
    def _():
        weight[...] = jnp.zeros_like(weight)

        @pl.loop(0, steps)
        def _(i):
            at = pl.ds(pl.multiple_of(i * tile, tile), tile)
            cosine, sine = cos_ref[:, at], sin_ref[:, at]

            def turn_back(value):
                front, back = value[:HALF], value[HALF:]
                return [front * cosine + back * sine, back * cosine - front * sine]

            low = lambda value: value.astype(BF).astype(F32)
            projected = jnp.concatenate(
                [
                    *turn_back(queries[:, at].astype(F32)),
                    *turn_back(low(sums[:HD, at])),
                    low(sums[HD:, at]),
                ],
                axis=0,
            ).astype(BF)
            part = dot(projected, w_ref[...], 0, 1).astype(BF)
            for k in range(per_tile):
                out_ref[i * per_tile + k] = part[k * rows : (k + 1) * rows]
            weight[...] += dot(projected, x_ref[at, :], 1, 0)

        shard = weight_ref.shape[2]
        for c in range(lines):
            weight_ref[c] = weight[:, c * shard : (c + 1) * shard].astype(BF)
        halving.halve(1)
        line.finish()
        for k in range(2):
            q = length - 3 + k
            mlp_ref[k] = (
                terms[line.spot, k].astype(F32)
                + line.land[0, q].astype(F32)
                + line.land[1, q].astype(F32)
            ).astype(BF)
        swap.finish()
        attn_out_ref[...] = functools.reduce(
            jnp.add, [attn_land[c].astype(F32) for c in range(lines)]
        ).astype(BF)
        halving.finish()


def attend_back(qkv, grad, wide, lse, x, w, cosine, sine, forward, terms, carry, attn, groups, reach, tile):
    count, width = x.shape
    blocks, _, rows = grad.shape
    lines, shard, lanes = attn.shape
    whole = lambda *shape: pl.BlockSpec(shape, lambda i: (0,) * len(shape))
    operands = (qkv, grad, wide, lse, x, w, cosine, sine, forward, terms, carry)
    return pl.pallas_call(
        functools.partial(attend_back_kernel, groups, reach, lines, tile),
        grid=(count // tile,),
        in_specs=[*[whole(*operand.shape) for operand in operands], ANY],
        out_specs=[
            whole(blocks, rows, width),
            whole(lines, 3 * HD, shard),
            whole(rows, width),
            whole(shard, lanes),
            whole(*terms.shape[1:]),
        ],
        out_shape=[
            jax.ShapeDtypeStruct((blocks, rows, width), BF),
            jax.ShapeDtypeStruct((lines, 3 * HD, shard), BF),
            jax.ShapeDtypeStruct((rows, width), F32),
            jax.ShapeDtypeStruct((shard, lanes), BF),
            jax.ShapeDtypeStruct(terms.shape[1:], BF),
        ],
        scratch_shapes=[
            pltpu.VMEM((2 * HD, count), F32),
            pltpu.VMEM((HD, count), BF),
            pltpu.VMEM((3 * HD, width), F32),
            pltpu.VMEM((lines, shard, lanes), BF),
            *Halving.scratch(2, rows, width),
            *Lines.scratch(lines),
            *Sum.scratch(terms.shape[0] - 1, terms.shape[2:]),
        ],
        compiler_params=pltpu.CompilerParams(
            collective_id=4, has_side_effects=True, vmem_limit_bytes=44 << 20
        ),
        cost_estimate=pl.CostEstimate(
            flops=count * count * HD * 20, bytes_accessed=count * 6144, transcendentals=count * count
        ),
        name="attend_back",
    )(*operands, attn)


class Collect:
    def __init__(self, groups, pieces, far_send, far_recv, near_send, near_recv):
        head = lax.axis_index("heads")
        self.half = half = groups // 2
        pair = {"heads": flip(head, 1)}
        self.far, self.near = [], []
        for n, (piece, where) in enumerate(pieces):
            self.far.append(
                [
                    remote(
                        piece,
                        where(head),
                        {"heads": (head + 2 * k) % groups},
                        far_send.at[n, k - 1],
                        far_recv.at[n, k - 1],
                    )
                    for k in range(1, half)
                ]
            )
            sides = [(piece, where(head))]
            for k in range(1, half):
                got = where((head - 2 * k + groups) % groups)
                sides.append((got, got))
            self.near.append(
                [
                    remote(source, target, pair, near_send.at[n, k], near_recv.at[n, k])
                    for k, (source, target) in enumerate(sides)
                ]
            )

    @staticmethod
    def scratch(count, groups):
        far, near = (count, max(groups // 2 - 1, 1)), (count, groups // 2)
        return [DMA(far), DMA(far), DMA(near), DMA(near)]

    def start(self, n):
        for copy in self.far[n]:
            copy.start()
        self.near[n][0].start()

    def forward(self, n):
        for k, copy in enumerate(self.far[n]):
            copy.wait_recv()
            self.near[n][k + 1].start()

    def finish(self):
        for copies in self.far:
            for copy in copies:
                copy.wait_send()
        for copies in self.near:
            for copy in copies:
                copy.wait()


def end_kernel(
    groups,
    reach,
    lines,
    partial,
    weight,
    mlp,
    attn,
    total,
    mlp_all,
    weight_all,
    attn_all,
    lined,
    summed,
    swap_send,
    swap_recv,
    own,
    *rest,
):
    place = Place(groups, reach)
    sub = mlp.shape[0]
    mine, head = place.ctx % sub, place.head
    meet(everyone(place, lines))
    wide = Halving(place, 3, partial, total, rest[:7], [2, 1])
    swap = Lines(lines, weight, lined, *rest[7:10])
    wide.start()
    swaps = []
    for step in range(1, sub):
        peer = (mine + step) % sub
        swaps.append(
            push(
                mlp.at[peer],
                mlp_all.at[mine, head],
                {"ctx": place.ctx - mine + peer},
                swap_send.at[step - 1],
                swap_recv.at[step - 1],
            )
        )
    pieces = [(mlp.at[mine], lambda h: mlp_all.at[mine, h]), (attn, lambda h: attn_all.at[h])]
    for step in range(1, sub):
        source = (mine - step + sub) % sub
        pieces.append(
            (mlp_all.at[source, head], lambda h, source=source: mlp_all.at[source, h])
        )
    pieces.append((summed, lambda h: weight_all.at[h]))
    collect = Collect(groups, pieces, *rest[10:14])
    swap.start()
    local = [
        pltpu.make_async_copy(mlp.at[mine], mlp_all.at[mine, head], own.at[0]),
        pltpu.make_async_copy(attn, attn_all.at[head], own.at[1]),
        pltpu.make_async_copy(summed, weight_all.at[head], own.at[2]),
    ]
    local[0].start()
    local[1].start()
    collect.start(0)
    collect.start(1)
    wide.pair()
    for step in range(1, sub):
        swaps[step - 1].wait_recv()
        collect.start(step + 1)
    wide.halve(0)
    swap.finish()
    for r in range(reach):
        summed[r] = functools.reduce(
            jnp.add, [lined[r + reach * g].astype(F32) for g in range(lines // reach)]
        ).astype(BF)
    local[2].start()
    collect.start(sub + 1)
    wide.halve(1)
    collect.forward(0)
    collect.forward(1)
    wide.halve(2)
    for n in range(2, sub + 2):
        collect.forward(n)
    for copy in local:
        copy.wait()
    for copy in swaps:
        copy.wait_send()
    collect.finish()
    wide.finish()


def end_step(partial, weight, mlp, attn, groups, reach):
    rows, width = partial.shape[2:]
    lines, _, shard = weight.shape
    sub = mlp.shape[0]
    return pl.pallas_call(
        functools.partial(end_kernel, groups, reach, lines),
        in_specs=[VMEM, ANY, ANY, ANY],
        out_specs=[VMEM, ANY, ANY, ANY],
        out_shape=[
            jax.ShapeDtypeStruct((rows, width), F32),
            jax.ShapeDtypeStruct((sub, groups, *mlp.shape[1:]), BF),
            jax.ShapeDtypeStruct((groups, reach, 3 * HD, shard), BF),
            jax.ShapeDtypeStruct((groups, *attn.shape), BF),
        ],
        scratch_shapes=[
            pltpu.VMEM((lines, 3 * HD, shard), BF),
            pltpu.VMEM((reach, 3 * HD, shard), BF),
            DMA((max(sub - 1, 1),)),
            DMA((max(sub - 1, 1),)),
            DMA((3,)),
            *Halving.scratch(3, rows, width),
            *Lines.scratch(lines),
            *Collect.scratch(sub + 2, groups),
        ],
        compiler_params=pltpu.CompilerParams(
            collective_id=3, has_side_effects=True, vmem_limit_bytes=20 << 20
        ),
        cost_estimate=pl.CostEstimate(flops=0, bytes_accessed=24 << 20, transcendentals=0),
        name="end_step",
    )(partial, weight, mlp, attn)


def assemble_kernel(
    upstream,
    tokens,
    grad_middle,
    gains,
    middle,
    ahead,
    weight_all,
    attn_all,
    mlp_all,
    w_qkv,
    w_in,
    own_gains,
    result,
    grad,
    sum_qkv,
    sum_attn,
    sum_in,
    sum_out,
    gain_sums,
):
    groups, reach, _, shard = weight_all.shape
    lanes = attn_all.shape[2]
    result[...] = (middle[...] + ahead[...]).astype(BF)
    normed, inverse_std = norm_parts(tokens[...].astype(F32))
    grad[...] = grad_middle[...] + norm_back(upstream[...], normed, inverse_std, gains[0:1, :])
    for g in range(groups):
        sum_attn[:, g * lanes : (g + 1) * lanes] = attn_all[g].astype(F32)
    gain_one = jnp.zeros((shard, 128), F32)
    for third in range(3):
        part = slice(third * HD, (third + 1) * HD)
        for pair in range(H // 2):
            r, g = 2 * pair // groups, 2 * pair % groups
            tile = (
                jnp.concatenate([weight_all[g, r, part], weight_all[g + 1, r, part]], axis=0)
                .astype(F32)
                .T
            )
            at = third * H * HD + pair * 2 * HD
            sum_qkv[:, at : at + 2 * HD] = tile
            gain_one += tile * w_qkv[:, at : at + 2 * HD].astype(F32)
    gain_two = jnp.zeros((shard, 1), F32)
    for t in range(8):
        start, wide = slice_place(t)
        for half in range(2):
            piece = mlp_all[t, :, half * SLICE : half * SLICE + wide].astype(F32)
            at = half * FF + start
            sum_in[:, at : at + wide] = piece
            gain_two += jnp.sum(
                piece * w_in[:, at : at + wide].astype(F32), axis=1, keepdims=True
            )
        sum_out[start : start + wide, :] = (
            mlp_all[t, :, 2 * SLICE : 3 * SLICE].astype(F32).T[:wide]
        )
    one = jnp.sum(gain_one, axis=1, keepdims=True)
    lane = lax.broadcasted_iota(jnp.int32, (shard, 128), 1)
    both = jnp.where(lane == 0, one, gain_two).T
    gain_sums[...] = both[:8] / own_gains[...]


def assemble(upstream, tokens, grad_middle, gains, middle, ahead, weight_all, attn_all, mlp_all, w_qkv, w_in, own_gains):
    rows, width = tokens.shape
    shard = w_qkv.shape[0]
    return pl.pallas_call(
        assemble_kernel,
        in_specs=[VMEM] * 12,
        out_specs=[VMEM] * 7,
        out_shape=[
            jax.ShapeDtypeStruct((rows, width), BF),
            jax.ShapeDtypeStruct((rows, width), F32),
            jax.ShapeDtypeStruct((shard, 3 * width), F32),
            jax.ShapeDtypeStruct((shard, width), F32),
            jax.ShapeDtypeStruct((shard, 2 * FF), F32),
            jax.ShapeDtypeStruct((FF, shard), F32),
            jax.ShapeDtypeStruct((8, shard), F32),
        ],
        compiler_params=pltpu.CompilerParams(vmem_limit_bytes=24 << 20),
        cost_estimate=pl.CostEstimate(flops=1 << 24, bytes_accessed=20 << 20, transcendentals=0),
        name="assemble",
    )(upstream, tokens, grad_middle, gains, middle, ahead, weight_all, attn_all, mlp_all, w_qkv, w_in, own_gains)


def slice_start(t):
    return 128 * jnp.minimum(3 * t, 2 * t + 5)


def slice_place(t):
    start = 128 * min(3 * t, 2 * t + 5)
    return start, min(128 * min(3 * t + 3, 2 * t + 7), FF) - start


def body(count, tokens, d_out, segment_ids, position_ids, w_qkv, w_attn, w_in, w_out, gain_attn, gain_mlp):
    groups = lax.axis_size("heads")
    rows, width = tokens.shape
    shard = w_qkv.shape[0]
    reach = SEQ_MAX // (rows * groups)
    group = reach * groups
    sub = 8 // groups
    ctx, head = lax.axis_index("ctx"), lax.axis_index("heads")
    assert group == H and sub * groups == 8
    total = group * rows
    tile = 512

    def mlp_slice(value, axis, start, t):
        pads = [(0, 0), (0, 0)]
        pads[axis] = (0, SLICE)
        piece = lax.dynamic_slice_in_dim(jnp.pad(value, pads), start + slice_start(t), SLICE, axis)
        wide = jnp.minimum(slice_start(t + 1), FF) - slice_start(t)
        shape = [1, 1]
        shape[axis] = SLICE
        return jnp.where(jnp.arange(SLICE).reshape(shape) < wide, piece, jnp.zeros_like(piece))

    def mlp_part(t):
        return jnp.concatenate(
            [mlp_slice(w_in, 1, 0, t), mlp_slice(w_in, 1, FF, t), mlp_slice(w_out, 0, 0, t).T], axis=1
        )

    mlp = jnp.stack([mlp_part(x * groups + head) for x in range(sub)])
    gains_own = jnp.pad(jnp.stack([gain_attn, gain_mlp]).astype(F32), ((0, 6), (0, -shard % 128)))
    ids = jnp.pad(jnp.stack([position_ids, segment_ids]), ((0, 6), (0, 0)))
    freqs = jnp.power(160000.0, -(2.0 * jnp.arange(HALF, dtype=F32)) / HD)[:, None]
    input_all, gains, w_head, cosine, sine, marks, attn_half = begin(
        tokens, gains_own, ids, w_qkv, w_attn, freqs, count // sub, count, groups, reach
    )
    x = input_all.reshape(total, width)

    attended, wide, lse, qkv, attn_weights, mlp_pair, mlp_near = attend(
        x,
        w_head,
        cosine,
        sine,
        marks,
        attn_half,
        mlp.reshape(2, sub * shard // 2, 3 * SLICE),
        count,
        groups,
        reach,
        rows,
        tile,
    )
    attn_weights = attn_weights.reshape(width, width)
    mlp_all, upstream, middle, attended, mlp_weights = middle_step(
        attended, tokens, d_out, attn_weights, gains, mlp_pair, mlp_near, count, groups, reach
    )
    mlp_weights = mlp_weights.reshape(width, 3 * SLICE)
    split = lambda value, blocks: value.reshape(blocks // 2, 2, rows, width)
    back, forward, mlp_terms = mlp_step(
        mlp_all.reshape(8 * rows, width), upstream.reshape(8 * rows, width), mlp_weights, 512
    )
    mlp_terms = mlp_terms.reshape(count // sub, 2, sub * shard // 2, 3 * SLICE)
    grad_heads, grad_middle, attn_part, carry = turn_step(
        split(back, 8),
        middle,
        d_out,
        attn_weights,
        gains,
        attended.reshape(groups, width, rows),
        mlp_terms,
        groups,
        reach,
    )
    attn_part = attn_part.reshape(count, shard, width // groups)
    forward = split(forward, 8)
    grad_input_parts, weight, ahead, attn_sum, mlp_sum = attend_back(
        qkv,
        grad_heads,
        wide,
        lse,
        x,
        w_head,
        cosine,
        sine,
        forward,
        mlp_terms,
        carry,
        attn_part,
        groups,
        reach,
        tile,
    )
    mlp_sum = mlp_sum.reshape(sub, shard, 3 * SLICE)
    upstream_in, mlp_all, weight_all, attn_all = end_step(
        split(grad_input_parts, group), weight, mlp_sum, attn_sum, groups, reach
    )
    result, grad_input, sum_qkv, sum_attn, sum_in, sum_out, gain_sums = assemble(
        upstream_in,
        tokens,
        grad_middle,
        gains,
        middle,
        ahead,
        weight_all,
        attn_all,
        mlp_all.reshape(8, shard, 3 * SLICE),
        w_qkv,
        w_in,
        jnp.pad(gains_own[:2, :shard], ((0, 6), (0, 0)), constant_values=1.0),
    )
    return (
        result,
        grad_input,
        sum_qkv,
        sum_attn,
        sum_in,
        sum_out,
        gain_sums[0],
        gain_sums[1],
    )


def solution(mesh):
    return jax.shard_map(
        functools.partial(body, mesh.shape["ctx"]),
        mesh=mesh,
        in_specs=(
            P(("ctx", "heads"), None),
            P(("ctx", "heads"), None),
            P(("ctx", "heads")),
            P(("ctx", "heads")),
            P("ctx", None),
            P("ctx", None),
            P("ctx", None),
            P(None, "ctx"),
            P("ctx"),
            P("ctx"),
        ),
        out_specs=(
            P(("ctx", "heads"), None),
            P(("ctx", "heads"), None),
            P("ctx", None),
            P("ctx", None),
            P("ctx", None),
            P(None, "ctx"),
            P("ctx"),
            P("ctx"),
        ),
        check_vma=False,
    )
```

```python
import functools

import jax
import jax.numpy as jnp
from jax import lax
from jax.experimental import pallas as pl
from jax.experimental.pallas import tpu as pltpu
from jax.sharding import PartitionSpec as P

H = 16
HD = 64
HALF = HD // 2
FF = 2624
SEQ_MAX = 2048
MASKED = -1e30
MARKS = 16
QM_END = HD + MARKS
K_END = QM_END + HD
KM_END = K_END + MARKS
V_END = KM_END + HD
SLICE = 384
BF = jnp.bfloat16
F32 = jnp.float32
MESH = pl.DeviceIdType.MESH
VMEM = pl.BlockSpec(memory_space=pltpu.VMEM)
ANY = pl.BlockSpec(memory_space=pl.ANY)
DMA = pltpu.SemaphoreType.DMA


def dot(left, right, left_dim, right_dim):
    return lax.dot_general(
        left, right, (((left_dim,), (right_dim,)), ((), ())), preferred_element_type=F32
    )


def norm_parts(values):
    average = jnp.mean(values, axis=-1, keepdims=True)
    centred = values - average
    inverse_std = lax.rsqrt(jnp.mean(centred * centred, axis=-1, keepdims=True) + 1e-05)
    return centred * inverse_std, inverse_std


def norm_back(upstream, normed, inverse_std, gain):
    scaled = upstream * gain
    return inverse_std * (
        scaled
        - jnp.mean(scaled, axis=-1, keepdims=True)
        - normed * jnp.mean(scaled * normed, axis=-1, keepdims=True)
    )


def flip(value, bit):
    return value + bit - 2 * bit * (value // bit % 2)


class Place:
    def __init__(self, groups, reach):
        self.groups, self.reach = groups, reach
        self.ctx = lax.axis_index("ctx")
        self.head = lax.axis_index("heads")
        self.local = self.ctx % reach
        self.base = self.ctx - self.local
        self.idx = self.local * groups + self.head

    def member(self, j):
        return {"ctx": self.base + j // self.groups, "heads": j % self.groups}


def greet(devices):
    barrier = pltpu.get_barrier_semaphore()
    for device in devices:
        pl.semaphore_signal(barrier, inc=1, device_id=device, device_id_type=MESH)


def meet(devices):
    greet(devices)
    pl.semaphore_wait(pltpu.get_barrier_semaphore(), len(devices))


def remote(source, target, device, send, recv):
    return pltpu.make_async_remote_copy(
        src_ref=source,
        dst_ref=target,
        send_sem=send,
        recv_sem=recv,
        device_id=device,
        device_id_type=MESH,
    )


def push(*operands):
    copy = remote(*operands)
    copy.start()
    return copy


def tree_parts(axes, rows):
    part = -(-rows // axes // 16) * 16
    starts = [min(part * a, rows) for a in range(axes + 1)]
    return [(starts[a], starts[a + 1] - starts[a]) for a in range(axes)]


class Tree:
    def __init__(self, place, axes, source, target, sems):
        self.place, self.axes, self.source, self.target = place, axes, source, target
        self.send, self.recv, self.core_send, self.core_recv, self.own = sems
        self.slots = 2 << axes
        self.levels, self.cores = [], []

    @staticmethod
    def scratch(axes):
        far, near = axes * axes, axes * axes + 1
        return [DMA((far,)), DMA((far,)), DMA((near,)), DMA((near,)), DMA]

    def origin(self, level, first):
        value = self.place.idx
        for k in range(level):
            value = flip(value, 2 << ((first + k) % self.axes))
        return value % self.slots

    def neighbour(self, axis):
        return self.place.member(flip(self.place.idx, 2 << (axis % self.axes)))

    def piece(self, slot, part):
        return self.target.at[slot] if part is None else self.target.at[slot, pl.ds(*part)]

    def to_core(self, source, slot, part):
        at = len(self.cores)
        self.cores.append(
            push(
                source,
                self.piece(slot, part),
                self.place.member(flip(self.place.idx, 1)),
                self.core_send.at[at],
                self.core_recv.at[at],
            )
        )

    def start(self):
        me = self.place.idx % self.slots
        self.levels.append(
            [
                push(
                    self.source, self.target.at[me], self.neighbour(a), self.send.at[a], self.recv.at[a]
                )
                for a in range(self.axes)
            ]
        )
        self.to_core(self.source, me, None)
        self.local = pltpu.make_async_copy(self.source, self.target.at[me], self.own)
        self.local.start()

    def forward(self, level):
        axes = self.axes
        parts = tree_parts(axes, self.target.shape[1])
        onward = []
        for a in range(axes):
            self.levels[level - 1][a].wait_recv()
            slot = self.origin(level, a)
            if level < axes:
                part = parts[a] if level + 1 == axes else None
                at = level * axes + a
                piece = self.piece(slot, part)
                onward.append(
                    push(piece, piece, self.neighbour(a + level), self.send.at[at], self.recv.at[at])
                )
                self.to_core(self.target.at[slot], slot, None)
            else:
                self.to_core(self.piece(slot, parts[a]), slot, parts[a])
        self.levels.append(onward)

    def finish(self):
        self.local.wait()
        for level in self.levels:
            for copy in level:
                copy.wait_send()
        for copy in self.cores:
            copy.wait()


class Halving:
    def __init__(self, place, axes, value, result, scratch, firsts=None):
        self.firsts = firsts = firsts or list(range(axes))
        self.axes, self.value, self.result = axes, value, result
        self.other, self.held, self.land, send, recv, send0, recv0 = scratch
        self.blocks = 1 << axes
        width = value.shape[-1]
        part = width // len(firsts)
        self.columns = [pl.ds(part * a, part) for a in range(len(firsts))]
        self.core = place.idx % 2
        self.chip = place.idx // 2 % self.blocks
        self.sources = []
        for j in range(self.blocks):
            k = self.chip
            for a in range(axes):
                if j >> a & 1:
                    k = flip(k, 1 << a)
            self.sources.append(k)
        self.first, self.copies = [], {}
        for p in range(len(firsts)):
            self.first.append(
                remote(
                    value.at[:, 1 - self.core, :, self.columns[p]],
                    self.other.at[:, :, self.columns[p]],
                    place.member(flip(place.idx, 1)),
                    send0.at[p],
                    recv0.at[p],
                )
            )
            for step in range(axes):
                bit, sent = self.sent(p, step)
                for j in sent:
                    self.copies[p, j] = remote(
                        self.held.at[j, :, self.columns[p]],
                        self.land.at[j, :, self.columns[p]],
                        place.member(flip(place.idx, 2 * bit)),
                        send.at[p, j],
                        recv.at[p, j],
                    )

    @staticmethod
    def scratch(axes, rows, width):
        blocks = 1 << axes
        return [
            pltpu.VMEM((blocks, rows, width), BF),
            pltpu.VMEM((blocks, rows, width), BF),
            pltpu.VMEM((blocks, rows, width), BF),
            DMA((axes, blocks)),
            DMA((axes, blocks)),
            DMA((axes,)),
            DMA((axes,)),
        ]

    def sent(self, part, step):
        first = self.firsts[part]
        seen = [1 << ((first + s) % self.axes) for s in range(step)]
        bit = 1 << ((first + step) % self.axes)
        return bit, [j for j in range(self.blocks) if j & bit and not any(j & s for s in seen)]

    def start(self):
        for copy in self.first:
            copy.start()

    def pair(self):
        for p in range(len(self.firsts)):
            cols = self.columns[p]
            self.first[p].wait_recv()
            _, early = self.sent(p, 0)
            for j in early + [j for j in range(self.blocks) if j not in early]:
                k = self.sources[j]
                self.held[j, :, cols] = (
                    self.value[k, self.core, :, cols].astype(F32) + self.other[k, :, cols].astype(F32)
                ).astype(BF)
                if j in early:
                    self.copies[p, j].start()

    def halve(self, step):
        for p in range(len(self.firsts)):
            cols = self.columns[p]
            bit, arrived = self.sent(p, step)
            onward = self.sent(p, step + 1)[1] if step + 1 < self.axes else []
            for j in sorted(arrived, key=lambda j: (j - bit) not in onward):
                self.copies[p, j].wait_recv()
                k = j - bit
                total = self.held[k, :, cols].astype(F32) + self.land[j, :, cols].astype(F32)
                if step + 1 < self.axes:
                    self.held[k, :, cols] = total.astype(BF)
                    if k in onward:
                        self.copies[p, k].start()
                else:
                    self.result[:, cols] = total

    def run(self):
        self.start()
        self.pair()
        for step in range(self.axes):
            self.halve(step)
        self.finish()

    def finish(self):
        for copy in self.first:
            copy.wait_send()
        for copy in self.copies.values():
            copy.wait_send()


class Lines:
    def __init__(self, count, source, target, send, recv, own):
        me = lax.axis_index("ctx")
        self.copies = [pltpu.make_async_copy(source.at[me], target.at[me], own)]
        for step in range(1, count):
            peer = (me + step) % count
            self.copies.append(
                remote(source.at[peer], target.at[me], {"ctx": peer}, send.at[step - 1], recv.at[step - 1])
            )

    @staticmethod
    def scratch(count):
        return [DMA((count - 1,)), DMA((count - 1,)), DMA]

    def start(self):
        for copy in self.copies:
            copy.start()

    def finish(self):
        for copy in self.copies:
            copy.wait()


def everyone(place, count):
    group = place.reach * place.groups
    mates = [place.member((place.idx + step) % group) for step in range(1, group)]
    outside = [{"ctx": (place.base + place.reach + step) % count} for step in range(count - place.reach)]
    return mates + outside


def spread(place, source, target, sems, me=None):
    send, recv, own = sems
    count = target.shape[0]
    copies = []
    for step in range(1, count):
        peer = (place.idx + step) % count
        copies.append(
            push(
                source.at[peer],
                target.at[place.idx],
                place.member(peer),
                send.at[step - 1],
                recv.at[step - 1],
            )
        )
    local = pltpu.make_async_copy(source.at[place.idx], target.at[place.idx], own)
    local.start()
    copies.append(local)
    return copies


def begin_kernel(
    groups,
    reach,
    count,
    tokens,
    gains,
    ids,
    w_qkv,
    w_attn,
    freqs,
    input_all,
    gains_all,
    w_head,
    cosine,
    sine,
    marks,
    attn_half,
    ids_all,
    slab,
    mine,
    gain_land,
    own_sems,
    ids_send,
    ids_recv,
    gain_send,
    gain_recv,
    slab_send,
    slab_recv,
    wide_send,
    wide_recv,
    core_send,
    core_recv,
    *tree_sems,
):
    place = Place(groups, reach)
    group = reach * groups
    ctx, head, idx = place.ctx, place.head, place.idx
    shard = w_qkv.shape[0]
    ring = attn_half.shape[0]
    sub = count // ring
    side, spot = ctx % sub, ctx // sub
    lanes = attn_half.shape[2] // groups
    core = {"heads": flip(head, 1)}
    mates = [place.member((idx + step) % group) for step in range(1, group)]
    lines = [{"ctx": (ctx + step) % count} for step in range(1, count)]
    meet(everyone(place, count))
    first = [
        push(gains, gain_land.at[ctx], lines[step - 1], gain_send.at[step - 1], gain_recv.at[step - 1])
        for step in range(1, count)
    ]
    small = [
        push(ids, ids_all.at[idx], mates[step - 1], ids_send.at[step - 1], ids_recv.at[step - 1])
        for step in range(1, group)
    ]
    half = pl.ds(pl.multiple_of(head % 2 * (shard // 2), 16), shard // 2)
    thirds = []
    for step in range(1, count):
        peer = (ctx + step) % count
        column = ((peer % reach) * groups + head) // 2 * 128
        for third in range(3):
            start = pl.multiple_of(third * 1024 + column, 128)
            thirds.append(
                push(
                    w_qkv.at[half, pl.ds(start, 128)],
                    slab.at[ctx, half, pl.ds(third * 128, 128)],
                    lines[step - 1],
                    slab_send.at[step - 1, third],
                    slab_recv.at[step - 1, third],
                )
            )
    gain_land[ctx] = gains[...]
    where = lambda h: pl.ds(pl.multiple_of(h * lanes, 128), lanes)
    across = where(head)
    own = [
        pltpu.make_async_copy(ids, ids_all.at[idx], own_sems.at[3]),
        pltpu.make_async_copy(w_attn.at[:, across], attn_half.at[spot, :, across], own_sems.at[4]),
    ]
    for third in range(3):
        start = pl.multiple_of(third * 1024 + idx // 2 * 128, 128)
        own.append(
            pltpu.make_async_copy(
                w_qkv.at[half, pl.ds(start, 128)],
                slab.at[ctx, half, pl.ds(third * 128, 128)],
                own_sems.at[third],
            )
        )
    for copy in own:
        copy.start()
    for copy in first:
        copy.wait_recv()
    gain, gain_two = (
        jnp.concatenate([gain_land[c, k : k + 1, :shard] for c in range(count)], axis=1)
        for k in range(2)
    )
    normed, _ = norm_parts(tokens[...].astype(F32))
    mine[...] = (normed * gain).astype(BF)
    tree = Tree(place, 3, mine, input_all, tree_sems[:5])
    tree.start()
    gains_all[0:1, :] = gain
    gains_all[1:2, :] = gain_two
    late = []
    for step in range(1, ring):
        late.append(
            push(
                w_attn.at[:, across],
                attn_half.at[spot, :, across],
                {"ctx": (spot + step) % ring * sub + side},
                wide_send.at[step - 1],
                wide_recv.at[step - 1],
            )
        )
    tree.forward(1)
    for copy in own:
        copy.wait()
    for copy in thirds:
        copy.wait_recv()
    for copy in late:
        copy.wait_recv()
    collect = Collect(
        groups, [(attn_half.at[:, :, across], lambda h: attn_half.at[:, :, where(h)])], *tree_sems[5:]
    )
    collect.start(0)
    shared = push(slab.at[:, half], slab.at[:, half], core, core_send, core_recv)
    for copy in small:
        copy.wait()
    row = lambda k: jnp.concatenate([ids_all[j, k : k + 1, :] for j in range(group)], axis=1)
    angles = freqs[...] * row(0).astype(F32)
    cosine[...] = jnp.cos(angles)
    sine[...] = jnp.sin(angles)
    parity = (row(1) % 2).astype(F32)
    blank = jnp.zeros((MARKS - 2, parity.shape[1]), F32)
    marks[...] = jnp.concatenate(
        [parity, 1.0 - parity, blank, (1.0 - parity) * MASKED, parity * MASKED, blank], axis=0
    ).astype(BF)
    tree.forward(2)
    shared.wait()
    odd = head % 2 == 1
    for c in range(count):
        rows = slice(c * shard, (c + 1) * shard)
        block = slab[c].astype(F32)
        parts = []
        for third in range(3):
            at = third * 128
            parts.append(jnp.where(odd, block[:, at + HD : at + 128], block[:, at : at + HD]))
        w_head[rows] = jnp.concatenate(parts, axis=1).astype(BF)
    collect.forward(0)
    tree.forward(3)
    tree.finish()
    collect.finish()
    for copy in first + thirds + late:
        copy.wait_send()


def begin(tokens, gains, ids, w_qkv, w_attn, freqs, ring, count, groups, reach):
    rows, width = tokens.shape
    shard = w_qkv.shape[0]
    group = groups * reach
    sems = lambda *shape: [DMA(shape), DMA(shape)]
    return pl.pallas_call(
        functools.partial(begin_kernel, groups, reach, count),
        in_specs=[VMEM, VMEM, ANY, ANY, ANY, VMEM],
        out_specs=[ANY, VMEM, VMEM, VMEM, VMEM, VMEM, ANY],
        out_shape=[
            jax.ShapeDtypeStruct((group, rows, width), BF),
            jax.ShapeDtypeStruct((8, width), F32),
            jax.ShapeDtypeStruct((width, 3 * HD), BF),
            jax.ShapeDtypeStruct((HALF, group * rows), F32),
            jax.ShapeDtypeStruct((HALF, group * rows), F32),
            jax.ShapeDtypeStruct((2 * MARKS, group * rows), BF),
            jax.ShapeDtypeStruct((ring, shard, width), BF),
        ],
        scratch_shapes=[
            pltpu.VMEM((group, 8, rows), jnp.int32),
            pltpu.VMEM((count, shard, 3 * 128), BF),
            pltpu.VMEM((rows, width), BF),
            pltpu.VMEM((count, 8, gains.shape[1]), F32),
            DMA((5,)),
            *sems(group - 1),
            *sems(count - 1),
            *sems(count - 1, 3),
            *sems(ring - 1),
            DMA,
            DMA,
            *Tree.scratch(3),
            *Collect.scratch(1, groups),
        ],
        compiler_params=pltpu.CompilerParams(
            collective_id=0, has_side_effects=True, vmem_limit_bytes=12 << 20
        ),
        cost_estimate=pl.CostEstimate(flops=0, bytes_accessed=30 << 20, transcendentals=0),
        name="begin",
    )(tokens, gains, ids, w_qkv, w_attn, freqs)


class Line:
    def __init__(self, length, sub, first, sources, targets, send, recv):
        ctx = lax.axis_index("ctx")
        spot, side = ctx // sub, ctx % sub
        self.length, self.spot, self.first = length, spot, first
        self.waited = 0
        beside = [{"ctx": (spot + 1) % length * sub + side}, {"ctx": (spot + length - 1) % length * sub + side}]
        self.copies = [
            [
                remote(sources[d][q], targets[d][q], beside[d], send.at[d, q], recv.at[d, q])
                for q in range(len(sources[d]))
            ]
            for d in range(2)
        ]

    def sends(self, d, q):
        s, spot, last = (q + self.first) // 2, self.spot, self.length - 1
        if d:
            return jnp.logical_and(spot + s <= last, spot > 0)
        return jnp.logical_and(spot >= s, spot < last)

    def receives(self, d, q):
        s = (q + self.first) // 2
        return self.spot + s + 1 < self.length if d else self.spot > s

    def arrive(self, q):
        for d in range(2):
            pl.when(self.receives(d, q))(self.copies[d][q].wait_recv)
        self.waited = q + 1

    def start(self, q):
        if q >= 2:
            self.arrive(q - 2)
        for d in range(2):
            pl.when(self.sends(d, q))(self.copies[d][q].start)

    def finish(self):
        for q in range(self.waited, len(self.copies[0])):
            self.arrive(q)
        for d in range(2):
            for q, copy in enumerate(self.copies[d]):
                pl.when(self.sends(d, q))(copy.wait_send)


def ring_half(sub, side, k):
    return (side + k) % 2 if sub == 2 else k


class Columns:
    def __init__(self, place, part, whole, own, side_send, side_recv, near_send, near_recv):
        _, sub, _, width = whole.shape
        side = place.ctx % sub
        half = pl.ds(pl.multiple_of(place.head % 2 * (width // 2), 128), width // 2)
        self.own = pltpu.make_async_copy(part, whole.at[:, side], own)
        self.sides, self.near = [], []
        for step in range(1, sub):
            peer, source = (side + step) % sub, (side - step + sub) % sub
            self.sides.append(
                remote(
                    part.at[:, :, half],
                    whole.at[:, side, :, half],
                    {"ctx": place.ctx - side + peer},
                    side_send.at[step - 1],
                    side_recv.at[step - 1],
                )
            )
            here = whole.at[:, source, :, half]
            self.near.append(
                remote(
                    here, here, {"heads": flip(place.head, 1)}, near_send.at[step - 1], near_recv.at[step - 1]
                )
            )

    @staticmethod
    def scratch(sub):
        count = (max(sub - 1, 1),)
        return [DMA, DMA(count), DMA(count), DMA(count), DMA(count)]

    def start(self):
        self.own.start()
        for copy in self.sides:
            copy.start()

    def across(self):
        for side, near in zip(self.sides, self.near):
            side.wait_recv()
            near.start()

    def finish(self):
        self.own.wait()
        for side, near in zip(self.sides, self.near):
            side.wait_send()
            near.wait()


def attend_kernel(
    groups,
    reach,
    lines,
    tile,
    x_ref,
    w_ref,
    cos_ref,
    sin_ref,
    mark_ref,
    attn_half,
    mlp,
    out_ref,
    wide_ref,
    lse_ref,
    qkv_ref,
    attn_all,
    mlp_pair,
    mlp_near,
    ring_send,
    ring_recv,
    swap_send,
    swap_recv,
    swap_own,
    *sems,
):
    count = x_ref.shape[0]
    step = pl.program_id(0)
    steps = count // tile
    place = Place(groups, reach)
    ring_size, sub = attn_all.shape[:2]
    side = place.ctx % sub
    early = mlp_near.shape[1]
    if sub == 2:
        kept = pltpu.make_async_copy(mlp.at[side], mlp_pair.at[side], swap_own)
        swap = [
            remote(
                mlp.at[1 - side],
                mlp_pair.at[side],
                {"ctx": place.ctx + 1 - 2 * side},
                swap_send,
                swap_recv,
            )
        ]
        sources = [mlp.at[side], mlp_pair.at[1 - side]]
    else:
        kept = pltpu.make_async_copy(mlp, mlp_pair, swap_own)
        swap = []
        sources = [mlp.at[0], mlp.at[1]]
    ring = Line(
        ring_size,
        sub,
        0,
        [sources + [mlp_near.at[d, q] for q in range(early - 2)] for d in range(2)],
        [[mlp_near.at[d, q] for q in range(early)] for d in range(2)],
        ring_send,
        ring_recv,
    )
    columns = Columns(place, attn_half, attn_all, *sems)

    @pl.when(step == 0)
    def _():
        meet(everyone(place, lines))
        for copy in swap:
            copy.start()
        ring.start(0)
        kept.start()
        columns.start()
        qkv_ref[HD:QM_END, :] = mark_ref[:MARKS, :]
        qkv_ref[K_END:KM_END, :] = mark_ref[MARKS:, :]

        @pl.loop(0, steps)
        def _(i):
            at = pl.ds(pl.multiple_of(i * tile, tile), tile)
            cosine, sine = cos_ref[:, at], sin_ref[:, at]
            part = dot(w_ref[...], x_ref[at, :], 0, 1)

            def turn(value):
                front, back = value[:HALF], value[HALF:]
                return jnp.concatenate(
                    [front * cosine - back * sine, back * cosine + front * sine], axis=0
                )

            qkv_ref[:HD, at] = (turn(part[:HD]) * 0.125).astype(BF)
            qkv_ref[QM_END:K_END, at] = turn(part[HD : 2 * HD]).astype(BF)
            qkv_ref[KM_END:, at] = part[2 * HD :].astype(BF)

    here = pl.ds(pl.multiple_of(step * tile, tile), tile)
    query = qkv_ref[:QM_END, here]
    keys = [slice(j * tile, (j + 1) * tile) for j in range(steps)]
    scores = [dot(qkv_ref[QM_END:KM_END, at], query, 0, 0) for at in keys]
    top = functools.reduce(jnp.maximum, [jnp.max(s, axis=0, keepdims=True) for s in scores])
    raised = [jnp.exp(s - top) for s in scores]
    total = functools.reduce(jnp.add, [jnp.sum(e, axis=0, keepdims=True) for e in raised])
    scale = 1.0 / total
    result = jnp.zeros((HD, tile), F32)
    for j in range(steps):
        result += dot(qkv_ref[KM_END:, keys[j]], (raised[j] * scale).astype(BF), 1, 0)
    rows = out_ref.shape[2]
    for k in range(tile // rows):
        out_ref[step * (tile // rows) + k] = result[:, k * rows : (k + 1) * rows].astype(BF)
    wide_ref[:, here] = result
    lse_ref[:, here] = top + jnp.log(total)

    @pl.when(step == min(1, steps - 1))
    def _():
        for copy in swap:
            copy.wait_recv()
        for q in range(1, min(early, 3)):
            ring.start(q)

    @pl.when(step == steps - 1)
    def _():
        columns.across()
        for q in range(3, early):
            ring.start(q)
        ring.finish()
        for copy in swap:
            copy.wait_send()
        kept.wait()
        columns.finish()


def attend(x, w, cosine, sine, marks, attn_half, mlp, lines, groups, reach, rows, tile):
    count, width = x.shape
    ring, shard, _ = attn_half.shape
    sub = lines // ring
    early = ring - 1
    whole = lambda *shape: pl.BlockSpec(shape, lambda i: (0,) * len(shape))
    return pl.pallas_call(
        functools.partial(attend_kernel, groups, reach, lines, tile),
        grid=(count // tile,),
        in_specs=[
            whole(count, width),
            whole(*w.shape),
            whole(HALF, count),
            whole(HALF, count),
            whole(2 * MARKS, count),
            ANY,
            ANY,
        ],
        out_specs=[
            whole(count // rows, HD, rows),
            whole(HD, count),
            whole(1, count),
            whole(V_END, count),
            ANY,
            ANY,
            ANY,
        ],
        out_shape=[
            jax.ShapeDtypeStruct((count // rows, HD, rows), BF),
            jax.ShapeDtypeStruct((HD, count), F32),
            jax.ShapeDtypeStruct((1, count), F32),
            jax.ShapeDtypeStruct((V_END, count), BF),
            jax.ShapeDtypeStruct((ring, sub, shard, width), BF),
            jax.ShapeDtypeStruct(mlp.shape, BF),
            jax.ShapeDtypeStruct((2, early, *mlp.shape[1:]), BF),
        ],
        scratch_shapes=[DMA((2, early)), DMA((2, early)), DMA, DMA, DMA, *Columns.scratch(sub)],
        compiler_params=pltpu.CompilerParams(
            collective_id=5, has_side_effects=True, vmem_limit_bytes=32 << 20
        ),
        cost_estimate=pl.CostEstimate(
            flops=count * count * HD * 8, bytes_accessed=count * 4096, transcendentals=count * count
        ),
        name="attend",
    )(x, w, cosine, sine, marks, attn_half, mlp)


def middle_kernel(
    groups,
    reach,
    lines,
    outgoing,
    tokens,
    d_out,
    w_attn,
    gains,
    mlp_pair,
    mlp_near,
    mlp_all,
    upstream_all,
    middle,
    attended,
    mlp_weights,
    land,
    mine,
    a2a_send,
    a2a_recv,
    own,
    ring_send,
    ring_recv,
    ring_own,
    land_own,
    *tree_sems,
):
    place = Place(groups, reach)
    group = groups * reach
    early, count = mlp_near.shape[1], mlp_weights.shape[0]
    sub = lines // count
    spot, side = place.ctx // sub, place.ctx % sub

    def slot(d, q, ahead):
        block = (spot + (q // 2 + ahead if d else count - q // 2 - ahead)) % count
        return mlp_weights.at[block, ring_half(sub, side, q % 2)]

    rest = range(early, 2 * (count - 1))
    ring = Line(
        count,
        sub,
        early,
        [[mlp_near.at[d, q - 2] if q - 2 < early else slot(d, q, 0) for q in rest] for d in range(2)],
        [[slot(d, q, 0) for q in rest] for d in range(2)],
        ring_send,
        ring_recv,
    )
    local = [pltpu.make_async_copy(mlp_pair, mlp_weights.at[spot], ring_own.at[0])]
    near = []
    for d in range(2):
        for q in range(early):
            copy = pltpu.make_async_copy(
                mlp_near.at[d, q], slot(d, q, 1), ring_own.at[1 + d * early + q]
            )
            there = spot + q // 2 + 1 < count if d else spot > q // 2
            near.append((there, copy))
    meet(everyone(place, lines))
    copies = spread(place, outgoing, land, (a2a_send, a2a_recv, own))
    ring.start(0)
    ring.start(1)
    up = Tree(place, 2, d_out, upstream_all, tree_sems[5:10])
    up.start()
    for copy in local:
        copy.start()
    for there, copy in near:
        pl.when(there)(copy.start)
    for copy in copies:
        copy.wait()
    collect = Collect(groups, [(land, lambda h: attended.at[h])], *tree_sems[10:])
    collect.start(0)
    local.append(pltpu.make_async_copy(land, attended.at[place.head], land_own))
    local[-1].start()
    value = tokens[...].astype(F32) + dot(
        land[...].reshape(group * HD, tokens.shape[0]), w_attn[...], 0, 0
    )
    middle[...] = value
    normed, _ = norm_parts(value)
    mine[...] = (normed * gains[1:2, :]).astype(BF)
    tree = Tree(place, 2, mine, mlp_all, tree_sems[:5])
    tree.start()
    up.forward(1)
    for q in range(2, len(rest)):
        ring.start(q)
    tree.forward(1)
    up.forward(2)
    tree.forward(2)
    collect.forward(0)
    up.finish()
    tree.finish()
    collect.finish()
    for copy in local:
        copy.wait()
    for there, copy in near:
        pl.when(there)(copy.wait)
    ring.finish()


def middle_step(outgoing, tokens, d_out, w_attn, gains, mlp_pair, mlp_near, lines, groups, reach):
    rows, width = tokens.shape
    group = groups * reach
    early, sub = mlp_near.shape[1], 8 // groups
    ring = lines // sub
    left = 2 * (ring - 1) - early
    return pl.pallas_call(
        functools.partial(middle_kernel, groups, reach, lines),
        in_specs=[ANY, VMEM, ANY, VMEM, VMEM, ANY, ANY],
        out_specs=[ANY, ANY, VMEM, ANY, ANY],
        out_shape=[
            jax.ShapeDtypeStruct((8, rows, width), BF),
            jax.ShapeDtypeStruct((8, rows, width), BF),
            jax.ShapeDtypeStruct((rows, width), F32),
            jax.ShapeDtypeStruct((groups, group, HD, rows), BF),
            jax.ShapeDtypeStruct((ring, *mlp_pair.shape), BF),
        ],
        scratch_shapes=[
            pltpu.VMEM((group, HD, rows), BF),
            pltpu.VMEM((rows, width), BF),
            DMA((group - 1,)),
            DMA((group - 1,)),
            DMA,
            DMA((2, left)),
            DMA((2, left)),
            DMA((2 * early + 1,)),
            DMA,
            *Tree.scratch(2),
            *Tree.scratch(2),
            *Collect.scratch(1, groups),
        ],
        compiler_params=pltpu.CompilerParams(
            collective_id=1, has_side_effects=True, vmem_limit_bytes=12 << 20
        ),
        cost_estimate=pl.CostEstimate(flops=1 << 28, bytes_accessed=12 << 20, transcendentals=0),
        name="middle_step",
    )(outgoing, tokens, d_out, w_attn, gains, mlp_pair, mlp_near)


class Sum:
    def __init__(self, place, terms, first, held, stage, land, send, recv):
        self.terms, self.first, self.stage, self.land = terms, first, stage, land
        self.half = stage.shape[2]
        length = terms.shape[0] // (2 * self.half)
        lines_sub = 8 // place.groups
        spot, side = place.ctx // lines_sub, place.ctx % lines_sub
        self.length, self.spot = length, spot
        self.held = lambda d, q: land.at[d, q] if q >= 0 else held.at[d, q + 2]
        beside = [
            {"ctx": (spot + 1) % length * lines_sub + side},
            {"ctx": (spot + length - 1) % length * lines_sub + side},
        ]
        self.copies = [
            [
                remote(stage.at[d, q], land.at[d, q], beside[d], send.at[d, q], recv.at[d, q])
                for q in range(stage.shape[1])
            ]
            for d in range(2)
        ]

    @staticmethod
    def scratch(count, half):
        return [
            pltpu.VMEM((2, count, *half), BF),
            pltpu.VMEM((2, count, *half), BF),
            DMA((2, count)),
            DMA((2, count)),
        ]

    def sends(self, d, q):
        s, spot, last = (q + self.first) // 2, self.spot, self.length - 1
        if d:
            return jnp.logical_and(spot >= last - s, spot > 0)
        return jnp.logical_and(spot <= s, spot < last)

    def receives(self, d, q):
        s, spot, last = (q + self.first) // 2, self.spot, self.length - 1
        if d:
            return jnp.logical_and(spot >= last - 1 - s, spot < last)
        return jnp.logical_and(spot <= s + 1, spot > 0)

    def clear(self):
        for d in range(2):
            for q in range(len(self.copies[d])):

                @pl.when(jnp.logical_not(self.receives(d, q)))
                def _():
                    self.land[d, q] = jnp.zeros(self.land.shape[2:], BF)

    def block(self, at, k):
        return self.terms[pl.ds(pl.multiple_of((2 * at + k) * self.half, 16), self.half), :]

    def arrive(self, q):
        for d in range(2):
            pl.when(self.receives(d, q))(self.copies[d][q].wait_recv)

    def start(self, q):
        if q >= 2:
            self.arrive(q - 2)
        step, k = (q + self.first) // 2, (q + self.first) % 2
        for d in range(2):
            at = self.spot + (step + 1 if d else self.length - 1 - step)

            @pl.when(self.sends(d, q))
            def _():
                value = self.block(at % self.length, k)
                if q + self.first >= 2:
                    value = (value.astype(F32) + self.held(d, q - 2)[...].astype(F32)).astype(BF)
                self.stage[d, q] = value
                self.copies[d][q].start()

    def finish(self):
        count = len(self.copies[0])
        for q in range(max(count - 2, 0), count):
            self.arrive(q)
        for d in range(2):
            for q, copy in enumerate(self.copies[d]):
                pl.when(self.sends(d, q))(copy.wait_send)


def mlp_rows(chunk, x_ref, up_ref, w_ref, back_ref, forward_ref, kept):
    count = x_ref.shape[0]
    rows = back_ref.shape[2]

    @pl.loop(0, count // chunk)
    def _(i):
        at = pl.ds(pl.multiple_of(i * chunk, chunk), chunk)
        gate_up = dot(x_ref[at, :], w_ref[:, : 2 * SLICE], 1, 0)
        left, right = gate_up[:, :SLICE], gate_up[:, SLICE:]
        grad_mixed = dot(up_ref[at, :], w_ref[:, 2 * SLICE :], 1, 0)
        normal_cdf = 0.5 * (1.0 + lax.erf(left * 0.7071067811865476))
        gelu = left * normal_cdf
        density = jnp.exp(-0.5 * left * left) * 0.3989422804014327
        kept[at, :SLICE] = (grad_mixed * right * (normal_cdf + left * density)).astype(BF)
        kept[at, SLICE : 2 * SLICE] = (grad_mixed * gelu).astype(BF)
        kept[at, 2 * SLICE :] = (gelu * right).astype(BF)
        back = dot(kept[at, : 2 * SLICE], w_ref[:, : 2 * SLICE], 1, 1).astype(BF)
        forward = dot(kept[at, 2 * SLICE :], w_ref[:, 2 * SLICE :], 1, 1).astype(BF)
        pairs = chunk // rows // 2
        for j in range(chunk // rows):
            piece = slice(j * rows, (j + 1) * rows)
            back_ref[i * pairs + j // 2, j % 2] = back[piece]
            forward_ref[i * pairs + j // 2, j % 2] = forward[piece]


def mlp_weights_back(chunk, x_ref, up_ref, kept, terms_ref):
    @pl.loop(0, x_ref.shape[1] // chunk)
    def _(i):
        at = pl.ds(pl.multiple_of(i * chunk, chunk), chunk)
        terms_ref[at, : 2 * SLICE] = dot(x_ref[:, at], kept[:, : 2 * SLICE], 0, 0).astype(BF)
        terms_ref[at, 2 * SLICE :] = dot(up_ref[:, at], kept[:, 2 * SLICE :], 0, 0).astype(BF)


def turn_kernel(
    groups,
    reach,
    lines,
    x,
    up,
    mlp_weights,
    middle,
    d_out,
    w_attn,
    gains,
    attended,
    grads,
    grad_middle,
    attn_part,
    carry,
    forward,
    terms,
    kept,
    partial,
    columns,
    total,
    outgoing,
    branch,
    a2a_send,
    a2a_recv,
    own,
    side_send,
    side_recv,
    side_own,
    *rest,
):
    place = Place(groups, reach)
    group = groups * reach
    lanes = branch.shape[2]
    sums = Sum(place, terms, 0, None, *rest[7:])
    count = rest[7].shape[1]
    devices = everyone(place, lines)
    sums.clear()
    greet(devices)
    mlp_rows(512, x, up, mlp_weights, partial, forward, kept)
    pl.semaphore_wait(pltpu.get_barrier_semaphore(), len(devices))
    halving = Halving(place, 2, partial, total, rest[:7])
    halving.start()
    mlp_weights_back(512, x, up, kept, terms)
    sums.start(0)
    sums.start(1)
    halving.pair()
    halving.halve(0)
    halving.halve(1)
    for q in range(2, count):
        sums.start(q)
    halving.finish()
    normed, inverse_std = norm_parts(middle[...])
    upstream = total[...]
    grad = d_out[...].astype(F32) + norm_back(upstream, normed, inverse_std, gains[1:2, :])
    grad_middle[...] = grad
    low = grad.astype(BF)
    for g in range(groups):
        branch[g] = low[:, g * lanes : (g + 1) * lanes]
    outgoing[...] = dot(w_attn[...], low, 1, 1).astype(BF).reshape(outgoing.shape)
    copies = spread(place, outgoing, grads, (a2a_send, a2a_recv, own))
    for step in range(1, groups):
        peer = (place.head + step) % groups
        copies.append(
            push(
                branch.at[peer],
                columns.at[place.head],
                {"heads": peer},
                side_send.at[step - 1],
                side_recv.at[step - 1],
            )
        )
    local = pltpu.make_async_copy(branch.at[place.head], columns.at[place.head], side_own)
    local.start()
    for copy in copies[-(groups - 1) :]:
        copy.wait()
    local.wait()
    attn_part[...] = functools.reduce(
        jnp.add, [dot(attended[g], columns[g], 1, 0) for g in range(groups)]
    ).astype(BF)
    for copy in copies[: -(groups - 1)]:
        copy.wait()
    sums.finish()
    for d in range(2):
        for q in range(2):
            carry[d, q] = sums.land[d, count - 2 + q]


def turn_step(x, up, mlp_weights, middle, d_out, w_attn, gains, attended, lines, groups, reach):
    rows, width = middle.shape
    count = lines * groups // 8 - 1
    half = (width // (2 * (count + 1)), 3 * SLICE)
    group = groups * reach
    return pl.pallas_call(
        functools.partial(turn_kernel, groups, reach, lines),
        in_specs=[VMEM] * 8,
        out_specs=[ANY, VMEM, VMEM, VMEM, VMEM, VMEM],
        out_shape=[
            jax.ShapeDtypeStruct((group, HD, rows), BF),
            jax.ShapeDtypeStruct((rows, width), F32),
            jax.ShapeDtypeStruct((width, width // groups), BF),
            jax.ShapeDtypeStruct((2, 2, *half), BF),
            jax.ShapeDtypeStruct((4, 2, rows, width), BF),
            jax.ShapeDtypeStruct((width, 3 * SLICE), BF),
        ],
        scratch_shapes=[
            pltpu.VMEM((8 * rows, 3 * SLICE), BF),
            pltpu.VMEM((4, 2, rows, width), BF),
            pltpu.VMEM((groups, rows, width // groups), BF),
            pltpu.VMEM((rows, width), F32),
            pltpu.VMEM((group, HD, rows), BF),
            pltpu.VMEM((groups, rows, width // groups), BF),
            DMA((group - 1,)),
            DMA((group - 1,)),
            DMA,
            DMA((groups - 1,)),
            DMA((groups - 1,)),
            DMA,
            *Halving.scratch(2, rows, width),
            *Sum.scratch(count, half),
        ],
        compiler_params=pltpu.CompilerParams(
            collective_id=2, has_side_effects=True, vmem_limit_bytes=40 << 20
        ),
        cost_estimate=pl.CostEstimate(flops=1 << 33, bytes_accessed=12 << 20, transcendentals=0),
        name="turn_step",
    )(x, up, mlp_weights, middle, d_out, w_attn, gains, attended)


def end_part(
    place,
    lines,
    partial,
    weight,
    mlp,
    attn,
    total,
    mlp_all,
    weight_all,
    attn_all,
    sum_line,
    sum_attn,
    lined,
    summed,
    swap_send,
    swap_recv,
    own,
    *rest,
):
    groups, reach = place.groups, place.reach
    sub = mlp.shape[0]
    mine, head = place.ctx % sub, place.head
    wide = Halving(place, 3, partial, total, rest[:7], [2, 1])
    swap = Lines(lines, weight, lined, *rest[7:10])
    wide.start()
    swap.start()
    wide.pair()
    sum_line()
    swaps = []
    for step in range(1, sub):
        peer = (mine + step) % sub
        swaps.append(
            push(
                mlp.at[peer],
                mlp_all.at[mine, head],
                {"ctx": place.ctx - mine + peer},
                swap_send.at[step - 1],
                swap_recv.at[step - 1],
            )
        )
    pieces = [(mlp.at[mine], lambda h: mlp_all.at[mine, h]), (attn, lambda h: attn_all.at[h])]
    for step in range(1, sub):
        source = (mine - step + sub) % sub
        pieces.append(
            (mlp_all.at[source, head], lambda h, source=source: mlp_all.at[source, h])
        )
    pieces.append((summed, lambda h: weight_all.at[h]))
    collect = Collect(groups, pieces, *rest[10:14])
    local = [
        pltpu.make_async_copy(mlp.at[mine], mlp_all.at[mine, head], own.at[0]),
        pltpu.make_async_copy(attn, attn_all.at[head], own.at[1]),
        pltpu.make_async_copy(summed, weight_all.at[head], own.at[2]),
    ]
    local[0].start()
    collect.start(0)
    sum_attn()
    local[1].start()
    collect.start(1)
    for step in range(1, sub):
        swaps[step - 1].wait_recv()
        collect.start(step + 1)
    wide.halve(0)
    swap.finish()
    for r in range(reach):
        summed[r] = functools.reduce(
            jnp.add, [lined[r + reach * g].astype(F32) for g in range(lines // reach)]
        ).astype(BF)
    local[2].start()
    collect.start(sub + 1)
    wide.halve(1)
    collect.forward(0)
    collect.forward(1)
    wide.halve(2)
    for n in range(2, sub + 2):
        collect.forward(n)
    for copy in local:
        copy.wait()
    for copy in swaps:
        copy.wait_send()
    collect.finish()
    wide.finish()


def attend_back_kernel(
    groups,
    reach,
    lines,
    tile,
    qkv_ref,
    grad_ref,
    wide_ref,
    lse_ref,
    x_ref,
    w_ref,
    cos_ref,
    sin_ref,
    forward_ref,
    terms,
    carry,
    attn_ref,
    ahead_ref,
    total,
    mlp_all,
    weight_all,
    attn_all,
    out_ref,
    weight_ref,
    attn_out_ref,
    mlp_ref,
    sums,
    queries,
    weight,
    attn_land,
    *sems,
):
    count = x_ref.shape[0]
    rows = grad_ref.shape[2]
    steps, per_tile = count // tile, tile // rows
    step = pl.program_id(0)
    place = Place(groups, reach)
    halving = Halving(place, 2, forward_ref, ahead_ref, sems[:7])
    swap = Lines(lines, attn_ref, attn_land, *sems[7:10])
    length = lines * groups // 8
    line = Sum(place, terms, length - 1, carry, *sems[10:14])

    @pl.when(step == 0)
    def _():
        line.clear()
        meet(everyone(place, lines))
        line.start(0)
        line.start(1)
        halving.start()
        swap.start()
        sums[...] = jnp.zeros_like(sums)

    here = pl.ds(pl.multiple_of(step * tile, tile), tile)
    query = qkv_ref[:QM_END, here]
    grad = jnp.concatenate([grad_ref[step * per_tile + k] for k in range(per_tile)], axis=1)
    delta = jnp.sum(grad.astype(F32) * wide_ref[:, here], axis=0, keepdims=True)
    lse = lse_ref[:, here]
    grad_query = jnp.zeros((HD, tile), F32)
    for j in range(steps):
        keys = slice(j * tile, (j + 1) * tile)
        prob = jnp.exp(dot(qkv_ref[QM_END:KM_END, keys], query, 0, 0) - lse)
        grad_prob = dot(qkv_ref[KM_END:, keys], grad, 0, 0)
        grad_score = (prob * (grad_prob - delta)).astype(BF)
        grad_query += dot(qkv_ref[QM_END:K_END, keys], grad_score, 1, 0)
        sums[:HD, keys] += dot(query[:HD], grad_score, 1, 1)
        sums[HD:, keys] += dot(grad, prob.astype(BF), 1, 1)
    queries[:, here] = (grad_query * 0.125).astype(BF)

    pl.when(step == 0)(halving.pair)

    @pl.when(step == min(2, steps - 1))
    def _():
        halving.halve(0)
        for q in range(2, length - 1):
            line.start(q)


    @pl.when(step == steps - 1)
    def _():
        weight[...] = jnp.zeros_like(weight)

        @pl.loop(0, steps)
        def _(i):
            at = pl.ds(pl.multiple_of(i * tile, tile), tile)
            cosine, sine = cos_ref[:, at], sin_ref[:, at]

            def turn_back(value):
                front, back = value[:HALF], value[HALF:]
                return [front * cosine + back * sine, back * cosine - front * sine]

            low = lambda value: value.astype(BF).astype(F32)
            projected = jnp.concatenate(
                [
                    *turn_back(queries[:, at].astype(F32)),
                    *turn_back(low(sums[:HD, at])),
                    low(sums[HD:, at]),
                ],
                axis=0,
            ).astype(BF)
            part = dot(projected, w_ref[...], 0, 1).astype(BF)
            for k in range(per_tile):
                out_ref[(i * per_tile + k) // 2, k % 2] = part[k * rows : (k + 1) * rows]
            weight[...] += dot(projected, x_ref[at, :], 1, 0)

        shard = weight_ref.shape[2]
        for c in range(lines):
            weight_ref[c] = weight[:, c * shard : (c + 1) * shard].astype(BF)
        halving.halve(1)
        half = line.half

        def sum_line():
            line.finish()
            for k in range(2):
                q = length - 3 + k
                value = (
                    line.block(line.spot, k).astype(F32)
                    + line.land[0, q].astype(F32)
                    + line.land[1, q].astype(F32)
                ).astype(BF)
                if mlp_ref.shape[0] == 2:
                    mlp_ref[k] = value
                else:
                    mlp_ref[0, k * half : (k + 1) * half] = value

        def sum_attn():
            swap.finish()
            attn_out_ref[...] = functools.reduce(
                jnp.add, [attn_land[c].astype(F32) for c in range(lines)]
            ).astype(BF)

        end_part(
            place,
            lines,
            out_ref,
            weight_ref,
            mlp_ref,
            attn_out_ref,
            total,
            mlp_all,
            weight_all,
            attn_all,
            sum_line,
            sum_attn,
            *sems[14:],
        )
        halving.finish()


def attend_back(qkv, grad, wide, lse, x, w, cosine, sine, forward, terms, carry, attn, groups, reach, tile):
    count, width = x.shape
    blocks, _, rows = grad.shape
    lines, shard, lanes = attn.shape
    sub = 8 // groups
    length = lines // sub
    whole = lambda *shape: pl.BlockSpec(shape, lambda i: (0,) * len(shape))
    operands = (qkv, grad, wide, lse, x, w, cosine, sine, forward, terms, carry)
    return pl.pallas_call(
        functools.partial(attend_back_kernel, groups, reach, lines, tile),
        grid=(count // tile,),
        in_specs=[*[whole(*operand.shape) for operand in operands], ANY],
        out_specs=[whole(rows, width), whole(rows, width), ANY, ANY, ANY],
        out_shape=[
            jax.ShapeDtypeStruct((rows, width), F32),
            jax.ShapeDtypeStruct((rows, width), F32),
            jax.ShapeDtypeStruct((sub, groups, shard, 3 * SLICE), BF),
            jax.ShapeDtypeStruct((groups, reach, 3 * HD, shard), BF),
            jax.ShapeDtypeStruct((groups, shard, lanes), BF),
        ],
        scratch_shapes=[
            pltpu.VMEM((blocks // 2, 2, rows, width), BF),
            pltpu.VMEM((lines, 3 * HD, shard), BF),
            pltpu.VMEM((shard, lanes), BF),
            pltpu.VMEM((sub, shard, 3 * SLICE), BF),
            pltpu.VMEM((2 * HD, count), F32),
            pltpu.VMEM((HD, count), BF),
            pltpu.VMEM((3 * HD, width), F32),
            pltpu.VMEM((lines, shard, lanes), BF),
            *Halving.scratch(2, rows, width),
            *Lines.scratch(lines),
            *Sum.scratch(length - 1, (width // (2 * length), 3 * SLICE)),
            pltpu.VMEM((lines, 3 * HD, shard), BF),
            pltpu.VMEM((reach, 3 * HD, shard), BF),
            DMA((max(sub - 1, 1),)),
            DMA((max(sub - 1, 1),)),
            DMA((3,)),
            *Halving.scratch(3, rows, width),
            *Lines.scratch(lines),
            *Collect.scratch(sub + 2, groups),
        ],
        compiler_params=pltpu.CompilerParams(
            collective_id=4, has_side_effects=True, vmem_limit_bytes=44 << 20
        ),
        cost_estimate=pl.CostEstimate(
            flops=count * count * HD * 20, bytes_accessed=count * 6144, transcendentals=count * count
        ),
        name="attend_back",
    )(*operands, attn)


class Collect:
    def __init__(self, groups, pieces, far_send, far_recv, near_send, near_recv):
        head = lax.axis_index("heads")
        self.half = half = groups // 2
        pair = {"heads": flip(head, 1)}
        self.far, self.near = [], []
        for n, (piece, where) in enumerate(pieces):
            self.far.append(
                [
                    remote(
                        piece,
                        where(head),
                        {"heads": (head + 2 * k) % groups},
                        far_send.at[n, k - 1],
                        far_recv.at[n, k - 1],
                    )
                    for k in range(1, half)
                ]
            )
            sides = [(piece, where(head))]
            for k in range(1, half):
                got = where((head - 2 * k + groups) % groups)
                sides.append((got, got))
            self.near.append(
                [
                    remote(source, target, pair, near_send.at[n, k], near_recv.at[n, k])
                    for k, (source, target) in enumerate(sides)
                ]
            )

    @staticmethod
    def scratch(count, groups):
        far, near = (count, max(groups // 2 - 1, 1)), (count, groups // 2)
        return [DMA(far), DMA(far), DMA(near), DMA(near)]

    def start(self, n):
        for copy in self.far[n]:
            copy.start()
        self.near[n][0].start()

    def forward(self, n):
        for k, copy in enumerate(self.far[n]):
            copy.wait_recv()
            self.near[n][k + 1].start()

    def finish(self):
        for copies in self.far:
            for copy in copies:
                copy.wait_send()
        for copies in self.near:
            for copy in copies:
                copy.wait()


def assemble_kernel(
    upstream,
    tokens,
    grad_middle,
    gains,
    middle,
    ahead,
    weight_all,
    attn_all,
    mlp_all,
    w_qkv,
    w_in,
    own_gains,
    result,
    grad,
    sum_qkv,
    sum_attn,
    sum_in,
    sum_out,
    gain_sums,
):
    groups, reach, _, shard = weight_all.shape
    lanes = attn_all.shape[2]
    result[...] = (middle[...] + ahead[...]).astype(BF)
    normed, inverse_std = norm_parts(tokens[...].astype(F32))
    grad[...] = grad_middle[...] + norm_back(upstream[...], normed, inverse_std, gains[0:1, :])
    for g in range(groups):
        sum_attn[:, g * lanes : (g + 1) * lanes] = attn_all[g].astype(F32)
    gain_one = jnp.zeros((shard, 128), F32)
    for third in range(3):
        part = slice(third * HD, (third + 1) * HD)
        for pair in range(H // 2):
            r, g = 2 * pair // groups, 2 * pair % groups
            tile = (
                jnp.concatenate([weight_all[g, r, part], weight_all[g + 1, r, part]], axis=0)
                .astype(F32)
                .T
            )
            at = third * H * HD + pair * 2 * HD
            sum_qkv[:, at : at + 2 * HD] = tile
            gain_one += tile * w_qkv[:, at : at + 2 * HD].astype(F32)
    gain_two = jnp.zeros((shard, 1), F32)
    for t in range(8):
        start, wide = slice_place(t)
        for half in range(2):
            piece = mlp_all[t, :, half * SLICE : half * SLICE + wide].astype(F32)
            at = half * FF + start
            sum_in[:, at : at + wide] = piece
            gain_two += jnp.sum(
                piece * w_in[:, at : at + wide].astype(F32), axis=1, keepdims=True
            )
        sum_out[start : start + wide, :] = (
            mlp_all[t, :, 2 * SLICE : 3 * SLICE].astype(F32).T[:wide]
        )
    one = jnp.sum(gain_one, axis=1, keepdims=True)
    lane = lax.broadcasted_iota(jnp.int32, (shard, 128), 1)
    both = jnp.where(lane == 0, one, gain_two).T
    gain_sums[...] = both[:8] / own_gains[...]


def assemble(upstream, tokens, grad_middle, gains, middle, ahead, weight_all, attn_all, mlp_all, w_qkv, w_in, own_gains):
    rows, width = tokens.shape
    shard = w_qkv.shape[0]
    return pl.pallas_call(
        assemble_kernel,
        in_specs=[VMEM] * 12,
        out_specs=[VMEM] * 7,
        out_shape=[
            jax.ShapeDtypeStruct((rows, width), BF),
            jax.ShapeDtypeStruct((rows, width), F32),
            jax.ShapeDtypeStruct((shard, 3 * width), F32),
            jax.ShapeDtypeStruct((shard, width), F32),
            jax.ShapeDtypeStruct((shard, 2 * FF), F32),
            jax.ShapeDtypeStruct((FF, shard), F32),
            jax.ShapeDtypeStruct((8, shard), F32),
        ],
        compiler_params=pltpu.CompilerParams(vmem_limit_bytes=24 << 20),
        cost_estimate=pl.CostEstimate(flops=1 << 24, bytes_accessed=20 << 20, transcendentals=0),
        name="assemble",
    )(upstream, tokens, grad_middle, gains, middle, ahead, weight_all, attn_all, mlp_all, w_qkv, w_in, own_gains)


def slice_start(t):
    return 128 * jnp.minimum(3 * t, 2 * t + 5)


def slice_place(t):
    start = 128 * min(3 * t, 2 * t + 5)
    return start, min(128 * min(3 * t + 3, 2 * t + 7), FF) - start


def body(count, tokens, d_out, segment_ids, position_ids, w_qkv, w_attn, w_in, w_out, gain_attn, gain_mlp):
    groups = lax.axis_size("heads")
    rows, width = tokens.shape
    shard = w_qkv.shape[0]
    reach = SEQ_MAX // (rows * groups)
    group = reach * groups
    sub = 8 // groups
    ctx, head = lax.axis_index("ctx"), lax.axis_index("heads")
    assert group == H and sub * groups == 8
    total = group * rows
    tile = 512

    def mlp_slice(value, axis, start, t):
        pads = [(0, 0), (0, 0)]
        pads[axis] = (0, SLICE)
        piece = lax.dynamic_slice_in_dim(jnp.pad(value, pads), start + slice_start(t), SLICE, axis)
        wide = jnp.minimum(slice_start(t + 1), FF) - slice_start(t)
        shape = [1, 1]
        shape[axis] = SLICE
        return jnp.where(jnp.arange(SLICE).reshape(shape) < wide, piece, jnp.zeros_like(piece))

    def mlp_part(t):
        return jnp.concatenate(
            [mlp_slice(w_in, 1, 0, t), mlp_slice(w_in, 1, FF, t), mlp_slice(w_out, 0, 0, t).T], axis=1
        )

    mlp = jnp.stack([mlp_part(x * groups + head) for x in range(sub)])
    gains_own = jnp.pad(jnp.stack([gain_attn, gain_mlp]).astype(F32), ((0, 6), (0, -shard % 128)))
    ids = jnp.pad(jnp.stack([position_ids, segment_ids]), ((0, 6), (0, 0)))
    freqs = jnp.power(160000.0, -(2.0 * jnp.arange(HALF, dtype=F32)) / HD)[:, None]
    input_all, gains, w_head, cosine, sine, marks, attn_half = begin(
        tokens, gains_own, ids, w_qkv, w_attn, freqs, count // sub, count, groups, reach
    )
    x = input_all.reshape(total, width)

    attended, wide, lse, qkv, attn_weights, mlp_pair, mlp_near = attend(
        x,
        w_head,
        cosine,
        sine,
        marks,
        attn_half,
        mlp.reshape(2, sub * shard // 2, 3 * SLICE),
        count,
        groups,
        reach,
        rows,
        tile,
    )
    attn_weights = attn_weights.reshape(width, width)
    mlp_all, upstream, middle, attended, mlp_weights = middle_step(
        attended, tokens, d_out, attn_weights, gains, mlp_pair, mlp_near, count, groups, reach
    )
    mlp_weights = mlp_weights.reshape(width, 3 * SLICE)
    grad_heads, grad_middle, attn_part, carry, forward, mlp_terms = turn_step(
        mlp_all.reshape(8 * rows, width),
        upstream.reshape(8 * rows, width),
        mlp_weights,
        middle,
        d_out,
        attn_weights,
        gains,
        attended.reshape(groups, width, rows),
        count,
        groups,
        reach,
    )
    attn_part = attn_part.reshape(count, shard, width // groups)
    ahead, upstream_in, mlp_all, weight_all, attn_all = attend_back(
        qkv,
        grad_heads,
        wide,
        lse,
        x,
        w_head,
        cosine,
        sine,
        forward,
        mlp_terms,
        carry,
        attn_part,
        groups,
        reach,
        tile,
    )
    result, grad_input, sum_qkv, sum_attn, sum_in, sum_out, gain_sums = assemble(
        upstream_in,
        tokens,
        grad_middle,
        gains,
        middle,
        ahead,
        weight_all,
        attn_all,
        mlp_all.reshape(8, shard, 3 * SLICE),
        w_qkv,
        w_in,
        jnp.pad(gains_own[:2, :shard], ((0, 6), (0, 0)), constant_values=1.0),
    )
    return (
        result,
        grad_input,
        sum_qkv,
        sum_attn,
        sum_in,
        sum_out,
        gain_sums[0],
        gain_sums[1],
    )


def solution(mesh):
    return jax.shard_map(
        functools.partial(body, mesh.shape["ctx"]),
        mesh=mesh,
        in_specs=(
            P(("ctx", "heads"), None),
            P(("ctx", "heads"), None),
            P(("ctx", "heads")),
            P(("ctx", "heads")),
            P("ctx", None),
            P("ctx", None),
            P("ctx", None),
            P(None, "ctx"),
            P("ctx"),
            P("ctx"),
        ),
        out_specs=(
            P(("ctx", "heads"), None),
            P(("ctx", "heads"), None),
            P("ctx", None),
            P("ctx", None),
            P("ctx", None),
            P(None, "ctx"),
            P("ctx"),
            P("ctx"),
        ),
        check_vma=False,
    )
```

```python
import functools

import jax
import jax.numpy as jnp
from jax import lax
from jax.experimental import pallas as pl
from jax.experimental.pallas import tpu as pltpu
from jax.sharding import PartitionSpec as P

H = 16
HD = 64
HALF = HD // 2
FF = 2624
SEQ_MAX = 2048
MASKED = -1e30
MARKS = 16
QM_END = HD + MARKS
K_END = QM_END + HD
KM_END = K_END + MARKS
V_END = KM_END + HD
SLICE = 384
BF = jnp.bfloat16
F32 = jnp.float32
MESH = pl.DeviceIdType.MESH
VMEM = pl.BlockSpec(memory_space=pltpu.VMEM)
ANY = pl.BlockSpec(memory_space=pl.ANY)
DMA = pltpu.SemaphoreType.DMA


def dot(left, right, left_dim, right_dim):
    return lax.dot_general(
        left, right, (((left_dim,), (right_dim,)), ((), ())), preferred_element_type=F32
    )


def norm_parts(values):
    average = jnp.mean(values, axis=-1, keepdims=True)
    centred = values - average
    inverse_std = lax.rsqrt(jnp.mean(centred * centred, axis=-1, keepdims=True) + 1e-05)
    return centred * inverse_std, inverse_std


def norm_back(upstream, normed, inverse_std, gain):
    scaled = upstream * gain
    return inverse_std * (
        scaled
        - jnp.mean(scaled, axis=-1, keepdims=True)
        - normed * jnp.mean(scaled * normed, axis=-1, keepdims=True)
    )


def flip(value, bit):
    return value + bit - 2 * bit * (value // bit % 2)


class Place:
    def __init__(self, groups, reach):
        self.groups, self.reach = groups, reach
        self.ctx = lax.axis_index("ctx")
        self.head = lax.axis_index("heads")
        self.local = self.ctx % reach
        self.base = self.ctx - self.local
        self.idx = self.local * groups + self.head

    def member(self, j):
        return {"ctx": self.base + j // self.groups, "heads": j % self.groups}


def greet(devices):
    barrier = pltpu.get_barrier_semaphore()
    for device in devices:
        pl.semaphore_signal(barrier, inc=1, device_id=device, device_id_type=MESH)


def meet(devices):
    greet(devices)
    pl.semaphore_wait(pltpu.get_barrier_semaphore(), len(devices))


def remote(source, target, device, send, recv):
    return pltpu.make_async_remote_copy(
        src_ref=source,
        dst_ref=target,
        send_sem=send,
        recv_sem=recv,
        device_id=device,
        device_id_type=MESH,
    )


def push(*operands):
    copy = remote(*operands)
    copy.start()
    return copy


def tree_parts(axes, rows):
    part = -(-rows // axes // 16) * 16
    starts = [min(part * a, rows) for a in range(axes + 1)]
    return [(starts[a], starts[a + 1] - starts[a]) for a in range(axes)]


class Tree:
    def __init__(self, place, axes, source, target, sems):
        self.place, self.axes, self.source, self.target = place, axes, source, target
        self.send, self.recv, self.core_send, self.core_recv, self.own = sems
        self.slots = 2 << axes
        self.levels, self.cores = [], []

    @staticmethod
    def scratch(axes):
        far, near = axes * axes, axes * axes + 1
        return [DMA((far,)), DMA((far,)), DMA((near,)), DMA((near,)), DMA]

    def origin(self, level, first):
        value = self.place.idx
        for k in range(level):
            value = flip(value, 2 << ((first + k) % self.axes))
        return value % self.slots

    def neighbour(self, axis):
        return self.place.member(flip(self.place.idx, 2 << (axis % self.axes)))

    def piece(self, slot, part):
        return self.target.at[slot] if part is None else self.target.at[slot, pl.ds(*part)]

    def to_core(self, source, slot, part):
        at = len(self.cores)
        self.cores.append(
            push(
                source,
                self.piece(slot, part),
                self.place.member(flip(self.place.idx, 1)),
                self.core_send.at[at],
                self.core_recv.at[at],
            )
        )

    def start(self):
        me = self.place.idx % self.slots
        self.levels.append(
            [
                push(
                    self.source, self.target.at[me], self.neighbour(a), self.send.at[a], self.recv.at[a]
                )
                for a in range(self.axes)
            ]
        )
        self.to_core(self.source, me, None)
        self.local = pltpu.make_async_copy(self.source, self.target.at[me], self.own)
        self.local.start()

    def forward(self, level):
        axes = self.axes
        parts = tree_parts(axes, self.target.shape[1])
        onward = []
        for a in range(axes):
            self.levels[level - 1][a].wait_recv()
            slot = self.origin(level, a)
            if level < axes:
                part = parts[a] if level + 1 == axes else None
                at = level * axes + a
                piece = self.piece(slot, part)
                onward.append(
                    push(piece, piece, self.neighbour(a + level), self.send.at[at], self.recv.at[at])
                )
                self.to_core(self.target.at[slot], slot, None)
            else:
                self.to_core(self.piece(slot, parts[a]), slot, parts[a])
        self.levels.append(onward)

    def finish(self):
        self.local.wait()
        for level in self.levels:
            for copy in level:
                copy.wait_send()
        for copy in self.cores:
            copy.wait()


class Halving:
    def __init__(self, place, axes, value, result, scratch, firsts=None):
        self.firsts = firsts = firsts or list(range(axes))
        self.axes, self.value, self.result = axes, value, result
        self.other, self.held, self.land, send, recv, send0, recv0 = scratch
        self.blocks = 1 << axes
        width = value.shape[-1]
        part = width // len(firsts)
        self.columns = [pl.ds(part * a, part) for a in range(len(firsts))]
        self.core = place.idx % 2
        self.chip = place.idx // 2 % self.blocks
        self.sources = []
        for j in range(self.blocks):
            k = self.chip
            for a in range(axes):
                if j >> a & 1:
                    k = flip(k, 1 << a)
            self.sources.append(k)
        self.first, self.copies = [], {}
        for p in range(len(firsts)):
            self.first.append(
                remote(
                    value.at[:, 1 - self.core, :, self.columns[p]],
                    self.other.at[:, :, self.columns[p]],
                    place.member(flip(place.idx, 1)),
                    send0.at[p],
                    recv0.at[p],
                )
            )
            for step in range(axes):
                bit, sent = self.sent(p, step)
                for j in sent:
                    self.copies[p, j] = remote(
                        self.held.at[j, :, self.columns[p]],
                        self.land.at[j, :, self.columns[p]],
                        place.member(flip(place.idx, 2 * bit)),
                        send.at[p, j],
                        recv.at[p, j],
                    )

    @staticmethod
    def scratch(axes, rows, width):
        blocks = 1 << axes
        return [
            pltpu.VMEM((blocks, rows, width), BF),
            pltpu.VMEM((blocks, rows, width), BF),
            pltpu.VMEM((blocks, rows, width), BF),
            DMA((axes, blocks)),
            DMA((axes, blocks)),
            DMA((axes,)),
            DMA((axes,)),
        ]

    def sent(self, part, step):
        first = self.firsts[part]
        seen = [1 << ((first + s) % self.axes) for s in range(step)]
        bit = 1 << ((first + step) % self.axes)
        return bit, [j for j in range(self.blocks) if j & bit and not any(j & s for s in seen)]

    def start(self):
        for copy in self.first:
            copy.start()

    def pair(self):
        for p in range(len(self.firsts)):
            cols = self.columns[p]
            self.first[p].wait_recv()
            _, early = self.sent(p, 0)
            for j in early + [j for j in range(self.blocks) if j not in early]:
                k = self.sources[j]
                self.held[j, :, cols] = (
                    self.value[k, self.core, :, cols].astype(F32) + self.other[k, :, cols].astype(F32)
                ).astype(BF)
                if j in early:
                    self.copies[p, j].start()

    def halve(self, step):
        for p in range(len(self.firsts)):
            cols = self.columns[p]
            bit, arrived = self.sent(p, step)
            onward = self.sent(p, step + 1)[1] if step + 1 < self.axes else []
            for j in sorted(arrived, key=lambda j: (j - bit) not in onward):
                self.copies[p, j].wait_recv()
                k = j - bit
                total = self.held[k, :, cols].astype(F32) + self.land[j, :, cols].astype(F32)
                if step + 1 < self.axes:
                    self.held[k, :, cols] = total.astype(BF)
                    if k in onward:
                        self.copies[p, k].start()
                else:
                    self.result[:, cols] = total

    def run(self):
        self.start()
        self.pair()
        for step in range(self.axes):
            self.halve(step)
        self.finish()

    def finish(self):
        for copy in self.first:
            copy.wait_send()
        for copy in self.copies.values():
            copy.wait_send()


class Lines:
    def __init__(self, count, source, target, send, recv, own):
        me = lax.axis_index("ctx")
        self.copies = [pltpu.make_async_copy(source.at[me], target.at[me], own)]
        for step in range(1, count):
            peer = (me + step) % count
            self.copies.append(
                remote(source.at[peer], target.at[me], {"ctx": peer}, send.at[step - 1], recv.at[step - 1])
            )

    @staticmethod
    def scratch(count):
        return [DMA((count - 1,)), DMA((count - 1,)), DMA]

    def start(self):
        for copy in self.copies:
            copy.start()

    def finish(self):
        for copy in self.copies:
            copy.wait()


def everyone(place, count):
    group = place.reach * place.groups
    mates = [place.member((place.idx + step) % group) for step in range(1, group)]
    outside = [{"ctx": (place.base + place.reach + step) % count} for step in range(count - place.reach)]
    return mates + outside


def spread(place, source, target, sems, me=None):
    send, recv, own = sems
    count = target.shape[0]
    copies = []
    for step in range(1, count):
        peer = (place.idx + step) % count
        copies.append(
            push(
                source.at[peer],
                target.at[place.idx],
                place.member(peer),
                send.at[step - 1],
                recv.at[step - 1],
            )
        )
    local = pltpu.make_async_copy(source.at[place.idx], target.at[place.idx], own)
    local.start()
    copies.append(local)
    return copies


def begin_kernel(
    groups,
    reach,
    count,
    tokens,
    gains,
    ids,
    w_qkv,
    w_attn,
    freqs,
    input_all,
    gains_all,
    w_head,
    cosine,
    sine,
    marks,
    attn_half,
    ids_all,
    slab,
    mine,
    gain_land,
    own_sems,
    ids_send,
    ids_recv,
    gain_send,
    gain_recv,
    slab_send,
    slab_recv,
    wide_send,
    wide_recv,
    core_send,
    core_recv,
    *tree_sems,
):
    place = Place(groups, reach)
    group = reach * groups
    ctx, head, idx = place.ctx, place.head, place.idx
    shard = w_qkv.shape[0]
    ring = attn_half.shape[0]
    sub = count // ring
    side, spot = ctx % sub, ctx // sub
    lanes = attn_half.shape[2] // groups
    core = {"heads": flip(head, 1)}
    mates = [place.member((idx + step) % group) for step in range(1, group)]
    lines = [{"ctx": (ctx + step) % count} for step in range(1, count)]
    meet(everyone(place, count))
    first = [
        push(gains, gain_land.at[ctx], lines[step - 1], gain_send.at[step - 1], gain_recv.at[step - 1])
        for step in range(1, count)
    ]
    small = [
        push(ids, ids_all.at[idx], mates[step - 1], ids_send.at[step - 1], ids_recv.at[step - 1])
        for step in range(1, group)
    ]
    half = pl.ds(pl.multiple_of(head % 2 * (shard // 2), 16), shard // 2)
    thirds = []
    for step in range(1, count):
        peer = (ctx + step) % count
        column = ((peer % reach) * groups + head) // 2 * 128
        for third in range(3):
            start = pl.multiple_of(third * 1024 + column, 128)
            thirds.append(
                push(
                    w_qkv.at[half, pl.ds(start, 128)],
                    slab.at[ctx, half, pl.ds(third * 128, 128)],
                    lines[step - 1],
                    slab_send.at[step - 1, third],
                    slab_recv.at[step - 1, third],
                )
            )
    gain_land[ctx] = gains[...]
    where = lambda h: pl.ds(pl.multiple_of(h * lanes, 128), lanes)
    across = where(head)
    own = [
        pltpu.make_async_copy(ids, ids_all.at[idx], own_sems.at[3]),
        pltpu.make_async_copy(w_attn.at[:, across], attn_half.at[spot, :, across], own_sems.at[4]),
    ]
    for third in range(3):
        start = pl.multiple_of(third * 1024 + idx // 2 * 128, 128)
        own.append(
            pltpu.make_async_copy(
                w_qkv.at[half, pl.ds(start, 128)],
                slab.at[ctx, half, pl.ds(third * 128, 128)],
                own_sems.at[third],
            )
        )
    for copy in own:
        copy.start()
    for copy in first:
        copy.wait_recv()
    gain, gain_two = (
        jnp.concatenate([gain_land[c, k : k + 1, :shard] for c in range(count)], axis=1)
        for k in range(2)
    )
    normed, _ = norm_parts(tokens[...].astype(F32))
    mine[...] = (normed * gain).astype(BF)
    tree = Tree(place, 3, mine, input_all, tree_sems[:5])
    tree.start()
    gains_all[0:1, :] = gain
    gains_all[1:2, :] = gain_two
    late = []
    for step in range(1, ring):
        late.append(
            push(
                w_attn.at[:, across],
                attn_half.at[spot, :, across],
                {"ctx": (spot + step) % ring * sub + side},
                wide_send.at[step - 1],
                wide_recv.at[step - 1],
            )
        )
    tree.forward(1)
    for copy in own:
        copy.wait()
    for copy in thirds:
        copy.wait_recv()
    for copy in late:
        copy.wait_recv()
    collect = Collect(
        groups, [(attn_half.at[:, :, across], lambda h: attn_half.at[:, :, where(h)])], *tree_sems[5:]
    )
    collect.start(0)
    shared = push(slab.at[:, half], slab.at[:, half], core, core_send, core_recv)
    for copy in small:
        copy.wait()
    row = lambda k: jnp.concatenate([ids_all[j, k : k + 1, :] for j in range(group)], axis=1)
    angles = freqs[...] * row(0).astype(F32)
    cosine[...] = jnp.cos(angles)
    sine[...] = jnp.sin(angles)
    parity = (row(1) % 2).astype(F32)
    blank = jnp.zeros((MARKS - 2, parity.shape[1]), F32)
    marks[...] = jnp.concatenate(
        [parity, 1.0 - parity, blank, (1.0 - parity) * MASKED, parity * MASKED, blank], axis=0
    ).astype(BF)
    tree.forward(2)
    shared.wait()
    odd = head % 2 == 1
    for c in range(count):
        rows = slice(c * shard, (c + 1) * shard)
        block = slab[c].astype(F32)
        parts = []
        for third in range(3):
            at = third * 128
            parts.append(jnp.where(odd, block[:, at + HD : at + 128], block[:, at : at + HD]))
        w_head[rows] = jnp.concatenate(parts, axis=1).astype(BF)
    collect.forward(0)
    tree.forward(3)
    tree.finish()
    collect.finish()
    for copy in first + thirds + late:
        copy.wait_send()


def begin(tokens, gains, ids, w_qkv, w_attn, freqs, ring, count, groups, reach):
    rows, width = tokens.shape
    shard = w_qkv.shape[0]
    group = groups * reach
    sems = lambda *shape: [DMA(shape), DMA(shape)]
    return pl.pallas_call(
        functools.partial(begin_kernel, groups, reach, count),
        in_specs=[VMEM, VMEM, ANY, ANY, ANY, VMEM],
        out_specs=[ANY, VMEM, VMEM, VMEM, VMEM, VMEM, ANY],
        out_shape=[
            jax.ShapeDtypeStruct((group, rows, width), BF),
            jax.ShapeDtypeStruct((8, width), F32),
            jax.ShapeDtypeStruct((width, 3 * HD), BF),
            jax.ShapeDtypeStruct((HALF, group * rows), F32),
            jax.ShapeDtypeStruct((HALF, group * rows), F32),
            jax.ShapeDtypeStruct((2 * MARKS, group * rows), BF),
            jax.ShapeDtypeStruct((ring, shard, width), BF),
        ],
        scratch_shapes=[
            pltpu.VMEM((group, 8, rows), jnp.int32),
            pltpu.VMEM((count, shard, 3 * 128), BF),
            pltpu.VMEM((rows, width), BF),
            pltpu.VMEM((count, 8, gains.shape[1]), F32),
            DMA((5,)),
            *sems(group - 1),
            *sems(count - 1),
            *sems(count - 1, 3),
            *sems(ring - 1),
            DMA,
            DMA,
            *Tree.scratch(3),
            *Collect.scratch(1, groups),
        ],
        compiler_params=pltpu.CompilerParams(
            collective_id=0, has_side_effects=True, vmem_limit_bytes=12 << 20
        ),
        cost_estimate=pl.CostEstimate(flops=0, bytes_accessed=30 << 20, transcendentals=0),
        name="begin",
    )(tokens, gains, ids, w_qkv, w_attn, freqs)


class Line:
    def __init__(self, length, sub, first, sources, targets, send, recv):
        ctx = lax.axis_index("ctx")
        spot, side = ctx // sub, ctx % sub
        self.length, self.spot, self.first = length, spot, first
        self.waited = 0
        beside = [{"ctx": (spot + 1) % length * sub + side}, {"ctx": (spot + length - 1) % length * sub + side}]
        self.copies = [
            [
                remote(sources[d][q], targets[d][q], beside[d], send.at[d, q], recv.at[d, q])
                for q in range(len(sources[d]))
            ]
            for d in range(2)
        ]

    def sends(self, d, q):
        s, spot, last = (q + self.first) // 2, self.spot, self.length - 1
        if d:
            return jnp.logical_and(spot + s <= last, spot > 0)
        return jnp.logical_and(spot >= s, spot < last)

    def receives(self, d, q):
        s = (q + self.first) // 2
        return self.spot + s + 1 < self.length if d else self.spot > s

    def arrive(self, q):
        for d in range(2):
            pl.when(self.receives(d, q))(self.copies[d][q].wait_recv)
        self.waited = q + 1

    def start(self, q):
        if q >= 2:
            self.arrive(q - 2)
        for d in range(2):
            pl.when(self.sends(d, q))(self.copies[d][q].start)

    def finish(self):
        for q in range(self.waited, len(self.copies[0])):
            self.arrive(q)
        for d in range(2):
            for q, copy in enumerate(self.copies[d]):
                pl.when(self.sends(d, q))(copy.wait_send)


def ring_half(sub, side, k):
    return (side + k) % 2 if sub == 2 else k


class Columns:
    def __init__(self, place, part, whole, own, side_send, side_recv, near_send, near_recv):
        _, sub, _, width = whole.shape
        side = place.ctx % sub
        half = pl.ds(pl.multiple_of(place.head % 2 * (width // 2), 128), width // 2)
        self.own = pltpu.make_async_copy(part, whole.at[:, side], own)
        self.sides, self.near = [], []
        for step in range(1, sub):
            peer, source = (side + step) % sub, (side - step + sub) % sub
            self.sides.append(
                remote(
                    part.at[:, :, half],
                    whole.at[:, side, :, half],
                    {"ctx": place.ctx - side + peer},
                    side_send.at[step - 1],
                    side_recv.at[step - 1],
                )
            )
            here = whole.at[:, source, :, half]
            self.near.append(
                remote(
                    here, here, {"heads": flip(place.head, 1)}, near_send.at[step - 1], near_recv.at[step - 1]
                )
            )

    @staticmethod
    def scratch(sub):
        count = (max(sub - 1, 1),)
        return [DMA, DMA(count), DMA(count), DMA(count), DMA(count)]

    def start(self):
        self.own.start()
        for copy in self.sides:
            copy.start()

    def across(self):
        for side, near in zip(self.sides, self.near):
            side.wait_recv()
            near.start()

    def finish(self):
        self.own.wait()
        for side, near in zip(self.sides, self.near):
            side.wait_send()
            near.wait()


def attend_kernel(
    groups,
    reach,
    lines,
    tile,
    x_ref,
    w_ref,
    cos_ref,
    sin_ref,
    mark_ref,
    attn_half,
    mlp,
    out_ref,
    wide_ref,
    lse_ref,
    qkv_ref,
    attn_all,
    mlp_pair,
    mlp_near,
    ring_send,
    ring_recv,
    swap_send,
    swap_recv,
    swap_own,
    *sems,
):
    count = x_ref.shape[0]
    step = pl.program_id(0)
    steps = count // tile
    place = Place(groups, reach)
    ring_size, sub = attn_all.shape[:2]
    side = place.ctx % sub
    early = mlp_near.shape[1]
    if sub == 2:
        kept = pltpu.make_async_copy(mlp.at[side], mlp_pair.at[side], swap_own)
        swap = [
            remote(
                mlp.at[1 - side],
                mlp_pair.at[side],
                {"ctx": place.ctx + 1 - 2 * side},
                swap_send,
                swap_recv,
            )
        ]
        sources = [mlp.at[side], mlp_pair.at[1 - side]]
    else:
        kept = pltpu.make_async_copy(mlp, mlp_pair, swap_own)
        swap = []
        sources = [mlp.at[0], mlp.at[1]]
    ring = Line(
        ring_size,
        sub,
        0,
        [sources + [mlp_near.at[d, q] for q in range(early - 2)] for d in range(2)],
        [[mlp_near.at[d, q] for q in range(early)] for d in range(2)],
        ring_send,
        ring_recv,
    )
    columns = Columns(place, attn_half, attn_all, *sems)

    @pl.when(step == 0)
    def _():
        meet(everyone(place, lines))
        for copy in swap:
            copy.start()
        ring.start(0)
        kept.start()
        columns.start()
        qkv_ref[HD:QM_END, :] = mark_ref[:MARKS, :]
        qkv_ref[K_END:KM_END, :] = mark_ref[MARKS:, :]

        @pl.loop(0, steps)
        def _(i):
            at = pl.ds(pl.multiple_of(i * tile, tile), tile)
            cosine, sine = cos_ref[:, at], sin_ref[:, at]
            part = dot(w_ref[...], x_ref[at, :], 0, 1)

            def turn(value):
                front, back = value[:HALF], value[HALF:]
                return jnp.concatenate(
                    [front * cosine - back * sine, back * cosine + front * sine], axis=0
                )

            qkv_ref[:HD, at] = (turn(part[:HD]) * 0.125).astype(BF)
            qkv_ref[QM_END:K_END, at] = turn(part[HD : 2 * HD]).astype(BF)
            qkv_ref[KM_END:, at] = part[2 * HD :].astype(BF)

    here = pl.ds(pl.multiple_of(step * tile, tile), tile)
    query = qkv_ref[:QM_END, here]
    keys = [slice(j * tile, (j + 1) * tile) for j in range(steps)]
    scores = [dot(qkv_ref[QM_END:KM_END, at], query, 0, 0) for at in keys]
    top = functools.reduce(jnp.maximum, [jnp.max(s, axis=0, keepdims=True) for s in scores])
    raised = [jnp.exp(s - top) for s in scores]
    total = functools.reduce(jnp.add, [jnp.sum(e, axis=0, keepdims=True) for e in raised])
    scale = 1.0 / total
    result = jnp.zeros((HD, tile), F32)
    for j in range(steps):
        result += dot(qkv_ref[KM_END:, keys[j]], (raised[j] * scale).astype(BF), 1, 0)
    rows = out_ref.shape[2]
    for k in range(tile // rows):
        out_ref[step * (tile // rows) + k] = result[:, k * rows : (k + 1) * rows].astype(BF)
    wide_ref[:, here] = result
    lse_ref[:, here] = top + jnp.log(total)

    @pl.when(step == min(1, steps - 1))
    def _():
        for copy in swap:
            copy.wait_recv()
        for q in range(1, min(early, 3)):
            ring.start(q)

    @pl.when(step == steps - 1)
    def _():
        columns.across()
        for q in range(3, early):
            ring.start(q)
        ring.finish()
        for copy in swap:
            copy.wait_send()
        kept.wait()
        columns.finish()


def attend(x, w, cosine, sine, marks, attn_half, mlp, lines, groups, reach, rows, tile):
    count, width = x.shape
    ring, shard, _ = attn_half.shape
    sub = lines // ring
    early = ring - 1
    return pl.pallas_call(
        functools.partial(attend_kernel, groups, reach, lines, tile),
        grid=(count // tile,),
        in_specs=[
            VMEM,
            VMEM,
            VMEM,
            VMEM,
            VMEM,
            ANY,
            ANY,
        ],
        out_specs=[
            VMEM,
            VMEM,
            VMEM,
            VMEM,
            ANY,
            ANY,
            ANY,
        ],
        out_shape=[
            jax.ShapeDtypeStruct((count // rows, HD, rows), BF),
            jax.ShapeDtypeStruct((HD, count), F32),
            jax.ShapeDtypeStruct((1, count), F32),
            jax.ShapeDtypeStruct((V_END, count), BF),
            jax.ShapeDtypeStruct((ring, sub, shard, width), BF),
            jax.ShapeDtypeStruct(mlp.shape, BF),
            jax.ShapeDtypeStruct((2, early, *mlp.shape[1:]), BF),
        ],
        scratch_shapes=[DMA((2, early)), DMA((2, early)), DMA, DMA, DMA, *Columns.scratch(sub)],
        compiler_params=pltpu.CompilerParams(
            collective_id=5, has_side_effects=True, vmem_limit_bytes=20 << 20
        ),
        cost_estimate=pl.CostEstimate(
            flops=count * count * HD * 8, bytes_accessed=count * 4096, transcendentals=count * count
        ),
        name="attend",
    )(x, w, cosine, sine, marks, attn_half, mlp)


def middle_kernel(
    groups,
    reach,
    lines,
    outgoing,
    tokens,
    d_out,
    w_attn,
    gains,
    mlp_pair,
    mlp_near,
    mlp_all,
    upstream_all,
    middle,
    attended,
    mlp_weights,
    land,
    mine,
    a2a_send,
    a2a_recv,
    own,
    ring_send,
    ring_recv,
    ring_own,
    land_own,
    *tree_sems,
):
    place = Place(groups, reach)
    group = groups * reach
    early, count = mlp_near.shape[1], mlp_weights.shape[0]
    sub = lines // count
    spot, side = place.ctx // sub, place.ctx % sub

    def slot(d, q, ahead):
        block = (spot + (q // 2 + ahead if d else count - q // 2 - ahead)) % count
        return mlp_weights.at[block, ring_half(sub, side, q % 2)]

    rest = range(early, 2 * (count - 1))
    ring = Line(
        count,
        sub,
        early,
        [[mlp_near.at[d, q - 2] if q - 2 < early else slot(d, q, 0) for q in rest] for d in range(2)],
        [[slot(d, q, 0) for q in rest] for d in range(2)],
        ring_send,
        ring_recv,
    )
    local = [pltpu.make_async_copy(mlp_pair, mlp_weights.at[spot], ring_own.at[0])]
    near = []
    for d in range(2):
        for q in range(early):
            copy = pltpu.make_async_copy(
                mlp_near.at[d, q], slot(d, q, 1), ring_own.at[1 + d * early + q]
            )
            there = spot + q // 2 + 1 < count if d else spot > q // 2
            near.append((there, copy))
    meet(everyone(place, lines))
    copies = spread(place, outgoing, land, (a2a_send, a2a_recv, own))
    ring.start(0)
    ring.start(1)
    up = Tree(place, 2, d_out, upstream_all, tree_sems[5:10])
    up.start()
    for copy in local:
        copy.start()
    for there, copy in near:
        pl.when(there)(copy.start)
    for copy in copies:
        copy.wait()
    collect = Collect(groups, [(land, lambda h: attended.at[h])], *tree_sems[10:])
    collect.start(0)
    local.append(pltpu.make_async_copy(land, attended.at[place.head], land_own))
    local[-1].start()
    value = tokens[...].astype(F32) + dot(
        land[...].reshape(group * HD, tokens.shape[0]), w_attn[...], 0, 0
    )
    middle[...] = value
    normed, _ = norm_parts(value)
    mine[...] = (normed * gains[1:2, :]).astype(BF)
    tree = Tree(place, 2, mine, mlp_all, tree_sems[:5])
    tree.start()
    up.forward(1)
    for q in range(2, len(rest)):
        ring.start(q)
    tree.forward(1)
    up.forward(2)
    tree.forward(2)
    collect.forward(0)
    up.finish()
    tree.finish()
    collect.finish()
    for copy in local:
        copy.wait()
    for there, copy in near:
        pl.when(there)(copy.wait)
    ring.finish()


def middle_step(outgoing, tokens, d_out, w_attn, gains, mlp_pair, mlp_near, lines, groups, reach):
    rows, width = tokens.shape
    group = groups * reach
    early, sub = mlp_near.shape[1], 8 // groups
    ring = lines // sub
    left = 2 * (ring - 1) - early
    return pl.pallas_call(
        functools.partial(middle_kernel, groups, reach, lines),
        in_specs=[ANY, VMEM, ANY, VMEM, VMEM, ANY, ANY],
        out_specs=[ANY, ANY, VMEM, ANY, ANY],
        out_shape=[
            jax.ShapeDtypeStruct((8, rows, width), BF),
            jax.ShapeDtypeStruct((8, rows, width), BF),
            jax.ShapeDtypeStruct((rows, width), F32),
            jax.ShapeDtypeStruct((groups, group, HD, rows), BF),
            jax.ShapeDtypeStruct((ring, *mlp_pair.shape), BF),
        ],
        scratch_shapes=[
            pltpu.VMEM((group, HD, rows), BF),
            pltpu.VMEM((rows, width), BF),
            DMA((group - 1,)),
            DMA((group - 1,)),
            DMA,
            DMA((2, left)),
            DMA((2, left)),
            DMA((2 * early + 1,)),
            DMA,
            *Tree.scratch(2),
            *Tree.scratch(2),
            *Collect.scratch(1, groups),
        ],
        compiler_params=pltpu.CompilerParams(
            collective_id=1, has_side_effects=True, vmem_limit_bytes=12 << 20
        ),
        cost_estimate=pl.CostEstimate(flops=1 << 28, bytes_accessed=12 << 20, transcendentals=0),
        name="middle_step",
    )(outgoing, tokens, d_out, w_attn, gains, mlp_pair, mlp_near)


class Sum:
    def __init__(self, place, terms, first, held, stage, land, send, recv):
        self.terms, self.first, self.stage, self.land = terms, first, stage, land
        self.half = stage.shape[2]
        length = terms.shape[0] // (2 * self.half)
        lines_sub = 8 // place.groups
        spot, side = place.ctx // lines_sub, place.ctx % lines_sub
        self.length, self.spot = length, spot
        self.held = lambda d, q: land.at[d, q] if q >= 0 else held.at[d, q + 2]
        beside = [
            {"ctx": (spot + 1) % length * lines_sub + side},
            {"ctx": (spot + length - 1) % length * lines_sub + side},
        ]
        self.copies = [
            [
                remote(stage.at[d, q], land.at[d, q], beside[d], send.at[d, q], recv.at[d, q])
                for q in range(stage.shape[1])
            ]
            for d in range(2)
        ]

    @staticmethod
    def scratch(count, half):
        return [
            pltpu.VMEM((2, count, *half), BF),
            pltpu.VMEM((2, count, *half), BF),
            DMA((2, count)),
            DMA((2, count)),
        ]

    def sends(self, d, q):
        s, spot, last = (q + self.first) // 2, self.spot, self.length - 1
        if d:
            return jnp.logical_and(spot >= last - s, spot > 0)
        return jnp.logical_and(spot <= s, spot < last)

    def receives(self, d, q):
        s, spot, last = (q + self.first) // 2, self.spot, self.length - 1
        if d:
            return jnp.logical_and(spot >= last - 1 - s, spot < last)
        return jnp.logical_and(spot <= s + 1, spot > 0)

    def clear(self):
        for d in range(2):
            for q in range(len(self.copies[d])):

                @pl.when(jnp.logical_not(self.receives(d, q)))
                def _():
                    self.land[d, q] = jnp.zeros(self.land.shape[2:], BF)

    def block(self, at, k):
        return self.terms[pl.ds(pl.multiple_of((2 * at + k) * self.half, 16), self.half), :]

    def arrive(self, q):
        for d in range(2):
            pl.when(self.receives(d, q))(self.copies[d][q].wait_recv)

    def start(self, q):
        if q >= 2:
            self.arrive(q - 2)
        step, k = (q + self.first) // 2, (q + self.first) % 2
        for d in range(2):
            at = self.spot + (step + 1 if d else self.length - 1 - step)

            @pl.when(self.sends(d, q))
            def _():
                value = self.block(at % self.length, k)
                if q + self.first >= 2:
                    value = (value.astype(F32) + self.held(d, q - 2)[...].astype(F32)).astype(BF)
                self.stage[d, q] = value
                self.copies[d][q].start()

    def finish(self):
        count = len(self.copies[0])
        for q in range(max(count - 2, 0), count):
            self.arrive(q)
        for d in range(2):
            for q, copy in enumerate(self.copies[d]):
                pl.when(self.sends(d, q))(copy.wait_send)


def mlp_rows(chunk, x_ref, up_ref, w_ref, back_ref, forward_ref, kept):
    count = x_ref.shape[0]
    rows = back_ref.shape[2]

    @pl.loop(0, count // chunk)
    def _(i):
        at = pl.ds(pl.multiple_of(i * chunk, chunk), chunk)
        gate_up = dot(x_ref[at, :], w_ref[:, : 2 * SLICE], 1, 0)
        left, right = gate_up[:, :SLICE], gate_up[:, SLICE:]
        grad_mixed = dot(up_ref[at, :], w_ref[:, 2 * SLICE :], 1, 0)
        normal_cdf = 0.5 * (1.0 + lax.erf(left * 0.7071067811865476))
        gelu = left * normal_cdf
        density = jnp.exp(-0.5 * left * left) * 0.3989422804014327
        kept[at, :SLICE] = (grad_mixed * right * (normal_cdf + left * density)).astype(BF)
        kept[at, SLICE : 2 * SLICE] = (grad_mixed * gelu).astype(BF)
        kept[at, 2 * SLICE :] = (gelu * right).astype(BF)
        back = dot(kept[at, : 2 * SLICE], w_ref[:, : 2 * SLICE], 1, 1).astype(BF)
        forward = dot(kept[at, 2 * SLICE :], w_ref[:, 2 * SLICE :], 1, 1).astype(BF)
        pairs = chunk // rows // 2
        for j in range(chunk // rows):
            piece = slice(j * rows, (j + 1) * rows)
            back_ref[i * pairs + j // 2, j % 2] = back[piece]
            forward_ref[i * pairs + j // 2, j % 2] = forward[piece]


def mlp_weights_back(chunk, x_ref, up_ref, kept, terms_ref):
    @pl.loop(0, x_ref.shape[1] // chunk)
    def _(i):
        at = pl.ds(pl.multiple_of(i * chunk, chunk), chunk)
        terms_ref[at, : 2 * SLICE] = dot(x_ref[:, at], kept[:, : 2 * SLICE], 0, 0).astype(BF)
        terms_ref[at, 2 * SLICE :] = dot(up_ref[:, at], kept[:, 2 * SLICE :], 0, 0).astype(BF)


def turn_kernel(
    groups,
    reach,
    lines,
    x,
    up,
    mlp_weights,
    middle,
    d_out,
    w_attn,
    gains,
    attended,
    grads,
    grad_middle,
    attn_part,
    carry,
    forward,
    terms,
    kept,
    partial,
    columns,
    total,
    outgoing,
    branch,
    a2a_send,
    a2a_recv,
    own,
    side_send,
    side_recv,
    side_own,
    *rest,
):
    place = Place(groups, reach)
    group = groups * reach
    lanes = branch.shape[2]
    sums = Sum(place, terms, 0, None, *rest[7:])
    count = rest[7].shape[1]
    devices = everyone(place, lines)
    sums.clear()
    greet(devices)
    mlp_rows(512, x, up, mlp_weights, partial, forward, kept)
    pl.semaphore_wait(pltpu.get_barrier_semaphore(), len(devices))
    halving = Halving(place, 2, partial, total, rest[:7])
    halving.start()
    mlp_weights_back(512, x, up, kept, terms)
    sums.start(0)
    sums.start(1)
    halving.pair()
    halving.halve(0)
    halving.halve(1)
    for q in range(2, count):
        sums.start(q)
    halving.finish()
    normed, inverse_std = norm_parts(middle[...])
    upstream = total[...]
    grad = d_out[...].astype(F32) + norm_back(upstream, normed, inverse_std, gains[1:2, :])
    grad_middle[...] = grad
    low = grad.astype(BF)
    for g in range(groups):
        branch[g] = low[:, g * lanes : (g + 1) * lanes]
    outgoing[...] = dot(w_attn[...], low, 1, 1).astype(BF).reshape(outgoing.shape)
    copies = spread(place, outgoing, grads, (a2a_send, a2a_recv, own))
    for step in range(1, groups):
        peer = (place.head + step) % groups
        copies.append(
            push(
                branch.at[peer],
                columns.at[place.head],
                {"heads": peer},
                side_send.at[step - 1],
                side_recv.at[step - 1],
            )
        )
    local = pltpu.make_async_copy(branch.at[place.head], columns.at[place.head], side_own)
    local.start()
    for copy in copies[-(groups - 1) :]:
        copy.wait()
    local.wait()
    attn_part[...] = functools.reduce(
        jnp.add, [dot(attended[g], columns[g], 1, 0) for g in range(groups)]
    ).astype(BF)
    for copy in copies[: -(groups - 1)]:
        copy.wait()
    sums.finish()
    for d in range(2):
        for q in range(2):
            carry[d, q] = sums.land[d, count - 2 + q]


def turn_step(x, up, mlp_weights, middle, d_out, w_attn, gains, attended, lines, groups, reach):
    rows, width = middle.shape
    count = lines * groups // 8 - 1
    half = (width // (2 * (count + 1)), 3 * SLICE)
    group = groups * reach
    return pl.pallas_call(
        functools.partial(turn_kernel, groups, reach, lines),
        in_specs=[VMEM] * 8,
        out_specs=[ANY, VMEM, VMEM, VMEM, VMEM, VMEM],
        out_shape=[
            jax.ShapeDtypeStruct((group, HD, rows), BF),
            jax.ShapeDtypeStruct((rows, width), F32),
            jax.ShapeDtypeStruct((width, width // groups), BF),
            jax.ShapeDtypeStruct((2, 2, *half), BF),
            jax.ShapeDtypeStruct((4, 2, rows, width), BF),
            jax.ShapeDtypeStruct((width, 3 * SLICE), BF),
        ],
        scratch_shapes=[
            pltpu.VMEM((8 * rows, 3 * SLICE), BF),
            pltpu.VMEM((4, 2, rows, width), BF),
            pltpu.VMEM((groups, rows, width // groups), BF),
            pltpu.VMEM((rows, width), F32),
            pltpu.VMEM((group, HD, rows), BF),
            pltpu.VMEM((groups, rows, width // groups), BF),
            DMA((group - 1,)),
            DMA((group - 1,)),
            DMA,
            DMA((groups - 1,)),
            DMA((groups - 1,)),
            DMA,
            *Halving.scratch(2, rows, width),
            *Sum.scratch(count, half),
        ],
        compiler_params=pltpu.CompilerParams(
            collective_id=2, has_side_effects=True, vmem_limit_bytes=24 << 20
        ),
        cost_estimate=pl.CostEstimate(flops=1 << 33, bytes_accessed=12 << 20, transcendentals=0),
        name="turn_step",
    )(x, up, mlp_weights, middle, d_out, w_attn, gains, attended)


def end_part(
    place,
    lines,
    partial,
    weight,
    mlp,
    attn,
    total,
    mlp_all,
    weight_all,
    attn_all,
    sum_line,
    sum_attn,
    lined,
    summed,
    swap_send,
    swap_recv,
    own,
    *rest,
):
    groups, reach = place.groups, place.reach
    sub = mlp.shape[0]
    mine, head = place.ctx % sub, place.head
    wide = Halving(place, 3, partial, total, rest[:7], [2, 1])
    swap = Lines(lines, weight, lined, *rest[7:10])
    wide.start()
    swap.start()
    wide.pair()
    sum_line()
    swaps = []
    for step in range(1, sub):
        peer = (mine + step) % sub
        swaps.append(
            push(
                mlp.at[peer],
                mlp_all.at[mine, head],
                {"ctx": place.ctx - mine + peer},
                swap_send.at[step - 1],
                swap_recv.at[step - 1],
            )
        )
    pieces = [(mlp.at[mine], lambda h: mlp_all.at[mine, h]), (attn, lambda h: attn_all.at[h])]
    for step in range(1, sub):
        source = (mine - step + sub) % sub
        pieces.append(
            (mlp_all.at[source, head], lambda h, source=source: mlp_all.at[source, h])
        )
    pieces.append((summed, lambda h: weight_all.at[h]))
    collect = Collect(groups, pieces, *rest[10:14])
    local = [
        pltpu.make_async_copy(mlp.at[mine], mlp_all.at[mine, head], own.at[0]),
        pltpu.make_async_copy(attn, attn_all.at[head], own.at[1]),
        pltpu.make_async_copy(summed, weight_all.at[head], own.at[2]),
    ]
    local[0].start()
    collect.start(0)
    sum_attn()
    local[1].start()
    collect.start(1)
    for step in range(1, sub):
        swaps[step - 1].wait_recv()
        collect.start(step + 1)
    wide.halve(0)
    swap.finish()
    for r in range(reach):
        summed[r] = functools.reduce(
            jnp.add, [lined[r + reach * g].astype(F32) for g in range(lines // reach)]
        ).astype(BF)
    local[2].start()
    collect.start(sub + 1)
    wide.halve(1)
    collect.forward(0)
    collect.forward(1)
    wide.halve(2)
    for n in range(2, sub + 2):
        collect.forward(n)
    for copy in local:
        copy.wait()
    for copy in swaps:
        copy.wait_send()
    collect.finish()
    wide.finish()


def attend_back_kernel(
    groups,
    reach,
    lines,
    tile,
    qkv_ref,
    grad_ref,
    wide_ref,
    lse_ref,
    x_ref,
    w_ref,
    cos_ref,
    sin_ref,
    forward_ref,
    terms,
    carry,
    attn_ref,
    ahead_ref,
    total,
    mlp_all,
    weight_all,
    attn_all,
    out_ref,
    weight_ref,
    attn_out_ref,
    mlp_ref,
    sums,
    queries,
    weight,
    attn_land,
    *sems,
):
    count = x_ref.shape[0]
    rows = grad_ref.shape[2]
    steps, per_tile = count // tile, tile // rows
    step = pl.program_id(0)
    place = Place(groups, reach)
    halving = Halving(place, 2, forward_ref, ahead_ref, sems[:7])
    swap = Lines(lines, attn_ref, attn_land, *sems[7:10])
    length = lines * groups // 8
    line = Sum(place, terms, length - 1, carry, *sems[10:14])

    @pl.when(step == 0)
    def _():
        line.clear()
        meet(everyone(place, lines))
        line.start(0)
        line.start(1)
        halving.start()
        swap.start()
        sums[...] = jnp.zeros_like(sums)

    here = pl.ds(pl.multiple_of(step * tile, tile), tile)
    query = qkv_ref[:QM_END, here]
    grad = jnp.concatenate([grad_ref[step * per_tile + k] for k in range(per_tile)], axis=1)
    delta = jnp.sum(grad.astype(F32) * wide_ref[:, here], axis=0, keepdims=True)
    lse = lse_ref[:, here]
    grad_query = jnp.zeros((HD, tile), F32)
    for j in range(steps):
        keys = slice(j * tile, (j + 1) * tile)
        prob = jnp.exp(dot(qkv_ref[QM_END:KM_END, keys], query, 0, 0) - lse)
        grad_prob = dot(qkv_ref[KM_END:, keys], grad, 0, 0)
        grad_score = (prob * (grad_prob - delta)).astype(BF)
        grad_query += dot(qkv_ref[QM_END:K_END, keys], grad_score, 1, 0)
        sums[:HD, keys] += dot(query[:HD], grad_score, 1, 1)
        sums[HD:, keys] += dot(grad, prob.astype(BF), 1, 1)
    queries[:, here] = (grad_query * 0.125).astype(BF)

    pl.when(step == 0)(halving.pair)

    @pl.when(step == min(2, steps - 1))
    def _():
        halving.halve(0)
        for q in range(2, length - 1):
            line.start(q)


    @pl.when(step == steps - 1)
    def _():
        weight[...] = jnp.zeros_like(weight)

        @pl.loop(0, steps)
        def _(i):
            at = pl.ds(pl.multiple_of(i * tile, tile), tile)
            cosine, sine = cos_ref[:, at], sin_ref[:, at]

            def turn_back(value):
                front, back = value[:HALF], value[HALF:]
                return [front * cosine + back * sine, back * cosine - front * sine]

            low = lambda value: value.astype(BF).astype(F32)
            projected = jnp.concatenate(
                [
                    *turn_back(queries[:, at].astype(F32)),
                    *turn_back(low(sums[:HD, at])),
                    low(sums[HD:, at]),
                ],
                axis=0,
            ).astype(BF)
            part = dot(projected, w_ref[...], 0, 1).astype(BF)
            for k in range(per_tile):
                out_ref[(i * per_tile + k) // 2, k % 2] = part[k * rows : (k + 1) * rows]
            weight[...] += dot(projected, x_ref[at, :], 1, 0)

        shard = weight_ref.shape[2]
        for c in range(lines):
            weight_ref[c] = weight[:, c * shard : (c + 1) * shard].astype(BF)
        halving.halve(1)
        half = line.half

        def sum_line():
            line.finish()
            for k in range(2):
                q = length - 3 + k
                value = (
                    line.block(line.spot, k).astype(F32)
                    + line.land[0, q].astype(F32)
                    + line.land[1, q].astype(F32)
                ).astype(BF)
                if mlp_ref.shape[0] == 2:
                    mlp_ref[k] = value
                else:
                    mlp_ref[0, k * half : (k + 1) * half] = value

        def sum_attn():
            swap.finish()
            attn_out_ref[...] = functools.reduce(
                jnp.add, [attn_land[c].astype(F32) for c in range(lines)]
            ).astype(BF)

        end_part(
            place,
            lines,
            out_ref,
            weight_ref,
            mlp_ref,
            attn_out_ref,
            total,
            mlp_all,
            weight_all,
            attn_all,
            sum_line,
            sum_attn,
            *sems[14:],
        )
        halving.finish()


def attend_back(qkv, grad, wide, lse, x, w, cosine, sine, forward, terms, carry, attn, groups, reach, tile):
    count, width = x.shape
    blocks, _, rows = grad.shape
    lines, shard, lanes = attn.shape
    sub = 8 // groups
    length = lines // sub
    operands = (qkv, grad, wide, lse, x, w, cosine, sine, forward, terms, carry)
    return pl.pallas_call(
        functools.partial(attend_back_kernel, groups, reach, lines, tile),
        grid=(count // tile,),
        in_specs=[*[VMEM] * len(operands), ANY],
        out_specs=[VMEM, VMEM, ANY, ANY, ANY],
        out_shape=[
            jax.ShapeDtypeStruct((rows, width), F32),
            jax.ShapeDtypeStruct((rows, width), F32),
            jax.ShapeDtypeStruct((sub, groups, shard, 3 * SLICE), BF),
            jax.ShapeDtypeStruct((groups, reach, 3 * HD, shard), BF),
            jax.ShapeDtypeStruct((groups, shard, lanes), BF),
        ],
        scratch_shapes=[
            pltpu.VMEM((blocks // 2, 2, rows, width), BF),
            pltpu.VMEM((lines, 3 * HD, shard), BF),
            pltpu.VMEM((shard, lanes), BF),
            pltpu.VMEM((sub, shard, 3 * SLICE), BF),
            pltpu.VMEM((2 * HD, count), F32),
            pltpu.VMEM((HD, count), BF),
            pltpu.VMEM((3 * HD, width), F32),
            pltpu.VMEM((lines, shard, lanes), BF),
            *Halving.scratch(2, rows, width),
            *Lines.scratch(lines),
            *Sum.scratch(length - 1, (width // (2 * length), 3 * SLICE)),
            pltpu.VMEM((lines, 3 * HD, shard), BF),
            pltpu.VMEM((reach, 3 * HD, shard), BF),
            DMA((max(sub - 1, 1),)),
            DMA((max(sub - 1, 1),)),
            DMA((3,)),
            *Halving.scratch(3, rows, width),
            *Lines.scratch(lines),
            *Collect.scratch(sub + 2, groups),
        ],
        compiler_params=pltpu.CompilerParams(
            collective_id=4, has_side_effects=True, vmem_limit_bytes=36 << 20
        ),
        cost_estimate=pl.CostEstimate(
            flops=count * count * HD * 20, bytes_accessed=count * 6144, transcendentals=count * count
        ),
        name="attend_back",
    )(*operands, attn)


class Collect:
    def __init__(self, groups, pieces, far_send, far_recv, near_send, near_recv):
        head = lax.axis_index("heads")
        self.half = half = groups // 2
        pair = {"heads": flip(head, 1)}
        self.far, self.near = [], []
        for n, (piece, where) in enumerate(pieces):
            self.far.append(
                [
                    remote(
                        piece,
                        where(head),
                        {"heads": (head + 2 * k) % groups},
                        far_send.at[n, k - 1],
                        far_recv.at[n, k - 1],
                    )
                    for k in range(1, half)
                ]
            )
            sides = [(piece, where(head))]
            for k in range(1, half):
                got = where((head - 2 * k + groups) % groups)
                sides.append((got, got))
            self.near.append(
                [
                    remote(source, target, pair, near_send.at[n, k], near_recv.at[n, k])
                    for k, (source, target) in enumerate(sides)
                ]
            )

    @staticmethod
    def scratch(count, groups):
        far, near = (count, max(groups // 2 - 1, 1)), (count, groups // 2)
        return [DMA(far), DMA(far), DMA(near), DMA(near)]

    def start(self, n):
        for copy in self.far[n]:
            copy.start()
        self.near[n][0].start()

    def forward(self, n):
        for k, copy in enumerate(self.far[n]):
            copy.wait_recv()
            self.near[n][k + 1].start()

    def finish(self):
        for copies in self.far:
            for copy in copies:
                copy.wait_send()
        for copies in self.near:
            for copy in copies:
                copy.wait()


def assemble_kernel(
    upstream,
    tokens,
    grad_middle,
    gains,
    middle,
    ahead,
    weight_all,
    attn_all,
    mlp_all,
    w_qkv,
    w_in,
    own_gains,
    result,
    grad,
    sum_qkv,
    sum_attn,
    sum_in,
    sum_out,
    gain_sums,
):
    groups, reach, _, shard = weight_all.shape
    lanes = attn_all.shape[2]
    result[...] = (middle[...] + ahead[...]).astype(BF)
    normed, inverse_std = norm_parts(tokens[...].astype(F32))
    grad[...] = grad_middle[...] + norm_back(upstream[...], normed, inverse_std, gains[0:1, :])
    for g in range(groups):
        sum_attn[:, g * lanes : (g + 1) * lanes] = attn_all[g].astype(F32)
    gain_one = jnp.zeros((shard, 128), F32)
    for third in range(3):
        part = slice(third * HD, (third + 1) * HD)
        for pair in range(H // 2):
            r, g = 2 * pair // groups, 2 * pair % groups
            tile = (
                jnp.concatenate([weight_all[g, r, part], weight_all[g + 1, r, part]], axis=0)
                .astype(F32)
                .T
            )
            at = third * H * HD + pair * 2 * HD
            sum_qkv[:, at : at + 2 * HD] = tile
            gain_one += tile * w_qkv[:, at : at + 2 * HD].astype(F32)
    gain_two = jnp.zeros((shard, 1), F32)
    for t in range(8):
        start, wide = slice_place(t)
        for half in range(2):
            piece = mlp_all[t, :, half * SLICE : half * SLICE + wide].astype(F32)
            at = half * FF + start
            sum_in[:, at : at + wide] = piece
            gain_two += jnp.sum(
                piece * w_in[:, at : at + wide].astype(F32), axis=1, keepdims=True
            )
        sum_out[start : start + wide, :] = (
            mlp_all[t, :, 2 * SLICE : 3 * SLICE].astype(F32).T[:wide]
        )
    one = jnp.sum(gain_one, axis=1, keepdims=True)
    lane = lax.broadcasted_iota(jnp.int32, (shard, 128), 1)
    both = jnp.where(lane == 0, one, gain_two).T
    gain_sums[...] = both[:8] / own_gains[...]


def assemble(upstream, tokens, grad_middle, gains, middle, ahead, weight_all, attn_all, mlp_all, w_qkv, w_in, own_gains):
    rows, width = tokens.shape
    shard = w_qkv.shape[0]
    return pl.pallas_call(
        assemble_kernel,
        in_specs=[VMEM] * 12,
        out_specs=[VMEM] * 7,
        out_shape=[
            jax.ShapeDtypeStruct((rows, width), BF),
            jax.ShapeDtypeStruct((rows, width), F32),
            jax.ShapeDtypeStruct((shard, 3 * width), F32),
            jax.ShapeDtypeStruct((shard, width), F32),
            jax.ShapeDtypeStruct((shard, 2 * FF), F32),
            jax.ShapeDtypeStruct((FF, shard), F32),
            jax.ShapeDtypeStruct((8, shard), F32),
        ],
        compiler_params=pltpu.CompilerParams(vmem_limit_bytes=20 << 20),
        cost_estimate=pl.CostEstimate(flops=1 << 24, bytes_accessed=20 << 20, transcendentals=0),
        name="assemble",
    )(upstream, tokens, grad_middle, gains, middle, ahead, weight_all, attn_all, mlp_all, w_qkv, w_in, own_gains)


def slice_start(t):
    return 128 * jnp.minimum(3 * t, 2 * t + 5)


def slice_place(t):
    start = 128 * min(3 * t, 2 * t + 5)
    return start, min(128 * min(3 * t + 3, 2 * t + 7), FF) - start


def body(count, tokens, d_out, segment_ids, position_ids, w_qkv, w_attn, w_in, w_out, gain_attn, gain_mlp):
    groups = lax.axis_size("heads")
    rows, width = tokens.shape
    shard = w_qkv.shape[0]
    reach = SEQ_MAX // (rows * groups)
    group = reach * groups
    sub = 8 // groups
    ctx, head = lax.axis_index("ctx"), lax.axis_index("heads")
    assert group == H and sub * groups == 8
    total = group * rows
    tile = 512

    def mlp_slice(value, axis, start, t):
        pads = [(0, 0), (0, 0)]
        pads[axis] = (0, SLICE)
        piece = lax.dynamic_slice_in_dim(jnp.pad(value, pads), start + slice_start(t), SLICE, axis)
        wide = jnp.minimum(slice_start(t + 1), FF) - slice_start(t)
        shape = [1, 1]
        shape[axis] = SLICE
        return jnp.where(jnp.arange(SLICE).reshape(shape) < wide, piece, jnp.zeros_like(piece))

    def mlp_part(t):
        return jnp.concatenate(
            [mlp_slice(w_in, 1, 0, t), mlp_slice(w_in, 1, FF, t), mlp_slice(w_out, 0, 0, t).T], axis=1
        )

    mlp = jnp.stack([mlp_part(x * groups + head) for x in range(sub)])
    gains_own = jnp.pad(jnp.stack([gain_attn, gain_mlp]).astype(F32), ((0, 6), (0, -shard % 128)))
    ids = jnp.pad(jnp.stack([position_ids, segment_ids]), ((0, 6), (0, 0)))
    freqs = jnp.power(160000.0, -(2.0 * jnp.arange(HALF, dtype=F32)) / HD)[:, None]
    input_all, gains, w_head, cosine, sine, marks, attn_half = begin(
        tokens, gains_own, ids, w_qkv, w_attn, freqs, count // sub, count, groups, reach
    )
    x = input_all.reshape(total, width)

    attended, wide, lse, qkv, attn_weights, mlp_pair, mlp_near = attend(
        x,
        w_head,
        cosine,
        sine,
        marks,
        attn_half,
        mlp.reshape(2, sub * shard // 2, 3 * SLICE),
        count,
        groups,
        reach,
        rows,
        tile,
    )
    attn_weights = attn_weights.reshape(width, width)
    mlp_all, upstream, middle, attended, mlp_weights = middle_step(
        attended, tokens, d_out, attn_weights, gains, mlp_pair, mlp_near, count, groups, reach
    )
    mlp_weights = mlp_weights.reshape(width, 3 * SLICE)
    grad_heads, grad_middle, attn_part, carry, forward, mlp_terms = turn_step(
        mlp_all.reshape(8 * rows, width),
        upstream.reshape(8 * rows, width),
        mlp_weights,
        middle,
        d_out,
        attn_weights,
        gains,
        attended.reshape(groups, width, rows),
        count,
        groups,
        reach,
    )
    attn_part = attn_part.reshape(count, shard, width // groups)
    ahead, upstream_in, mlp_all, weight_all, attn_all = attend_back(
        qkv,
        grad_heads,
        wide,
        lse,
        x,
        w_head,
        cosine,
        sine,
        forward,
        mlp_terms,
        carry,
        attn_part,
        groups,
        reach,
        tile,
    )
    result, grad_input, sum_qkv, sum_attn, sum_in, sum_out, gain_sums = assemble(
        upstream_in,
        tokens,
        grad_middle,
        gains,
        middle,
        ahead,
        weight_all,
        attn_all,
        mlp_all.reshape(8, shard, 3 * SLICE),
        w_qkv,
        w_in,
        jnp.pad(gains_own[:2, :shard], ((0, 6), (0, 0)), constant_values=1.0),
    )
    return (
        result,
        grad_input,
        sum_qkv,
        sum_attn,
        sum_in,
        sum_out,
        gain_sums[0],
        gain_sums[1],
    )


def solution(mesh):
    return jax.shard_map(
        functools.partial(body, mesh.shape["ctx"]),
        mesh=mesh,
        in_specs=(
            P(("ctx", "heads"), None),
            P(("ctx", "heads"), None),
            P(("ctx", "heads")),
            P(("ctx", "heads")),
            P("ctx", None),
            P("ctx", None),
            P("ctx", None),
            P(None, "ctx"),
            P("ctx"),
            P("ctx"),
        ),
        out_specs=(
            P(("ctx", "heads"), None),
            P(("ctx", "heads"), None),
            P("ctx", None),
            P("ctx", None),
            P("ctx", None),
            P(None, "ctx"),
            P("ctx"),
            P("ctx"),
        ),
        check_vma=False,
    )
```

```python
import functools

import jax
import jax.numpy as jnp
from jax import lax
from jax.experimental import pallas as pl
from jax.experimental.pallas import tpu as pltpu
from jax.sharding import PartitionSpec as P

H = 16
HD = 64
HALF = HD // 2
FF = 2624
SEQ_MAX = 2048
MASKED = -1e30
MARKS = 16
QM_END = HD + MARKS
K_END = QM_END + HD
KM_END = K_END + MARKS
V_END = KM_END + HD
SLICE = 384
BF = jnp.bfloat16
F32 = jnp.float32
MESH = pl.DeviceIdType.MESH
VMEM = pl.BlockSpec(memory_space=pltpu.VMEM)
ANY = pl.BlockSpec(memory_space=pl.ANY)
DMA = pltpu.SemaphoreType.DMA


def dot(left, right, left_dim, right_dim):
    return lax.dot_general(
        left, right, (((left_dim,), (right_dim,)), ((), ())), preferred_element_type=F32
    )


def norm_parts(values):
    average = jnp.mean(values, axis=-1, keepdims=True)
    centred = values - average
    inverse_std = lax.rsqrt(jnp.mean(centred * centred, axis=-1, keepdims=True) + 1e-05)
    return centred * inverse_std, inverse_std


def norm_back(upstream, normed, inverse_std, gain):
    scaled = upstream * gain
    return inverse_std * (
        scaled
        - jnp.mean(scaled, axis=-1, keepdims=True)
        - normed * jnp.mean(scaled * normed, axis=-1, keepdims=True)
    )


def flip(value, bit):
    return value + bit - 2 * bit * (value // bit % 2)


class Place:
    def __init__(self, groups, reach):
        self.groups, self.reach = groups, reach
        self.ctx = lax.axis_index("ctx")
        self.head = lax.axis_index("heads")
        self.local = self.ctx % reach
        self.base = self.ctx - self.local
        self.idx = self.local * groups + self.head

    def member(self, j):
        return {"ctx": self.base + j // self.groups, "heads": j % self.groups}


def greet(devices):
    barrier = pltpu.get_barrier_semaphore()
    for device in devices:
        pl.semaphore_signal(barrier, inc=1, device_id=device, device_id_type=MESH)


def meet(devices):
    greet(devices)
    pl.semaphore_wait(pltpu.get_barrier_semaphore(), len(devices))


def remote(source, target, device, send, recv):
    return pltpu.make_async_remote_copy(
        src_ref=source,
        dst_ref=target,
        send_sem=send,
        recv_sem=recv,
        device_id=device,
        device_id_type=MESH,
    )


def push(*operands):
    copy = remote(*operands)
    copy.start()
    return copy


def tree_parts(axes, rows):
    part = -(-rows // axes // 16) * 16
    starts = [min(part * a, rows) for a in range(axes + 1)]
    return [(starts[a], starts[a + 1] - starts[a]) for a in range(axes)]


class Tree:
    def __init__(self, place, axes, source, target, sems):
        self.place, self.axes, self.source, self.target = place, axes, source, target
        self.send, self.recv, self.core_send, self.core_recv, self.own = sems
        self.slots = 2 << axes
        self.levels, self.cores = [], []

    @staticmethod
    def scratch(axes):
        far, near = axes * axes, axes * axes + 1
        return [DMA((far,)), DMA((far,)), DMA((near,)), DMA((near,)), DMA]

    def origin(self, level, first):
        value = self.place.idx
        for k in range(level):
            value = flip(value, 2 << ((first + k) % self.axes))
        return value % self.slots

    def neighbour(self, axis):
        return self.place.member(flip(self.place.idx, 2 << (axis % self.axes)))

    def piece(self, slot, part):
        return self.target.at[slot] if part is None else self.target.at[slot, pl.ds(*part)]

    def to_core(self, source, slot, part):
        at = len(self.cores)
        self.cores.append(
            push(
                source,
                self.piece(slot, part),
                self.place.member(flip(self.place.idx, 1)),
                self.core_send.at[at],
                self.core_recv.at[at],
            )
        )

    def start(self):
        me = self.place.idx % self.slots
        self.levels.append(
            [
                push(
                    self.source, self.target.at[me], self.neighbour(a), self.send.at[a], self.recv.at[a]
                )
                for a in range(self.axes)
            ]
        )
        self.to_core(self.source, me, None)
        self.local = pltpu.make_async_copy(self.source, self.target.at[me], self.own)
        self.local.start()

    def forward(self, level):
        axes = self.axes
        parts = tree_parts(axes, self.target.shape[1])
        onward = []
        for a in range(axes):
            self.levels[level - 1][a].wait_recv()
            slot = self.origin(level, a)
            if level < axes:
                part = parts[a] if level + 1 == axes else None
                at = level * axes + a
                piece = self.piece(slot, part)
                onward.append(
                    push(piece, piece, self.neighbour(a + level), self.send.at[at], self.recv.at[at])
                )
                self.to_core(self.target.at[slot], slot, None)
            else:
                self.to_core(self.piece(slot, parts[a]), slot, parts[a])
        self.levels.append(onward)

    def finish(self):
        self.local.wait()
        for level in self.levels:
            for copy in level:
                copy.wait_send()
        for copy in self.cores:
            copy.wait()


class Halving:
    def __init__(self, place, axes, value, result, scratch, firsts=None):
        self.firsts = firsts = firsts or list(range(axes))
        self.axes, self.value, self.result = axes, value, result
        self.other, self.held, self.land, send, recv, send0, recv0 = scratch
        self.blocks = 1 << axes
        width = value.shape[-1]
        part = width // len(firsts)
        self.columns = [pl.ds(part * a, part) for a in range(len(firsts))]
        self.core = place.idx % 2
        self.chip = place.idx // 2 % self.blocks
        self.sources = []
        for j in range(self.blocks):
            k = self.chip
            for a in range(axes):
                if j >> a & 1:
                    k = flip(k, 1 << a)
            self.sources.append(k)
        self.first, self.copies = [], {}
        for p in range(len(firsts)):
            self.first.append(
                remote(
                    value.at[:, 1 - self.core, :, self.columns[p]],
                    self.other.at[:, :, self.columns[p]],
                    place.member(flip(place.idx, 1)),
                    send0.at[p],
                    recv0.at[p],
                )
            )
            for step in range(axes):
                bit, sent = self.sent(p, step)
                for j in sent:
                    self.copies[p, j] = remote(
                        self.held.at[j, :, self.columns[p]],
                        self.land.at[j, :, self.columns[p]],
                        place.member(flip(place.idx, 2 * bit)),
                        send.at[p, j],
                        recv.at[p, j],
                    )

    @staticmethod
    def scratch(axes, rows, width):
        blocks = 1 << axes
        return [
            pltpu.VMEM((blocks, rows, width), BF),
            pltpu.VMEM((blocks, rows, width), BF),
            pltpu.VMEM((blocks, rows, width), BF),
            DMA((axes, blocks)),
            DMA((axes, blocks)),
            DMA((axes,)),
            DMA((axes,)),
        ]

    def sent(self, part, step):
        first = self.firsts[part]
        seen = [1 << ((first + s) % self.axes) for s in range(step)]
        bit = 1 << ((first + step) % self.axes)
        return bit, [j for j in range(self.blocks) if j & bit and not any(j & s for s in seen)]

    def start(self):
        for copy in self.first:
            copy.start()

    def pair(self):
        for p in range(len(self.firsts)):
            cols = self.columns[p]
            self.first[p].wait_recv()
            _, early = self.sent(p, 0)
            for j in early + [j for j in range(self.blocks) if j not in early]:
                k = self.sources[j]
                self.held[j, :, cols] = (
                    self.value[k, self.core, :, cols].astype(F32) + self.other[k, :, cols].astype(F32)
                ).astype(BF)
                if j in early:
                    self.copies[p, j].start()

    def halve(self, step):
        for p in range(len(self.firsts)):
            cols = self.columns[p]
            bit, arrived = self.sent(p, step)
            onward = self.sent(p, step + 1)[1] if step + 1 < self.axes else []
            for j in sorted(arrived, key=lambda j: (j - bit) not in onward):
                self.copies[p, j].wait_recv()
                k = j - bit
                total = self.held[k, :, cols].astype(F32) + self.land[j, :, cols].astype(F32)
                if step + 1 < self.axes:
                    self.held[k, :, cols] = total.astype(BF)
                    if k in onward:
                        self.copies[p, k].start()
                else:
                    self.result[:, cols] = total

    def run(self):
        self.start()
        self.pair()
        for step in range(self.axes):
            self.halve(step)
        self.finish()

    def finish(self):
        for copy in self.first:
            copy.wait_send()
        for copy in self.copies.values():
            copy.wait_send()


class Lines:
    def __init__(self, count, source, target, send, recv, own):
        me = lax.axis_index("ctx")
        self.copies = [pltpu.make_async_copy(source.at[me], target.at[me], own)]
        for step in range(1, count):
            peer = (me + step) % count
            self.copies.append(
                remote(source.at[peer], target.at[me], {"ctx": peer}, send.at[step - 1], recv.at[step - 1])
            )

    @staticmethod
    def scratch(count):
        return [DMA((count - 1,)), DMA((count - 1,)), DMA]

    def start(self):
        for copy in self.copies:
            copy.start()

    def finish(self):
        for copy in self.copies:
            copy.wait()


def everyone(place, count):
    group = place.reach * place.groups
    mates = [place.member((place.idx + step) % group) for step in range(1, group)]
    outside = [{"ctx": (place.base + place.reach + step) % count} for step in range(count - place.reach)]
    return mates + outside


def spread(place, source, target, sems, me=None):
    send, recv, own = sems
    count = target.shape[0]
    copies = []
    for step in range(1, count):
        peer = (place.idx + step) % count
        copies.append(
            push(
                source.at[peer],
                target.at[place.idx],
                place.member(peer),
                send.at[step - 1],
                recv.at[step - 1],
            )
        )
    local = pltpu.make_async_copy(source.at[place.idx], target.at[place.idx], own)
    local.start()
    copies.append(local)
    return copies


def begin_kernel(
    groups,
    reach,
    count,
    tokens,
    gains,
    ids,
    w_qkv,
    w_attn,
    freqs,
    input_all,
    gains_all,
    w_head,
    cosine,
    sine,
    marks,
    attn_half,
    ids_all,
    slab,
    mine,
    gain_land,
    own_sems,
    ids_send,
    ids_recv,
    gain_send,
    gain_recv,
    slab_send,
    slab_recv,
    wide_send,
    wide_recv,
    core_send,
    core_recv,
    *tree_sems,
):
    place = Place(groups, reach)
    group = reach * groups
    ctx, head, idx = place.ctx, place.head, place.idx
    shard = w_qkv.shape[0]
    ring = attn_half.shape[0]
    sub = count // ring
    side, spot = ctx % sub, ctx // sub
    lanes = attn_half.shape[2] // groups
    core = {"heads": flip(head, 1)}
    mates = [place.member((idx + step) % group) for step in range(1, group)]
    lines = [{"ctx": (ctx + step) % count} for step in range(1, count)]
    meet(everyone(place, count))
    first = [
        push(gains, gain_land.at[ctx], lines[step - 1], gain_send.at[step - 1], gain_recv.at[step - 1])
        for step in range(1, count)
    ]
    half = pl.ds(pl.multiple_of(head % 2 * (shard // 2), 16), shard // 2)
    gain_land[ctx] = gains[...]
    where = lambda h: pl.ds(pl.multiple_of(h * lanes, 128), lanes)
    across = where(head)
    own = [
        pltpu.make_async_copy(ids, ids_all.at[idx], own_sems.at[3]),
        pltpu.make_async_copy(w_attn.at[:, across], attn_half.at[spot, :, across], own_sems.at[4]),
    ]
    for third in range(3):
        start = pl.multiple_of(third * 1024 + idx // 2 * 128, 128)
        own.append(
            pltpu.make_async_copy(
                w_qkv.at[half, pl.ds(start, 128)],
                slab.at[ctx, half, pl.ds(third * 128, 128)],
                own_sems.at[third],
            )
        )
    for copy in own:
        copy.start()
    for copy in first:
        copy.wait_recv()
    gain, gain_two = (
        jnp.concatenate([gain_land[c, k : k + 1, :shard] for c in range(count)], axis=1)
        for k in range(2)
    )
    normed, _ = norm_parts(tokens[...].astype(F32))
    mine[...] = (normed * gain).astype(BF)
    tree = Tree(place, 3, mine, input_all, tree_sems[:5])
    tree.start()
    small = [
        push(ids, ids_all.at[idx], mates[step - 1], ids_send.at[step - 1], ids_recv.at[step - 1])
        for step in range(1, group)
    ]
    thirds = []
    for step in range(1, count):
        peer = (ctx + step) % count
        column = ((peer % reach) * groups + head) // 2 * 128
        for third in range(3):
            start = pl.multiple_of(third * 1024 + column, 128)
            thirds.append(
                push(
                    w_qkv.at[half, pl.ds(start, 128)],
                    slab.at[ctx, half, pl.ds(third * 128, 128)],
                    lines[step - 1],
                    slab_send.at[step - 1, third],
                    slab_recv.at[step - 1, third],
                )
            )
    gains_all[0:1, :] = gain
    gains_all[1:2, :] = gain_two
    late = []
    for step in range(1, ring):
        late.append(
            push(
                w_attn.at[:, across],
                attn_half.at[spot, :, across],
                {"ctx": (spot + step) % ring * sub + side},
                wide_send.at[step - 1],
                wide_recv.at[step - 1],
            )
        )
    tree.forward(1)
    for copy in own:
        copy.wait()
    for copy in thirds:
        copy.wait_recv()
    for copy in late:
        copy.wait_recv()
    collect = Collect(
        groups, [(attn_half.at[:, :, across], lambda h: attn_half.at[:, :, where(h)])], *tree_sems[5:]
    )
    collect.start(0)
    shared = push(slab.at[:, half], slab.at[:, half], core, core_send, core_recv)
    for copy in small:
        copy.wait()
    row = lambda k: jnp.concatenate([ids_all[j, k : k + 1, :] for j in range(group)], axis=1)
    angles = freqs[...] * row(0).astype(F32)
    cosine[...] = jnp.cos(angles)
    sine[...] = jnp.sin(angles)
    parity = (row(1) % 2).astype(F32)
    blank = jnp.zeros((MARKS - 2, parity.shape[1]), F32)
    marks[...] = jnp.concatenate(
        [parity, 1.0 - parity, blank, (1.0 - parity) * MASKED, parity * MASKED, blank], axis=0
    ).astype(BF)
    tree.forward(2)
    shared.wait()
    odd = head % 2 == 1
    for c in range(count):
        rows = slice(c * shard, (c + 1) * shard)
        block = slab[c].astype(F32)
        parts = []
        for third in range(3):
            at = third * 128
            parts.append(jnp.where(odd, block[:, at + HD : at + 128], block[:, at : at + HD]))
        w_head[rows] = jnp.concatenate(parts, axis=1).astype(BF)
    collect.forward(0)
    tree.forward(3)
    tree.finish()
    collect.finish()
    for copy in first + thirds + late:
        copy.wait_send()


def begin(tokens, gains, ids, w_qkv, w_attn, freqs, ring, count, groups, reach):
    rows, width = tokens.shape
    shard = w_qkv.shape[0]
    group = groups * reach
    sems = lambda *shape: [DMA(shape), DMA(shape)]
    return pl.pallas_call(
        functools.partial(begin_kernel, groups, reach, count),
        in_specs=[VMEM, VMEM, ANY, ANY, ANY, VMEM],
        out_specs=[ANY, VMEM, VMEM, VMEM, VMEM, VMEM, ANY],
        out_shape=[
            jax.ShapeDtypeStruct((group, rows, width), BF),
            jax.ShapeDtypeStruct((8, width), F32),
            jax.ShapeDtypeStruct((width, 3 * HD), BF),
            jax.ShapeDtypeStruct((HALF, group * rows), F32),
            jax.ShapeDtypeStruct((HALF, group * rows), F32),
            jax.ShapeDtypeStruct((2 * MARKS, group * rows), BF),
            jax.ShapeDtypeStruct((ring, shard, width), BF),
        ],
        scratch_shapes=[
            pltpu.VMEM((group, 8, rows), jnp.int32),
            pltpu.VMEM((count, shard, 3 * 128), BF),
            pltpu.VMEM((rows, width), BF),
            pltpu.VMEM((count, 8, gains.shape[1]), F32),
            DMA((5,)),
            *sems(group - 1),
            *sems(count - 1),
            *sems(count - 1, 3),
            *sems(ring - 1),
            DMA,
            DMA,
            *Tree.scratch(3),
            *Collect.scratch(1, groups),
        ],
        compiler_params=pltpu.CompilerParams(
            collective_id=0, has_side_effects=True, vmem_limit_bytes=12 << 20
        ),
        cost_estimate=pl.CostEstimate(flops=0, bytes_accessed=30 << 20, transcendentals=0),
        name="begin",
    )(tokens, gains, ids, w_qkv, w_attn, freqs)


class Line:
    def __init__(self, length, sub, first, sources, targets, send, recv):
        ctx = lax.axis_index("ctx")
        spot, side = ctx // sub, ctx % sub
        self.length, self.spot, self.first = length, spot, first
        self.waited = 0
        beside = [{"ctx": (spot + 1) % length * sub + side}, {"ctx": (spot + length - 1) % length * sub + side}]
        self.copies = [
            [
                remote(sources[d][q], targets[d][q], beside[d], send.at[d, q], recv.at[d, q])
                for q in range(len(sources[d]))
            ]
            for d in range(2)
        ]

    def sends(self, d, q):
        s, spot, last = (q + self.first) // 2, self.spot, self.length - 1
        if d:
            return jnp.logical_and(spot + s <= last, spot > 0)
        return jnp.logical_and(spot >= s, spot < last)

    def receives(self, d, q):
        s = (q + self.first) // 2
        return self.spot + s + 1 < self.length if d else self.spot > s

    def arrive(self, q):
        for d in range(2):
            pl.when(self.receives(d, q))(self.copies[d][q].wait_recv)
        self.waited = q + 1

    def start(self, q):
        if q >= 2:
            self.arrive(q - 2)
        for d in range(2):
            pl.when(self.sends(d, q))(self.copies[d][q].start)

    def finish(self):
        for q in range(self.waited, len(self.copies[0])):
            self.arrive(q)
        for d in range(2):
            for q, copy in enumerate(self.copies[d]):
                pl.when(self.sends(d, q))(copy.wait_send)


def ring_half(sub, side, k):
    return (side + k) % 2 if sub == 2 else k


class Columns:
    def __init__(self, place, part, whole, own, side_send, side_recv, near_send, near_recv):
        _, sub, _, width = whole.shape
        side = place.ctx % sub
        half = pl.ds(pl.multiple_of(place.head % 2 * (width // 2), 128), width // 2)
        self.own = pltpu.make_async_copy(part, whole.at[:, side], own)
        self.sides, self.near = [], []
        for step in range(1, sub):
            peer, source = (side + step) % sub, (side - step + sub) % sub
            self.sides.append(
                remote(
                    part.at[:, :, half],
                    whole.at[:, side, :, half],
                    {"ctx": place.ctx - side + peer},
                    side_send.at[step - 1],
                    side_recv.at[step - 1],
                )
            )
            here = whole.at[:, source, :, half]
            self.near.append(
                remote(
                    here, here, {"heads": flip(place.head, 1)}, near_send.at[step - 1], near_recv.at[step - 1]
                )
            )

    @staticmethod
    def scratch(sub):
        count = (max(sub - 1, 1),)
        return [DMA, DMA(count), DMA(count), DMA(count), DMA(count)]

    def start(self):
        self.own.start()
        for copy in self.sides:
            copy.start()

    def across(self):
        for side, near in zip(self.sides, self.near):
            side.wait_recv()
            near.start()

    def finish(self):
        self.own.wait()
        for side, near in zip(self.sides, self.near):
            side.wait_send()
            near.wait()


def attend_kernel(
    groups,
    reach,
    lines,
    tile,
    x_ref,
    w_ref,
    cos_ref,
    sin_ref,
    mark_ref,
    attn_half,
    mlp,
    out_ref,
    wide_ref,
    lse_ref,
    qkv_ref,
    attn_all,
    mlp_pair,
    mlp_near,
    ring_send,
    ring_recv,
    swap_send,
    swap_recv,
    swap_own,
    *sems,
):
    count = x_ref.shape[0]
    step = pl.program_id(0)
    steps = count // tile
    place = Place(groups, reach)
    ring_size, sub = attn_all.shape[:2]
    side = place.ctx % sub
    early = mlp_near.shape[1]
    if sub == 2:
        kept = pltpu.make_async_copy(mlp.at[side], mlp_pair.at[side], swap_own)
        swap = [
            remote(
                mlp.at[1 - side],
                mlp_pair.at[side],
                {"ctx": place.ctx + 1 - 2 * side},
                swap_send,
                swap_recv,
            )
        ]
        sources = [mlp.at[side], mlp_pair.at[1 - side]]
    else:
        kept = pltpu.make_async_copy(mlp, mlp_pair, swap_own)
        swap = []
        sources = [mlp.at[0], mlp.at[1]]
    ring = Line(
        ring_size,
        sub,
        0,
        [sources + [mlp_near.at[d, q] for q in range(early - 2)] for d in range(2)],
        [[mlp_near.at[d, q] for q in range(early)] for d in range(2)],
        ring_send,
        ring_recv,
    )
    columns = Columns(place, attn_half, attn_all, *sems)

    @pl.when(step == 0)
    def _():
        meet(everyone(place, lines))
        for copy in swap:
            copy.start()
        ring.start(0)
        kept.start()
        columns.start()
        qkv_ref[HD:QM_END, :] = mark_ref[:MARKS, :]
        qkv_ref[K_END:KM_END, :] = mark_ref[MARKS:, :]

        @pl.loop(0, steps)
        def _(i):
            at = pl.ds(pl.multiple_of(i * tile, tile), tile)
            cosine, sine = cos_ref[:, at], sin_ref[:, at]
            part = dot(w_ref[...], x_ref[at, :], 0, 1)

            def turn(value):
                front, back = value[:HALF], value[HALF:]
                return jnp.concatenate(
                    [front * cosine - back * sine, back * cosine + front * sine], axis=0
                )

            qkv_ref[:HD, at] = (turn(part[:HD]) * 0.125).astype(BF)
            qkv_ref[QM_END:K_END, at] = turn(part[HD : 2 * HD]).astype(BF)
            qkv_ref[KM_END:, at] = part[2 * HD :].astype(BF)

    here = pl.ds(pl.multiple_of(step * tile, tile), tile)
    query = qkv_ref[:QM_END, here]
    keys = [slice(j * tile, (j + 1) * tile) for j in range(steps)]
    scores = [dot(qkv_ref[QM_END:KM_END, at], query, 0, 0) for at in keys]
    top = functools.reduce(jnp.maximum, [jnp.max(s, axis=0, keepdims=True) for s in scores])
    raised = [jnp.exp(s - top) for s in scores]
    total = functools.reduce(jnp.add, [jnp.sum(e, axis=0, keepdims=True) for e in raised])
    scale = 1.0 / total
    result = jnp.zeros((HD, tile), F32)
    for j in range(steps):
        result += dot(qkv_ref[KM_END:, keys[j]], (raised[j] * scale).astype(BF), 1, 0)
    rows = out_ref.shape[2]
    for k in range(tile // rows):
        out_ref[step * (tile // rows) + k] = result[:, k * rows : (k + 1) * rows].astype(BF)
    wide_ref[:, here] = result
    lse_ref[:, here] = top + jnp.log(total)

    @pl.when(step == min(1, steps - 1))
    def _():
        for copy in swap:
            copy.wait_recv()
        for q in range(1, min(early, 3)):
            ring.start(q)

    @pl.when(step == steps - 1)
    def _():
        columns.across()
        for q in range(3, early):
            ring.start(q)
        ring.finish()
        for copy in swap:
            copy.wait_send()
        kept.wait()
        columns.finish()


def attend(x, w, cosine, sine, marks, attn_half, mlp, lines, groups, reach, rows, tile):
    count, width = x.shape
    ring, shard, _ = attn_half.shape
    sub = lines // ring
    early = ring - 1
    return pl.pallas_call(
        functools.partial(attend_kernel, groups, reach, lines, tile),
        grid=(count // tile,),
        in_specs=[
            VMEM,
            VMEM,
            VMEM,
            VMEM,
            VMEM,
            ANY,
            ANY,
        ],
        out_specs=[
            VMEM,
            VMEM,
            VMEM,
            VMEM,
            ANY,
            ANY,
            ANY,
        ],
        out_shape=[
            jax.ShapeDtypeStruct((count // rows, HD, rows), BF),
            jax.ShapeDtypeStruct((HD, count), F32),
            jax.ShapeDtypeStruct((1, count), F32),
            jax.ShapeDtypeStruct((V_END, count), BF),
            jax.ShapeDtypeStruct((ring, sub, shard, width), BF),
            jax.ShapeDtypeStruct(mlp.shape, BF),
            jax.ShapeDtypeStruct((2, early, *mlp.shape[1:]), BF),
        ],
        scratch_shapes=[DMA((2, early)), DMA((2, early)), DMA, DMA, DMA, *Columns.scratch(sub)],
        compiler_params=pltpu.CompilerParams(
            collective_id=5, has_side_effects=True, vmem_limit_bytes=20 << 20
        ),
        cost_estimate=pl.CostEstimate(
            flops=count * count * HD * 8, bytes_accessed=count * 4096, transcendentals=count * count
        ),
        name="attend",
    )(x, w, cosine, sine, marks, attn_half, mlp)


def middle_kernel(
    groups,
    reach,
    lines,
    outgoing,
    tokens,
    d_out,
    w_attn,
    gains,
    mlp_pair,
    mlp_near,
    mlp_all,
    upstream_all,
    middle,
    attended,
    mlp_weights,
    land,
    mine,
    a2a_send,
    a2a_recv,
    own,
    ring_send,
    ring_recv,
    ring_own,
    land_own,
    *tree_sems,
):
    place = Place(groups, reach)
    group = groups * reach
    early, count = mlp_near.shape[1], mlp_weights.shape[0]
    sub = lines // count
    spot, side = place.ctx // sub, place.ctx % sub

    def slot(d, q, ahead):
        block = (spot + (q // 2 + ahead if d else count - q // 2 - ahead)) % count
        return mlp_weights.at[block, ring_half(sub, side, q % 2)]

    rest = range(early, 2 * (count - 1))
    ring = Line(
        count,
        sub,
        early,
        [[mlp_near.at[d, q - 2] if q - 2 < early else slot(d, q, 0) for q in rest] for d in range(2)],
        [[slot(d, q, 0) for q in rest] for d in range(2)],
        ring_send,
        ring_recv,
    )
    local = [pltpu.make_async_copy(mlp_pair, mlp_weights.at[spot], ring_own.at[0])]
    near = []
    for d in range(2):
        for q in range(early):
            copy = pltpu.make_async_copy(
                mlp_near.at[d, q], slot(d, q, 1), ring_own.at[1 + d * early + q]
            )
            there = spot + q // 2 + 1 < count if d else spot > q // 2
            near.append((there, copy))
    meet(everyone(place, lines))
    copies = spread(place, outgoing, land, (a2a_send, a2a_recv, own))
    ring.start(0)
    ring.start(1)
    up = Tree(place, 2, d_out, upstream_all, tree_sems[5:10])
    up.start()
    for copy in local:
        copy.start()
    for there, copy in near:
        pl.when(there)(copy.start)
    for copy in copies:
        copy.wait()
    collect = Collect(groups, [(land, lambda h: attended.at[h])], *tree_sems[10:])
    collect.start(0)
    local.append(pltpu.make_async_copy(land, attended.at[place.head], land_own))
    local[-1].start()
    value = tokens[...].astype(F32) + dot(
        land[...].reshape(group * HD, tokens.shape[0]), w_attn[...], 0, 0
    )
    middle[...] = value
    normed, _ = norm_parts(value)
    mine[...] = (normed * gains[1:2, :]).astype(BF)
    tree = Tree(place, 2, mine, mlp_all, tree_sems[:5])
    tree.start()
    up.forward(1)
    for q in range(2, len(rest)):
        ring.start(q)
    tree.forward(1)
    up.forward(2)
    tree.forward(2)
    collect.forward(0)
    up.finish()
    tree.finish()
    collect.finish()
    for copy in local:
        copy.wait()
    for there, copy in near:
        pl.when(there)(copy.wait)
    ring.finish()


def middle_step(outgoing, tokens, d_out, w_attn, gains, mlp_pair, mlp_near, lines, groups, reach):
    rows, width = tokens.shape
    group = groups * reach
    early, sub = mlp_near.shape[1], 8 // groups
    ring = lines // sub
    left = 2 * (ring - 1) - early
    return pl.pallas_call(
        functools.partial(middle_kernel, groups, reach, lines),
        in_specs=[ANY, VMEM, ANY, VMEM, VMEM, ANY, ANY],
        out_specs=[ANY, ANY, VMEM, ANY, ANY],
        out_shape=[
            jax.ShapeDtypeStruct((8, rows, width), BF),
            jax.ShapeDtypeStruct((8, rows, width), BF),
            jax.ShapeDtypeStruct((rows, width), F32),
            jax.ShapeDtypeStruct((groups, group, HD, rows), BF),
            jax.ShapeDtypeStruct((ring, *mlp_pair.shape), BF),
        ],
        scratch_shapes=[
            pltpu.VMEM((group, HD, rows), BF),
            pltpu.VMEM((rows, width), BF),
            DMA((group - 1,)),
            DMA((group - 1,)),
            DMA,
            DMA((2, left)),
            DMA((2, left)),
            DMA((2 * early + 1,)),
            DMA,
            *Tree.scratch(2),
            *Tree.scratch(2),
            *Collect.scratch(1, groups),
        ],
        compiler_params=pltpu.CompilerParams(
            collective_id=1, has_side_effects=True, vmem_limit_bytes=12 << 20
        ),
        cost_estimate=pl.CostEstimate(flops=1 << 28, bytes_accessed=12 << 20, transcendentals=0),
        name="middle_step",
    )(outgoing, tokens, d_out, w_attn, gains, mlp_pair, mlp_near)


class Sum:
    def __init__(self, place, terms, first, held, stage, land, send, recv):
        self.terms, self.first, self.stage, self.land = terms, first, stage, land
        self.half = stage.shape[2]
        length = terms.shape[0] // (2 * self.half)
        lines_sub = 8 // place.groups
        spot, side = place.ctx // lines_sub, place.ctx % lines_sub
        self.length, self.spot = length, spot
        self.held = lambda d, q: land.at[d, q] if q >= 0 else held.at[d, q + 2]
        beside = [
            {"ctx": (spot + 1) % length * lines_sub + side},
            {"ctx": (spot + length - 1) % length * lines_sub + side},
        ]
        self.copies = [
            [
                remote(stage.at[d, q], land.at[d, q], beside[d], send.at[d, q], recv.at[d, q])
                for q in range(stage.shape[1])
            ]
            for d in range(2)
        ]

    @staticmethod
    def scratch(count, half):
        return [
            pltpu.VMEM((2, count, *half), BF),
            pltpu.VMEM((2, count, *half), BF),
            DMA((2, count)),
            DMA((2, count)),
        ]

    def sends(self, d, q):
        s, spot, last = (q + self.first) // 2, self.spot, self.length - 1
        if d:
            return jnp.logical_and(spot >= last - s, spot > 0)
        return jnp.logical_and(spot <= s, spot < last)

    def receives(self, d, q):
        s, spot, last = (q + self.first) // 2, self.spot, self.length - 1
        if d:
            return jnp.logical_and(spot >= last - 1 - s, spot < last)
        return jnp.logical_and(spot <= s + 1, spot > 0)

    def clear(self):
        for d in range(2):
            for q in range(len(self.copies[d])):

                @pl.when(jnp.logical_not(self.receives(d, q)))
                def _():
                    self.land[d, q] = jnp.zeros(self.land.shape[2:], BF)

    def block(self, at, k):
        return self.terms[pl.ds(pl.multiple_of((2 * at + k) * self.half, 16), self.half), :]

    def arrive(self, q):
        for d in range(2):
            pl.when(self.receives(d, q))(self.copies[d][q].wait_recv)

    def start(self, q):
        if q >= 2:
            self.arrive(q - 2)
        step, k = (q + self.first) // 2, (q + self.first) % 2
        for d in range(2):
            at = self.spot + (step + 1 if d else self.length - 1 - step)

            @pl.when(self.sends(d, q))
            def _():
                value = self.block(at % self.length, k)
                if q + self.first >= 2:
                    value = (value.astype(F32) + self.held(d, q - 2)[...].astype(F32)).astype(BF)
                self.stage[d, q] = value
                self.copies[d][q].start()

    def finish(self):
        count = len(self.copies[0])
        for q in range(max(count - 2, 0), count):
            self.arrive(q)
        for d in range(2):
            for q, copy in enumerate(self.copies[d]):
                pl.when(self.sends(d, q))(copy.wait_send)


def mlp_rows(chunk, x_ref, up_ref, w_ref, back_ref, forward_ref, kept):
    count = x_ref.shape[0]
    rows = back_ref.shape[2]

    @pl.loop(0, count // chunk)
    def _(i):
        at = pl.ds(pl.multiple_of(i * chunk, chunk), chunk)
        gate_up = dot(x_ref[at, :], w_ref[:, : 2 * SLICE], 1, 0)
        left, right = gate_up[:, :SLICE], gate_up[:, SLICE:]
        grad_mixed = dot(up_ref[at, :], w_ref[:, 2 * SLICE :], 1, 0)
        normal_cdf = 0.5 * (1.0 + lax.erf(left * 0.7071067811865476))
        gelu = left * normal_cdf
        density = jnp.exp(-0.5 * left * left) * 0.3989422804014327
        kept[at, :SLICE] = (grad_mixed * right * (normal_cdf + left * density)).astype(BF)
        kept[at, SLICE : 2 * SLICE] = (grad_mixed * gelu).astype(BF)
        kept[at, 2 * SLICE :] = (gelu * right).astype(BF)
        back = dot(kept[at, : 2 * SLICE], w_ref[:, : 2 * SLICE], 1, 1).astype(BF)
        forward = dot(kept[at, 2 * SLICE :], w_ref[:, 2 * SLICE :], 1, 1).astype(BF)
        pairs = chunk // rows // 2
        for j in range(chunk // rows):
            piece = slice(j * rows, (j + 1) * rows)
            back_ref[i * pairs + j // 2, j % 2] = back[piece]
            forward_ref[i * pairs + j // 2, j % 2] = forward[piece]


def mlp_weights_back(chunk, x_ref, up_ref, kept, terms_ref):
    @pl.loop(0, x_ref.shape[1] // chunk)
    def _(i):
        at = pl.ds(pl.multiple_of(i * chunk, chunk), chunk)
        terms_ref[at, : 2 * SLICE] = dot(x_ref[:, at], kept[:, : 2 * SLICE], 0, 0).astype(BF)
        terms_ref[at, 2 * SLICE :] = dot(up_ref[:, at], kept[:, 2 * SLICE :], 0, 0).astype(BF)


def turn_kernel(
    groups,
    reach,
    lines,
    x,
    up,
    mlp_weights,
    middle,
    d_out,
    w_attn,
    gains,
    attended,
    grads,
    grad_middle,
    attn_part,
    carry,
    forward,
    terms,
    kept,
    partial,
    columns,
    total,
    outgoing,
    branch,
    a2a_send,
    a2a_recv,
    own,
    side_send,
    side_recv,
    side_own,
    *rest,
):
    place = Place(groups, reach)
    group = groups * reach
    lanes = branch.shape[2]
    sums = Sum(place, terms, 0, None, *rest[7:])
    count = rest[7].shape[1]
    devices = everyone(place, lines)
    sums.clear()
    greet(devices)
    mlp_rows(512, x, up, mlp_weights, partial, forward, kept)
    pl.semaphore_wait(pltpu.get_barrier_semaphore(), len(devices))
    halving = Halving(place, 2, partial, total, rest[:7])
    halving.start()
    mlp_weights_back(512, x, up, kept, terms)
    sums.start(0)
    sums.start(1)
    halving.pair()
    halving.halve(0)
    halving.halve(1)
    for q in range(2, count):
        sums.start(q)
    halving.finish()
    normed, inverse_std = norm_parts(middle[...])
    upstream = total[...]
    grad = d_out[...].astype(F32) + norm_back(upstream, normed, inverse_std, gains[1:2, :])
    grad_middle[...] = grad
    low = grad.astype(BF)
    for g in range(groups):
        branch[g] = low[:, g * lanes : (g + 1) * lanes]
    outgoing[...] = dot(w_attn[...], low, 1, 1).astype(BF).reshape(outgoing.shape)
    copies = spread(place, outgoing, grads, (a2a_send, a2a_recv, own))
    for step in range(1, groups):
        peer = (place.head + step) % groups
        copies.append(
            push(
                branch.at[peer],
                columns.at[place.head],
                {"heads": peer},
                side_send.at[step - 1],
                side_recv.at[step - 1],
            )
        )
    local = pltpu.make_async_copy(branch.at[place.head], columns.at[place.head], side_own)
    local.start()
    for copy in copies[-(groups - 1) :]:
        copy.wait()
    local.wait()
    attn_part[...] = functools.reduce(
        jnp.add, [dot(attended[g], columns[g], 1, 0) for g in range(groups)]
    ).astype(BF)
    for copy in copies[: -(groups - 1)]:
        copy.wait()
    sums.finish()
    for d in range(2):
        for q in range(2):
            carry[d, q] = sums.land[d, count - 2 + q]


def turn_step(x, up, mlp_weights, middle, d_out, w_attn, gains, attended, lines, groups, reach):
    rows, width = middle.shape
    count = lines * groups // 8 - 1
    half = (width // (2 * (count + 1)), 3 * SLICE)
    group = groups * reach
    return pl.pallas_call(
        functools.partial(turn_kernel, groups, reach, lines),
        in_specs=[VMEM] * 8,
        out_specs=[ANY, VMEM, VMEM, VMEM, VMEM, VMEM],
        out_shape=[
            jax.ShapeDtypeStruct((group, HD, rows), BF),
            jax.ShapeDtypeStruct((rows, width), F32),
            jax.ShapeDtypeStruct((width, width // groups), BF),
            jax.ShapeDtypeStruct((2, 2, *half), BF),
            jax.ShapeDtypeStruct((4, 2, rows, width), BF),
            jax.ShapeDtypeStruct((width, 3 * SLICE), BF),
        ],
        scratch_shapes=[
            pltpu.VMEM((8 * rows, 3 * SLICE), BF),
            pltpu.VMEM((4, 2, rows, width), BF),
            pltpu.VMEM((groups, rows, width // groups), BF),
            pltpu.VMEM((rows, width), F32),
            pltpu.VMEM((group, HD, rows), BF),
            pltpu.VMEM((groups, rows, width // groups), BF),
            DMA((group - 1,)),
            DMA((group - 1,)),
            DMA,
            DMA((groups - 1,)),
            DMA((groups - 1,)),
            DMA,
            *Halving.scratch(2, rows, width),
            *Sum.scratch(count, half),
        ],
        compiler_params=pltpu.CompilerParams(
            collective_id=2, has_side_effects=True, vmem_limit_bytes=24 << 20
        ),
        cost_estimate=pl.CostEstimate(flops=1 << 33, bytes_accessed=12 << 20, transcendentals=0),
        name="turn_step",
    )(x, up, mlp_weights, middle, d_out, w_attn, gains, attended)


def end_part(
    place,
    lines,
    partial,
    weight,
    mlp,
    attn,
    total,
    mlp_all,
    weight_all,
    attn_all,
    sum_line,
    sum_attn,
    lined,
    summed,
    swap_send,
    swap_recv,
    own,
    *rest,
):
    groups, reach = place.groups, place.reach
    sub = mlp.shape[0]
    mine, head = place.ctx % sub, place.head
    wide = Halving(place, 3, partial, total, rest[:7], [2, 1])
    swap = Lines(lines, weight, lined, *rest[7:10])
    wide.start()
    swap.start()
    wide.pair()
    sum_line()
    swaps = []
    for step in range(1, sub):
        peer = (mine + step) % sub
        swaps.append(
            push(
                mlp.at[peer],
                mlp_all.at[mine, head],
                {"ctx": place.ctx - mine + peer},
                swap_send.at[step - 1],
                swap_recv.at[step - 1],
            )
        )
    pieces = [(mlp.at[mine], lambda h: mlp_all.at[mine, h]), (attn, lambda h: attn_all.at[h])]
    for step in range(1, sub):
        source = (mine - step + sub) % sub
        pieces.append(
            (mlp_all.at[source, head], lambda h, source=source: mlp_all.at[source, h])
        )
    pieces.append((summed, lambda h: weight_all.at[h]))
    collect = Collect(groups, pieces, *rest[10:14])
    local = [
        pltpu.make_async_copy(mlp.at[mine], mlp_all.at[mine, head], own.at[0]),
        pltpu.make_async_copy(attn, attn_all.at[head], own.at[1]),
        pltpu.make_async_copy(summed, weight_all.at[head], own.at[2]),
    ]
    local[0].start()
    collect.start(0)
    sum_attn()
    local[1].start()
    collect.start(1)
    for step in range(1, sub):
        swaps[step - 1].wait_recv()
        collect.start(step + 1)
    wide.halve(0)
    swap.finish()
    for r in range(reach):
        summed[r] = functools.reduce(
            jnp.add, [lined[r + reach * g].astype(F32) for g in range(lines // reach)]
        ).astype(BF)
    local[2].start()
    collect.start(sub + 1)
    wide.halve(1)
    collect.forward(0)
    collect.forward(1)
    wide.halve(2)
    for n in range(2, sub + 2):
        collect.forward(n)
    for copy in local:
        copy.wait()
    for copy in swaps:
        copy.wait_send()
    collect.finish()
    wide.finish()


def attend_back_kernel(
    groups,
    reach,
    lines,
    tile,
    qkv_ref,
    grad_ref,
    wide_ref,
    lse_ref,
    x_ref,
    w_ref,
    cos_ref,
    sin_ref,
    forward_ref,
    terms,
    carry,
    attn_ref,
    ahead_ref,
    total,
    mlp_all,
    weight_all,
    attn_all,
    out_ref,
    weight_ref,
    attn_out_ref,
    mlp_ref,
    sums,
    queries,
    weight,
    attn_land,
    *sems,
):
    count = x_ref.shape[0]
    rows = grad_ref.shape[2]
    steps, per_tile = count // tile, tile // rows
    step = pl.program_id(0)
    place = Place(groups, reach)
    halving = Halving(place, 2, forward_ref, ahead_ref, sems[:7])
    swap = Lines(lines, attn_ref, attn_land, *sems[7:10])
    length = lines * groups // 8
    line = Sum(place, terms, length - 1, carry, *sems[10:14])

    @pl.when(step == 0)
    def _():
        line.clear()
        meet(everyone(place, lines))
        line.start(0)
        line.start(1)
        halving.start()
        swap.start()
        sums[...] = jnp.zeros_like(sums)

    here = pl.ds(pl.multiple_of(step * tile, tile), tile)
    query = qkv_ref[:QM_END, here]
    grad = jnp.concatenate([grad_ref[step * per_tile + k] for k in range(per_tile)], axis=1)
    delta = jnp.sum(grad.astype(F32) * wide_ref[:, here], axis=0, keepdims=True)
    lse = lse_ref[:, here]
    grad_query = jnp.zeros((HD, tile), F32)
    for j in range(steps):
        keys = slice(j * tile, (j + 1) * tile)
        prob = jnp.exp(dot(qkv_ref[QM_END:KM_END, keys], query, 0, 0) - lse)
        grad_prob = dot(qkv_ref[KM_END:, keys], grad, 0, 0)
        grad_score = (prob * (grad_prob - delta)).astype(BF)
        grad_query += dot(qkv_ref[QM_END:K_END, keys], grad_score, 1, 0)
        sums[:HD, keys] += dot(query[:HD], grad_score, 1, 1)
        sums[HD:, keys] += dot(grad, prob.astype(BF), 1, 1)
    queries[:, here] = (grad_query * 0.125).astype(BF)

    pl.when(step == 0)(halving.pair)

    @pl.when(step == min(2, steps - 1))
    def _():
        halving.halve(0)
        for q in range(2, length - 1):
            line.start(q)


    @pl.when(step == steps - 1)
    def _():
        weight[...] = jnp.zeros_like(weight)

        @pl.loop(0, steps)
        def _(i):
            at = pl.ds(pl.multiple_of(i * tile, tile), tile)
            cosine, sine = cos_ref[:, at], sin_ref[:, at]

            def turn_back(value):
                front, back = value[:HALF], value[HALF:]
                return [front * cosine + back * sine, back * cosine - front * sine]

            low = lambda value: value.astype(BF).astype(F32)
            projected = jnp.concatenate(
                [
                    *turn_back(queries[:, at].astype(F32)),
                    *turn_back(low(sums[:HD, at])),
                    low(sums[HD:, at]),
                ],
                axis=0,
            ).astype(BF)
            part = dot(projected, w_ref[...], 0, 1).astype(BF)
            for k in range(per_tile):
                out_ref[(i * per_tile + k) // 2, k % 2] = part[k * rows : (k + 1) * rows]
            weight[...] += dot(projected, x_ref[at, :], 1, 0)

        shard = weight_ref.shape[2]
        for c in range(lines):
            weight_ref[c] = weight[:, c * shard : (c + 1) * shard].astype(BF)
        halving.halve(1)
        half = line.half

        def sum_line():
            line.finish()
            for k in range(2):
                q = length - 3 + k
                value = (
                    line.block(line.spot, k).astype(F32)
                    + line.land[0, q].astype(F32)
                    + line.land[1, q].astype(F32)
                ).astype(BF)
                if mlp_ref.shape[0] == 2:
                    mlp_ref[k] = value
                else:
                    mlp_ref[0, k * half : (k + 1) * half] = value

        def sum_attn():
            swap.finish()
            attn_out_ref[...] = functools.reduce(
                jnp.add, [attn_land[c].astype(F32) for c in range(lines)]
            ).astype(BF)

        end_part(
            place,
            lines,
            out_ref,
            weight_ref,
            mlp_ref,
            attn_out_ref,
            total,
            mlp_all,
            weight_all,
            attn_all,
            sum_line,
            sum_attn,
            *sems[14:],
        )
        halving.finish()


def attend_back(qkv, grad, wide, lse, x, w, cosine, sine, forward, terms, carry, attn, groups, reach, tile):
    count, width = x.shape
    blocks, _, rows = grad.shape
    lines, shard, lanes = attn.shape
    sub = 8 // groups
    length = lines // sub
    operands = (qkv, grad, wide, lse, x, w, cosine, sine, forward, terms, carry)
    return pl.pallas_call(
        functools.partial(attend_back_kernel, groups, reach, lines, tile),
        grid=(count // tile,),
        in_specs=[*[VMEM] * len(operands), ANY],
        out_specs=[VMEM, VMEM, ANY, ANY, ANY],
        out_shape=[
            jax.ShapeDtypeStruct((rows, width), F32),
            jax.ShapeDtypeStruct((rows, width), F32),
            jax.ShapeDtypeStruct((sub, groups, shard, 3 * SLICE), BF),
            jax.ShapeDtypeStruct((groups, reach, 3 * HD, shard), BF),
            jax.ShapeDtypeStruct((groups, shard, lanes), BF),
        ],
        scratch_shapes=[
            pltpu.VMEM((blocks // 2, 2, rows, width), BF),
            pltpu.VMEM((lines, 3 * HD, shard), BF),
            pltpu.VMEM((shard, lanes), BF),
            pltpu.VMEM((sub, shard, 3 * SLICE), BF),
            pltpu.VMEM((2 * HD, count), F32),
            pltpu.VMEM((HD, count), BF),
            pltpu.VMEM((3 * HD, width), F32),
            pltpu.VMEM((lines, shard, lanes), BF),
            *Halving.scratch(2, rows, width),
            *Lines.scratch(lines),
            *Sum.scratch(length - 1, (width // (2 * length), 3 * SLICE)),
            pltpu.VMEM((lines, 3 * HD, shard), BF),
            pltpu.VMEM((reach, 3 * HD, shard), BF),
            DMA((max(sub - 1, 1),)),
            DMA((max(sub - 1, 1),)),
            DMA((3,)),
            *Halving.scratch(3, rows, width),
            *Lines.scratch(lines),
            *Collect.scratch(sub + 2, groups),
        ],
        compiler_params=pltpu.CompilerParams(
            collective_id=4, has_side_effects=True, vmem_limit_bytes=36 << 20
        ),
        cost_estimate=pl.CostEstimate(
            flops=count * count * HD * 20, bytes_accessed=count * 6144, transcendentals=count * count
        ),
        name="attend_back",
    )(*operands, attn)


class Collect:
    def __init__(self, groups, pieces, far_send, far_recv, near_send, near_recv):
        head = lax.axis_index("heads")
        self.half = half = groups // 2
        pair = {"heads": flip(head, 1)}
        self.far, self.near = [], []
        for n, (piece, where) in enumerate(pieces):
            self.far.append(
                [
                    remote(
                        piece,
                        where(head),
                        {"heads": (head + 2 * k) % groups},
                        far_send.at[n, k - 1],
                        far_recv.at[n, k - 1],
                    )
                    for k in range(1, half)
                ]
            )
            sides = [(piece, where(head))]
            for k in range(1, half):
                got = where((head - 2 * k + groups) % groups)
                sides.append((got, got))
            self.near.append(
                [
                    remote(source, target, pair, near_send.at[n, k], near_recv.at[n, k])
                    for k, (source, target) in enumerate(sides)
                ]
            )

    @staticmethod
    def scratch(count, groups):
        far, near = (count, max(groups // 2 - 1, 1)), (count, groups // 2)
        return [DMA(far), DMA(far), DMA(near), DMA(near)]

    def start(self, n):
        for copy in self.far[n]:
            copy.start()
        self.near[n][0].start()

    def forward(self, n):
        for k, copy in enumerate(self.far[n]):
            copy.wait_recv()
            self.near[n][k + 1].start()

    def finish(self):
        for copies in self.far:
            for copy in copies:
                copy.wait_send()
        for copies in self.near:
            for copy in copies:
                copy.wait()


def assemble_kernel(
    upstream,
    tokens,
    grad_middle,
    gains,
    middle,
    ahead,
    weight_all,
    attn_all,
    mlp_all,
    w_qkv,
    w_in,
    own_gains,
    result,
    grad,
    sum_qkv,
    sum_attn,
    sum_in,
    sum_out,
    gain_sums,
):
    groups, reach, _, shard = weight_all.shape
    lanes = attn_all.shape[2]
    result[...] = (middle[...] + ahead[...]).astype(BF)
    normed, inverse_std = norm_parts(tokens[...].astype(F32))
    grad[...] = grad_middle[...] + norm_back(upstream[...], normed, inverse_std, gains[0:1, :])
    for g in range(groups):
        sum_attn[:, g * lanes : (g + 1) * lanes] = attn_all[g].astype(F32)
    gain_one = jnp.zeros((shard, 128), F32)
    for third in range(3):
        part = slice(third * HD, (third + 1) * HD)
        for pair in range(H // 2):
            r, g = 2 * pair // groups, 2 * pair % groups
            tile = (
                jnp.concatenate([weight_all[g, r, part], weight_all[g + 1, r, part]], axis=0)
                .astype(F32)
                .T
            )
            at = third * H * HD + pair * 2 * HD
            sum_qkv[:, at : at + 2 * HD] = tile
            gain_one += tile * w_qkv[:, at : at + 2 * HD].astype(F32)
    gain_two = jnp.zeros((shard, 1), F32)
    for t in range(8):
        start, wide = slice_place(t)
        for half in range(2):
            piece = mlp_all[t, :, half * SLICE : half * SLICE + wide].astype(F32)
            at = half * FF + start
            sum_in[:, at : at + wide] = piece
            gain_two += jnp.sum(
                piece * w_in[:, at : at + wide].astype(F32), axis=1, keepdims=True
            )
        sum_out[start : start + wide, :] = (
            mlp_all[t, :, 2 * SLICE : 3 * SLICE].astype(F32).T[:wide]
        )
    one = jnp.sum(gain_one, axis=1, keepdims=True)
    lane = lax.broadcasted_iota(jnp.int32, (shard, 128), 1)
    both = jnp.where(lane == 0, one, gain_two).T
    gain_sums[...] = both[:8] / own_gains[...]


def assemble(upstream, tokens, grad_middle, gains, middle, ahead, weight_all, attn_all, mlp_all, w_qkv, w_in, own_gains):
    rows, width = tokens.shape
    shard = w_qkv.shape[0]
    return pl.pallas_call(
        assemble_kernel,
        in_specs=[VMEM] * 12,
        out_specs=[VMEM] * 7,
        out_shape=[
            jax.ShapeDtypeStruct((rows, width), BF),
            jax.ShapeDtypeStruct((rows, width), F32),
            jax.ShapeDtypeStruct((shard, 3 * width), F32),
            jax.ShapeDtypeStruct((shard, width), F32),
            jax.ShapeDtypeStruct((shard, 2 * FF), F32),
            jax.ShapeDtypeStruct((FF, shard), F32),
            jax.ShapeDtypeStruct((8, shard), F32),
        ],
        compiler_params=pltpu.CompilerParams(vmem_limit_bytes=20 << 20),
        cost_estimate=pl.CostEstimate(flops=1 << 24, bytes_accessed=20 << 20, transcendentals=0),
        name="assemble",
    )(upstream, tokens, grad_middle, gains, middle, ahead, weight_all, attn_all, mlp_all, w_qkv, w_in, own_gains)


def slice_start(t):
    return 128 * jnp.minimum(3 * t, 2 * t + 5)


def slice_place(t):
    start = 128 * min(3 * t, 2 * t + 5)
    return start, min(128 * min(3 * t + 3, 2 * t + 7), FF) - start


def body(count, tokens, d_out, segment_ids, position_ids, w_qkv, w_attn, w_in, w_out, gain_attn, gain_mlp):
    groups = lax.axis_size("heads")
    rows, width = tokens.shape
    shard = w_qkv.shape[0]
    reach = SEQ_MAX // (rows * groups)
    group = reach * groups
    sub = 8 // groups
    ctx, head = lax.axis_index("ctx"), lax.axis_index("heads")
    assert group == H and sub * groups == 8
    total = group * rows
    tile = 512

    def mlp_slice(value, axis, start, t):
        pads = [(0, 0), (0, 0)]
        pads[axis] = (0, SLICE)
        piece = lax.dynamic_slice_in_dim(jnp.pad(value, pads), start + slice_start(t), SLICE, axis)
        wide = jnp.minimum(slice_start(t + 1), FF) - slice_start(t)
        shape = [1, 1]
        shape[axis] = SLICE
        return jnp.where(jnp.arange(SLICE).reshape(shape) < wide, piece, jnp.zeros_like(piece))

    def mlp_part(t):
        return jnp.concatenate(
            [mlp_slice(w_in, 1, 0, t), mlp_slice(w_in, 1, FF, t), mlp_slice(w_out, 0, 0, t).T], axis=1
        )

    mlp = jnp.stack([mlp_part(x * groups + head) for x in range(sub)])
    gains_own = jnp.pad(jnp.stack([gain_attn, gain_mlp]).astype(F32), ((0, 6), (0, -shard % 128)))
    ids = jnp.pad(jnp.stack([position_ids, segment_ids]), ((0, 6), (0, 0)))
    freqs = jnp.power(160000.0, -(2.0 * jnp.arange(HALF, dtype=F32)) / HD)[:, None]
    input_all, gains, w_head, cosine, sine, marks, attn_half = begin(
        tokens, gains_own, ids, w_qkv, w_attn, freqs, count // sub, count, groups, reach
    )
    x = input_all.reshape(total, width)

    attended, wide, lse, qkv, attn_weights, mlp_pair, mlp_near = attend(
        x,
        w_head,
        cosine,
        sine,
        marks,
        attn_half,
        mlp.reshape(2, sub * shard // 2, 3 * SLICE),
        count,
        groups,
        reach,
        rows,
        tile,
    )
    attn_weights = attn_weights.reshape(width, width)
    mlp_all, upstream, middle, attended, mlp_weights = middle_step(
        attended, tokens, d_out, attn_weights, gains, mlp_pair, mlp_near, count, groups, reach
    )
    mlp_weights = mlp_weights.reshape(width, 3 * SLICE)
    grad_heads, grad_middle, attn_part, carry, forward, mlp_terms = turn_step(
        mlp_all.reshape(8 * rows, width),
        upstream.reshape(8 * rows, width),
        mlp_weights,
        middle,
        d_out,
        attn_weights,
        gains,
        attended.reshape(groups, width, rows),
        count,
        groups,
        reach,
    )
    attn_part = attn_part.reshape(count, shard, width // groups)
    ahead, upstream_in, mlp_all, weight_all, attn_all = attend_back(
        qkv,
        grad_heads,
        wide,
        lse,
        x,
        w_head,
        cosine,
        sine,
        forward,
        mlp_terms,
        carry,
        attn_part,
        groups,
        reach,
        tile,
    )
    result, grad_input, sum_qkv, sum_attn, sum_in, sum_out, gain_sums = assemble(
        upstream_in,
        tokens,
        grad_middle,
        gains,
        middle,
        ahead,
        weight_all,
        attn_all,
        mlp_all.reshape(8, shard, 3 * SLICE),
        w_qkv,
        w_in,
        jnp.pad(gains_own[:2, :shard], ((0, 6), (0, 0)), constant_values=1.0),
    )
    return (
        result,
        grad_input,
        sum_qkv,
        sum_attn,
        sum_in,
        sum_out,
        gain_sums[0],
        gain_sums[1],
    )


def solution(mesh):
    return jax.shard_map(
        functools.partial(body, mesh.shape["ctx"]),
        mesh=mesh,
        in_specs=(
            P(("ctx", "heads"), None),
            P(("ctx", "heads"), None),
            P(("ctx", "heads")),
            P(("ctx", "heads")),
            P("ctx", None),
            P("ctx", None),
            P("ctx", None),
            P(None, "ctx"),
            P("ctx"),
            P("ctx"),
        ),
        out_specs=(
            P(("ctx", "heads"), None),
            P(("ctx", "heads"), None),
            P("ctx", None),
            P("ctx", None),
            P("ctx", None),
            P(None, "ctx"),
            P("ctx"),
            P("ctx"),
        ),
        check_vma=False,
    )
```

```python
import functools

import jax
import jax.numpy as jnp
from jax import lax
from jax.experimental import pallas as pl
from jax.experimental.pallas import tpu as pltpu
from jax.sharding import PartitionSpec as P

H = 16
HD = 64
HALF = HD // 2
FF = 2624
SEQ_MAX = 2048
MASKED = -1e30
MARKS = 16
QM_END = HD + MARKS
K_END = QM_END + HD
KM_END = K_END + MARKS
V_END = KM_END + HD
SLICE = 384
BF = jnp.bfloat16
F32 = jnp.float32
MESH = pl.DeviceIdType.MESH
VMEM = pl.BlockSpec(memory_space=pltpu.VMEM)
ANY = pl.BlockSpec(memory_space=pl.ANY)
DMA = pltpu.SemaphoreType.DMA


def dot(left, right, left_dim, right_dim):
    return lax.dot_general(
        left, right, (((left_dim,), (right_dim,)), ((), ())), preferred_element_type=F32
    )


def norm_parts(values):
    average = jnp.mean(values, axis=-1, keepdims=True)
    centred = values - average
    inverse_std = lax.rsqrt(jnp.mean(centred * centred, axis=-1, keepdims=True) + 1e-05)
    return centred * inverse_std, inverse_std


def norm_back(upstream, normed, inverse_std, gain):
    scaled = upstream * gain
    return inverse_std * (
        scaled
        - jnp.mean(scaled, axis=-1, keepdims=True)
        - normed * jnp.mean(scaled * normed, axis=-1, keepdims=True)
    )


def flip(value, bit):
    return value + bit - 2 * bit * (value // bit % 2)


class Place:
    def __init__(self, groups, reach):
        self.groups, self.reach = groups, reach
        self.ctx = lax.axis_index("ctx")
        self.head = lax.axis_index("heads")
        self.local = self.ctx % reach
        self.base = self.ctx - self.local
        self.idx = self.local * groups + self.head

    def member(self, j):
        return {"ctx": self.base + j // self.groups, "heads": j % self.groups}


def greet(devices):
    barrier = pltpu.get_barrier_semaphore()
    for device in devices:
        pl.semaphore_signal(barrier, inc=1, device_id=device, device_id_type=MESH)


def meet(devices):
    greet(devices)
    pl.semaphore_wait(pltpu.get_barrier_semaphore(), len(devices))


def remote(source, target, device, send, recv):
    return pltpu.make_async_remote_copy(
        src_ref=source,
        dst_ref=target,
        send_sem=send,
        recv_sem=recv,
        device_id=device,
        device_id_type=MESH,
    )


def push(*operands):
    copy = remote(*operands)
    copy.start()
    return copy


def tree_parts(axes, rows):
    part = -(-rows // axes // 16) * 16
    starts = [min(part * a, rows) for a in range(axes + 1)]
    return [(starts[a], starts[a + 1] - starts[a]) for a in range(axes)]


class Tree:
    def __init__(self, place, axes, source, target, sems):
        self.place, self.axes, self.source, self.target = place, axes, source, target
        self.send, self.recv, self.core_send, self.core_recv, self.own = sems
        self.slots = 2 << axes
        self.levels, self.cores = [], []

    @staticmethod
    def scratch(axes):
        far, near = axes * axes, axes * axes + 1
        return [DMA((far,)), DMA((far,)), DMA((near,)), DMA((near,)), DMA]

    def origin(self, level, first):
        value = self.place.idx
        for k in range(level):
            value = flip(value, 2 << ((first + k) % self.axes))
        return value % self.slots

    def neighbour(self, axis):
        return self.place.member(flip(self.place.idx, 2 << (axis % self.axes)))

    def piece(self, slot, part):
        return self.target.at[slot] if part is None else self.target.at[slot, pl.ds(*part)]

    def to_core(self, source, slot, part):
        at = len(self.cores)
        self.cores.append(
            push(
                source,
                self.piece(slot, part),
                self.place.member(flip(self.place.idx, 1)),
                self.core_send.at[at],
                self.core_recv.at[at],
            )
        )

    def start(self):
        me = self.place.idx % self.slots
        self.levels.append(
            [
                push(
                    self.source, self.target.at[me], self.neighbour(a), self.send.at[a], self.recv.at[a]
                )
                for a in range(self.axes)
            ]
        )
        self.to_core(self.source, me, None)
        self.local = pltpu.make_async_copy(self.source, self.target.at[me], self.own)
        self.local.start()

    def forward(self, level):
        axes = self.axes
        parts = tree_parts(axes, self.target.shape[1])
        onward = []
        for a in range(axes):
            self.levels[level - 1][a].wait_recv()
            slot = self.origin(level, a)
            if level < axes:
                part = parts[a] if level + 1 == axes else None
                at = level * axes + a
                piece = self.piece(slot, part)
                onward.append(
                    push(piece, piece, self.neighbour(a + level), self.send.at[at], self.recv.at[at])
                )
                self.to_core(self.target.at[slot], slot, None)
            else:
                self.to_core(self.piece(slot, parts[a]), slot, parts[a])
        self.levels.append(onward)

    def finish(self):
        self.local.wait()
        for level in self.levels:
            for copy in level:
                copy.wait_send()
        for copy in self.cores:
            copy.wait()


class Halving:
    def __init__(self, place, axes, value, result, scratch, firsts=None):
        self.firsts = firsts = firsts or list(range(axes))
        self.axes, self.value, self.result = axes, value, result
        self.other, self.held, self.land, send, recv, send0, recv0 = scratch
        self.blocks = 1 << axes
        width = value.shape[-1]
        part = width // len(firsts)
        self.columns = [pl.ds(part * a, part) for a in range(len(firsts))]
        self.core = place.idx % 2
        self.chip = place.idx // 2 % self.blocks
        self.sources = []
        for j in range(self.blocks):
            k = self.chip
            for a in range(axes):
                if j >> a & 1:
                    k = flip(k, 1 << a)
            self.sources.append(k)
        self.first, self.copies = [], {}
        for p in range(len(firsts)):
            self.first.append(
                remote(
                    value.at[:, 1 - self.core, :, self.columns[p]],
                    self.other.at[:, :, self.columns[p]],
                    place.member(flip(place.idx, 1)),
                    send0.at[p],
                    recv0.at[p],
                )
            )
            for step in range(axes):
                bit, sent = self.sent(p, step)
                for j in sent:
                    self.copies[p, j] = remote(
                        self.held.at[j, :, self.columns[p]],
                        self.land.at[j, :, self.columns[p]],
                        place.member(flip(place.idx, 2 * bit)),
                        send.at[p, j],
                        recv.at[p, j],
                    )

    @staticmethod
    def scratch(axes, rows, width):
        blocks = 1 << axes
        return [
            pltpu.VMEM((blocks, rows, width), BF),
            pltpu.VMEM((blocks, rows, width), BF),
            pltpu.VMEM((blocks, rows, width), BF),
            DMA((axes, blocks)),
            DMA((axes, blocks)),
            DMA((axes,)),
            DMA((axes,)),
        ]

    def sent(self, part, step):
        first = self.firsts[part]
        seen = [1 << ((first + s) % self.axes) for s in range(step)]
        bit = 1 << ((first + step) % self.axes)
        return bit, [j for j in range(self.blocks) if j & bit and not any(j & s for s in seen)]

    def start(self):
        for copy in self.first:
            copy.start()

    def pair(self):
        for p in range(len(self.firsts)):
            cols = self.columns[p]
            self.first[p].wait_recv()
            _, early = self.sent(p, 0)
            for j in early + [j for j in range(self.blocks) if j not in early]:
                k = self.sources[j]
                self.held[j, :, cols] = (
                    self.value[k, self.core, :, cols].astype(F32) + self.other[k, :, cols].astype(F32)
                ).astype(BF)
                if j in early:
                    self.copies[p, j].start()

    def halve(self, step):
        for p in range(len(self.firsts)):
            cols = self.columns[p]
            bit, arrived = self.sent(p, step)
            onward = self.sent(p, step + 1)[1] if step + 1 < self.axes else []
            for j in sorted(arrived, key=lambda j: (j - bit) not in onward):
                self.copies[p, j].wait_recv()
                k = j - bit
                total = self.held[k, :, cols].astype(F32) + self.land[j, :, cols].astype(F32)
                if step + 1 < self.axes:
                    self.held[k, :, cols] = total.astype(BF)
                    if k in onward:
                        self.copies[p, k].start()
                else:
                    self.result[:, cols] = total

    def run(self):
        self.start()
        self.pair()
        for step in range(self.axes):
            self.halve(step)
        self.finish()

    def finish(self):
        for copy in self.first:
            copy.wait_send()
        for copy in self.copies.values():
            copy.wait_send()


class Lines:
    def __init__(self, count, source, target, send, recv, own):
        me = lax.axis_index("ctx")
        self.copies = [pltpu.make_async_copy(source.at[me], target.at[me], own)]
        for step in range(1, count):
            peer = (me + step) % count
            self.copies.append(
                remote(source.at[peer], target.at[me], {"ctx": peer}, send.at[step - 1], recv.at[step - 1])
            )

    @staticmethod
    def scratch(count):
        return [DMA((count - 1,)), DMA((count - 1,)), DMA]

    def start(self):
        for copy in self.copies:
            copy.start()

    def finish(self):
        for copy in self.copies:
            copy.wait()


def everyone(place, count):
    group = place.reach * place.groups
    mates = [place.member((place.idx + step) % group) for step in range(1, group)]
    outside = [{"ctx": (place.base + place.reach + step) % count} for step in range(count - place.reach)]
    return mates + outside


def spread(place, source, target, sems, me=None):
    send, recv, own = sems
    count = target.shape[0]
    copies = []
    for step in range(1, count):
        peer = (place.idx + step) % count
        copies.append(
            push(
                source.at[peer],
                target.at[place.idx],
                place.member(peer),
                send.at[step - 1],
                recv.at[step - 1],
            )
        )
    local = pltpu.make_async_copy(source.at[place.idx], target.at[place.idx], own)
    local.start()
    copies.append(local)
    return copies


def begin_kernel(
    groups,
    reach,
    count,
    tokens,
    gains,
    ids,
    w_qkv,
    w_attn,
    freqs,
    input_all,
    gains_all,
    w_head,
    cosine,
    sine,
    marks,
    attn_half,
    ids_all,
    slab,
    mine,
    gain_land,
    own_sems,
    ids_send,
    ids_recv,
    gain_send,
    gain_recv,
    slab_send,
    slab_recv,
    wide_send,
    wide_recv,
    core_send,
    core_recv,
    *tree_sems,
):
    place = Place(groups, reach)
    group = reach * groups
    ctx, head, idx = place.ctx, place.head, place.idx
    shard = w_qkv.shape[0]
    ring = attn_half.shape[0]
    sub = count // ring
    side, spot = ctx % sub, ctx // sub
    lanes = attn_half.shape[2] // groups
    core = {"heads": flip(head, 1)}
    mates = [place.member((idx + step) % group) for step in range(1, group)]
    lines = [{"ctx": (ctx + step) % count} for step in range(1, count)]
    meet(everyone(place, count))
    first = [
        push(gains, gain_land.at[ctx], lines[step - 1], gain_send.at[step - 1], gain_recv.at[step - 1])
        for step in range(1, count)
    ]
    small = [
        push(ids, ids_all.at[idx], mates[step - 1], ids_send.at[step - 1], ids_recv.at[step - 1])
        for step in range(1, group)
    ]
    half = pl.ds(pl.multiple_of(head % 2 * (shard // 2), 16), shard // 2)
    thirds = []
    for step in range(1, count):
        peer = (ctx + step) % count
        column = ((peer % reach) * groups + head) // 2 * 128
        for third in range(3):
            start = pl.multiple_of(third * 1024 + column, 128)
            thirds.append(
                push(
                    w_qkv.at[half, pl.ds(start, 128)],
                    slab.at[ctx, half, pl.ds(third * 128, 128)],
                    lines[step - 1],
                    slab_send.at[step - 1, third],
                    slab_recv.at[step - 1, third],
                )
            )
    gain_land[ctx] = gains[...]
    where = lambda h: pl.ds(pl.multiple_of(h * lanes, 128), lanes)
    across = where(head)
    own = [
        pltpu.make_async_copy(ids, ids_all.at[idx], own_sems.at[3]),
        pltpu.make_async_copy(w_attn.at[:, across], attn_half.at[spot, :, across], own_sems.at[4]),
    ]
    for third in range(3):
        start = pl.multiple_of(third * 1024 + idx // 2 * 128, 128)
        own.append(
            pltpu.make_async_copy(
                w_qkv.at[half, pl.ds(start, 128)],
                slab.at[ctx, half, pl.ds(third * 128, 128)],
                own_sems.at[third],
            )
        )
    for copy in own:
        copy.start()
    for copy in first:
        copy.wait_recv()
    gain, gain_two = (
        jnp.concatenate([gain_land[c, k : k + 1, :shard] for c in range(count)], axis=1)
        for k in range(2)
    )
    normed, _ = norm_parts(tokens[...].astype(F32))
    mine[...] = (normed * gain).astype(BF)
    tree = Tree(place, 3, mine, input_all, tree_sems[:5])
    tree.start()
    gains_all[0:1, :] = gain
    gains_all[1:2, :] = gain_two
    late = []
    for step in range(1, ring):
        late.append(
            push(
                w_attn.at[:, across],
                attn_half.at[spot, :, across],
                {"ctx": (spot + step) % ring * sub + side},
                wide_send.at[step - 1],
                wide_recv.at[step - 1],
            )
        )
    tree.forward(1)
    for copy in own:
        copy.wait()
    for copy in thirds:
        copy.wait_recv()
    for copy in late:
        copy.wait_recv()
    collect = Collect(
        groups, [(attn_half.at[:, :, across], lambda h: attn_half.at[:, :, where(h)])], *tree_sems[5:]
    )
    collect.start(0)
    shared = push(slab.at[:, half], slab.at[:, half], core, core_send, core_recv)
    for copy in small:
        copy.wait()
    row = lambda k: jnp.concatenate([ids_all[j, k : k + 1, :] for j in range(group)], axis=1)
    angles = freqs[...] * row(0).astype(F32)
    cosine[...] = jnp.cos(angles)
    sine[...] = jnp.sin(angles)
    parity = (row(1) % 2).astype(F32)
    blank = jnp.zeros((MARKS - 2, parity.shape[1]), F32)
    marks[...] = jnp.concatenate(
        [parity, 1.0 - parity, blank, (1.0 - parity) * MASKED, parity * MASKED, blank], axis=0
    ).astype(BF)
    tree.forward(2)
    shared.wait()
    odd = head % 2 == 1
    for c in range(count):
        rows = slice(c * shard, (c + 1) * shard)
        block = slab[c].astype(F32)
        parts = []
        for third in range(3):
            at = third * 128
            parts.append(jnp.where(odd, block[:, at + HD : at + 128], block[:, at : at + HD]))
        w_head[rows] = jnp.concatenate(parts, axis=1).astype(BF)
    collect.forward(0)
    tree.forward(3)
    tree.finish()
    collect.finish()
    for copy in first + thirds + late:
        copy.wait_send()


def begin(tokens, gains, ids, w_qkv, w_attn, freqs, ring, count, groups, reach):
    rows, width = tokens.shape
    shard = w_qkv.shape[0]
    group = groups * reach
    sems = lambda *shape: [DMA(shape), DMA(shape)]
    return pl.pallas_call(
        functools.partial(begin_kernel, groups, reach, count),
        in_specs=[VMEM, VMEM, ANY, ANY, ANY, VMEM],
        out_specs=[ANY, VMEM, VMEM, VMEM, VMEM, VMEM, ANY],
        out_shape=[
            jax.ShapeDtypeStruct((group, rows, width), BF),
            jax.ShapeDtypeStruct((8, width), F32),
            jax.ShapeDtypeStruct((width, 3 * HD), BF),
            jax.ShapeDtypeStruct((HALF, group * rows), F32),
            jax.ShapeDtypeStruct((HALF, group * rows), F32),
            jax.ShapeDtypeStruct((2 * MARKS, group * rows), BF),
            jax.ShapeDtypeStruct((ring, shard, width), BF),
        ],
        scratch_shapes=[
            pltpu.VMEM((group, 8, rows), jnp.int32),
            pltpu.VMEM((count, shard, 3 * 128), BF),
            pltpu.VMEM((rows, width), BF),
            pltpu.VMEM((count, 8, gains.shape[1]), F32),
            DMA((5,)),
            *sems(group - 1),
            *sems(count - 1),
            *sems(count - 1, 3),
            *sems(ring - 1),
            DMA,
            DMA,
            *Tree.scratch(3),
            *Collect.scratch(1, groups),
        ],
        compiler_params=pltpu.CompilerParams(
            collective_id=0, has_side_effects=True, vmem_limit_bytes=12 << 20
        ),
        cost_estimate=pl.CostEstimate(flops=0, bytes_accessed=30 << 20, transcendentals=0),
        name="begin",
    )(tokens, gains, ids, w_qkv, w_attn, freqs)


class Line:
    def __init__(self, length, sub, first, sources, targets, send, recv):
        ctx = lax.axis_index("ctx")
        spot, side = ctx // sub, ctx % sub
        self.length, self.spot, self.first = length, spot, first
        self.waited = 0
        beside = [{"ctx": (spot + 1) % length * sub + side}, {"ctx": (spot + length - 1) % length * sub + side}]
        self.copies = [
            [
                remote(sources[d][q], targets[d][q], beside[d], send.at[d, q], recv.at[d, q])
                for q in range(len(sources[d]))
            ]
            for d in range(2)
        ]

    def sends(self, d, q):
        s, spot, last = (q + self.first) // 2, self.spot, self.length - 1
        if d:
            return jnp.logical_and(spot + s <= last, spot > 0)
        return jnp.logical_and(spot >= s, spot < last)

    def receives(self, d, q):
        s = (q + self.first) // 2
        return self.spot + s + 1 < self.length if d else self.spot > s

    def arrive(self, q):
        for d in range(2):
            pl.when(self.receives(d, q))(self.copies[d][q].wait_recv)
        self.waited = q + 1

    def start(self, q):
        if q >= 2:
            self.arrive(q - 2)
        for d in range(2):
            pl.when(self.sends(d, q))(self.copies[d][q].start)

    def finish(self):
        for q in range(self.waited, len(self.copies[0])):
            self.arrive(q)
        for d in range(2):
            for q, copy in enumerate(self.copies[d]):
                pl.when(self.sends(d, q))(copy.wait_send)


def ring_half(sub, side, k):
    return (side + k) % 2 if sub == 2 else k


class Columns:
    def __init__(self, place, part, whole, own, side_send, side_recv, near_send, near_recv):
        _, sub, _, width = whole.shape
        side = place.ctx % sub
        half = pl.ds(pl.multiple_of(place.head % 2 * (width // 2), 128), width // 2)
        self.own = pltpu.make_async_copy(part, whole.at[:, side], own)
        self.sides, self.near = [], []
        for step in range(1, sub):
            peer, source = (side + step) % sub, (side - step + sub) % sub
            self.sides.append(
                remote(
                    part.at[:, :, half],
                    whole.at[:, side, :, half],
                    {"ctx": place.ctx - side + peer},
                    side_send.at[step - 1],
                    side_recv.at[step - 1],
                )
            )
            here = whole.at[:, source, :, half]
            self.near.append(
                remote(
                    here, here, {"heads": flip(place.head, 1)}, near_send.at[step - 1], near_recv.at[step - 1]
                )
            )

    @staticmethod
    def scratch(sub):
        count = (max(sub - 1, 1),)
        return [DMA, DMA(count), DMA(count), DMA(count), DMA(count)]

    def start(self):
        self.own.start()
        for copy in self.sides:
            copy.start()

    def across(self):
        for side, near in zip(self.sides, self.near):
            side.wait_recv()
            near.start()

    def finish(self):
        self.own.wait()
        for side, near in zip(self.sides, self.near):
            side.wait_send()
            near.wait()


def attend_kernel(
    groups,
    reach,
    lines,
    tile,
    x_ref,
    w_ref,
    cos_ref,
    sin_ref,
    mark_ref,
    attn_half,
    mlp,
    out_ref,
    wide_ref,
    lse_ref,
    qkv_ref,
    attn_all,
    mlp_pair,
    mlp_near,
    ring_send,
    ring_recv,
    swap_send,
    swap_recv,
    swap_own,
    *sems,
):
    count = x_ref.shape[0]
    step = pl.program_id(0)
    steps = count // tile
    place = Place(groups, reach)
    ring_size, sub = attn_all.shape[:2]
    side = place.ctx % sub
    early = mlp_near.shape[1]
    if sub == 2:
        kept = pltpu.make_async_copy(mlp.at[side], mlp_pair.at[side], swap_own)
        swap = [
            remote(
                mlp.at[1 - side],
                mlp_pair.at[side],
                {"ctx": place.ctx + 1 - 2 * side},
                swap_send,
                swap_recv,
            )
        ]
        sources = [mlp.at[side], mlp_pair.at[1 - side]]
    else:
        kept = pltpu.make_async_copy(mlp, mlp_pair, swap_own)
        swap = []
        sources = [mlp.at[0], mlp.at[1]]
    ring = Line(
        ring_size,
        sub,
        0,
        [sources + [mlp_near.at[d, q] for q in range(early - 2)] for d in range(2)],
        [[mlp_near.at[d, q] for q in range(early)] for d in range(2)],
        ring_send,
        ring_recv,
    )
    columns = Columns(place, attn_half, attn_all, *sems)

    @pl.when(step == 0)
    def _():
        meet(everyone(place, lines))
        for copy in swap:
            copy.start()
        ring.start(0)
        kept.start()
        columns.start()
        qkv_ref[HD:QM_END, :] = mark_ref[:MARKS, :]
        qkv_ref[K_END:KM_END, :] = mark_ref[MARKS:, :]

        @pl.loop(0, steps)
        def _(i):
            at = pl.ds(pl.multiple_of(i * tile, tile), tile)
            cosine, sine = cos_ref[:, at], sin_ref[:, at]
            part = dot(w_ref[...], x_ref[at, :], 0, 1)

            def turn(value):
                front, back = value[:HALF], value[HALF:]
                return jnp.concatenate(
                    [front * cosine - back * sine, back * cosine + front * sine], axis=0
                )

            qkv_ref[:HD, at] = (turn(part[:HD]) * 0.125).astype(BF)
            qkv_ref[QM_END:K_END, at] = turn(part[HD : 2 * HD]).astype(BF)
            qkv_ref[KM_END:, at] = part[2 * HD :].astype(BF)

    here = pl.ds(pl.multiple_of(step * tile, tile), tile)
    query = qkv_ref[:QM_END, here]
    keys = [slice(j * tile, (j + 1) * tile) for j in range(steps)]
    scores = [dot(qkv_ref[QM_END:KM_END, at], query, 0, 0) for at in keys]
    top = functools.reduce(jnp.maximum, [jnp.max(s, axis=0, keepdims=True) for s in scores])
    raised = [jnp.exp(s - top) for s in scores]
    total = functools.reduce(jnp.add, [jnp.sum(e, axis=0, keepdims=True) for e in raised])
    scale = 1.0 / total
    result = jnp.zeros((HD, tile), F32)
    for j in range(steps):
        result += dot(qkv_ref[KM_END:, keys[j]], (raised[j] * scale).astype(BF), 1, 0)
    rows = out_ref.shape[2]
    for k in range(tile // rows):
        out_ref[step * (tile // rows) + k] = result[:, k * rows : (k + 1) * rows].astype(BF)
    wide_ref[:, here] = result
    lse_ref[:, here] = top + jnp.log(total)

    @pl.when(step == min(1, steps - 1))
    def _():
        for copy in swap:
            copy.wait_recv()
        for q in range(1, min(early, 3)):
            ring.start(q)

    @pl.when(step == steps - 1)
    def _():
        columns.across()
        for q in range(3, early):
            ring.start(q)
        ring.finish()
        for copy in swap:
            copy.wait_send()
        kept.wait()
        columns.finish()


def attend(x, w, cosine, sine, marks, attn_half, mlp, lines, groups, reach, rows, tile):
    count, width = x.shape
    ring, shard, _ = attn_half.shape
    sub = lines // ring
    early = ring - 1
    return pl.pallas_call(
        functools.partial(attend_kernel, groups, reach, lines, tile),
        grid=(count // tile,),
        in_specs=[
            VMEM,
            VMEM,
            VMEM,
            VMEM,
            VMEM,
            ANY,
            ANY,
        ],
        out_specs=[
            VMEM,
            VMEM,
            VMEM,
            VMEM,
            ANY,
            ANY,
            ANY,
        ],
        out_shape=[
            jax.ShapeDtypeStruct((count // rows, HD, rows), BF),
            jax.ShapeDtypeStruct((HD, count), F32),
            jax.ShapeDtypeStruct((1, count), F32),
            jax.ShapeDtypeStruct((V_END, count), BF),
            jax.ShapeDtypeStruct((ring, sub, shard, width), BF),
            jax.ShapeDtypeStruct(mlp.shape, BF),
            jax.ShapeDtypeStruct((2, early, *mlp.shape[1:]), BF),
        ],
        scratch_shapes=[DMA((2, early)), DMA((2, early)), DMA, DMA, DMA, *Columns.scratch(sub)],
        compiler_params=pltpu.CompilerParams(
            collective_id=5, has_side_effects=True, vmem_limit_bytes=20 << 20
        ),
        cost_estimate=pl.CostEstimate(
            flops=count * count * HD * 8, bytes_accessed=count * 4096, transcendentals=count * count
        ),
        name="attend",
    )(x, w, cosine, sine, marks, attn_half, mlp)


def middle_kernel(
    groups,
    reach,
    lines,
    outgoing,
    tokens,
    d_out,
    w_attn,
    gains,
    mlp_pair,
    mlp_near,
    mlp_all,
    upstream_all,
    middle,
    attended,
    mlp_weights,
    land,
    mine,
    a2a_send,
    a2a_recv,
    own,
    ring_send,
    ring_recv,
    ring_own,
    land_own,
    *tree_sems,
):
    place = Place(groups, reach)
    group = groups * reach
    early, count = mlp_near.shape[1], mlp_weights.shape[0]
    sub = lines // count
    spot, side = place.ctx // sub, place.ctx % sub

    def slot(d, q, ahead):
        block = (spot + (q // 2 + ahead if d else count - q // 2 - ahead)) % count
        return mlp_weights.at[block, ring_half(sub, side, q % 2)]

    rest = range(early, 2 * (count - 1))
    ring = Line(
        count,
        sub,
        early,
        [[mlp_near.at[d, q - 2] if q - 2 < early else slot(d, q, 0) for q in rest] for d in range(2)],
        [[slot(d, q, 0) for q in rest] for d in range(2)],
        ring_send,
        ring_recv,
    )
    local = [pltpu.make_async_copy(mlp_pair, mlp_weights.at[spot], ring_own.at[0])]
    near = []
    for d in range(2):
        for q in range(early):
            copy = pltpu.make_async_copy(
                mlp_near.at[d, q], slot(d, q, 1), ring_own.at[1 + d * early + q]
            )
            there = spot + q // 2 + 1 < count if d else spot > q // 2
            near.append((there, copy))
    meet(everyone(place, lines))
    copies = spread(place, outgoing, land, (a2a_send, a2a_recv, own))
    ring.start(0)
    ring.start(1)
    up = Tree(place, 2, d_out, upstream_all, tree_sems[5:10])
    up.start()
    for copy in local:
        copy.start()
    for there, copy in near:
        pl.when(there)(copy.start)
    for copy in copies:
        copy.wait()
    collect = Collect(groups, [(land, lambda h: attended.at[h])], *tree_sems[10:])
    local.append(pltpu.make_async_copy(land, attended.at[place.head], land_own))
    local[-1].start()
    value = tokens[...].astype(F32) + dot(
        land[...].reshape(group * HD, tokens.shape[0]), w_attn[...], 0, 0
    )
    middle[...] = value
    normed, _ = norm_parts(value)
    mine[...] = (normed * gains[1:2, :]).astype(BF)
    tree = Tree(place, 2, mine, mlp_all, tree_sems[:5])
    tree.start()
    up.forward(1)
    for q in range(2, len(rest)):
        ring.start(q)
    tree.forward(1)
    collect.start(0)
    up.forward(2)
    tree.forward(2)
    collect.forward(0)
    up.finish()
    tree.finish()
    collect.finish()
    for copy in local:
        copy.wait()
    for there, copy in near:
        pl.when(there)(copy.wait)
    ring.finish()


def middle_step(outgoing, tokens, d_out, w_attn, gains, mlp_pair, mlp_near, lines, groups, reach):
    rows, width = tokens.shape
    group = groups * reach
    early, sub = mlp_near.shape[1], 8 // groups
    ring = lines // sub
    left = 2 * (ring - 1) - early
    return pl.pallas_call(
        functools.partial(middle_kernel, groups, reach, lines),
        in_specs=[ANY, VMEM, ANY, VMEM, VMEM, ANY, ANY],
        out_specs=[ANY, ANY, VMEM, ANY, ANY],
        out_shape=[
            jax.ShapeDtypeStruct((8, rows, width), BF),
            jax.ShapeDtypeStruct((8, rows, width), BF),
            jax.ShapeDtypeStruct((rows, width), F32),
            jax.ShapeDtypeStruct((groups, group, HD, rows), BF),
            jax.ShapeDtypeStruct((ring, *mlp_pair.shape), BF),
        ],
        scratch_shapes=[
            pltpu.VMEM((group, HD, rows), BF),
            pltpu.VMEM((rows, width), BF),
            DMA((group - 1,)),
            DMA((group - 1,)),
            DMA,
            DMA((2, left)),
            DMA((2, left)),
            DMA((2 * early + 1,)),
            DMA,
            *Tree.scratch(2),
            *Tree.scratch(2),
            *Collect.scratch(1, groups),
        ],
        compiler_params=pltpu.CompilerParams(
            collective_id=1, has_side_effects=True, vmem_limit_bytes=12 << 20
        ),
        cost_estimate=pl.CostEstimate(flops=1 << 28, bytes_accessed=12 << 20, transcendentals=0),
        name="middle_step",
    )(outgoing, tokens, d_out, w_attn, gains, mlp_pair, mlp_near)


class Sum:
    def __init__(self, place, terms, first, held, stage, land, send, recv):
        self.terms, self.first, self.stage, self.land = terms, first, stage, land
        self.half = stage.shape[2]
        length = terms.shape[0] // (2 * self.half)
        lines_sub = 8 // place.groups
        spot, side = place.ctx // lines_sub, place.ctx % lines_sub
        self.length, self.spot = length, spot
        self.held = lambda d, q: land.at[d, q] if q >= 0 else held.at[d, q + 2]
        beside = [
            {"ctx": (spot + 1) % length * lines_sub + side},
            {"ctx": (spot + length - 1) % length * lines_sub + side},
        ]
        self.copies = [
            [
                remote(stage.at[d, q], land.at[d, q], beside[d], send.at[d, q], recv.at[d, q])
                for q in range(stage.shape[1])
            ]
            for d in range(2)
        ]

    @staticmethod
    def scratch(count, half):
        return [
            pltpu.VMEM((2, count, *half), BF),
            pltpu.VMEM((2, count, *half), BF),
            DMA((2, count)),
            DMA((2, count)),
        ]

    def sends(self, d, q):
        s, spot, last = (q + self.first) // 2, self.spot, self.length - 1
        if d:
            return jnp.logical_and(spot >= last - s, spot > 0)
        return jnp.logical_and(spot <= s, spot < last)

    def receives(self, d, q):
        s, spot, last = (q + self.first) // 2, self.spot, self.length - 1
        if d:
            return jnp.logical_and(spot >= last - 1 - s, spot < last)
        return jnp.logical_and(spot <= s + 1, spot > 0)

    def clear(self):
        for d in range(2):
            for q in range(len(self.copies[d])):

                @pl.when(jnp.logical_not(self.receives(d, q)))
                def _():
                    self.land[d, q] = jnp.zeros(self.land.shape[2:], BF)

    def block(self, at, k):
        return self.terms[pl.ds(pl.multiple_of((2 * at + k) * self.half, 16), self.half), :]

    def arrive(self, q):
        for d in range(2):
            pl.when(self.receives(d, q))(self.copies[d][q].wait_recv)

    def start(self, q):
        if q >= 2:
            self.arrive(q - 2)
        step, k = (q + self.first) // 2, (q + self.first) % 2
        for d in range(2):
            at = self.spot + (step + 1 if d else self.length - 1 - step)

            @pl.when(self.sends(d, q))
            def _():
                value = self.block(at % self.length, k)
                if q + self.first >= 2:
                    value = (value.astype(F32) + self.held(d, q - 2)[...].astype(F32)).astype(BF)
                self.stage[d, q] = value
                self.copies[d][q].start()

    def finish(self):
        count = len(self.copies[0])
        for q in range(max(count - 2, 0), count):
            self.arrive(q)
        for d in range(2):
            for q, copy in enumerate(self.copies[d]):
                pl.when(self.sends(d, q))(copy.wait_send)


def mlp_rows(chunk, x_ref, up_ref, w_ref, back_ref, forward_ref, kept):
    count = x_ref.shape[0]
    rows = back_ref.shape[2]

    @pl.loop(0, count // chunk)
    def _(i):
        at = pl.ds(pl.multiple_of(i * chunk, chunk), chunk)
        gate_up = dot(x_ref[at, :], w_ref[:, : 2 * SLICE], 1, 0)
        left, right = gate_up[:, :SLICE], gate_up[:, SLICE:]
        grad_mixed = dot(up_ref[at, :], w_ref[:, 2 * SLICE :], 1, 0)
        normal_cdf = 0.5 * (1.0 + lax.erf(left * 0.7071067811865476))
        gelu = left * normal_cdf
        density = jnp.exp(-0.5 * left * left) * 0.3989422804014327
        kept[at, :SLICE] = (grad_mixed * right * (normal_cdf + left * density)).astype(BF)
        kept[at, SLICE : 2 * SLICE] = (grad_mixed * gelu).astype(BF)
        kept[at, 2 * SLICE :] = (gelu * right).astype(BF)
        back = dot(kept[at, : 2 * SLICE], w_ref[:, : 2 * SLICE], 1, 1).astype(BF)
        forward = dot(kept[at, 2 * SLICE :], w_ref[:, 2 * SLICE :], 1, 1).astype(BF)
        pairs = chunk // rows // 2
        for j in range(chunk // rows):
            piece = slice(j * rows, (j + 1) * rows)
            back_ref[i * pairs + j // 2, j % 2] = back[piece]
            forward_ref[i * pairs + j // 2, j % 2] = forward[piece]


def mlp_weights_back(chunk, x_ref, up_ref, kept, terms_ref):
    @pl.loop(0, x_ref.shape[1] // chunk)
    def _(i):
        at = pl.ds(pl.multiple_of(i * chunk, chunk), chunk)
        terms_ref[at, : 2 * SLICE] = dot(x_ref[:, at], kept[:, : 2 * SLICE], 0, 0).astype(BF)
        terms_ref[at, 2 * SLICE :] = dot(up_ref[:, at], kept[:, 2 * SLICE :], 0, 0).astype(BF)


def turn_kernel(
    groups,
    reach,
    lines,
    x,
    up,
    mlp_weights,
    middle,
    d_out,
    w_attn,
    gains,
    attended,
    grads,
    grad_middle,
    attn_part,
    carry,
    forward,
    terms,
    kept,
    partial,
    columns,
    total,
    outgoing,
    branch,
    a2a_send,
    a2a_recv,
    own,
    side_send,
    side_recv,
    side_own,
    *rest,
):
    place = Place(groups, reach)
    group = groups * reach
    lanes = branch.shape[2]
    sums = Sum(place, terms, 0, None, *rest[7:])
    count = rest[7].shape[1]
    devices = everyone(place, lines)
    sums.clear()
    greet(devices)
    mlp_rows(512, x, up, mlp_weights, partial, forward, kept)
    pl.semaphore_wait(pltpu.get_barrier_semaphore(), len(devices))
    halving = Halving(place, 2, partial, total, rest[:7])
    halving.start()
    mlp_weights_back(512, x, up, kept, terms)
    sums.start(0)
    sums.start(1)
    halving.pair()
    halving.halve(0)
    halving.halve(1)
    for q in range(2, count):
        sums.start(q)
    halving.finish()
    normed, inverse_std = norm_parts(middle[...])
    upstream = total[...]
    grad = d_out[...].astype(F32) + norm_back(upstream, normed, inverse_std, gains[1:2, :])
    grad_middle[...] = grad
    low = grad.astype(BF)
    for g in range(groups):
        branch[g] = low[:, g * lanes : (g + 1) * lanes]
    outgoing[...] = dot(w_attn[...], low, 1, 1).astype(BF).reshape(outgoing.shape)
    copies = spread(place, outgoing, grads, (a2a_send, a2a_recv, own))
    for step in range(1, groups):
        peer = (place.head + step) % groups
        copies.append(
            push(
                branch.at[peer],
                columns.at[place.head],
                {"heads": peer},
                side_send.at[step - 1],
                side_recv.at[step - 1],
            )
        )
    local = pltpu.make_async_copy(branch.at[place.head], columns.at[place.head], side_own)
    local.start()
    for copy in copies[-(groups - 1) :]:
        copy.wait()
    local.wait()
    attn_part[...] = functools.reduce(
        jnp.add, [dot(attended[g], columns[g], 1, 0) for g in range(groups)]
    ).astype(BF)
    for copy in copies[: -(groups - 1)]:
        copy.wait()
    sums.finish()
    for d in range(2):
        for q in range(2):
            carry[d, q] = sums.land[d, count - 2 + q]


def turn_step(x, up, mlp_weights, middle, d_out, w_attn, gains, attended, lines, groups, reach):
    rows, width = middle.shape
    count = lines * groups // 8 - 1
    half = (width // (2 * (count + 1)), 3 * SLICE)
    group = groups * reach
    return pl.pallas_call(
        functools.partial(turn_kernel, groups, reach, lines),
        in_specs=[VMEM] * 8,
        out_specs=[ANY, VMEM, VMEM, VMEM, VMEM, VMEM],
        out_shape=[
            jax.ShapeDtypeStruct((group, HD, rows), BF),
            jax.ShapeDtypeStruct((rows, width), F32),
            jax.ShapeDtypeStruct((width, width // groups), BF),
            jax.ShapeDtypeStruct((2, 2, *half), BF),
            jax.ShapeDtypeStruct((4, 2, rows, width), BF),
            jax.ShapeDtypeStruct((width, 3 * SLICE), BF),
        ],
        scratch_shapes=[
            pltpu.VMEM((8 * rows, 3 * SLICE), BF),
            pltpu.VMEM((4, 2, rows, width), BF),
            pltpu.VMEM((groups, rows, width // groups), BF),
            pltpu.VMEM((rows, width), F32),
            pltpu.VMEM((group, HD, rows), BF),
            pltpu.VMEM((groups, rows, width // groups), BF),
            DMA((group - 1,)),
            DMA((group - 1,)),
            DMA,
            DMA((groups - 1,)),
            DMA((groups - 1,)),
            DMA,
            *Halving.scratch(2, rows, width),
            *Sum.scratch(count, half),
        ],
        compiler_params=pltpu.CompilerParams(
            collective_id=2, has_side_effects=True, vmem_limit_bytes=24 << 20
        ),
        cost_estimate=pl.CostEstimate(flops=1 << 33, bytes_accessed=12 << 20, transcendentals=0),
        name="turn_step",
    )(x, up, mlp_weights, middle, d_out, w_attn, gains, attended)


def end_part(
    place,
    lines,
    partial,
    weight,
    mlp,
    attn,
    total,
    mlp_all,
    weight_all,
    attn_all,
    sum_line,
    sum_attn,
    lined,
    summed,
    swap_send,
    swap_recv,
    own,
    *rest,
):
    groups, reach = place.groups, place.reach
    sub = mlp.shape[0]
    mine, head = place.ctx % sub, place.head
    wide = Halving(place, 3, partial, total, rest[:7], [2, 1])
    swap = Lines(lines, weight, lined, *rest[7:10])
    wide.start()
    swap.start()
    wide.pair()
    sum_line()
    swaps = []
    for step in range(1, sub):
        peer = (mine + step) % sub
        swaps.append(
            push(
                mlp.at[peer],
                mlp_all.at[mine, head],
                {"ctx": place.ctx - mine + peer},
                swap_send.at[step - 1],
                swap_recv.at[step - 1],
            )
        )
    pieces = [(mlp.at[mine], lambda h: mlp_all.at[mine, h]), (attn, lambda h: attn_all.at[h])]
    for step in range(1, sub):
        source = (mine - step + sub) % sub
        pieces.append(
            (mlp_all.at[source, head], lambda h, source=source: mlp_all.at[source, h])
        )
    pieces.append((summed, lambda h: weight_all.at[h]))
    collect = Collect(groups, pieces, *rest[10:14])
    local = [
        pltpu.make_async_copy(mlp.at[mine], mlp_all.at[mine, head], own.at[0]),
        pltpu.make_async_copy(attn, attn_all.at[head], own.at[1]),
        pltpu.make_async_copy(summed, weight_all.at[head], own.at[2]),
    ]
    local[0].start()
    collect.start(0)
    sum_attn()
    local[1].start()
    collect.start(1)
    for step in range(1, sub):
        swaps[step - 1].wait_recv()
        collect.start(step + 1)
    wide.halve(0)
    swap.finish()
    for r in range(reach):
        summed[r] = functools.reduce(
            jnp.add, [lined[r + reach * g].astype(F32) for g in range(lines // reach)]
        ).astype(BF)
    local[2].start()
    collect.start(sub + 1)
    wide.halve(1)
    collect.forward(0)
    collect.forward(1)
    wide.halve(2)
    for n in range(2, sub + 2):
        collect.forward(n)
    for copy in local:
        copy.wait()
    for copy in swaps:
        copy.wait_send()
    collect.finish()
    wide.finish()


def attend_back_kernel(
    groups,
    reach,
    lines,
    tile,
    qkv_ref,
    grad_ref,
    wide_ref,
    lse_ref,
    x_ref,
    w_ref,
    cos_ref,
    sin_ref,
    forward_ref,
    terms,
    carry,
    attn_ref,
    ahead_ref,
    total,
    mlp_all,
    weight_all,
    attn_all,
    out_ref,
    weight_ref,
    attn_out_ref,
    mlp_ref,
    sums,
    queries,
    weight,
    attn_land,
    *sems,
):
    count = x_ref.shape[0]
    rows = grad_ref.shape[2]
    steps, per_tile = count // tile, tile // rows
    step = pl.program_id(0)
    place = Place(groups, reach)
    halving = Halving(place, 2, forward_ref, ahead_ref, sems[:7])
    swap = Lines(lines, attn_ref, attn_land, *sems[7:10])
    length = lines * groups // 8
    line = Sum(place, terms, length - 1, carry, *sems[10:14])

    @pl.when(step == 0)
    def _():
        line.clear()
        meet(everyone(place, lines))
        line.start(0)
        line.start(1)
        halving.start()
        swap.start()
        sums[...] = jnp.zeros_like(sums)

    here = pl.ds(pl.multiple_of(step * tile, tile), tile)
    query = qkv_ref[:QM_END, here]
    grad = jnp.concatenate([grad_ref[step * per_tile + k] for k in range(per_tile)], axis=1)
    delta = jnp.sum(grad.astype(F32) * wide_ref[:, here], axis=0, keepdims=True)
    lse = lse_ref[:, here]
    grad_query = jnp.zeros((HD, tile), F32)
    for j in range(steps):
        keys = slice(j * tile, (j + 1) * tile)
        prob = jnp.exp(dot(qkv_ref[QM_END:KM_END, keys], query, 0, 0) - lse)
        grad_prob = dot(qkv_ref[KM_END:, keys], grad, 0, 0)
        grad_score = (prob * (grad_prob - delta)).astype(BF)
        grad_query += dot(qkv_ref[QM_END:K_END, keys], grad_score, 1, 0)
        sums[:HD, keys] += dot(query[:HD], grad_score, 1, 1)
        sums[HD:, keys] += dot(grad, prob.astype(BF), 1, 1)
    queries[:, here] = (grad_query * 0.125).astype(BF)

    pl.when(step == 0)(halving.pair)

    @pl.when(step == min(2, steps - 1))
    def _():
        halving.halve(0)
        for q in range(2, length - 1):
            line.start(q)


    @pl.when(step == steps - 1)
    def _():
        weight[...] = jnp.zeros_like(weight)

        @pl.loop(0, steps)
        def _(i):
            at = pl.ds(pl.multiple_of(i * tile, tile), tile)
            cosine, sine = cos_ref[:, at], sin_ref[:, at]

            def turn_back(value):
                front, back = value[:HALF], value[HALF:]
                return [front * cosine + back * sine, back * cosine - front * sine]

            low = lambda value: value.astype(BF).astype(F32)
            projected = jnp.concatenate(
                [
                    *turn_back(queries[:, at].astype(F32)),
                    *turn_back(low(sums[:HD, at])),
                    low(sums[HD:, at]),
                ],
                axis=0,
            ).astype(BF)
            part = dot(projected, w_ref[...], 0, 1).astype(BF)
            for k in range(per_tile):
                out_ref[(i * per_tile + k) // 2, k % 2] = part[k * rows : (k + 1) * rows]
            weight[...] += dot(projected, x_ref[at, :], 1, 0)

        shard = weight_ref.shape[2]
        for c in range(lines):
            weight_ref[c] = weight[:, c * shard : (c + 1) * shard].astype(BF)
        halving.halve(1)
        half = line.half

        def sum_line():
            line.finish()
            for k in range(2):
                q = length - 3 + k
                value = (
                    line.block(line.spot, k).astype(F32)
                    + line.land[0, q].astype(F32)
                    + line.land[1, q].astype(F32)
                ).astype(BF)
                if mlp_ref.shape[0] == 2:
                    mlp_ref[k] = value
                else:
                    mlp_ref[0, k * half : (k + 1) * half] = value

        def sum_attn():
            swap.finish()
            attn_out_ref[...] = functools.reduce(
                jnp.add, [attn_land[c].astype(F32) for c in range(lines)]
            ).astype(BF)

        end_part(
            place,
            lines,
            out_ref,
            weight_ref,
            mlp_ref,
            attn_out_ref,
            total,
            mlp_all,
            weight_all,
            attn_all,
            sum_line,
            sum_attn,
            *sems[14:],
        )
        halving.finish()


def attend_back(qkv, grad, wide, lse, x, w, cosine, sine, forward, terms, carry, attn, groups, reach, tile):
    count, width = x.shape
    blocks, _, rows = grad.shape
    lines, shard, lanes = attn.shape
    sub = 8 // groups
    length = lines // sub
    operands = (qkv, grad, wide, lse, x, w, cosine, sine, forward, terms, carry)
    return pl.pallas_call(
        functools.partial(attend_back_kernel, groups, reach, lines, tile),
        grid=(count // tile,),
        in_specs=[*[VMEM] * len(operands), ANY],
        out_specs=[VMEM, VMEM, ANY, ANY, ANY],
        out_shape=[
            jax.ShapeDtypeStruct((rows, width), F32),
            jax.ShapeDtypeStruct((rows, width), F32),
            jax.ShapeDtypeStruct((sub, groups, shard, 3 * SLICE), BF),
            jax.ShapeDtypeStruct((groups, reach, 3 * HD, shard), BF),
            jax.ShapeDtypeStruct((groups, shard, lanes), BF),
        ],
        scratch_shapes=[
            pltpu.VMEM((blocks // 2, 2, rows, width), BF),
            pltpu.VMEM((lines, 3 * HD, shard), BF),
            pltpu.VMEM((shard, lanes), BF),
            pltpu.VMEM((sub, shard, 3 * SLICE), BF),
            pltpu.VMEM((2 * HD, count), F32),
            pltpu.VMEM((HD, count), BF),
            pltpu.VMEM((3 * HD, width), F32),
            pltpu.VMEM((lines, shard, lanes), BF),
            *Halving.scratch(2, rows, width),
            *Lines.scratch(lines),
            *Sum.scratch(length - 1, (width // (2 * length), 3 * SLICE)),
            pltpu.VMEM((lines, 3 * HD, shard), BF),
            pltpu.VMEM((reach, 3 * HD, shard), BF),
            DMA((max(sub - 1, 1),)),
            DMA((max(sub - 1, 1),)),
            DMA((3,)),
            *Halving.scratch(3, rows, width),
            *Lines.scratch(lines),
            *Collect.scratch(sub + 2, groups),
        ],
        compiler_params=pltpu.CompilerParams(
            collective_id=4, has_side_effects=True, vmem_limit_bytes=36 << 20
        ),
        cost_estimate=pl.CostEstimate(
            flops=count * count * HD * 20, bytes_accessed=count * 6144, transcendentals=count * count
        ),
        name="attend_back",
    )(*operands, attn)


class Collect:
    def __init__(self, groups, pieces, far_send, far_recv, near_send, near_recv):
        head = lax.axis_index("heads")
        self.half = half = groups // 2
        pair = {"heads": flip(head, 1)}
        self.far, self.near = [], []
        for n, (piece, where) in enumerate(pieces):
            self.far.append(
                [
                    remote(
                        piece,
                        where(head),
                        {"heads": (head + 2 * k) % groups},
                        far_send.at[n, k - 1],
                        far_recv.at[n, k - 1],
                    )
                    for k in range(1, half)
                ]
            )
            sides = [(piece, where(head))]
            for k in range(1, half):
                got = where((head - 2 * k + groups) % groups)
                sides.append((got, got))
            self.near.append(
                [
                    remote(source, target, pair, near_send.at[n, k], near_recv.at[n, k])
                    for k, (source, target) in enumerate(sides)
                ]
            )

    @staticmethod
    def scratch(count, groups):
        far, near = (count, max(groups // 2 - 1, 1)), (count, groups // 2)
        return [DMA(far), DMA(far), DMA(near), DMA(near)]

    def start(self, n):
        for copy in self.far[n]:
            copy.start()
        self.near[n][0].start()

    def forward(self, n):
        for k, copy in enumerate(self.far[n]):
            copy.wait_recv()
            self.near[n][k + 1].start()

    def finish(self):
        for copies in self.far:
            for copy in copies:
                copy.wait_send()
        for copies in self.near:
            for copy in copies:
                copy.wait()


def assemble_kernel(
    upstream,
    tokens,
    grad_middle,
    gains,
    middle,
    ahead,
    weight_all,
    attn_all,
    mlp_all,
    w_qkv,
    w_in,
    own_gains,
    result,
    grad,
    sum_qkv,
    sum_attn,
    sum_in,
    sum_out,
    gain_sums,
):
    groups, reach, _, shard = weight_all.shape
    lanes = attn_all.shape[2]
    result[...] = (middle[...] + ahead[...]).astype(BF)
    normed, inverse_std = norm_parts(tokens[...].astype(F32))
    grad[...] = grad_middle[...] + norm_back(upstream[...], normed, inverse_std, gains[0:1, :])
    for g in range(groups):
        sum_attn[:, g * lanes : (g + 1) * lanes] = attn_all[g].astype(F32)
    gain_one = jnp.zeros((shard, 128), F32)
    for third in range(3):
        part = slice(third * HD, (third + 1) * HD)
        for pair in range(H // 2):
            r, g = 2 * pair // groups, 2 * pair % groups
            tile = (
                jnp.concatenate([weight_all[g, r, part], weight_all[g + 1, r, part]], axis=0)
                .astype(F32)
                .T
            )
            at = third * H * HD + pair * 2 * HD
            sum_qkv[:, at : at + 2 * HD] = tile
            gain_one += tile * w_qkv[:, at : at + 2 * HD].astype(F32)
    gain_two = jnp.zeros((shard, 1), F32)
    for t in range(8):
        start, wide = slice_place(t)
        for half in range(2):
            piece = mlp_all[t, :, half * SLICE : half * SLICE + wide].astype(F32)
            at = half * FF + start
            sum_in[:, at : at + wide] = piece
            gain_two += jnp.sum(
                piece * w_in[:, at : at + wide].astype(F32), axis=1, keepdims=True
            )
        sum_out[start : start + wide, :] = (
            mlp_all[t, :, 2 * SLICE : 3 * SLICE].astype(F32).T[:wide]
        )
    one = jnp.sum(gain_one, axis=1, keepdims=True)
    lane = lax.broadcasted_iota(jnp.int32, (shard, 128), 1)
    both = jnp.where(lane == 0, one, gain_two).T
    gain_sums[...] = both[:8] / own_gains[...]


def assemble(upstream, tokens, grad_middle, gains, middle, ahead, weight_all, attn_all, mlp_all, w_qkv, w_in, own_gains):
    rows, width = tokens.shape
    shard = w_qkv.shape[0]
    return pl.pallas_call(
        assemble_kernel,
        in_specs=[VMEM] * 12,
        out_specs=[VMEM] * 7,
        out_shape=[
            jax.ShapeDtypeStruct((rows, width), BF),
            jax.ShapeDtypeStruct((rows, width), F32),
            jax.ShapeDtypeStruct((shard, 3 * width), F32),
            jax.ShapeDtypeStruct((shard, width), F32),
            jax.ShapeDtypeStruct((shard, 2 * FF), F32),
            jax.ShapeDtypeStruct((FF, shard), F32),
            jax.ShapeDtypeStruct((8, shard), F32),
        ],
        compiler_params=pltpu.CompilerParams(vmem_limit_bytes=20 << 20),
        cost_estimate=pl.CostEstimate(flops=1 << 24, bytes_accessed=20 << 20, transcendentals=0),
        name="assemble",
    )(upstream, tokens, grad_middle, gains, middle, ahead, weight_all, attn_all, mlp_all, w_qkv, w_in, own_gains)


def slice_start(t):
    return 128 * jnp.minimum(3 * t, 2 * t + 5)


def slice_place(t):
    start = 128 * min(3 * t, 2 * t + 5)
    return start, min(128 * min(3 * t + 3, 2 * t + 7), FF) - start


def body(count, tokens, d_out, segment_ids, position_ids, w_qkv, w_attn, w_in, w_out, gain_attn, gain_mlp):
    groups = lax.axis_size("heads")
    rows, width = tokens.shape
    shard = w_qkv.shape[0]
    reach = SEQ_MAX // (rows * groups)
    group = reach * groups
    sub = 8 // groups
    ctx, head = lax.axis_index("ctx"), lax.axis_index("heads")
    assert group == H and sub * groups == 8
    total = group * rows
    tile = 512

    def mlp_slice(value, axis, start, t):
        pads = [(0, 0), (0, 0)]
        pads[axis] = (0, SLICE)
        piece = lax.dynamic_slice_in_dim(jnp.pad(value, pads), start + slice_start(t), SLICE, axis)
        wide = jnp.minimum(slice_start(t + 1), FF) - slice_start(t)
        shape = [1, 1]
        shape[axis] = SLICE
        return jnp.where(jnp.arange(SLICE).reshape(shape) < wide, piece, jnp.zeros_like(piece))

    def mlp_part(t):
        return jnp.concatenate(
            [mlp_slice(w_in, 1, 0, t), mlp_slice(w_in, 1, FF, t), mlp_slice(w_out, 0, 0, t).T], axis=1
        )

    mlp = jnp.stack([mlp_part(x * groups + head) for x in range(sub)])
    gains_own = jnp.pad(jnp.stack([gain_attn, gain_mlp]).astype(F32), ((0, 6), (0, -shard % 128)))
    ids = jnp.pad(jnp.stack([position_ids, segment_ids]), ((0, 6), (0, 0)))
    freqs = jnp.power(160000.0, -(2.0 * jnp.arange(HALF, dtype=F32)) / HD)[:, None]
    input_all, gains, w_head, cosine, sine, marks, attn_half = begin(
        tokens, gains_own, ids, w_qkv, w_attn, freqs, count // sub, count, groups, reach
    )
    x = input_all.reshape(total, width)

    attended, wide, lse, qkv, attn_weights, mlp_pair, mlp_near = attend(
        x,
        w_head,
        cosine,
        sine,
        marks,
        attn_half,
        mlp.reshape(2, sub * shard // 2, 3 * SLICE),
        count,
        groups,
        reach,
        rows,
        tile,
    )
    attn_weights = attn_weights.reshape(width, width)
    mlp_all, upstream, middle, attended, mlp_weights = middle_step(
        attended, tokens, d_out, attn_weights, gains, mlp_pair, mlp_near, count, groups, reach
    )
    mlp_weights = mlp_weights.reshape(width, 3 * SLICE)
    grad_heads, grad_middle, attn_part, carry, forward, mlp_terms = turn_step(
        mlp_all.reshape(8 * rows, width),
        upstream.reshape(8 * rows, width),
        mlp_weights,
        middle,
        d_out,
        attn_weights,
        gains,
        attended.reshape(groups, width, rows),
        count,
        groups,
        reach,
    )
    attn_part = attn_part.reshape(count, shard, width // groups)
    ahead, upstream_in, mlp_all, weight_all, attn_all = attend_back(
        qkv,
        grad_heads,
        wide,
        lse,
        x,
        w_head,
        cosine,
        sine,
        forward,
        mlp_terms,
        carry,
        attn_part,
        groups,
        reach,
        tile,
    )
    result, grad_input, sum_qkv, sum_attn, sum_in, sum_out, gain_sums = assemble(
        upstream_in,
        tokens,
        grad_middle,
        gains,
        middle,
        ahead,
        weight_all,
        attn_all,
        mlp_all.reshape(8, shard, 3 * SLICE),
        w_qkv,
        w_in,
        jnp.pad(gains_own[:2, :shard], ((0, 6), (0, 0)), constant_values=1.0),
    )
    return (
        result,
        grad_input,
        sum_qkv,
        sum_attn,
        sum_in,
        sum_out,
        gain_sums[0],
        gain_sums[1],
    )


def solution(mesh):
    return jax.shard_map(
        functools.partial(body, mesh.shape["ctx"]),
        mesh=mesh,
        in_specs=(
            P(("ctx", "heads"), None),
            P(("ctx", "heads"), None),
            P(("ctx", "heads")),
            P(("ctx", "heads")),
            P("ctx", None),
            P("ctx", None),
            P("ctx", None),
            P(None, "ctx"),
            P("ctx"),
            P("ctx"),
        ),
        out_specs=(
            P(("ctx", "heads"), None),
            P(("ctx", "heads"), None),
            P("ctx", None),
            P("ctx", None),
            P("ctx", None),
            P(None, "ctx"),
            P("ctx"),
            P("ctx"),
        ),
        check_vma=False,
    )
```
